128 devices in a mesh: slot: 2 (over x_lo), ctx: 32 (over y, x_hi, z), wsh: 2 (over core).
Axes of the slice: x: 4 (x_hi: 2, x_lo: 2; x = x_hi * 2 + x_lo), y: 4, z: 4, core: 2. Of those that a mesh axis runs over, the one named last changes fastest.
Arguments:
- tokens: bfloat16 [4, 4096, 1024], P(('slot', 'wsh'), 'ctx'), may hold values from -6 to 6
- lengths: int32 [4], P(('slot', 'wsh')), may hold values from 1 to 4096, 12288 in all
- ln_gain: float32 [1024], P(('slot', 'ctx', 'wsh')), may hold values from 0.5 to 1.5
- ln_bias: float32 [1024], P(('slot', 'ctx', 'wsh')), may hold values from -2 to 2
- w_qkv: float32 [1024, 3072], P(('slot', 'ctx', 'wsh')), may hold values from -0.1875 to 0.1875
- b_qkv: float32 [3072], P(('slot', 'ctx', 'wsh')), may hold values from -0.3 to 0.3
- w_out: float32 [1024, 1024], P(('slot', 'ctx', 'wsh')), may hold values from -3 to 3
- b_out: float32 [1024], P(('slot', 'ctx', 'wsh')), may hold values from -3 to 3
- w_fc1: float32 [1024, 4096], P(('slot', 'ctx', 'wsh')), may hold values from -0.1875 to 0.1875
- b_fc1: float32 [4096], P(('slot', 'ctx', 'wsh')), may hold values from -3 to 3
- w_fc2: float32 [4096, 1024], P(('slot', 'ctx', 'wsh')), may hold values from -0.09375 to 0.09375
- b_fc2: float32 [1024], P(('slot', 'ctx', 'wsh')), may hold values from -3 to 3
- cotangent: bfloat16 [4, 4096, 1024], P(('slot', 'wsh'), 'ctx'), may hold values from -6 to 6
Outputs:
- output: bfloat16 [4, 4096, 1024], P(('slot', 'wsh'), 'ctx')
- token_grad: bfloat16 [4, 4096, 1024], P(('slot', 'wsh'), 'ctx')
- ln_gain_grad: float32 [1024], P(('slot', 'ctx', 'wsh'))
- ln_bias_grad: float32 [1024], P(('slot', 'ctx', 'wsh'))
- w_qkv_grad: float32 [1024, 3072], P(('slot', 'ctx', 'wsh'))
- b_qkv_grad: float32 [2048], P(('slot', 'ctx', 'wsh'))
- b_v_grad: float32 [1024], P(('slot', 'ctx', 'wsh'))
- w_out_grad: float32 [1024, 1024], P(('slot', 'ctx', 'wsh'))
- b_out_grad: float32 [1024], P(('slot', 'ctx', 'wsh'))
- w_fc1_grad: float32 [1024, 4096], P(('slot', 'ctx', 'wsh'))
- b_fc1_grad: float32 [4096], P(('slot', 'ctx', 'wsh'))
- w_fc2_grad: float32 [4096, 1024], P(('slot', 'ctx', 'wsh'))
- b_fc2_grad: float32 [1024], P(('slot', 'ctx', 'wsh'))
The draws below stay inside these ranges and needn't reach their ends.
Inputs may be any that keep to these rules, and one draw needn't show every extreme that they name: The 4 lengths add up to 12288; the longest is exactly 4096.
All inputs are finite; a program needn't handle non-finite values. No bound on the sum of `lengths` on one device may be relied on, other than what follows from the above.
Results may differ from the reference program's by a relative error of at most 0.024.
Values may be sent and summed in bfloat16 or wider, within the bound.
A program may use at most 192 MiB of HBM per device.

```python
import math
import jax
import jax.numpy as jnp
import numpy as np
from jax import lax

D = 1024
HEADS = 16
HD = 64
ROT = 16
FF = 4096
HQ = 1024
SEQ = 4096
SLOTS = 4


def steps_of(key, dims, split, low, high):
    factor_of, own = 1.0, jax.random.fold_in(key, 6)
    for dim, shards_of in split:
        steps = jnp.exp(jax.random.uniform(jax.random.fold_in(own, dim), (shards_of,), jnp.float32, low / len(split), high / len(split)))
        factor_of = factor_of * jnp.repeat(steps, dims[dim] // shards_of).reshape([-1 if axis == dim else 1 for axis in range(len(dims))])
    return factor_of


def length_profile(number_of, total, most, slope):
    loads = [(1 << 20) // math.isqrt(rank ** slope) + 1 for rank in range(2, number_of + 1)]
    rest, given = total - most - (number_of - 1), [1] * (number_of - 1)
    while rest > 0:
        movable = [i for i in range(number_of - 1) if given[i] < most]
        pool, left = sum([loads[i] for i in movable]), rest
        for i in movable:
            extra = min(most - given[i], max(1, left * loads[i] // pool), rest)
            given[i] = given[i] + extra
            rest = rest - extra
    return np.array([most] + given)


def ragged(rng, amount, total, reach, skew):
    if amount == 2:
        one = jax.random.randint(rng, (), max(1, total - reach), min(reach, total - 1) + 1)
        return jnp.stack([one, total - one])
    sizes = jnp.asarray(length_profile(amount, total, reach, skew), jnp.int32)
    pairs = (amount - 1) // 2
    source_of, receiver = sizes[1:1 + 2 * pairs:2], sizes[2:2 + 2 * pairs:2]
    room = jnp.minimum(source_of - 1, reach - receiver)
    moved = jax.random.randint(jax.random.fold_in(rng, 1), (pairs,), 0, 1 << 20) % (room + 1)
    sizes = sizes.at[1:1 + 2 * pairs:2].set(source_of - moved).at[2:2 + 2 * pairs:2].set(receiver + moved)
    return sizes[jax.random.permutation(jax.random.fold_in(rng, 2), amount)]


def gaussian(rng, shape, scale, most, split=(), kind=jnp.bfloat16):
    drawn = jax.random.normal(rng, shape, jnp.float32) * scale
    if len(split) > 0:
        drawn = steps_of(rng, shape, split, -0.22, 0.18) * drawn
    return jnp.clip(drawn, min=-most, max=most).astype(kind)


def setup_inputs(seed: int = 0) -> dict:
    key_list = jax.random.split(jax.random.key(seed), 14)
    tokens = gaussian(key_list[0], (SLOTS, SEQ, D), 1.0, 6.0, ((0, 4), (1, 32)))
    lengths = ragged(key_list[1], SLOTS, 3 * SEQ, SEQ, 2).astype(jnp.int32)
    ln_gain = jnp.clip(1.0 + 0.1 * jax.random.normal(key_list[2], (D,), jnp.float32), 0.5, 1.5)
    ln_bias = gaussian(key_list[3], (D,), 0.3, 2.0, ((0, 128),), jnp.float32)
    w_qkv = gaussian(key_list[4], (D, 3 * HQ), D ** -0.5, 0.1875, ((0, 128),), jnp.float32)
    b_qkv = gaussian(key_list[5], (3 * HQ,), 0.05, 0.3, ((0, 128),), jnp.float32)
    w_out = gaussian(key_list[6], (HQ, D), (max(HQ // 256, 1)) ** -0.5, 3.0, ((0, 128),), jnp.float32)
    b_out = gaussian(key_list[7], (D,), 0.5, 3.0, ((0, 128),), jnp.float32)
    w_fc1 = gaussian(key_list[8], (D, FF), D ** -0.5, 0.1875, ((0, 128),), jnp.float32)
    b_fc1 = gaussian(key_list[9], (FF,), 0.5, 3.0, ((0, 128),), jnp.float32)
    w_fc2 = gaussian(key_list[10], (FF, D), FF ** -0.5, 0.09375, ((0, 128),), jnp.float32)
    b_fc2 = gaussian(key_list[11], (D,), 0.5, 3.0, ((0, 128),), jnp.float32)
    cotangent = gaussian(key_list[12], (SLOTS, SEQ, D), 1.0, 6.0, ((0, 4), (1, 32)))
    return {"tokens": tokens, "lengths": lengths, "ln_gain": ln_gain, "ln_bias": ln_bias, "w_qkv": w_qkv, "b_qkv": b_qkv, "w_out": w_out, "b_out": b_out, "w_fc1": w_fc1, "b_fc1": b_fc1, "w_fc2": w_fc2, "b_fc2": b_fc2, "cotangent": cotangent}


norm_eps = 1e-05
rope_base = 10000.0
neg_large = -1e+30

@jax.custom_vjp
def low(v):
    return lax.optimization_barrier(v.astype(jnp.bfloat16)).astype(jnp.float32)

@jax.custom_vjp
def low_back(v):
    return v

def low_keep(v):
    return (low(v), None)

def low_pass(kept, grad):
    return (grad,)

def back_keep(v):
    return (v, None)

def back_low(kept, grad):
    return (low(grad),)
low.defvjp(low_keep, low_pass)
low_back.defvjp(back_keep, back_low)

def rope_tables(positions):
    lanes = jnp.arange(HD)
    half_rot = ROT // 2
    freq_index = jnp.where(lanes < half_rot, lanes, lanes - half_rot).astype(jnp.float32)
    inverse = jnp.power(rope_base, -2.0 * freq_index / ROT)
    angles = positions.astype(jnp.float32)[:, None] * inverse[None, :]
    cosine = jnp.where(lanes < ROT, jnp.cos(angles), 1.0)
    sine = jnp.where(lanes < half_rot, -jnp.sin(angles), jnp.where(lanes < ROT, jnp.sin(angles), 0.0))
    return (cosine[:, None, :], sine[:, None, :])

def swap_lanes(field):
    half_rot = ROT // 2
    return jnp.concatenate([field[..., half_rot:ROT], field[..., :half_rot], field[..., ROT:]], axis=-1)

def rotate_fwd(field, cosine, sine):
    return field * cosine + swap_lanes(field) * sine

def gelu_tanh(values):
    return jax.nn.gelu(values, approximate=True)

def reference(tokens, lengths, ln_gain, ln_bias, w_qkv, b_qkv, w_out, b_out, w_fc1, b_fc1, w_fc2, b_fc2, cotangent):
    highest = lax.Precision.HIGHEST
    positions = jnp.arange(SEQ)
    cosine, sine = rope_tables(positions)
    query_block = min(512, SEQ)
    block_count = SEQ // query_block
    block_starts = jnp.arange(block_count) * query_block
    score_scale = HD ** (-0.5)
    valid = (positions[None, :] < lengths[:, None]).astype(jnp.float32)

    def layer(params, inputs):
        norm_gain, norm_shift, qkv_weight, qkv_bias, out_weight, out_bias, fc1_weight, fc1_bias, fc2_weight, fc2_bias = [low(parameter) for parameter in params]

        def one_slot(unused, entries):
            x_slot, length = entries
            row_mean = lax.optimization_barrier(jnp.mean(x_slot, axis=-1, keepdims=True))
            centered = x_slot - row_mean
            variance = lax.optimization_barrier(jnp.mean(centered * centered, axis=-1, keepdims=True))
            normed = centered * lax.rsqrt(variance + norm_eps)
            hidden_in = low(normed * norm_gain + norm_shift)
            qkv_all = low_back(jnp.dot(hidden_in, qkv_weight, precision=highest) + qkv_bias)
            heads_shape = (SEQ, HEADS, HD)
            query_r = low(rotate_fwd(qkv_all[:, :HQ].reshape(heads_shape), cosine, sine))
            key_r = low(rotate_fwd(qkv_all[:, HQ:2 * HQ].reshape(heads_shape), cosine, sine))
            value_r = low(qkv_all[:, 2 * HQ:].reshape(heads_shape))
            key_pos = jnp.arange(SEQ)

            def attend(block_args):
                query_rows, start_row = block_args
                scores = low_back(jnp.einsum('qhd,khd->qhk', query_rows, key_r, precision=highest) * score_scale)
                query_pos = start_row + jnp.arange(query_block)
                allowed = ((key_pos[None, :] <= query_pos[:, None]) & (key_pos[None, :] < length))[:, None, :]
                scores = jnp.where(allowed, scores, neg_large)
                probs = jax.nn.softmax(scores, axis=-1)
                return jnp.einsum('qhk,khd->qhd', low(probs), value_r, precision=highest)
            blocks_out = lax.map(jax.checkpoint(attend), (query_r.reshape(block_count, query_block, HEADS, HD), block_starts))
            query_valid = (key_pos < length).astype(jnp.float32)
            attn_heads = blocks_out.reshape(SEQ, HQ) * query_valid[:, None]
            attn_low = low_back(low(attn_heads))
            branch_attn = jnp.dot(attn_low, out_weight, precision=highest) + out_bias
            fc1_pre = low_back(jnp.dot(hidden_in, fc1_weight, precision=highest) + fc1_bias)
            act_low = low(gelu_tanh(fc1_pre))
            branch_mlp = jnp.dot(act_low, fc2_weight, precision=highest) + fc2_bias
            return (unused, x_slot + branch_attn + branch_mlp)
        _, outputs = lax.scan(one_slot, None, (inputs, lengths))
        return outputs
    params = (ln_gain, ln_bias, w_qkv, b_qkv, w_out, b_out, w_fc1, b_fc1, w_fc2, b_fc2)
    inputs = tokens.astype(jnp.float32)
    outputs, pullback = jax.vjp(layer, params, inputs)
    out_grad = cotangent.astype(jnp.float32) * valid[:, :, None]
    param_grads, token_grad = pullback(out_grad)
    bias_grad = param_grads[3]
    return (outputs.astype(jnp.bfloat16), token_grad.astype(jnp.bfloat16), param_grads[0], param_grads[1], param_grads[2], bias_grad[:2 * HQ], bias_grad[2 * HQ:], param_grads[4], param_grads[5], param_grads[6], param_grads[7], param_grads[8], param_grads[9])
```

```python
import functools

import jax
import jax.numpy as jnp
from jax import lax
from jax.experimental import pallas as pl
from jax.experimental.pallas import tpu as pltpu
from jax.sharding import PartitionSpec as P

HEADS = 16
HD = 64
ROT = 16
HQ = 1024
D = 1024
FF = 4096
BLK = 512

norm_eps = 1e-05
rope_base = 10000.0
MESH = pl.DeviceIdType.MESH
low = jnp.bfloat16
full = jnp.float32
VM = pl.BlockSpec(memory_space=pltpu.VMEM)
AN = pl.BlockSpec(memory_space=pl.ANY)


def place():
    s = lax.axis_index("slot")
    c = lax.axis_index("ctx")
    w = lax.axis_index("wsh")
    return s, c // 8, (c // 4) % 2, c % 4, w


def dev(s, y, xh, z, w):
    return (s, y * 8 + xh * 4 + z, w)


def x_dev(x, y, z, w):
    return dev(x % 2, y, x // 2, z, w)


def signal(barrier, target):
    pl.semaphore_signal(barrier, inc=1, device_id=target, device_id_type=MESH)


def remote(src, dst, send, recv, target):
    return pltpu.make_async_remote_copy(
        src_ref=src, dst_ref=dst, send_sem=send, recv_sem=recv,
        device_id=target, device_id_type=MESH,
    )


def iota(shape, axis):
    return lax.broadcasted_iota(jnp.int32, shape, axis)


def dot(a, b, ca, cb):
    return lax.dot_general(a, b, (((ca,), (cb,)), ((), ())), preferred_element_type=full)


def core_of(m):
    return ((m + 1) // 2) % 2


def owner_lanes(params, width, lanes, step):
    f, l = iota((128, width), 1), iota((128, width), 0)
    pick = (l == lanes[0] + (f & (step - 1)))
    for other in lanes[1:]:
        pick = pick | (l == other + (f & (step - 1)))
    return dot(params, pick.astype(full).astype(low), 1, 0), f, l


def lane_mix(tiles, shifts):
    lane = iota((8, 128), 1)
    out = jnp.zeros((8, 128), full)
    for g in range(4):
        t = tiles[g]
        if shifts[g] % 128:
            t = pltpu.roll(t, shifts[g] % 128, 1)
        out = jnp.where((lane >= 32 * g) & (lane < 32 * g + 32), t, out)
    return out


def front_kernel(lens, tok, cot, smallp, wq, wo, w1, w2, cosine, sine,
                 KV, QD, HB, XH, YY, GA, DU, W1, W2, WQT, WOF, VEC, VAL,
                 XX, Q, F, Qs, Fs, wos, WO, HT,
                 zs, zr, ys, yr, ps, pr, ts, tr, fs, fr, os, orr,
                 q1s, q1r, q2s, q2r, f1s, f1r, f2s, f2r, w1s, w1r, w2s, w2r,
                 hs, kr, qr, dr, ks, krp):
    s, y, xh, z, w = place()
    x = xh * 2 + s
    r = s * 8 + y * 2 + xh
    j = z * 2 + w
    jo = r // 2
    m = y * 2 + xh
    core, spot = core_of(m), m // 2
    keep = (j == jo).astype(jnp.int32)
    mine = ((y // 2 == w) & (core == w)).astype(jnp.int32)
    sib = dev(s, y, xh, z, 1 - w)

    barrier = pltpu.get_barrier_semaphore()
    for k in range(1, 8):
        q = (j + k) % 8
        signal(barrier, dev(s, y, xh, q // 2, q % 2))
    for k in range(1, 4):
        signal(barrier, x_dev((x + k) % 4, y, z, w))
        signal(barrier, dev(s, (y + k) % 4, xh, z, w))

    def wo_source(k):
        rr = 2 * j + k // 8
        return rr // 8, (rr // 2) % 4, rr % 2, (k % 8) // 2, k % 2

    def wo_mine(k):
        ss, sy, sxh, sz, sw = wo_source(k)
        return (ss == s) & (sy == y) & (sxh == xh) & (sz == z) & (sw == w)

    for k in range(16):
        @pl.when(jnp.logical_not(wo_mine(k)))
        def _():
            signal(barrier, dev(*wo_source(k)))

    def source(i):
        return dev(s, i, (i + w) % 2, z, y // 2)

    def my_source(i):
        return (y == i) & (xh == (i + w) % 2) & (w == y // 2)

    for i in range(4):
        @pl.when(jnp.logical_not(my_source(i)))
        def _():
            signal(barrier, source(i))

    XX[w, z] = tok[0]
    row = iota((128, 1024), 0) + (m * BLK + z * 128)
    YY[w, z] = jnp.where(row < lens[0], cot[0].astype(full), 0.0).astype(low)
    first_row = iota((8, 128), 0) == 0
    padded = jnp.where(first_row, jnp.broadcast_to(smallp[0:1, :], (8, 128)), 0.0)
    for q in range(8):
        c = 128 * q
        top = jnp.concatenate([wq[:, c:c + 128], wq[:, 1024 + c:1152 + c]], axis=1)
        bot = jnp.concatenate([wq[:, 2048 + c:2176 + c], padded], axis=1)
        Qs[q] = jnp.concatenate([top, bot], axis=0).astype(low)
    wos[...] = jnp.concatenate([wo[:, :512], wo[:, 512:]], axis=0).astype(low)
    W2[s, y, xh] = w2[...].astype(low)

    pl.semaphore_wait(barrier, 7 + 6 + 16 - keep + 4 - mine)

    slot = (r % 2) * 8 + j
    tq, tf, xc, yc, oc = [], [], [], [], []
    for k in range(1, 8):
        q = (j + k) % 8
        cp = remote(Qs.at[q], Q.at[s, y, xh, j], ts.at[k], tr.at[k], dev(s, y, xh, q // 2, q % 2))
        cp.start()
        tq.append(cp)
    for k in (1, 3, 2):
        cp = remote(XX.at[w, z], XX.at[w, z], zs.at[k], zr.at[k], dev(s, y, xh, (z + k) % 4, w))
        cp.start()
        xc.append(cp)
    for q in range(8):
        tiles = []
        for g in range(4):
            parts = [w1[:, 128 * (2 * (4 * g + n) + q // 4):128 * (2 * (4 * g + n) + q // 4) + 128] for n in range(4)]
            tiles.append(lane_mix(parts, [32 * (n - q % 4) for n in range(4)]))
        top = jnp.concatenate(tiles[:2], axis=1)
        bot = jnp.concatenate(tiles[2:], axis=1)
        Fs[q] = jnp.concatenate([top, bot], axis=0).astype(low)
    for k in range(1, 8):
        q = (j + k) % 8
        cp = remote(Fs.at[q], F.at[s, y, xh, j], fs.at[k], fr.at[k], dev(s, y, xh, q // 2, q % 2))
        cp.start()
        tf.append(cp)
    Q[s, y, xh, j] = Qs[j]
    F[s, y, xh, j] = Fs[j]

    for cp in tq:
        cp.wait_recv()

    def ring1(ref0, ref1, snd, rcv):
        out = []
        for k in (1, 3, 2):
            cp = remote(ref0, ref0, snd.at[0, k], rcv.at[0, k], x_dev((x + k) % 4, y, z, w))
            cp.start()
            out.append(cp)
            cp = remote(ref1, ref1, snd.at[1, k], rcv.at[1, k], dev(s, (y + k) % 4, xh, z, w))
            cp.start()
            out.append(cp)
        return out

    def ring2(ref0, ref1, snd, rcv):
        out = []
        for k in (1, 3, 2):
            cp = remote(ref0, ref0, snd.at[0, k], rcv.at[0, k], dev(s, (y + k) % 4, xh, z, w))
            cp.start()
            out.append(cp)
            cp = remote(ref1, ref1, snd.at[1, k], rcv.at[1, k], x_dev((x + k) % 4, y, z, w))
            cp.start()
            out.append(cp)
        return out

    lo4, hi4 = pl.ds(0, 4), pl.ds(4, 4)
    lo5, hi5 = pl.ds(0, 512), pl.ds(512, 512)
    q1 = ring1(Q.at[s, y, xh, lo4], Q.at[s, y, xh, hi4], q1s, q1r)
    for k in range(16):
        q = (r + k) % 16
        cp = remote(wos, WO.at[slot], os.at[k], orr.at[slot], dev(q // 8, (q // 2) % 4, q % 2, jo // 2, jo % 2))
        oc.append(cp)
        if k == 0:
            @pl.when(j != jo)
            def _():
                cp.start()

            @pl.when(j == jo)
            def _():
                WO[slot] = wos[...]
        else:
            cp.start()
    for cp in q1:
        cp.wait_recv()
    q2 = ring2(Q.at[:, y, :, lo4], Q.at[s, :, xh, hi4], q2s, q2r)
    for cp in tf:
        cp.wait_recv()
    f1 = ring1(F.at[s, y, xh, lo4], F.at[s, y, xh, hi4], f1s, f1r)
    g1 = ring1(W2.at[s, y, xh, :, lo5], W2.at[s, y, xh, :, hi5], w1s, w1r)
    for k in (1, 3, 2):
        cp = remote(YY.at[w, z], YY.at[w, z], ys.at[k], yr.at[k], dev(s, y, xh, (z + k) % 4, w))
        cp.start()
        yc.append(cp)
    for cp in xc:
        cp.wait_recv()
    xpair = remote(XX.at[w], XX.at[w], ps.at[0], pr.at[0], sib)
    xpair.start()
    for cp in f1 + g1:
        cp.wait_recv()
    for cp in q2:
        cp.wait_recv()
    f2 = ring2(F.at[:, y, :, lo4], F.at[s, :, xh, hi4], f2s, f2r)
    g2 = ring2(W2.at[:, y, :, :, lo5], W2.at[s, :, xh, :, hi5], w2s, w2r)

    units = Q[...].reshape(128, 16, 256).astype(full)
    left = units[:, :8].reshape(1024, 256)
    right = units[:, 8:].reshape(1024, 256)
    WQT[0:256, :] = left.T.astype(low)
    WQT[256:384, :] = right[:, :128].T.astype(low)
    owner_row = (iota((128, 1024), 1) == 8 * iota((128, 1024), 0)).astype(full).astype(low)
    params = dot(owner_row, right[:, 128:].astype(low), 1, 0).astype(low)

    def row_of(lanes):
        t, f, l = owner_lanes(params, 1024, lanes, 8)
        return jnp.sum(jnp.where((f >= 8 * l) & (f < 8 * l + 8), t, 0.0), axis=0, keepdims=True)

    gain = row_of((0,))
    shift = row_of((8,))
    VEC[0:1, :] = gain
    VEC[1:2, :] = row_of((40, 80))
    t, f, l = owner_lanes(params, 512, (48,), 32)
    base = f - 4 * (l - j)
    bias_1 = jnp.sum(
        jnp.where((((l - j) & 7) == 0) & (base >= 0) & (base < 32), t, 0.0), axis=0, keepdims=True
    )
    n0, p0 = iota((384, 128), 0), iota((384, 128), 1)
    n0 = (n0 // 128) * 1024 + 128 * j + (n0 & 127)
    at = n0 - 24 * p0
    inside = ((at >= 0) & (at < 24)).astype(full)
    t = dot(inside.astype(low), params, 1, 0)
    lane_want = jnp.sum(inside * at.astype(full), axis=1, keepdims=True) + 16.0
    bias_q = jnp.sum(jnp.where(p0.astype(full) == lane_want, t, 0.0), axis=1, keepdims=True)
    lp, ll = iota((128, 128), 0), iota((128, 128), 1)
    tok_pos = (iota((1, BLK), 1) + m * BLK).astype(full)
    pf = params.astype(full)
    for i in range(2):
        here = lp == s * 64 + i
        size = jnp.sum(jnp.where(here & (ll == 88), pf, 0.0)) * 64.0 + jnp.sum(jnp.where(here & (ll == 89), pf, 0.0))
        VAL[i:i + 1, :] = jnp.where(tok_pos < size, 1.0, 0.0)

    co, si = cosine[...], sine[...]

    def norm_slot(wi):
        def one(zi, carry):
            v = XX[wi, zi].astype(full)
            mean = jnp.mean(v, axis=-1, keepdims=True)
            c = v - mean
            var = jnp.mean(c * c, axis=-1, keepdims=True)
            h = c * lax.rsqrt(var + norm_eps)
            XH[wi, zi] = h.astype(low)
            HB[wi, zi] = (h * gain + shift).astype(low)
            return carry

        lax.fori_loop(0, 4, one, 0)

    def turn(v):
        a, b = v[0:8], v[8:16]
        return jnp.concatenate([a * co - b * si, b * co + a * si, v[16:]], axis=0)

    def qkv_slot(wi):
        t = dot(WQT[...], HB[wi].reshape(BLK, 1024), 1, 1) + bias_q
        for e in range(2):
            HT[e, wi, 0, 0] = turn(t[128 + 64 * e:192 + 64 * e]).astype(low)
            HT[e, wi, 0, 1] = t[256 + 64 * e:320 + 64 * e].astype(low)
            HT[e, wi, 1, 0] = (turn(t[64 * e:64 + 64 * e]).astype(low).astype(full) * 0.125).astype(low)

    def head_target(e, i):
        return dev(s, 2 * w + e, i, z, core), (y == 2 * w + e) & (xh == i) & (core == w)

    def kv_copy(e, i):
        return remote(HT.at[e, i, 0], KV.at[core, spot], hs.at[e, i, 0], kr.at[spot], head_target(e, i)[0])

    def q_copy(e, i):
        return remote(HT.at[e, i, 1, 0], QD.at[spot, 0], hs.at[e, i, 1], qr.at[spot], head_target(e, i)[0])

    def do_copy(e, i):
        return remote(HT.at[e, i, 1, 1], QD.at[spot, 1], hs.at[e, i, 2], dr.at[spot], head_target(e, i)[0])

    def send_qkv(i):
        for e in range(2):
            me = head_target(e, i)[1]

            @pl.when(jnp.logical_not(me))
            def _():
                kv_copy(e, i).start()
                q_copy(e, i).start()

            @pl.when(me)
            def _():
                KV[core, spot] = HT[e, i, 0]
                QD[spot, 0] = HT[e, i, 1, 0]

    def send_do(i):
        t = dot(WOF[...], YY[i].reshape(BLK, 1024), 1, 1)
        for e in range(2):
            HT[e, i, 1, 1] = t[64 * e:64 + 64 * e].astype(low)
            me = head_target(e, i)[1]

            @pl.when(jnp.logical_not(me))
            def _():
                do_copy(e, i).start()

            @pl.when(me)
            def _():
                QD[spot, 1] = HT[e, i, 1, 1]

    norm_slot(w)
    qkv_slot(w)
    send_qkv(w)
    xpair.wait_recv()
    norm_slot(1 - w)
    qkv_slot(1 - w)
    send_qkv(1 - w)

    for cp in yc:
        cp.wait_recv()
    ypair = remote(YY.at[w], YY.at[w], ps.at[1], pr.at[1], sib)
    ypair.start()
    for k in range(16):
        @pl.when(jnp.logical_not(wo_mine(k)))
        def _():
            remote(wos, WO.at[k], os.at[0], orr.at[k], dev(*wo_source(k))).wait_recv()
    units = WO[...].astype(full)
    WOF[:, :512] = units[:, :8].reshape(128, 512).astype(low)
    WOF[:, 512:] = units[:, 8:].reshape(128, 512).astype(low)
    send_do(w)
    ypair.wait_recv()
    send_do(1 - w)

    for cp in f2 + g2:
        cp.wait_recv()
    units = F[...].reshape(128, 16, 256).astype(full)
    W1[:, :256] = units[:, :8].reshape(1024, 256).astype(low)
    W1[:, 256:] = units[:, 8:].reshape(1024, 256).astype(low)

    def hidden(n, carry):
        wi, zi = n // 4, n % 4
        u = dot(HB[wi, zi], W1[...], 1, 0) + bias_1
        dg = dot(YY[wi, zi], W2[...].reshape(512, 1024), 1, 1)
        c0 = 0.7978845608028654
        t = jnp.tanh(c0 * (u + 0.044715 * (u * u * u)))
        GA[wi, zi] = (0.5 * u * (1.0 + t)).astype(low)
        slope = 0.5 * (1.0 + t) + (0.5 * c0) * u * (1.0 - t * t) * (1.0 + (3.0 * 0.044715) * (u * u))
        DU[wi, zi] = (dg * slope).astype(low)
        return carry

    lax.fori_loop(0, 2, hidden, 0)
    for i in range(4):
        @pl.when(jnp.logical_not(my_source(i)))
        def _():
            remote(HT.at[0, 0, 0], KV.at[w, i], hs.at[0, 0, 0], kr.at[i], source(i)).wait_recv()
    swap = remote(KV.at[w], KV.at[w], ks, krp, sib)
    swap.start()
    lax.fori_loop(2, 8, hidden, 0)
    for i in range(4):
        @pl.when(jnp.logical_not(my_source(i)))
        def _():
            remote(HT.at[0, 0, 1, 0], QD.at[i, 0], hs.at[0, 0, 1], qr.at[i], source(i)).wait_recv()
            remote(HT.at[0, 0, 1, 1], QD.at[i, 1], hs.at[0, 0, 2], dr.at[i], source(i)).wait_recv()
    for e in range(2):
        for i in range(2):
            @pl.when(jnp.logical_not(head_target(e, i)[1]))
            def _():
                kv_copy(e, i).wait_send()
                q_copy(e, i).wait_send()
                do_copy(e, i).wait_send()

    @pl.when(j != jo)
    def _():
        oc[0].wait_send()

    for cp in oc[1:] + tq + tf + xc + yc + q1 + q2 + f1 + f2 + g1 + g2 + [xpair, ypair]:
        cp.wait_send()
    swap.wait()


def front(lens, tok, cot, smallp, wq, wo, w1, w2, cosine, sine):
    S = pltpu.SemaphoreType.DMA
    V = pltpu.VMEM
    sds = jax.ShapeDtypeStruct
    return pl.pallas_call(
        front_kernel,
        name="front",
        out_shape=(
            sds((2, 4, 2, 64, BLK), low),
            sds((4, 2, 64, BLK), low),
            sds((2, 4, 128, 1024), low),
            sds((2, 4, 128, 1024), low),
            sds((2, 4, 128, 1024), low),
            sds((2, 4, 128, 512), low),
            sds((2, 4, 128, 512), low),
            sds((1024, 512), low),
            sds((2, 4, 2, 32, 1024), low),
            sds((384, 1024), low),
            sds((128, 1024), low),
            sds((8, 1024), full),
            sds((8, BLK), full),
        ),
        in_specs=[pl.BlockSpec(memory_space=pltpu.SMEM)] + [VM] * 9,
        out_specs=(VM,) * 13,
        scratch_shapes=[
            V((2, 4, 128, 1024), low),
            V((2, 4, 2, 8, 16, 256), low),
            V((2, 4, 2, 8, 16, 256), low),
            V((8, 16, 256), low),
            V((8, 16, 256), low),
            V((16, 512), low),
            V((16, 16, 512), low),
            V((2, 2, 2, 2, 64, BLK), low),
            S((4,)), S((4,)), S((4,)), S((4,)), S((2,)), S((2,)), S((8,)), S((8,)), S((8,)), S((8,)),
            S((16,)), S((16,)),
            S((2, 4)), S((2, 4)), S((2, 4)), S((2, 4)), S((2, 4)), S((2, 4)), S((2, 4)), S((2, 4)),
            S((2, 4)), S((2, 4)), S((2, 4)), S((2, 4)),
            S((2, 2, 3)), S((4,)), S((4,)), S((4,)), S, S,
        ],
        compiler_params=pltpu.CompilerParams(
            collective_id=0, has_side_effects=True, vmem_limit_bytes=56 << 20
        ),
    )(lens, tok, cot, smallp, wq, wo, w1, w2, cosine, sine)


def collect_kernel(OQ, DKV, RT, got, summed, loc, ss, rr, ps, pr):
    s, y, xh, z, w = place()
    m = y * 2 + xh
    core = core_of(m)
    barrier = pltpu.get_barrier_semaphore()
    pair = dev(s, y, xh, z, 1 - w)
    signal(barrier, pair)

    def home(i):
        return dev(s, i, (i + w) % 2, z, y // 2)

    def at_home(i):
        return (y == i) & (xh == (i + w) % 2) & (w == y // 2)

    mine = ((y // 2 == w) & (core == w)).astype(jnp.int32)
    for e in range(2):
        for i in range(2):
            me = (y == 2 * w + e) & (xh == i) & (core == w)

            @pl.when(jnp.logical_not(me))
            def _():
                signal(barrier, dev(s, 2 * w + e, i, z, core))
    pl.semaphore_wait(barrier, 5 - mine)

    e_me, i_me = y % 2, xh
    swap = remote(DKV.at[1 - w], got, ps, pr, pair)
    swap.start()
    for i in range(4):
        @pl.when(jnp.logical_not(at_home(i)))
        def _():
            remote(OQ.at[i], RT.at[e_me, i_me, 0], ss.at[i, 0], rr.at[e_me, i_me, 0], home(i)).start()

        @pl.when(at_home(i))
        def _():
            pltpu.make_async_copy(OQ.at[i], RT.at[e_me, i_me, 0], loc.at[0]).start()
    swap.wait_recv()
    for i in range(4):
        summed[i] = (DKV[w, i].astype(full) + got[i].astype(full)).astype(low)

        @pl.when(jnp.logical_not(at_home(i)))
        def _():
            remote(summed.at[i], RT.at[e_me, i_me, 1], ss.at[i, 1], rr.at[e_me, i_me, 1], home(i)).start()

        @pl.when(at_home(i))
        def _():
            pltpu.make_async_copy(summed.at[i], RT.at[e_me, i_me, 1], loc.at[1]).start()
    for e in range(2):
        for i in range(2):
            me = (y == 2 * w + e) & (xh == i) & (core == w)
            for g in range(2):
                @pl.when(jnp.logical_not(me))
                def _():
                    remote(summed.at[0], RT.at[e, i, g], ss.at[0, g], rr.at[e, i, g],
                           dev(s, 2 * w + e, i, z, core)).wait_recv()

                @pl.when(me)
                def _():
                    pltpu.make_async_copy(summed.at[0], RT.at[e, i, g], loc.at[g]).wait()
    for i in range(4):
        for g in range(2):
            @pl.when(jnp.logical_not(at_home(i)))
            def _():
                remote(summed.at[i], RT.at[e_me, i_me, g], ss.at[i, g], rr.at[e_me, i_me, g], home(i)).wait_send()
    swap.wait_send()


def collect(OQ, DKV):
    S = pltpu.SemaphoreType.DMA
    return pl.pallas_call(
        collect_kernel,
        name="collect",
        out_shape=jax.ShapeDtypeStruct((2, 2, 2, 2, 64, BLK), low),
        in_specs=[VM, VM],
        out_specs=VM,
        scratch_shapes=[
            pltpu.VMEM((4, 2, 64, BLK), low), pltpu.VMEM((4, 2, 64, BLK), low),
            S((2,)), S((4, 2)), S((2, 2, 2)), S, S,
        ],
        compiler_params=pltpu.CompilerParams(
            collective_id=2, has_side_effects=True, vmem_limit_bytes=32 << 20
        ),
    )(OQ, DKV)


def attend_kernel(KV, QD, OQ, DKV, acc):
    w = lax.axis_index("wsh")
    acc[...] = jnp.zeros_like(acc)
    causal = lax.broadcasted_iota(jnp.int32, (BLK, BLK), 0) <= lax.broadcasted_iota(
        jnp.int32, (BLK, BLK), 1
    )

    def query_block(i, carry):
        m = 2 * i + (i + w) % 2
        q = QD[i, 0]
        do = QD[i, 1]

        def fwd(n, state, masked):
            run_max, total, out = state
            c, t = core_of(n), n // 2
            sc = dot(KV[c, t, 0], q, 0, 0)
            if masked:
                sc = jnp.where(causal, sc, -1e30)
            new_max = jnp.maximum(run_max, jnp.max(sc, axis=0, keepdims=True))
            pr = jnp.exp(sc - new_max)
            fac = jnp.exp(run_max - new_max)
            total = total * fac + jnp.sum(pr, axis=0, keepdims=True)
            out = out * fac + dot(KV[c, t, 1], pr.astype(low), 1, 0)
            return new_max, total, out

        start = (
            jnp.full((1, BLK), -1e30, full),
            jnp.zeros((1, BLK), full),
            jnp.zeros((HD, BLK), full),
        )
        state = lax.fori_loop(0, m, lambda n, st: fwd(n, st, False), start)
        run_max, total, out = fwd(m, state, True)
        out = out / total
        lse = run_max + jnp.log(total)
        OQ[i, 0] = out.astype(low)
        delta = jnp.sum(do.astype(full) * out, axis=0, keepdims=True)

        def bwd(n, dq, masked):
            c, t = core_of(n), n // 2
            k = KV[c, t, 0]
            sc = dot(k, q, 0, 0)
            pr = jnp.exp(sc - lse)
            if masked:
                pr = jnp.where(causal, pr, 0.0)
            dp = dot(KV[c, t, 1], do, 0, 0)
            ds = (pr * (dp - delta)).astype(low)
            acc[c, t, 0] += dot(q, ds, 1, 1)
            acc[c, t, 1] += dot(do, pr.astype(low), 1, 1)
            return dq + dot(k, ds, 1, 0)

        dq = lax.fori_loop(0, m, lambda n, st: bwd(n, st, False), jnp.zeros((HD, BLK), full))
        dq = bwd(m, dq, True)
        OQ[i, 1] = (dq * 0.125).astype(low)
        return carry

    lax.fori_loop(0, 4, query_block, 0)
    for c in range(2):
        for t in range(4):
            DKV[c, t] = acc[c, t].astype(low)


def attend(KV, QD):
    return pl.pallas_call(
        attend_kernel,
        name="attend",
        out_shape=(
            jax.ShapeDtypeStruct((4, 2, 64, BLK), low),
            jax.ShapeDtypeStruct((2, 4, 2, 64, BLK), low),
        ),
        in_specs=[VM, VM],
        out_specs=(VM, VM),
        scratch_shapes=[pltpu.VMEM((2, 4, 2, 64, BLK), full)],
        compiler_params=pltpu.CompilerParams(vmem_limit_bytes=48 << 20),
    )(KV, QD)


def reduce_kernel(PT, GB, GO, SUM, W2F, W1F, FO,
                  pair_in, part, z_in, g_in, g_mid, m_in, fin, fo_in,
                  loc, ps, pr, zs, zr, g1s, g1r, g2s, g2r, ts, tr, os, orr):
    s, y, xh, z, w = place()
    x = xh * 2 + s
    r = s * 8 + y * 2 + xh
    j = z * 2 + w
    jo = r // 2
    keep = (j == jo).astype(jnp.int32)
    slot = (r % 2) * 8 + j

    barrier = pltpu.get_barrier_semaphore()
    for k in range(1, 8):
        q = (j + k) % 8
        signal(barrier, dev(s, y, xh, q // 2, q % 2))
    for k in range(1, 4):
        signal(barrier, x_dev((x + k) % 4, y, z, w))
        signal(barrier, dev(s, (y + k) % 4, xh, z, w))
    for k in range(16):
        q = (r + k) % 16
        if k == 0:
            @pl.when(j != jo)
            def _():
                signal(barrier, dev(s, y, xh, jo // 2, jo % 2))
        else:
            signal(barrier, dev(q // 8, (q // 2) % 4, q % 2, jo // 2, jo % 2))
    pl.semaphore_wait(barrier, 7 + 6 + 16 - keep)

    def owner(k):
        rr = 2 * j + k // 8
        return rr // 8, (rr // 2) % 4, rr % 2, (k % 8) // 2, k % 2

    pair = remote(PT.at[1 - w], pair_in, ps, pr, dev(s, y, xh, z, 1 - w))
    pair.start()
    g1 = []
    for k in range(1, 4):
        yy, xx = (y + k) % 4, (x + k) % 4
        cp = remote(GB.at[0, yy], g_in.at[0, k], g1s.at[0, k], g1r.at[0, k], dev(s, yy, xh, z, w))
        cp.start()
        g1.append(cp)
        cp = remote(GB.at[1, xx], g_in.at[1, k], g1s.at[1, k], g1r.at[1, k], x_dev(xx, y, z, w))
        cp.start()
        g1.append(cp)

    def owner_copy(k):
        os_, oy, oxh, oz, ow = owner(k)
        me = (os_ == s) & (oy == y) & (oxh == xh) & (oz == z) & (ow == w)
        return remote(GO.at[k], fo_in.at[r], os.at[k], orr.at[r], dev(os_, oy, oxh, oz, ow)), me

    for k in range(16):
        cp, me = owner_copy(k)

        @pl.when(jnp.logical_not(me))
        def _():
            cp.start()

        @pl.when(me)
        def _():
            pltpu.make_async_copy(GO.at[k], fo_in.at[r], loc.at[0]).start()

    pair.wait_recv()

    def add_pair(n, carry):
        a, b = n // 2, n % 2
        part[a, b] = (PT[w, a, b].astype(full) + pair_in[a, b].astype(full)).astype(low)
        return carry

    lax.fori_loop(0, 8, add_pair, 0)
    zc = []
    for k in range(1, 4):
        zz = (z + k) % 4
        cp = remote(part.at[zz], z_in.at[k], zs.at[k], zr.at[k], dev(s, y, xh, zz, w))
        cp.start()
        zc.append(cp)

    for cp in g1:
        cp.wait_recv()

    def add_g(n, carry):
        g_mid[0, n] = (
            GB[0, y, n].astype(full) + g_in[0, 1, n].astype(full)
            + g_in[0, 2, n].astype(full) + g_in[0, 3, n].astype(full)
        ).astype(low)
        g_mid[1, n] = (
            GB[1, x, n].astype(full) + g_in[1, 1, n].astype(full)
            + g_in[1, 2, n].astype(full) + g_in[1, 3, n].astype(full)
        ).astype(low)
        return carry

    lax.fori_loop(0, 4, add_g, 0)
    g2 = []
    for k in range(1, 4):
        yy, xx = (y + k) % 4, (x + k) % 4
        cp = remote(g_mid.at[0, xx], m_in.at[0, k], g2s.at[0, k], g2r.at[0, k], x_dev(xx, y, z, w))
        cp.start()
        g2.append(cp)
        cp = remote(g_mid.at[1, yy], m_in.at[1, k], g2s.at[1, k], g2r.at[1, k], dev(s, yy, xh, z, w))
        cp.start()
        g2.append(cp)

    for q in range(16):
        @pl.when((q == r) & (j == jo))
        def _():
            pltpu.make_async_copy(GO.at[0], fo_in.at[q], loc.at[0]).wait()

        @pl.when(jnp.logical_not((q == r) & (j == jo)))
        def _():
            remote(GO.at[0], fo_in.at[q], os.at[0], orr.at[q],
                   dev(q // 8, (q // 2) % 4, q % 2, jo // 2, jo % 2)).wait_recv()
    FO[...] = lax.fori_loop(
        0, 16, lambda q, t: t + fo_in[q].astype(full), jnp.zeros((16, 512), full)
    )

    for cp in g2:
        cp.wait_recv()
    for h in range(2):
        mine = x if h == 0 else y
        for b in range(6):
            t = (
                g_mid[h, mine, b].astype(full) + m_in[h, 1, b].astype(full)
                + m_in[h, 2, b].astype(full) + m_in[h, 3, b].astype(full)
            )
            if b < 4:
                fin[h * 4 + b] = t.astype(low)
            else:
                W2F[h, b - 4] = t
    tp = []
    for k in range(1, 8):
        q = (j + k) % 8
        cp = remote(fin.at[q], W1F.at[j], ts.at[k], tr.at[k], dev(s, y, xh, q // 2, q % 2))
        cp.start()
        tp.append(cp)
    W1F[j] = fin[j]

    for cp in zc:
        cp.wait_recv()
    for b in range(2):
        SUM[b] = (
            part[z, b].astype(full) + z_in[1, b].astype(full)
            + z_in[2, b].astype(full) + z_in[3, b].astype(full)
        )
    for k in range(16):
        cp, me = owner_copy(k)

        @pl.when(jnp.logical_not(me))
        def _():
            cp.wait_send()
    pair.wait_send()
    for cp in zc + g1 + g2:
        cp.wait_send()
    for cp in tp:
        cp.wait()


def reduce(PT, GB, GO):
    S = pltpu.SemaphoreType.DMA
    return pl.pallas_call(
        reduce_kernel,
        name="reduce",
        out_shape=(
            jax.ShapeDtypeStruct((2, 128, 1024), full),
            jax.ShapeDtypeStruct((2, 2, 16, 512), full),
            jax.ShapeDtypeStruct((8, 16, 512), low),
            jax.ShapeDtypeStruct((16, 512), full),
        ),
        in_specs=[VM] * 3,
        out_specs=(VM,) * 4,
        scratch_shapes=[
            pltpu.VMEM((4, 2, 128, 1024), low),
            pltpu.VMEM((4, 2, 128, 1024), low),
            pltpu.VMEM((4, 2, 128, 1024), low),
            pltpu.VMEM((2, 4, 4, 6, 16, 512), low),
            pltpu.VMEM((2, 4, 6, 16, 512), low),
            pltpu.VMEM((2, 4, 6, 16, 512), low),
            pltpu.VMEM((8, 16, 512), low),
            pltpu.VMEM((16, 16, 512), low),
            S((1,)), S, S, S((4,)), S((4,)), S((2, 4)), S((2, 4)), S((2, 4)), S((2, 4)),
            S((8,)), S((8,)), S((16,)), S((16,)),
        ],
        compiler_params=pltpu.CompilerParams(
            collective_id=3, has_side_effects=True, vmem_limit_bytes=48 << 20
        ),
    )(PT, GB, GO)


def rope(first, second, cosine, sine):
    return first * cosine - second * sine, second * cosine + first * sine


def shards(
    tokens, lengths, ln_gain, ln_bias, w_qkv, b_qkv, w_out, b_out, w_fc1, b_fc1, w_fc2, b_fc2, cotangent
):
    s, y, xh, z, w = place()
    j = z * 2 + w
    m = y * 2 + xh
    own_first = m * BLK + z * 128
    own_valid = (own_first + jnp.arange(128)) < lengths[0]
    own_dy = jnp.where(own_valid[:, None], cotangent[0], jnp.zeros((), low))
    small = jnp.concatenate(
        [
            ln_gain, ln_bias, b_qkv, b_out, b_fc1, b_fc2,
            (lengths // 64).astype(full), (lengths % 64).astype(full), jnp.zeros((38,), full),
        ]
    )[None]
    pos = (m * BLK + jnp.arange(BLK)).astype(full)
    freq = jnp.power(rope_base, -2.0 * jnp.arange(8).astype(full) / ROT)
    angle = freq[:, None] * pos[None, :]
    cosine, sine = jnp.cos(angle), jnp.sin(angle)

    KV, QD, HB, XH, YY, GA, DU, W1, W2, WQT, WOF, VEC, VAL = front(
        lengths, tokens, cotangent, small, w_qkv, w_out, w_fc1, w_fc2, cosine, sine
    )
    OQ, DKV = attend(KV, QD)
    RT = collect(OQ, DKV)

    hb = HB.reshape(1024, 1024)
    xhat = XH.reshape(1024, 1024).astype(full)
    dY = YY.reshape(1024, 1024)
    Gb = GA.reshape(1024, 512)
    dU = DU.reshape(1024, 512)
    W2 = W2.reshape(512, 1024)
    gain, bias_sum = VEC[0], VEC[1]
    cosine, sine = cosine[None, None, :, None, :], sine[None, None, :, None, :]
    gW2 = dot(Gb, dY, 0, 0)
    gW1 = dot(hb, dU, 0, 0)
    gb1 = jnp.sum(dU.astype(full), axis=0)

    R = RT.transpose(2, 3, 0, 4, 1, 5)
    Ob = (R[0, 0].astype(full) * VAL[:2]).astype(low).reshape(128, 1024)
    dqk = jnp.stack([R[0, 1], R[1, 0]]).astype(full)
    f, g = rope(dqk[:, :, :8], dqk[:, :, 8:16], cosine, -sine)
    dqk = jnp.concatenate([f, g, dqk[:, :, 16:]], axis=2).astype(low)
    dqkv = jnp.concatenate([dqk, R[1, 1][None]], axis=0).reshape(384, 1024)

    out_part = dot(Gb, W2, 1, 0) + dot(Ob, WOF, 0, 0)
    dH_part = dot(dU, W1, 1, 1) + dot(dqkv, WQT, 0, 0)
    gWo = dot(Ob, dY, 1, 0)
    gWq = dot(hb, dqkv, 0, 1)
    gbq = jnp.sum(dqkv.astype(full), axis=1)
    g_gain = jnp.sum(dH_part * xhat, axis=0)
    g_shift = jnp.sum(dH_part, axis=0)
    gb_out = jnp.sum(own_dy.astype(full), axis=0)

    place_q = lax.dynamic_update_slice(jnp.zeros((2048,), full), gbq[:128], (128 * j,))
    place_q = lax.dynamic_update_slice(place_q, gbq[128:256], (1024 + 128 * j,))
    place_v = lax.dynamic_update_slice(jnp.zeros((1024,), full), gbq[256:], (128 * j,))
    p1 = gb1.reshape(16, 1, 32)
    p1 = (p1 * (jnp.arange(8) == j).astype(full)[None, :, None]).reshape(128, 32)
    small_g = jnp.concatenate(
        [
            g_gain.reshape(128, 8), g_shift.reshape(128, 8), gb_out.reshape(128, 8),
            place_q.reshape(128, 16), place_v.reshape(128, 8), p1, jnp.zeros((128, 48), full),
        ],
        axis=1,
    ).astype(low)
    pad_g = jnp.zeros((128, 8, 128), low).at[:, 0, :].set(small_g).reshape(1024, 128)
    gq = jnp.concatenate([gWq.astype(low), pad_g], axis=1).reshape(2, 4, 2, 2, 4, 1, 8, 512)
    g1 = gW1.astype(low).reshape(2, 4, 2, 2, 4, 1, 8, 512)
    gg = jnp.concatenate([g1, gq], axis=5)
    g2 = gW2.astype(low).reshape(2, 4, 2, 2, 16, 2, 512)
    g2 = jnp.stack(
        [
            g2[:, :, :, 0].transpose(1, 2, 0, 4, 3, 5).reshape(4, 4, 2, 16, 512),
            g2[:, :, :, 1].transpose(2, 0, 1, 4, 3, 5).reshape(4, 4, 2, 16, 512),
        ]
    )
    h0 = gg[:, :, :, 0].transpose(1, 2, 0, 3, 4, 5, 6).reshape(4, 4, 4, 16, 512)
    h1 = gg[:, :, :, 1].transpose(2, 0, 1, 3, 4, 5, 6).reshape(4, 4, 4, 16, 512)
    GB = jnp.concatenate([jnp.stack([h0, h1]), g2], axis=3)
    GO = gWo.astype(low).reshape(16, 8, 2, 512).transpose(0, 2, 1, 3).reshape(16, 16, 512)
    PT = jnp.stack([out_part.astype(low).reshape(2, 4, 128, 1024), dH_part.astype(low).reshape(2, 4, 128, 1024)], axis=2)

    SUM, W2F, W1F, FO = reduce(PT, GB, GO)

    own_x = tokens[0].astype(full)
    output = (own_x + SUM[0] + bias_sum).astype(low)[None]
    om = jnp.mean(own_x, axis=-1, keepdims=True)
    oc = own_x - om
    ov = jnp.mean(oc * oc, axis=-1, keepdims=True)
    inv = lax.rsqrt(ov + norm_eps)
    ohat = oc * inv
    ng = SUM[1] * gain
    token_grad = own_dy.astype(full) + inv * (
        ng - jnp.mean(ng, axis=-1, keepdims=True) - ohat * jnp.mean(ng * ohat, axis=-1, keepdims=True)
    )
    token_grad = token_grad.astype(low)[None]

    W1F = W1F.astype(full)
    f1 = W1F[:, :8]
    f1 = f1.reshape(8, 8, 16, 32).transpose(1, 2, 0, 3).reshape(8, 4096)
    fq = W1F[:, 8:, :384].reshape(8, 8, 3, 128).transpose(1, 2, 0, 3).reshape(8, 3072)
    sm = jnp.sum(W1F[:, 8, 384:], axis=0)
    f2 = W2F.transpose(0, 2, 1, 3).reshape(32, 1024)
    fo = FO.reshape(2, 8, 512).transpose(1, 0, 2).reshape(8, 1024)
    return (
        output, token_grad, sm[0:8], sm[8:16], fq, sm[24:40], sm[40:48], fo, sm[16:24], f1, sm[48:80], f2, sm[16:24],
    )


def solution(mesh):
    rows, tok, par, vec = (
        P(("slot", "wsh")), P(("slot", "wsh"), "ctx", None), P(("slot", "ctx", "wsh"), None), P(("slot", "ctx", "wsh"))
    )
    return jax.shard_map(
        shards,
        mesh=mesh,
        in_specs=(tok, rows, vec, vec, par, vec, par, vec, par, vec, par, vec, tok),
        out_specs=(tok, tok, vec, vec, par, vec, vec, par, vec, par, vec, par, vec),
        check_vma=False,
    )
```

```python
import functools

import jax
import jax.numpy as jnp
from jax import lax
from jax.experimental import pallas as pl
from jax.experimental.pallas import tpu as pltpu
from jax.sharding import PartitionSpec as P

HEADS = 16
HD = 64
ROT = 16
HQ = 1024
D = 1024
FF = 4096
BLK = 512

norm_eps = 1e-05
rope_base = 10000.0
MESH = pl.DeviceIdType.MESH
low = jnp.bfloat16
full = jnp.float32
VM = pl.BlockSpec(memory_space=pltpu.VMEM)
AN = pl.BlockSpec(memory_space=pl.ANY)


def place():
    s = lax.axis_index("slot")
    c = lax.axis_index("ctx")
    w = lax.axis_index("wsh")
    return s, c // 8, (c // 4) % 2, c % 4, w


def dev(s, y, xh, z, w):
    return (s, y * 8 + xh * 4 + z, w)


def x_dev(x, y, z, w):
    return dev(x % 2, y, x // 2, z, w)


def signal(barrier, target):
    pl.semaphore_signal(barrier, inc=1, device_id=target, device_id_type=MESH)


def remote(src, dst, send, recv, target):
    return pltpu.make_async_remote_copy(
        src_ref=src, dst_ref=dst, send_sem=send, recv_sem=recv,
        device_id=target, device_id_type=MESH,
    )


def iota(shape, axis):
    return lax.broadcasted_iota(jnp.int32, shape, axis)


def dot(a, b, ca, cb):
    return lax.dot_general(a, b, (((ca,), (cb,)), ((), ())), preferred_element_type=full)


def core_of(m):
    return ((m + 1) // 2) % 2


def owner_lanes(params, width, lanes, step):
    f, l = iota((128, width), 1), iota((128, width), 0)
    pick = (l == lanes[0] + (f & (step - 1)))
    for other in lanes[1:]:
        pick = pick | (l == other + (f & (step - 1)))
    return dot(params, pick.astype(full).astype(low), 1, 0), f, l


def lane_mix(tiles, shifts):
    lane = iota((8, 128), 1)
    out = jnp.zeros((8, 128), full)
    for g in range(4):
        t = tiles[g]
        if shifts[g] % 128:
            t = pltpu.roll(t, shifts[g] % 128, 1)
        out = jnp.where((lane >= 32 * g) & (lane < 32 * g + 32), t, out)
    return out


def front_kernel(lens, tok, cot, smallp, wq, wo, w1, w2, cosine, sine,
                 KV, QD, HB, XH, YY, GA, DU, W1, W2, WQT, WOF, VEC, VAL,
                 XX, Q, F, Qs, Fs, wos, WO, HT,
                 zs, zr, ys, yr, ps, pr, ts, tr, fs, fr, os, orr,
                 q1s, q1r, q2s, q2r, f1s, f1r, f2s, f2r, w1s, w1r, w2s, w2r,
                 hs, kr, qr, dr, ks, krp):
    s, y, xh, z, w = place()
    x = xh * 2 + s
    r = s * 8 + y * 2 + xh
    j = z * 2 + w
    jo = r // 2
    m = y * 2 + xh
    core, spot = core_of(m), m // 2
    keep = (j == jo).astype(jnp.int32)
    mine = ((y // 2 == w) & (core == w)).astype(jnp.int32)
    sib = dev(s, y, xh, z, 1 - w)

    barrier = pltpu.get_barrier_semaphore()
    for k in range(1, 8):
        q = (j + k) % 8
        signal(barrier, dev(s, y, xh, q // 2, q % 2))
    for k in range(1, 4):
        signal(barrier, x_dev((x + k) % 4, y, z, w))
        signal(barrier, dev(s, (y + k) % 4, xh, z, w))

    def wo_source(k):
        rr = 2 * j + k // 8
        return rr // 8, (rr // 2) % 4, rr % 2, (k % 8) // 2, k % 2

    def wo_mine(k):
        ss, sy, sxh, sz, sw = wo_source(k)
        return (ss == s) & (sy == y) & (sxh == xh) & (sz == z) & (sw == w)

    for k in range(16):
        @pl.when(jnp.logical_not(wo_mine(k)))
        def _():
            signal(barrier, dev(*wo_source(k)))

    def source(i):
        return dev(s, i, (i + w) % 2, z, y // 2)

    def my_source(i):
        return (y == i) & (xh == (i + w) % 2) & (w == y // 2)

    for i in range(4):
        @pl.when(jnp.logical_not(my_source(i)))
        def _():
            signal(barrier, source(i))

    XX[w, z] = tok[0]
    row = iota((128, 1024), 0) + (m * BLK + z * 128)
    YY[w, z] = jnp.where(row < lens[0], cot[0].astype(full), 0.0).astype(low)
    first_row = iota((8, 128), 0) == 0
    padded = jnp.where(first_row, jnp.broadcast_to(smallp[0:1, :], (8, 128)), 0.0)
    for q in range(8):
        c = 128 * q
        top = jnp.concatenate([wq[:, c:c + 128], wq[:, 1024 + c:1152 + c]], axis=1)
        bot = jnp.concatenate([wq[:, 2048 + c:2176 + c], padded], axis=1)
        Qs[q] = jnp.concatenate([top, bot], axis=0).astype(low)
    wos[...] = jnp.concatenate([wo[:, :512], wo[:, 512:]], axis=0).astype(low)
    W2[s, y, xh] = w2[...].astype(low)

    pl.semaphore_wait(barrier, 7 + 6 + 16 - keep + 4 - mine)

    slot = (r % 2) * 8 + j
    tq, tf, xc, yc, oc = [], [], [], [], []
    for k in range(1, 8):
        q = (j + k) % 8
        cp = remote(Qs.at[q], Q.at[s, y, xh, j], ts.at[k], tr.at[k], dev(s, y, xh, q // 2, q % 2))
        cp.start()
        tq.append(cp)
    for k in (1, 3, 2):
        cp = remote(XX.at[w, z], XX.at[w, z], zs.at[k], zr.at[k], dev(s, y, xh, (z + k) % 4, w))
        cp.start()
        xc.append(cp)
    for q in range(8):
        tiles = []
        for g in range(4):
            parts = [w1[:, 128 * (2 * (4 * g + n) + q // 4):128 * (2 * (4 * g + n) + q // 4) + 128] for n in range(4)]
            tiles.append(lane_mix(parts, [32 * (n - q % 4) for n in range(4)]))
        top = jnp.concatenate(tiles[:2], axis=1)
        bot = jnp.concatenate(tiles[2:], axis=1)
        Fs[q] = jnp.concatenate([top, bot], axis=0).astype(low)
    for k in range(1, 8):
        q = (j + k) % 8
        cp = remote(Fs.at[q], F.at[s, y, xh, j], fs.at[k], fr.at[k], dev(s, y, xh, q // 2, q % 2))
        cp.start()
        tf.append(cp)
    Q[s, y, xh, j] = Qs[j]
    F[s, y, xh, j] = Fs[j]

    for cp in tq:
        cp.wait_recv()

    def ring1(ref0, ref1, snd, rcv):
        out = []
        for k in (1, 3, 2):
            cp = remote(ref0, ref0, snd.at[0, k], rcv.at[0, k], x_dev((x + k) % 4, y, z, w))
            cp.start()
            out.append(cp)
            cp = remote(ref1, ref1, snd.at[1, k], rcv.at[1, k], dev(s, (y + k) % 4, xh, z, w))
            cp.start()
            out.append(cp)
        return out

    def ring2(ref0, ref1, snd, rcv):
        out = []
        for k in (1, 3, 2):
            cp = remote(ref0, ref0, snd.at[0, k], rcv.at[0, k], dev(s, (y + k) % 4, xh, z, w))
            cp.start()
            out.append(cp)
            cp = remote(ref1, ref1, snd.at[1, k], rcv.at[1, k], x_dev((x + k) % 4, y, z, w))
            cp.start()
            out.append(cp)
        return out

    lo4, hi4 = pl.ds(0, 4), pl.ds(4, 4)
    lo5, hi5 = pl.ds(0, 512), pl.ds(512, 512)
    q1 = ring1(Q.at[s, y, xh, lo4], Q.at[s, y, xh, hi4], q1s, q1r)
    for k in range(16):
        q = (r + k) % 16
        cp = remote(wos, WO.at[slot], os.at[k], orr.at[slot], dev(q // 8, (q // 2) % 4, q % 2, jo // 2, jo % 2))
        oc.append(cp)
        if k == 0:
            @pl.when(j != jo)
            def _():
                cp.start()

            @pl.when(j == jo)
            def _():
                WO[slot] = wos[...]
        else:
            cp.start()
    for cp in q1:
        cp.wait_recv()
    q2 = ring2(Q.at[:, y, :, lo4], Q.at[s, :, xh, hi4], q2s, q2r)
    for cp in tf:
        cp.wait_recv()
    f1 = ring1(F.at[s, y, xh, lo4], F.at[s, y, xh, hi4], f1s, f1r)
    g1 = ring1(W2.at[s, y, xh, :, lo5], W2.at[s, y, xh, :, hi5], w1s, w1r)
    for k in (1, 3, 2):
        cp = remote(YY.at[w, z], YY.at[w, z], ys.at[k], yr.at[k], dev(s, y, xh, (z + k) % 4, w))
        cp.start()
        yc.append(cp)
    for cp in xc:
        cp.wait_recv()
    xpair = remote(XX.at[w], XX.at[w], ps.at[0], pr.at[0], sib)
    xpair.start()
    for cp in f1 + g1:
        cp.wait_recv()
    for cp in q2:
        cp.wait_recv()
    f2 = ring2(F.at[:, y, :, lo4], F.at[s, :, xh, hi4], f2s, f2r)
    g2 = ring2(W2.at[:, y, :, :, lo5], W2.at[s, :, xh, :, hi5], w2s, w2r)

    units = Q[...].reshape(128, 16, 256).astype(full)
    left = units[:, :8].reshape(1024, 256)
    right = units[:, 8:].reshape(1024, 256)
    WQT[0:256, :] = left.T.astype(low)
    WQT[256:384, :] = right[:, :128].T.astype(low)
    owner_row = (iota((128, 1024), 1) == 8 * iota((128, 1024), 0)).astype(full).astype(low)
    params = dot(owner_row, right[:, 128:].astype(low), 1, 0).astype(low)

    def row_of(lanes):
        t, f, l = owner_lanes(params, 1024, lanes, 8)
        return jnp.sum(jnp.where((f >= 8 * l) & (f < 8 * l + 8), t, 0.0), axis=0, keepdims=True)

    gain = row_of((0,))
    shift = row_of((8,))
    VEC[0:1, :] = gain
    VEC[1:2, :] = row_of((40, 80))
    t, f, l = owner_lanes(params, 512, (48,), 32)
    base = f - 4 * (l - j)
    bias_1 = jnp.sum(
        jnp.where((((l - j) & 7) == 0) & (base >= 0) & (base < 32), t, 0.0), axis=0, keepdims=True
    )
    n0, p0 = iota((384, 128), 0), iota((384, 128), 1)
    n0 = (n0 // 128) * 1024 + 128 * j + (n0 & 127)
    at = n0 - 24 * p0
    inside = ((at >= 0) & (at < 24)).astype(full)
    t = dot(inside.astype(low), params, 1, 0)
    lane_want = jnp.sum(inside * at.astype(full), axis=1, keepdims=True) + 16.0
    bias_q = jnp.sum(jnp.where(p0.astype(full) == lane_want, t, 0.0), axis=1, keepdims=True)
    lp, ll = iota((128, 128), 0), iota((128, 128), 1)
    tok_pos = (iota((1, BLK), 1) + m * BLK).astype(full)
    pf = params.astype(full)
    for i in range(2):
        here = lp == s * 64 + i
        size = jnp.sum(jnp.where(here & (ll == 88), pf, 0.0)) * 64.0 + jnp.sum(jnp.where(here & (ll == 89), pf, 0.0))
        VAL[i:i + 1, :] = jnp.where(tok_pos < size, 1.0, 0.0)

    co, si = cosine[...], sine[...]

    def norm_slot(wi):
        def one(zi, carry):
            v = XX[wi, zi].astype(full)
            mean = jnp.mean(v, axis=-1, keepdims=True)
            c = v - mean
            var = jnp.mean(c * c, axis=-1, keepdims=True)
            h = c * lax.rsqrt(var + norm_eps)
            XH[wi, zi] = h.astype(low)
            HB[wi, zi] = (h * gain + shift).astype(low)
            return carry

        lax.fori_loop(0, 4, one, 0)

    def turn(v):
        a, b = v[0:8], v[8:16]
        return jnp.concatenate([a * co - b * si, b * co + a * si, v[16:]], axis=0)

    def qkv_slot(wi):
        t = dot(WQT[...], HB[wi].reshape(BLK, 1024), 1, 1) + bias_q
        for e in range(2):
            HT[e, wi, 0, 0] = turn(t[128 + 64 * e:192 + 64 * e]).astype(low)
            HT[e, wi, 0, 1] = t[256 + 64 * e:320 + 64 * e].astype(low)
            HT[e, wi, 1, 0] = (turn(t[64 * e:64 + 64 * e]).astype(low).astype(full) * 0.125).astype(low)

    def head_target(e, i):
        return dev(s, 2 * w + e, i, z, core), (y == 2 * w + e) & (xh == i) & (core == w)

    def kv_copy(e, i):
        return remote(HT.at[e, i, 0], KV.at[core, spot], hs.at[e, i, 0], kr.at[spot], head_target(e, i)[0])

    def q_copy(e, i):
        return remote(HT.at[e, i, 1, 0], QD.at[spot, 0], hs.at[e, i, 1], qr.at[spot], head_target(e, i)[0])

    def do_copy(e, i):
        return remote(HT.at[e, i, 1, 1], QD.at[spot, 1], hs.at[e, i, 2], dr.at[spot], head_target(e, i)[0])

    def send_qkv(i):
        for e in range(2):
            me = head_target(e, i)[1]

            @pl.when(jnp.logical_not(me))
            def _():
                kv_copy(e, i).start()
                q_copy(e, i).start()

            @pl.when(me)
            def _():
                KV[core, spot] = HT[e, i, 0]
                QD[spot, 0] = HT[e, i, 1, 0]

    def send_do(i):
        t = dot(WOF[...], YY[i].reshape(BLK, 1024), 1, 1)
        for e in range(2):
            HT[e, i, 1, 1] = t[64 * e:64 + 64 * e].astype(low)
            me = head_target(e, i)[1]

            @pl.when(jnp.logical_not(me))
            def _():
                do_copy(e, i).start()

            @pl.when(me)
            def _():
                QD[spot, 1] = HT[e, i, 1, 1]

    norm_slot(w)
    qkv_slot(w)
    send_qkv(w)
    xpair.wait_recv()
    norm_slot(1 - w)
    qkv_slot(1 - w)
    send_qkv(1 - w)

    for cp in yc:
        cp.wait_recv()
    ypair = remote(YY.at[w], YY.at[w], ps.at[1], pr.at[1], sib)
    ypair.start()
    for k in range(16):
        @pl.when(jnp.logical_not(wo_mine(k)))
        def _():
            remote(wos, WO.at[k], os.at[0], orr.at[k], dev(*wo_source(k))).wait_recv()
    units = WO[...].astype(full)
    WOF[:, :512] = units[:, :8].reshape(128, 512).astype(low)
    WOF[:, 512:] = units[:, 8:].reshape(128, 512).astype(low)
    send_do(w)
    ypair.wait_recv()
    send_do(1 - w)

    for cp in f2 + g2:
        cp.wait_recv()
    units = F[...].reshape(128, 16, 256).astype(full)
    W1[:, :256] = units[:, :8].reshape(1024, 256).astype(low)
    W1[:, 256:] = units[:, 8:].reshape(1024, 256).astype(low)

    def hidden(n, carry):
        wi, zi = n // 4, n % 4
        u = dot(HB[wi, zi], W1[...], 1, 0) + bias_1
        dg = dot(YY[wi, zi], W2[...].reshape(512, 1024), 1, 1)
        c0 = 0.7978845608028654
        t = jnp.tanh(c0 * (u + 0.044715 * (u * u * u)))
        GA[wi, zi] = (0.5 * u * (1.0 + t)).astype(low)
        slope = 0.5 * (1.0 + t) + (0.5 * c0) * u * (1.0 - t * t) * (1.0 + (3.0 * 0.044715) * (u * u))
        DU[wi, zi] = (dg * slope).astype(low)
        return carry

    lax.fori_loop(0, 2, hidden, 0)
    for i in range(4):
        @pl.when(jnp.logical_not(my_source(i)))
        def _():
            remote(HT.at[0, 0, 0], KV.at[w, i], hs.at[0, 0, 0], kr.at[i], source(i)).wait_recv()
    swap = remote(KV.at[w], KV.at[w], ks, krp, sib)
    swap.start()
    lax.fori_loop(2, 8, hidden, 0)
    for i in range(4):
        @pl.when(jnp.logical_not(my_source(i)))
        def _():
            remote(HT.at[0, 0, 1, 0], QD.at[i, 0], hs.at[0, 0, 1], qr.at[i], source(i)).wait_recv()
            remote(HT.at[0, 0, 1, 1], QD.at[i, 1], hs.at[0, 0, 2], dr.at[i], source(i)).wait_recv()
    for e in range(2):
        for i in range(2):
            @pl.when(jnp.logical_not(head_target(e, i)[1]))
            def _():
                kv_copy(e, i).wait_send()
                q_copy(e, i).wait_send()
                do_copy(e, i).wait_send()

    @pl.when(j != jo)
    def _():
        oc[0].wait_send()

    for cp in oc[1:] + tq + tf + xc + yc + q1 + q2 + f1 + f2 + g1 + g2 + [xpair, ypair]:
        cp.wait_send()
    swap.wait()


def front(lens, tok, cot, smallp, wq, wo, w1, w2, cosine, sine):
    S = pltpu.SemaphoreType.DMA
    V = pltpu.VMEM
    sds = jax.ShapeDtypeStruct
    return pl.pallas_call(
        front_kernel,
        name="front",
        out_shape=(
            sds((2, 4, 2, 64, BLK), low),
            sds((4, 2, 64, BLK), low),
            sds((2, 4, 128, 1024), low),
            sds((2, 4, 128, 1024), low),
            sds((2, 4, 128, 1024), low),
            sds((2, 4, 128, 512), low),
            sds((2, 4, 128, 512), low),
            sds((1024, 512), low),
            sds((2, 4, 2, 32, 1024), low),
            sds((384, 1024), low),
            sds((128, 1024), low),
            sds((8, 1024), full),
            sds((8, BLK), full),
        ),
        in_specs=[pl.BlockSpec(memory_space=pltpu.SMEM)] + [VM] * 9,
        out_specs=(VM,) * 13,
        scratch_shapes=[
            V((2, 4, 128, 1024), low),
            V((2, 4, 2, 8, 16, 256), low),
            V((2, 4, 2, 8, 16, 256), low),
            V((8, 16, 256), low),
            V((8, 16, 256), low),
            V((16, 512), low),
            V((16, 16, 512), low),
            V((2, 2, 2, 2, 64, BLK), low),
            S((4,)), S((4,)), S((4,)), S((4,)), S((2,)), S((2,)), S((8,)), S((8,)), S((8,)), S((8,)),
            S((16,)), S((16,)),
            S((2, 4)), S((2, 4)), S((2, 4)), S((2, 4)), S((2, 4)), S((2, 4)), S((2, 4)), S((2, 4)),
            S((2, 4)), S((2, 4)), S((2, 4)), S((2, 4)),
            S((2, 2, 3)), S((4,)), S((4,)), S((4,)), S, S,
        ],
        compiler_params=pltpu.CompilerParams(
            collective_id=0, has_side_effects=True, vmem_limit_bytes=56 << 20
        ),
    )(lens, tok, cot, smallp, wq, wo, w1, w2, cosine, sine)


def attend_kernel(KV, QD, OQ, DKV, acc):
    w = lax.axis_index("wsh")
    acc[...] = jnp.zeros_like(acc)
    causal = lax.broadcasted_iota(jnp.int32, (BLK, BLK), 0) <= lax.broadcasted_iota(
        jnp.int32, (BLK, BLK), 1
    )

    def query_block(i, carry):
        m = 2 * i + (i + w) % 2
        q = QD[i, 0]
        do = QD[i, 1]

        def fwd(n, state, masked):
            run_max, total, out = state
            c, t = core_of(n), n // 2
            sc = dot(KV[c, t, 0], q, 0, 0)
            if masked:
                sc = jnp.where(causal, sc, -1e30)
            new_max = jnp.maximum(run_max, jnp.max(sc, axis=0, keepdims=True))
            pr = jnp.exp(sc - new_max)
            fac = jnp.exp(run_max - new_max)
            total = total * fac + jnp.sum(pr, axis=0, keepdims=True)
            out = out * fac + dot(KV[c, t, 1], pr.astype(low), 1, 0)
            return new_max, total, out

        start = (
            jnp.full((1, BLK), -1e30, full),
            jnp.zeros((1, BLK), full),
            jnp.zeros((HD, BLK), full),
        )
        state = lax.fori_loop(0, m, lambda n, st: fwd(n, st, False), start)
        run_max, total, out = fwd(m, state, True)
        out = out / total
        lse = run_max + jnp.log(total)
        OQ[i, 0] = out.astype(low)
        delta = jnp.sum(do.astype(full) * out, axis=0, keepdims=True)

        def bwd(n, dq, masked):
            c, t = core_of(n), n // 2
            k = KV[c, t, 0]
            sc = dot(k, q, 0, 0)
            pr = jnp.exp(sc - lse)
            if masked:
                pr = jnp.where(causal, pr, 0.0)
            dp = dot(KV[c, t, 1], do, 0, 0)
            ds = (pr * (dp - delta)).astype(low)
            acc[c, t, 0] += dot(q, ds, 1, 1)
            acc[c, t, 1] += dot(do, pr.astype(low), 1, 1)
            return dq + dot(k, ds, 1, 0)

        dq = lax.fori_loop(0, m, lambda n, st: bwd(n, st, False), jnp.zeros((HD, BLK), full))
        dq = bwd(m, dq, True)
        OQ[i, 1] = (dq * 0.125).astype(low)
        return carry

    lax.fori_loop(0, 4, query_block, 0)
    for c in range(2):
        for t in range(4):
            DKV[c, t] = acc[c, t].astype(low)


def attend(KV, QD):
    return pl.pallas_call(
        attend_kernel,
        name="attend",
        out_shape=(
            jax.ShapeDtypeStruct((4, 2, 64, BLK), low),
            jax.ShapeDtypeStruct((2, 4, 2, 64, BLK), low),
        ),
        in_specs=[VM, VM],
        out_specs=(VM, VM),
        scratch_shapes=[pltpu.VMEM((2, 4, 2, 64, BLK), full)],
        compiler_params=pltpu.CompilerParams(vmem_limit_bytes=48 << 20),
    )(KV, QD)


def back_kernel(tok, OQ, DKV, HB, XH, YY, GA, DU, W1, W2, WQT, WOF, VEC, VAL, cosine, sine,
                OUT, TG, GQKV, GFC1, GFC2, GWO, SM,
                RT, got, summed, PO, PH, DQ, TO, TH, pin, zin, GF, GQ, GW, gi0, gi1, wi0, wi1, gm, wm, gi2, wi2,
                Ff, Qf, RF, RQ, GO, fo_in,
                ks, kr, hs, hr, ps, pr, zs, zr, os, orr,
                g1s, g1r, g2s, g2r, ts, tr):
    s, y, xh, z, w = place()
    x = xh * 2 + s
    r = s * 8 + y * 2 + xh
    j = z * 2 + w
    jo = r // 2
    m = y * 2 + xh
    core = core_of(m)
    keep = (j == jo).astype(jnp.int32)
    mine = ((y // 2 == w) & (core == w)).astype(jnp.int32)
    sib = dev(s, y, xh, z, 1 - w)
    e_me, i_me = y % 2, xh
    lo4, hi4 = pl.ds(0, 4), pl.ds(4, 4)
    lo5, hi5 = pl.ds(0, 512), pl.ds(512, 512)

    barrier = pltpu.get_barrier_semaphore()
    for k in range(1, 8):
        q = (j + k) % 8
        signal(barrier, dev(s, y, xh, q // 2, q % 2))
    for k in range(1, 4):
        signal(barrier, x_dev((x + k) % 4, y, z, w))
        signal(barrier, dev(s, (y + k) % 4, xh, z, w))

    def sender(q):
        return dev(q // 8, (q // 2) % 4, q % 2, jo // 2, jo % 2)

    for k in range(16):
        q = (r + k) % 16
        if k == 0:
            @pl.when(j != jo)
            def _():
                signal(barrier, sender(q))
        else:
            signal(barrier, sender(q))

    def home(i):
        return dev(s, i, (i + w) % 2, z, y // 2)

    def at_home(i):
        return (y == i) & (xh == (i + w) % 2) & (w == y // 2)

    def head_at(e, i):
        return dev(s, 2 * w + e, i, z, core)

    def head_here(e, i):
        return (y == 2 * w + e) & (xh == i) & (core == w)

    for e in range(2):
        for i in range(2):
            @pl.when(jnp.logical_not(head_here(e, i)))
            def _():
                signal(barrier, head_at(e, i))
    pl.semaphore_wait(barrier, 7 + 6 + 16 - keep + 4 - mine)

    swap = remote(DKV.at[1 - w], got, ks, kr, sib)
    swap.start()
    for i in range(4):
        @pl.when(jnp.logical_not(at_home(i)))
        def _():
            remote(OQ.at[i], RT.at[e_me, i_me, 0], hs.at[i, 0], hr.at[e_me, i_me, 0], home(i)).start()

        @pl.when(at_home(i))
        def _():
            RT[e_me, i_me, 0] = OQ[i]

    ga = GA[...].reshape(1024, 512)

    def first_w2(h):
        t = dot(ga, YY[:, :, :, 512 * h:512 * h + 512].reshape(1024, 512), 0, 0).astype(low)
        GW[:, :, :, :, 512 * h:512 * h + 512] = t.reshape(2, 4, 2, 32, 512)
        out = []
        for k in (1, 3, 2):
            yy, xx = (y + k) % 4, (x + k) % 4
            if h == 0:
                cp = remote(GW.at[:, yy, :, :, lo5], wi0.at[k], g1s.at[2, 0, k], g1r.at[2, 0, k], dev(s, yy, xh, z, w))
            else:
                cp = remote(GW.at[xx % 2, :, xx // 2, :, hi5], wi1.at[k], g1s.at[2, 1, k], g1r.at[2, 1, k], x_dev(xx, y, z, w))
            cp.start()
            out.append(cp)
        return out

    def first_unit(g, buf):
        out = []
        for k in (1, 3, 2):
            yy, xx = (y + k) % 4, (x + k) % 4
            cp = remote(buf.at[:, yy, :, lo4], gi0.at[g, k], g1s.at[g, 0, k], g1r.at[g, 0, k], dev(s, yy, xh, z, w))
            cp.start()
            out.append(cp)
            cp = remote(buf.at[xx % 2, :, xx // 2, hi4], gi1.at[g, k], g1s.at[g, 1, k], g1r.at[g, 1, k], x_dev(xx, y, z, w))
            cp.start()
            out.append(cp)
        return out

    def add4(a, b, c, d):
        return a.astype(full) + b.astype(full) + c.astype(full) + d.astype(full)

    def second_unit(g, buf):
        gm[g, 0] = add4(
            buf[:, y, :, 0:4], gi0[g, 1], gi0[g, 2], gi0[g, 3]
        ).astype(low).reshape(4, 4, 16, 256)
        gm[g, 1] = add4(
            buf[s, :, xh, 4:8], gi1[g, 1], gi1[g, 2], gi1[g, 3]
        ).astype(low)
        out = []
        for k in (1, 3, 2):
            yy, xx = (y + k) % 4, (x + k) % 4
            cp = remote(gm.at[g, 0, 2 * (xx % 2) + xx // 2], gi2.at[g, 0, k], g2s.at[g, 0, k], g2r.at[g, 0, k], x_dev(xx, y, z, w))
            cp.start()
            out.append(cp)
            cp = remote(gm.at[g, 1, yy], gi2.at[g, 1, k], g2s.at[g, 1, k], g2r.at[g, 1, k], dev(s, yy, xh, z, w))
            cp.start()
            out.append(cp)
        return out

    def second_w2():
        wm[0] = add4(GW[:, y, :, :, :512], wi0[1], wi0[2], wi0[3]).astype(low).reshape(4, 32, 512)
        wm[1] = add4(GW[s, :, xh, :, 512:], wi1[1], wi1[2], wi1[3]).astype(low)
        out = []
        for k in (1, 3, 2):
            yy, xx = (y + k) % 4, (x + k) % 4
            cp = remote(wm.at[0, 2 * (xx % 2) + xx // 2], wi2.at[0, k], g2s.at[2, 0, k], g2r.at[2, 0, k], x_dev(xx, y, z, w))
            cp.start()
            out.append(cp)
            cp = remote(wm.at[1, yy], wi2.at[1, k], g2s.at[2, 1, k], g2r.at[2, 1, k], dev(s, yy, xh, z, w))
            cp.start()
            out.append(cp)
        return out

    def last_unit(g, fin, got_units):
        fin[0:4] = add4(gm[g, 0, 2 * s + xh], gi2[g, 0, 1], gi2[g, 0, 2], gi2[g, 0, 3]).astype(low)
        fin[4:8] = add4(gm[g, 1, y], gi2[g, 1, 1], gi2[g, 1, 2], gi2[g, 1, 3]).astype(low)
        out = []
        for k in range(1, 8):
            q = (j + k) % 8
            cp = remote(fin.at[q], got_units.at[j], ts.at[g, k], tr.at[g, k], dev(s, y, xh, q // 2, q % 2))
            cp.start()
            out.append(cp)
        got_units[j] = fin[j]
        return out

    c_w2 = first_w2(0)
    c_w2 += first_w2(1)

    swap.wait_recv()
    for i in range(4):
        summed[i] = (DKV[w, i].astype(full) + got[i].astype(full)).astype(low)

        @pl.when(jnp.logical_not(at_home(i)))
        def _():
            remote(summed.at[i], RT.at[e_me, i_me, 1], hs.at[i, 1], hr.at[e_me, i_me, 1], home(i)).start()

        @pl.when(at_home(i))
        def _():
            RT[e_me, i_me, 1] = summed[i]

    du = DU[...].reshape(1024, 512)
    for n in range(4):
        t = dot(HB[:, :, :, 256 * n:256 * n + 256].reshape(1024, 256), du, 0, 0)
        t = jnp.concatenate([t[:, :256].reshape(32, 8, 256), t[:, 256:].reshape(32, 8, 256)], axis=1)
        GF[n // 2, 2 * (n % 2):2 * (n % 2) + 2] = t.astype(low).reshape(2, 2, 8, 16, 256)
    c_f = first_unit(0, GF)
    gb1 = jnp.sum(du.astype(full), axis=0, keepdims=True)
    gb_out = jnp.sum(YY[w, z].astype(full), axis=0, keepdims=True)

    def mlp_parts(i, carry):
        PO[i] = dot(GA[i].reshape(BLK, 512), W2[...].reshape(512, 1024), 1, 0)
        PH[i] = dot(DU[i].reshape(BLK, 512), W1[...], 1, 1)
        return carry

    lax.fori_loop(0, 2, mlp_parts, 0)

    def wait_heads(g):
        for e in range(2):
            for i in range(2):
                @pl.when(jnp.logical_not(head_here(e, i)))
                def _():
                    remote(summed.at[0], RT.at[e, i, g], hs.at[0, g], hr.at[e, i, g], head_at(e, i)).wait_recv()

    wait_heads(0)

    def ob_of(i):
        t = jnp.concatenate([RT[0, i, 0, 0], RT[1, i, 0, 0]], axis=0).astype(full)
        return (t * VAL[pl.ds(i, 1), :]).astype(low)

    def out_slot(i):
        ob = ob_of(i)
        t = dot(ob, WOF[...], 0, 0) + PO[i]
        TO[i] = t.astype(low).reshape(4, 128, 1024)
        return dot(ob, YY[i].reshape(BLK, 1024), 1, 0)

    g_wo = out_slot(1 - w)
    opair = remote(TO.at[1 - w], pin.at[0], ps.at[0], pr.at[0], sib)
    opair.start()
    g_wo = g_wo + out_slot(w)
    GO[...] = jnp.concatenate(
        [g_wo[:, :512].reshape(16, 8, 512), g_wo[:, 512:].reshape(16, 8, 512)], axis=1
    ).astype(low)

    def owner(k):
        rr = 2 * j + k // 8
        return rr // 8, (rr // 2) % 4, rr % 2, (k % 8) // 2, k % 2

    def owner_copy(k):
        os_, oy, oxh, oz, ow = owner(k)
        me = (os_ == s) & (oy == y) & (oxh == xh) & (oz == z) & (ow == w)
        return remote(GO.at[k], fo_in.at[r], os.at[k], orr.at[r], dev(os_, oy, oxh, oz, ow)), me

    for cp in c_w2 + c_f:
        cp.wait_recv()
    d_w2 = second_w2()
    d_f = second_unit(0, GF)

    co, si = cosine[...], sine[...]

    def turn_back(v):
        a, b = v[0:8], v[8:16]
        return jnp.concatenate([a * co + b * si, b * co - a * si, v[16:]], axis=0)

    wait_heads(1)

    def dh_slot(i):
        for e in range(2):
            DQ[i, 64 * e:64 * e + 64] = turn_back(RT[e, i, 0, 1].astype(full)).astype(low)
            DQ[i, 128 + 64 * e:192 + 64 * e] = turn_back(RT[e, i, 1, 0].astype(full)).astype(low)
            DQ[i, 256 + 64 * e:320 + 64 * e] = RT[e, i, 1, 1]
        t = dot(DQ[i], WQT[...], 0, 0) + PH[i]
        TH[i] = t.astype(low).reshape(4, 128, 1024)
        g_shift = jnp.sum(t, axis=0, keepdims=True)
        g_gain = jnp.sum(t * XH[i].reshape(BLK, 1024).astype(full), axis=0, keepdims=True)
        return g_shift, g_gain, jnp.sum(DQ[i].astype(full), axis=1, keepdims=True)

    a_shift, a_gain, a_bq = dh_slot(1 - w)
    hpair = remote(TH.at[1 - w], pin.at[1], ps.at[1], pr.at[1], sib)
    hpair.start()
    opair.wait_recv()

    def pair_z(n, buf):
        def one(t, carry):
            buf[w, t] = (buf[w, t].astype(full) + pin[n, t].astype(full)).astype(low)
            return carry

        lax.fori_loop(0, 4, one, 0)
        out = []
        for k in (1, 3, 2):
            zz = (z + k) % 4
            cp = remote(buf.at[w, zz], zin.at[n, k], zs.at[n, k], zr.at[n, k], dev(s, y, xh, zz, w))
            cp.start()
            out.append(cp)
        return out

    zo = pair_z(0, TO)
    b_shift, b_gain, b_bq = dh_slot(w)
    for k in range(16):
        cp, me = owner_copy(k)

        @pl.when(jnp.logical_not(me))
        def _():
            cp.start()

        @pl.when(me)
        def _():
            fo_in[r] = GO[k]
    hpair.wait_recv()
    zh = pair_z(1, TH)

    gq = dot(DQ[0], HB[0].reshape(BLK, 1024), 1, 0) + dot(DQ[1], HB[1].reshape(BLK, 1024), 1, 0)
    d0, p0 = iota((128, 1024), 1), iota((128, 1024), 0)
    block = (d0 >= 8 * p0) & (d0 < 8 * p0 + 8)
    dt, lt = iota((1024, 128), 0), iota((1024, 128), 1)

    def spread_row(v, lane):
        a = jnp.where(block, jnp.broadcast_to(v, (128, 1024)), 0.0).astype(low)
        return dot(a, (lt == lane + (dt & 7)).astype(full).astype(low), 1, 0)

    small = spread_row(a_gain + b_gain, 0) + spread_row(a_shift + b_shift, 8) + spread_row(gb_out, 16)
    f0, pf = iota((128, 512), 1), iota((128, 512), 0)
    base = f0 - 4 * (pf - j)
    a = jnp.where(
        (((pf - j) & 7) == 0) & (base >= 0) & (base < 32), jnp.broadcast_to(gb1, (128, 512)), 0.0
    ).astype(low)
    ft, lf = iota((512, 128), 0), iota((512, 128), 1)
    small = small + dot(a, (lf == 48 + (ft & 31)).astype(full).astype(low), 1, 0)
    n0, pn = iota((128, 384), 1), iota((128, 384), 0)
    qk_at = (n0 // 128) * 1024 + 128 * j + (n0 & 127) - 16 * pn
    v_at = 128 * j + (n0 & 127) - 8 * pn
    owns = ((n0 < 256) & (qk_at >= 0) & (qk_at < 16)) | ((n0 >= 256) & (v_at >= 0) & (v_at < 8))
    nt, ln = iota((384, 128), 0), iota((384, 128), 1)
    lane = jnp.where(nt < 256, 24 + (nt & 15), 40 + (nt & 7))
    b = jnp.where(ln == lane, jnp.broadcast_to(a_bq + b_bq, (384, 128)), 0.0).astype(low)
    small = small + dot(owns.astype(full).astype(low), b, 1, 0)
    head_row = (dt == 8 * lt).astype(full).astype(low)
    pad = dot(head_row, small.astype(low), 1, 0)
    left = gq[:256].T
    right = jnp.concatenate([gq[256:].T, pad], axis=1)
    GQ[...] = jnp.concatenate(
        [left.reshape(128, 8, 256), right.reshape(128, 8, 256)], axis=1
    ).astype(low).reshape(2, 4, 2, 8, 16, 256)
    c_q = first_unit(1, GQ)

    for cp in d_w2 + d_f:
        cp.wait_recv()
    GFC2[:, :512] = add4(wm[0, 2 * s + xh], wi2[0, 1], wi2[0, 2], wi2[0, 3])
    GFC2[:, 512:] = add4(wm[1, y], wi2[1, 1], wi2[1, 2], wi2[1, 3])
    t_f = last_unit(0, Ff, RF)

    for q in range(16):
        @pl.when(jnp.logical_not((q == r) & (j == jo)))
        def _():
            remote(GO.at[0], fo_in.at[q], os.at[0], orr.at[q], sender(q)).wait_recv()
    t = lax.fori_loop(0, 16, lambda q, t: t + fo_in[q].astype(full), jnp.zeros((16, 512), full))
    GWO[:, :512] = t[:8]
    GWO[:, 512:] = t[8:]

    for cp in c_q:
        cp.wait_recv()
    d_q = second_unit(1, GQ)

    for cp in t_f:
        cp.wait_recv()
    for rr in range(16):
        g = rr // 4
        c, half = g // 2, g % 2
        for hi in range(2):
            tiles = [RF[4 * hi + n, 8 * c:8 * c + 8, 128 * half:128 * half + 128].astype(full) for n in range(4)]
            col = 128 * (2 * rr + hi)
            GFC1[:, col:col + 128] = lane_mix(tiles, [32 * (n - rr % 4) for n in range(4)])

    for cp in zo:
        cp.wait_recv()
    mine_x = tok[0].astype(full)
    t = add4(TO[w, z], zin[0, 1], zin[0, 2], zin[0, 3])
    OUT[0] = (mine_x + t + VEC[1:2, :]).astype(low)

    for cp in d_q:
        cp.wait_recv()
    t_q = last_unit(1, Qf, RQ)

    for cp in zh:
        cp.wait_recv()
    gh = add4(TH[w, z], zin[1, 1], zin[1, 2], zin[1, 3])
    mean = jnp.mean(mine_x, axis=-1, keepdims=True)
    cen = mine_x - mean
    inv = lax.rsqrt(jnp.mean(cen * cen, axis=-1, keepdims=True) + norm_eps)
    hat = cen * inv
    gx = gh * VEC[0:1, :]
    gx = gx - jnp.mean(gx, axis=-1, keepdims=True) - hat * jnp.mean(gx * hat, axis=-1, keepdims=True)
    TG[0] = (YY[w, z].astype(full) + inv * gx).astype(low)

    for cp in t_q:
        cp.wait_recv()
    tail = jnp.zeros((8, 128), full)
    for q in range(8):
        c = 128 * q
        GQKV[:, c:c + 128] = RQ[q, 0:8, 0:128].astype(full)
        GQKV[:, 1024 + c:1152 + c] = RQ[q, 0:8, 128:256].astype(full)
        GQKV[:, 2048 + c:2176 + c] = RQ[q, 8:16, 0:128].astype(full)
        tail = tail + RQ[q, 8:16, 128:256].astype(full)
    SM[...] = tail

    for i in range(4):
        @pl.when(jnp.logical_not(at_home(i)))
        def _():
            for g in range(2):
                remote(summed.at[i], RT.at[e_me, i_me, g], hs.at[i, g], hr.at[e_me, i_me, g], home(i)).wait_send()
    for k in range(16):
        cp, me = owner_copy(k)

        @pl.when(jnp.logical_not(me))
        def _():
            cp.wait_send()
    for cp in [swap, opair, hpair] + zo + zh + c_w2 + c_f + c_q + d_w2 + d_f + d_q + t_f + t_q:
        cp.wait_send()


def back(*args):
    S = pltpu.SemaphoreType.DMA
    V = pltpu.VMEM
    sds = jax.ShapeDtypeStruct
    return pl.pallas_call(
        back_kernel,
        name="back",
        out_shape=(
            sds((1, 128, 1024), low),
            sds((1, 128, 1024), low),
            sds((8, 3072), full),
            sds((8, 4096), full),
            sds((32, 1024), full),
            sds((8, 1024), full),
            sds((8, 128), full),
        ),
        in_specs=[VM] * 16,
        out_specs=(VM,) * 7,
        scratch_shapes=[
            V((2, 2, 2, 2, 64, BLK), low),
            V((4, 2, 64, BLK), low),
            V((4, 2, 64, BLK), low),
            V((2, BLK, 1024), full),
            V((2, BLK, 1024), full),
            V((2, 384, BLK), low),
            V((2, 4, 128, 1024), low),
            V((2, 4, 128, 1024), low),
            V((2, 4, 128, 1024), low),
            V((2, 4, 128, 1024), low),
            V((2, 4, 2, 8, 16, 256), low),
            V((2, 4, 2, 8, 16, 256), low),
            V((2, 4, 2, 32, 1024), low),
            V((2, 4, 2, 2, 4, 16, 256), low),
            V((2, 4, 4, 4, 16, 256), low),
            V((4, 2, 2, 32, 512), low),
            V((4, 4, 32, 512), low),
            V((2, 2, 4, 4, 16, 256), low),
            V((2, 4, 32, 512), low),
            V((2, 2, 4, 4, 16, 256), low),
            V((2, 4, 32, 512), low),
            V((8, 16, 256), low),
            V((8, 16, 256), low),
            V((8, 16, 256), low),
            V((8, 16, 256), low),
            V((16, 16, 512), low),
            V((16, 16, 512), low),
            S, S, S((4, 2)), S((2, 2, 2)), S((2,)), S((2,)), S((2, 4)), S((2, 4)), S((16,)), S((16,)),
            S((3, 2, 4)), S((3, 2, 4)), S((3, 2, 4)), S((3, 2, 4)), S((2, 8)), S((2, 8)),
        ],
        compiler_params=pltpu.CompilerParams(
            collective_id=1, has_side_effects=True, vmem_limit_bytes=60 << 20
        ),
    )(*args)


def shards(
    tokens, lengths, ln_gain, ln_bias, w_qkv, b_qkv, w_out, b_out, w_fc1, b_fc1, w_fc2, b_fc2, cotangent
):
    s, y, xh, z, w = place()
    j = z * 2 + w
    m = y * 2 + xh
    small = jnp.concatenate(
        [
            ln_gain, ln_bias, b_qkv, b_out, b_fc1, b_fc2,
            (lengths // 64).astype(full), (lengths % 64).astype(full), jnp.zeros((38,), full),
        ]
    )[None]
    pos = (m * BLK + jnp.arange(BLK)).astype(full)
    freq = jnp.power(rope_base, -2.0 * jnp.arange(8).astype(full) / ROT)
    angle = freq[:, None] * pos[None, :]
    cosine, sine = jnp.cos(angle), jnp.sin(angle)

    KV, QD, HB, XH, YY, GA, DU, W1, W2, WQT, WOF, VEC, VAL = front(
        lengths, tokens, cotangent, small, w_qkv, w_out, w_fc1, w_fc2, cosine, sine
    )
    OQ, DKV = attend(KV, QD)
    OUT, TG, GQKV, GFC1, GFC2, GWO, SM = back(
        tokens, OQ, DKV, HB, XH, YY, GA, DU, W1, W2, WQT, WOF, VEC, VAL, cosine, sine
    )
    sm = SM[0]
    return (
        OUT, TG, sm[0:8], sm[8:16], GQKV, sm[24:40], sm[40:48], GWO, sm[16:24], GFC1, sm[48:80], GFC2, sm[16:24],
    )


def solution(mesh):
    rows, tok, par, vec = (
        P(("slot", "wsh")), P(("slot", "wsh"), "ctx", None), P(("slot", "ctx", "wsh"), None), P(("slot", "ctx", "wsh"))
    )
    return jax.shard_map(
        shards,
        mesh=mesh,
        in_specs=(tok, rows, vec, vec, par, vec, par, vec, par, vec, par, vec, tok),
        out_specs=(tok, tok, vec, vec, par, vec, vec, par, vec, par, vec, par, vec),
        check_vma=False,
    )
```

```python
import functools

import jax
import jax.numpy as jnp
from jax import lax
from jax.experimental import pallas as pl
from jax.experimental.pallas import tpu as pltpu
from jax.sharding import PartitionSpec as P

HEADS = 16
HD = 64
ROT = 16
HQ = 1024
D = 1024
FF = 4096
BLK = 512

norm_eps = 1e-05
rope_base = 10000.0
MESH = pl.DeviceIdType.MESH
low = jnp.bfloat16
full = jnp.float32
VM = pl.BlockSpec(memory_space=pltpu.VMEM)
AN = pl.BlockSpec(memory_space=pl.ANY)


def place():
    s = lax.axis_index("slot")
    c = lax.axis_index("ctx")
    w = lax.axis_index("wsh")
    return s, c // 8, (c // 4) % 2, c % 4, w


def dev(s, y, xh, z, w):
    return (s, y * 8 + xh * 4 + z, w)


def x_dev(x, y, z, w):
    return dev(x % 2, y, x // 2, z, w)


def signal(barrier, target):
    pl.semaphore_signal(barrier, inc=1, device_id=target, device_id_type=MESH)


def remote(src, dst, send, recv, target):
    return pltpu.make_async_remote_copy(
        src_ref=src, dst_ref=dst, send_sem=send, recv_sem=recv,
        device_id=target, device_id_type=MESH,
    )


def iota(shape, axis):
    return lax.broadcasted_iota(jnp.int32, shape, axis)


def dot(a, b, ca, cb):
    return lax.dot_general(a, b, (((ca,), (cb,)), ((), ())), preferred_element_type=full)


def core_of(m):
    return ((m + 1) // 2) % 2


def owner_lanes(params, width, lanes, step):
    f, l = iota((128, width), 1), iota((128, width), 0)
    pick = (l == lanes[0] + (f & (step - 1)))
    for other in lanes[1:]:
        pick = pick | (l == other + (f & (step - 1)))
    return dot(params, pick.astype(full).astype(low), 1, 0), f, l


def lane_mix(tiles, shifts):
    lane = iota((8, 128), 1)
    out = jnp.zeros((8, 128), full)
    for g in range(4):
        t = tiles[g]
        if shifts[g] % 128:
            t = pltpu.roll(t, shifts[g] % 128, 1)
        out = jnp.where((lane >= 32 * g) & (lane < 32 * g + 32), t, out)
    return out


def layer_kernel(
    lens, tok, cot, smallp, wq, wo, w1, w2, cosine, sine, OUT, TG, RF, RQ, GFC2, GWO, XX, YY, HB, XH, GA, DU,
    W1, W2, WQT, WOF, VEC, VAL, KV, QD, Q, F, Qs, Fs, wos, WO, HT, OF, OB, LSE, DLT, RO, RQ1, RKV, acc,
    acc_own, dqa, DQB, other, got, summed, PH, DQ, TO, TH, pin, zin, GF, GQ, GW, gi0, gi1, wi0, wi1, gm, wm,
    gi2, wi2, Ff, Qf, GO, fo_in, zs, zr, ys, yr, ps, pr, ts, tr, fs, fr, os, orr, q1s, q1r, q2s, q2r, f1s, f1r,
    f2s, f2r, w1s, w1r, w2s, w2r, hs, kr, qr, dr, ks, krp, bs, br, br2, pps, ppr, kss, ksr, gos, gor, zzs, zzr,
    g1s, g1r, g2s, g2r, tts, ttr,
):
    s, y, xh, z, w = place()
    x = xh * 2 + s
    r = s * 8 + y * 2 + xh
    j = z * 2 + w
    jo = r // 2
    m = y * 2 + xh
    core, spot = core_of(m), m // 2
    keep = (j == jo).astype(jnp.int32)
    mine = ((y // 2 == w) & (core == w)).astype(jnp.int32)
    sib = dev(s, y, xh, z, 1 - w)

    barrier = pltpu.get_barrier_semaphore()
    for k in range(1, 8):
        q = (j + k) % 8
        signal(barrier, dev(s, y, xh, q // 2, q % 2))
    for k in range(1, 4):
        signal(barrier, x_dev((x + k) % 4, y, z, w))
        signal(barrier, dev(s, (y + k) % 4, xh, z, w))

    def wo_source(k):
        rr = 2 * j + k // 8
        return rr // 8, (rr // 2) % 4, rr % 2, (k % 8) // 2, k % 2

    def wo_mine(k):
        ss, sy, sxh, sz, sw = wo_source(k)
        return (ss == s) & (sy == y) & (sxh == xh) & (sz == z) & (sw == w)

    for k in range(16):
        @pl.when(jnp.logical_not(wo_mine(k)))
        def _():
            signal(barrier, dev(*wo_source(k)))

    def source(i):
        return dev(s, i, (i + w) % 2, z, y // 2)

    def my_source(i):
        return (y == i) & (xh == (i + w) % 2) & (w == y // 2)

    for i in range(4):
        @pl.when(jnp.logical_not(my_source(i)))
        def _():
            signal(barrier, source(i))

    def sender(q):
        return dev(q // 8, (q // 2) % 4, q % 2, jo // 2, jo % 2)

    def home(i):
        return dev(s, i, (i + w) % 2, z, y // 2)

    def at_home(i):
        return (y == i) & (xh == (i + w) % 2) & (w == y // 2)

    def head_at(e, i):
        return dev(s, 2 * w + e, i, z, core)

    def head_here(e, i):
        return (y == 2 * w + e) & (xh == i) & (core == w)

    e_me, i_me = y % 2, xh
    XX[w, z] = tok[0]
    row = iota((128, 1024), 0) + (m * BLK + z * 128)
    YY[w, z] = jnp.where(row < lens[0], cot[0].astype(full), 0.0).astype(low)
    first_row = iota((8, 128), 0) == 0
    padded = jnp.where(first_row, jnp.broadcast_to(smallp[0:1, :], (8, 128)), 0.0)
    for q in range(8):
        c = 128 * q
        top = jnp.concatenate([wq[:, c:c + 128], wq[:, 1024 + c:1152 + c]], axis=1)
        bot = jnp.concatenate([wq[:, 2048 + c:2176 + c], padded], axis=1)
        Qs[q] = jnp.concatenate([top, bot], axis=0).astype(low)
    wos[...] = jnp.concatenate([wo[:, :512], wo[:, 512:]], axis=0).astype(low)
    W2[s, y, xh] = w2[...].astype(low)

    pl.semaphore_wait(barrier, 7 + 6 + 16 - keep + 4 - mine)

    slot = (r % 2) * 8 + j
    tq, tf, xc, yc, oc = [], [], [], [], []
    for k in range(1, 8):
        q = (j + k) % 8
        cp = remote(Qs.at[q], Q.at[s, y, xh, j], ts.at[k], tr.at[k], dev(s, y, xh, q // 2, q % 2))
        cp.start()
        tq.append(cp)
    for k in (1, 3, 2):
        cp = remote(XX.at[w, z], XX.at[w, z], zs.at[k], zr.at[k], dev(s, y, xh, (z + k) % 4, w))
        cp.start()
        xc.append(cp)
    for q in range(8):
        tiles = []
        for g in range(4):
            parts = [w1[:, 128 * (2 * (4 * g + n) + q // 4):128 * (2 * (4 * g + n) + q // 4) + 128] for n in range(4)]
            tiles.append(lane_mix(parts, [32 * (n - q % 4) for n in range(4)]))
        top = jnp.concatenate(tiles[:2], axis=1)
        bot = jnp.concatenate(tiles[2:], axis=1)
        Fs[q] = jnp.concatenate([top, bot], axis=0).astype(low)
    for k in range(1, 8):
        q = (j + k) % 8
        cp = remote(Fs.at[q], F.at[s, y, xh, j], fs.at[k], fr.at[k], dev(s, y, xh, q // 2, q % 2))
        cp.start()
        tf.append(cp)
    Q[s, y, xh, j] = Qs[j]
    F[s, y, xh, j] = Fs[j]

    for cp in tq:
        cp.wait_recv()

    def ring1(ref0, ref1, snd, rcv):
        out = []
        for k in (1, 3, 2):
            cp = remote(ref0, ref0, snd.at[0, k], rcv.at[0, k], x_dev((x + k) % 4, y, z, w))
            cp.start()
            out.append(cp)
            cp = remote(ref1, ref1, snd.at[1, k], rcv.at[1, k], dev(s, (y + k) % 4, xh, z, w))
            cp.start()
            out.append(cp)
        return out

    def ring2(ref0, ref1, snd, rcv):
        out = []
        for k in (1, 3, 2):
            cp = remote(ref0, ref0, snd.at[0, k], rcv.at[0, k], dev(s, (y + k) % 4, xh, z, w))
            cp.start()
            out.append(cp)
            cp = remote(ref1, ref1, snd.at[1, k], rcv.at[1, k], x_dev((x + k) % 4, y, z, w))
            cp.start()
            out.append(cp)
        return out

    lo4, hi4 = pl.ds(0, 4), pl.ds(4, 4)
    lo5, hi5 = pl.ds(0, 512), pl.ds(512, 512)
    q1 = ring1(Q.at[s, y, xh, lo4], Q.at[s, y, xh, hi4], q1s, q1r)
    for k in range(16):
        q = (r + k) % 16
        cp = remote(wos, WO.at[slot], os.at[k], orr.at[slot], dev(q // 8, (q // 2) % 4, q % 2, jo // 2, jo % 2))
        oc.append(cp)
        if k == 0:
            @pl.when(j != jo)
            def _():
                cp.start()

            @pl.when(j == jo)
            def _():
                WO[slot] = wos[...]
        else:
            cp.start()
    for cp in q1:
        cp.wait_recv()
    q2 = ring2(Q.at[:, y, :, lo4], Q.at[s, :, xh, hi4], q2s, q2r)
    for k in (1, 3, 2):
        cp = remote(YY.at[w, z], YY.at[w, z], ys.at[k], yr.at[k], dev(s, y, xh, (z + k) % 4, w))
        cp.start()
        yc.append(cp)
    for cp in xc:
        cp.wait_recv()
    xpair = remote(XX.at[w], XX.at[w], ps.at[0], pr.at[0], sib)
    xpair.start()
    for cp in tf:
        cp.wait_recv()
    for cp in q2:
        cp.wait_recv()
    f1 = ring1(F.at[s, y, xh, lo4], F.at[s, y, xh, hi4], f1s, f1r)
    g1 = ring1(W2.at[s, y, xh, :, lo5], W2.at[s, y, xh, :, hi5], w1s, w1r)

    units = Q[...].reshape(128, 16, 256).astype(full)
    left = units[:, :8].reshape(1024, 256)
    right = units[:, 8:].reshape(1024, 256)
    WQT[0:256, :] = left.T.astype(low)
    WQT[256:384, :] = right[:, :128].T.astype(low)
    owner_row = (iota((128, 1024), 1) == 8 * iota((128, 1024), 0)).astype(full).astype(low)
    params = dot(owner_row, right[:, 128:].astype(low), 1, 0).astype(low)

    def row_of(lanes):
        t, f, l = owner_lanes(params, 1024, lanes, 8)
        return jnp.sum(jnp.where((f >= 8 * l) & (f < 8 * l + 8), t, 0.0), axis=0, keepdims=True)

    gain = row_of((0,))
    shift = row_of((8,))
    VEC[0:1, :] = gain
    VEC[1:2, :] = row_of((40, 80))
    t, f, l = owner_lanes(params, 512, (48,), 32)
    base = f - 4 * (l - j)
    bias_1 = jnp.sum(
        jnp.where((((l - j) & 7) == 0) & (base >= 0) & (base < 32), t, 0.0), axis=0, keepdims=True
    )
    n0, p0 = iota((384, 128), 0), iota((384, 128), 1)
    n0 = (n0 // 128) * 1024 + 128 * j + (n0 & 127)
    at = n0 - 24 * p0
    inside = ((at >= 0) & (at < 24)).astype(full)
    t = dot(inside.astype(low), params, 1, 0)
    lane_want = jnp.sum(inside * at.astype(full), axis=1, keepdims=True) + 16.0
    bias_q = jnp.sum(jnp.where(p0.astype(full) == lane_want, t, 0.0), axis=1, keepdims=True)
    lp, ll = iota((128, 128), 0), iota((128, 128), 1)
    tok_pos = (iota((1, BLK), 1) + m * BLK).astype(full)
    pf = params.astype(full)
    for i in range(2):
        here = lp == s * 64 + i
        size = jnp.sum(jnp.where(here & (ll == 88), pf, 0.0)) * 64.0 + jnp.sum(jnp.where(here & (ll == 89), pf, 0.0))
        VAL[i:i + 1, :] = jnp.where(tok_pos < size, 1.0, 0.0)

    co, si = cosine[...], sine[...]

    def norm_slot(wi):
        def one(zi, carry):
            v = XX[wi, zi].astype(full)
            mean = jnp.mean(v, axis=-1, keepdims=True)
            c = v - mean
            var = jnp.mean(c * c, axis=-1, keepdims=True)
            h = c * lax.rsqrt(var + norm_eps)
            XH[wi, zi] = h.astype(low)
            HB[wi, zi] = (h * gain + shift).astype(low)
            return carry

        lax.fori_loop(0, 4, one, 0)

    def turn(v):
        a, b = v[0:8], v[8:16]
        return jnp.concatenate([a * co - b * si, b * co + a * si, v[16:]], axis=0)

    def qkv_slot(wi):
        t = dot(WQT[...], HB[wi].reshape(BLK, 1024), 1, 1) + bias_q
        for e in range(2):
            HT[e, wi, 0, 0] = turn(t[128 + 64 * e:192 + 64 * e]).astype(low)
            HT[e, wi, 0, 1] = t[256 + 64 * e:320 + 64 * e].astype(low)
            HT[e, wi, 1, 0] = (turn(t[64 * e:64 + 64 * e]).astype(low).astype(full) * 0.125).astype(low)

    def head_target(e, i):
        return dev(s, 2 * w + e, i, z, core), (y == 2 * w + e) & (xh == i) & (core == w)

    def kv_copy(e, i):
        return remote(HT.at[e, i, 0], KV.at[core, spot], hs.at[e, i, 0], kr.at[spot], head_target(e, i)[0])

    def q_copy(e, i):
        return remote(HT.at[e, i, 1, 0], QD.at[spot, 0], hs.at[e, i, 1], qr.at[spot], head_target(e, i)[0])

    def do_copy(e, i):
        return remote(HT.at[e, i, 1, 1], QD.at[spot, 1], hs.at[e, i, 2], dr.at[spot], head_target(e, i)[0])

    def send_qkv(i):
        for e in range(2):
            me = head_target(e, i)[1]

            @pl.when(jnp.logical_not(me))
            def _():
                kv_copy(e, i).start()
                q_copy(e, i).start()

            @pl.when(me)
            def _():
                KV[core, spot] = HT[e, i, 0]
                QD[spot, 0] = HT[e, i, 1, 0]

    def send_do(i):
        t = dot(WOF[...], YY[i].reshape(BLK, 1024), 1, 1)
        for e in range(2):
            HT[e, i, 1, 1] = t[64 * e:64 + 64 * e].astype(low)
            me = head_target(e, i)[1]

            @pl.when(jnp.logical_not(me))
            def _():
                do_copy(e, i).start()

            @pl.when(me)
            def _():
                QD[spot, 1] = HT[e, i, 1, 1]

    norm_slot(w)
    qkv_slot(w)
    send_qkv(w)
    xpair.wait_recv()
    norm_slot(1 - w)
    qkv_slot(1 - w)
    send_qkv(1 - w)

    for cp in yc:
        cp.wait_recv()
    ypair = remote(YY.at[w], YY.at[w], ps.at[1], pr.at[1], sib)
    ypair.start()
    for k in range(16):
        @pl.when(jnp.logical_not(wo_mine(k)))
        def _():
            remote(wos, WO.at[k], os.at[0], orr.at[k], dev(*wo_source(k))).wait_recv()
    units = WO[...].astype(full)
    WOF[:, :512] = units[:, :8].reshape(128, 512).astype(low)
    WOF[:, 512:] = units[:, 8:].reshape(128, 512).astype(low)
    send_do(w)
    ypair.wait_recv()
    send_do(1 - w)

    for cp in f1 + g1:
        cp.wait_recv()
    f2 = ring2(F.at[:, y, :, lo4], F.at[s, :, xh, hi4], f2s, f2r)
    g2 = ring2(W2.at[:, y, :, :, lo5], W2.at[s, :, xh, :, hi5], w2s, w2r)
    for i in range(4):
        @pl.when(jnp.logical_not(my_source(i)))
        def _():
            remote(HT.at[0, 0, 0], KV.at[w, i], hs.at[0, 0, 0], kr.at[i], source(i)).wait_recv()
    swap = remote(KV.at[w], KV.at[w], ks, krp, sib)
    swap.start()
    for i in range(4):
        @pl.when(jnp.logical_not(my_source(i)))
        def _():
            remote(HT.at[0, 0, 1, 0], QD.at[i, 0], hs.at[0, 0, 1], qr.at[i], source(i)).wait_recv()
    swap.wait_recv()

    causal = iota((BLK, BLK), 0) <= iota((BLK, BLK), 1)

    def query_block(i, carry):
        mi = 2 * i + (i + w) % 2
        q = QD[i, 0]

        def fwd(n, state, masked):
            run_max, total, out = state
            c, t = core_of(n), n // 2
            sc = dot(KV[c, t, 0], q, 0, 0)
            if masked:
                sc = jnp.where(causal, sc, -1e30)
            new_max = jnp.maximum(run_max, jnp.max(sc, axis=0, keepdims=True))
            pr = jnp.exp(sc - new_max)
            fac = jnp.exp(run_max - new_max)
            total = total * fac + jnp.sum(pr, axis=0, keepdims=True)
            out = out * fac + dot(KV[c, t, 1], pr.astype(low), 1, 0)
            return new_max, total, out

        state = (
            jnp.full((1, BLK), -1e30, full),
            jnp.zeros((1, BLK), full),
            jnp.zeros((HD, BLK), full),
        )
        state = lax.fori_loop(0, mi, lambda n, st: fwd(n, st, False), state)
        run_max, total, out = fwd(mi, state, True)
        out = out / total
        OF[i] = out
        LSE[i] = run_max + jnp.log(total)
        OB[i] = out.astype(low)

        @pl.when(jnp.logical_not(at_home(i)))
        def _():
            remote(OB.at[i], RO.at[e_me, i_me], bs.at[i, 0], br.at[0, e_me, i_me], home(i)).start()

        @pl.when(at_home(i))
        def _():
            RO[e_me, i_me] = OB[i]

        return carry

    lax.fori_loop(0, 4, query_block, 0)

    for cp in f2 + g2:
        cp.wait_recv()
    units = F[...].reshape(128, 16, 256).astype(full)
    W1[:, :256] = units[:, :8].reshape(1024, 256).astype(low)
    W1[:, 256:] = units[:, 8:].reshape(1024, 256).astype(low)

    def hidden(n, carry):
        wi, zi = n // 4, n % 4
        u = dot(HB[wi, zi], W1[...], 1, 0) + bias_1
        dg = dot(YY[wi, zi], W2[...].reshape(512, 1024), 1, 1)
        c0 = 0.7978845608028654
        t = jnp.tanh(c0 * (u + 0.044715 * (u * u * u)))
        GA[wi, zi] = (0.5 * u * (1.0 + t)).astype(low)
        slope = 0.5 * (1.0 + t) + (0.5 * c0) * u * (1.0 - t * t) * (1.0 + (3.0 * 0.044715) * (u * u))
        DU[wi, zi] = (dg * slope).astype(low)
        return carry

    lax.fori_loop(0, 8, hidden, 0)

    ga = GA[...].reshape(1024, 512)

    def first_w2(h):
        t = dot(ga, YY[:, :, :, 512 * h:512 * h + 512].reshape(1024, 512), 0, 0).astype(low)
        GW[:, :, :, :, 512 * h:512 * h + 512] = t.reshape(2, 4, 2, 32, 512)
        out = []
        for k in (1, 3, 2):
            yy, xx = (y + k) % 4, (x + k) % 4
            if h == 0:
                cp = remote(GW.at[:, yy, :, :, lo5], wi0.at[k], g1s.at[2, 0, k], g1r.at[2, 0, k], dev(s, yy, xh, z, w))
            else:
                cp = remote(GW.at[xx % 2, :, xx // 2, :, hi5], wi1.at[k], g1s.at[2, 1, k], g1r.at[2, 1, k], x_dev(xx, y, z, w))
            cp.start()
            out.append(cp)
        return out

    def first_unit(g, buf):
        out = []
        for k in (1, 3, 2):
            yy, xx = (y + k) % 4, (x + k) % 4
            cp = remote(buf.at[:, yy, :, lo4], gi0.at[g, k], g1s.at[g, 0, k], g1r.at[g, 0, k], dev(s, yy, xh, z, w))
            cp.start()
            out.append(cp)
            cp = remote(buf.at[xx % 2, :, xx // 2, hi4], gi1.at[g, k], g1s.at[g, 1, k], g1r.at[g, 1, k], x_dev(xx, y, z, w))
            cp.start()
            out.append(cp)
        return out

    def add4(a, b, c, d):
        return a.astype(full) + b.astype(full) + c.astype(full) + d.astype(full)

    def second_unit(g, buf):
        gm[g, 0] = add4(
            buf[:, y, :, 0:4], gi0[g, 1], gi0[g, 2], gi0[g, 3]
        ).astype(low).reshape(4, 4, 16, 256)
        gm[g, 1] = add4(
            buf[s, :, xh, 4:8], gi1[g, 1], gi1[g, 2], gi1[g, 3]
        ).astype(low)
        out = []
        for k in (1, 3, 2):
            yy, xx = (y + k) % 4, (x + k) % 4
            cp = remote(gm.at[g, 0, 2 * (xx % 2) + xx // 2], gi2.at[g, 0, k], g2s.at[g, 0, k], g2r.at[g, 0, k], x_dev(xx, y, z, w))
            cp.start()
            out.append(cp)
            cp = remote(gm.at[g, 1, yy], gi2.at[g, 1, k], g2s.at[g, 1, k], g2r.at[g, 1, k], dev(s, yy, xh, z, w))
            cp.start()
            out.append(cp)
        return out

    def second_w2():
        wm[0] = add4(GW[:, y, :, :, :512], wi0[1], wi0[2], wi0[3]).astype(low).reshape(4, 32, 512)
        wm[1] = add4(GW[s, :, xh, :, 512:], wi1[1], wi1[2], wi1[3]).astype(low)
        out = []
        for k in (1, 3, 2):
            yy, xx = (y + k) % 4, (x + k) % 4
            cp = remote(wm.at[0, 2 * (xx % 2) + xx // 2], wi2.at[0, k], g2s.at[2, 0, k], g2r.at[2, 0, k], x_dev(xx, y, z, w))
            cp.start()
            out.append(cp)
            cp = remote(wm.at[1, yy], wi2.at[1, k], g2s.at[2, 1, k], g2r.at[2, 1, k], dev(s, yy, xh, z, w))
            cp.start()
            out.append(cp)
        return out

    def last_unit(g, fin, got_units):
        fin[0:4] = add4(gm[g, 0, 2 * s + xh], gi2[g, 0, 1], gi2[g, 0, 2], gi2[g, 0, 3]).astype(low)
        fin[4:8] = add4(gm[g, 1, y], gi2[g, 1, 1], gi2[g, 1, 2], gi2[g, 1, 3]).astype(low)
        out = []
        for k in range(1, 8):
            q = (j + k) % 8
            cp = remote(fin.at[q], got_units.at[j], tts.at[g, k], ttr.at[g, k], dev(s, y, xh, q // 2, q % 2))
            cp.start()
            out.append(cp)
        got_units[j] = fin[j]
        return out

    c_w2 = first_w2(0)
    c_w2 += first_w2(1)

    du = DU[...].reshape(1024, 512)
    for n in range(4):
        t = dot(HB[:, :, :, 256 * n:256 * n + 256].reshape(1024, 256), du, 0, 0)
        t = jnp.concatenate([t[:, :256].reshape(32, 8, 256), t[:, 256:].reshape(32, 8, 256)], axis=1)
        GF[n // 2, 2 * (n % 2):2 * (n % 2) + 2] = t.astype(low).reshape(2, 2, 8, 16, 256)
    c_f = first_unit(0, GF)
    gb1 = jnp.sum(du.astype(full), axis=0, keepdims=True)
    gb_out = jnp.sum(YY[w, z].astype(full), axis=0, keepdims=True)

    def mlp_parts(i, carry):
        PH[i] = dot(DU[i].reshape(BLK, 512), W1[...], 1, 1)
        return carry

    lax.fori_loop(0, 2, mlp_parts, 0)

    def wait_home(g, src, dst):
        for e in range(2):
            for i in range(2):
                @pl.when(jnp.logical_not(head_here(e, i)))
                def _():
                    remote(src.at[0], dst.at[e, i], bs.at[0, g], br.at[g, e, i], head_at(e, i)).wait_recv()

    wait_home(0, OB, RO)

    def out_slot(i):
        ob = jnp.concatenate([RO[0, i], RO[1, i]], axis=0).astype(full)
        ob = (ob * VAL[pl.ds(i, 1), :]).astype(low)
        t = dot(ob, WOF[...], 0, 0) + dot(GA[i].reshape(BLK, 512), W2[...].reshape(512, 1024), 1, 0)
        TO[i] = t.astype(low).reshape(4, 128, 1024)
        return dot(ob, YY[i].reshape(BLK, 1024), 1, 0)

    g_wo = out_slot(1 - w)
    opair = remote(TO.at[1 - w], pin.at[0], pps.at[0], ppr.at[0], sib)
    opair.start()
    g_wo = g_wo + out_slot(w)
    GO[...] = jnp.concatenate(
        [g_wo[:, :512].reshape(16, 8, 512), g_wo[:, 512:].reshape(16, 8, 512)], axis=1
    ).astype(low)

    def owner(k):
        rr = 2 * j + k // 8
        return rr // 8, (rr // 2) % 4, rr % 2, (k % 8) // 2, k % 2

    def owner_copy(k):
        os_, oy, oxh, oz, ow = owner(k)
        me = (os_ == s) & (oy == y) & (oxh == xh) & (oz == z) & (ow == w)
        return remote(GO.at[k], fo_in.at[r], gos.at[k], gor.at[r], dev(os_, oy, oxh, oz, ow)), me

    for k in range(16):
        cp, me = owner_copy(k)

        @pl.when(jnp.logical_not(me))
        def _():
            cp.start()

        @pl.when(me)
        def _():
            fo_in[r] = GO[k]

    for i in range(4):
        @pl.when(jnp.logical_not(my_source(i)))
        def _():
            remote(HT.at[0, 0, 1, 1], QD.at[i, 1], hs.at[0, 0, 2], dr.at[i], source(i)).wait_recv()
    for i in range(4):
        DLT[i] = jnp.sum(QD[i, 1].astype(full) * OF[i], axis=0, keepdims=True)
    dqa[...] = jnp.zeros_like(dqa)

    def pair_of(c, t, i, masked):
        k = KV[c, t, 0]
        q = QD[i, 0]
        do = QD[i, 1]
        pr = jnp.exp(dot(k, q, 0, 0) - LSE[i])
        if masked:
            pr = jnp.where(causal, pr, 0.0)
        dp = dot(KV[c, t, 1], do, 0, 0)
        ds = (pr * (dp - DLT[i])).astype(low)
        acc[c, 0] += dot(q, ds, 1, 1)
        acc[c, 1] += dot(do, pr.astype(low), 1, 1)
        dqa[i] += dot(k, ds, 1, 0)

    def kv_home(t):
        summed[t] = (acc_own[t] + got[t].astype(full)).astype(low)

        @pl.when(jnp.logical_not(at_home(t)))
        def _():
            remote(summed.at[t], RKV.at[e_me, i_me], bs.at[t, 2], br2.at[e_me, i_me], home(t)).start()

        @pl.when(at_home(t))
        def _():
            RKV[e_me, i_me] = summed[t]

    def step(t):
        acc[...] = jnp.zeros_like(acc)

        def rest(u, carry):
            pair_of(u % 2, t, t + 1 + u // 2, False)
            return carry

        if t < 3:
            lax.fori_loop(0, 2 * (3 - t), rest, 0)

        @pl.when((t + w) % 2 == 1)
        def _():
            pair_of(1 - w, t, t, False)

        pair_of(w, t, t, True)
        other[t] = acc[1 - w].astype(low)
        acc_own[t] = acc[w]
        cp = remote(other.at[t], got.at[t], kss.at[t], ksr.at[t], sib)
        cp.start()
        DQB[t] = (dqa[t] * 0.125).astype(low)

        @pl.when(jnp.logical_not(at_home(t)))
        def _():
            remote(DQB.at[t], RQ1.at[e_me, i_me], bs.at[t, 1], br.at[1, e_me, i_me], home(t)).start()

        @pl.when(at_home(t))
        def _():
            RQ1[e_me, i_me] = DQB[t]

        return cp

    k0 = step(0)
    opair.wait_recv()
    def pair_z(n, buf):
        def one(t, carry):
            buf[w, t] = (buf[w, t].astype(full) + pin[n, t].astype(full)).astype(low)
            return carry

        lax.fori_loop(0, 4, one, 0)
        out = []
        for k in (1, 3, 2):
            zz = (z + k) % 4
            cp = remote(buf.at[w, zz], zin.at[n, k], zzs.at[n, k], zzr.at[n, k], dev(s, y, xh, zz, w))
            cp.start()
            out.append(cp)
        return out

    zo = pair_z(0, TO)
    for cp in c_w2 + c_f:
        cp.wait_recv()
    d_w2 = second_w2()
    d_f = second_unit(0, GF)
    k0.wait_recv()
    kv_home(0)
    k1 = step(1)
    for cp in d_w2 + d_f:
        cp.wait_recv()
    GFC2[:, :512] = add4(wm[0, 2 * s + xh], wi2[0, 1], wi2[0, 2], wi2[0, 3])
    GFC2[:, 512:] = add4(wm[1, y], wi2[1, 1], wi2[1, 2], wi2[1, 3])
    t_f = last_unit(0, Ff, RF)
    k1.wait_recv()
    kv_home(1)
    k2 = step(2)
    for q in range(16):
        @pl.when(jnp.logical_not((q == r) & (j == jo)))
        def _():
            remote(GO.at[0], fo_in.at[q], gos.at[0], gor.at[q], sender(q)).wait_recv()
    t = lax.fori_loop(0, 16, lambda q, t: t + fo_in[q].astype(full), jnp.zeros((16, 512), full))
    GWO[:, :512] = t[:8]
    GWO[:, 512:] = t[8:]
    k2.wait_recv()
    kv_home(2)
    k3 = step(3)
    k3.wait_recv()
    kv_home(3)

    def turn_back(v):
        a, b = v[0:8], v[8:16]
        return jnp.concatenate([a * co + b * si, b * co - a * si, v[16:]], axis=0)

    def wait_kv():
        for e in range(2):
            for i in range(2):
                @pl.when(jnp.logical_not(head_here(e, i)))
                def _():
                    remote(summed.at[0], RKV.at[e, i], bs.at[0, 2], br2.at[e, i], head_at(e, i)).wait_recv()

    wait_home(1, DQB, RQ1)
    wait_kv()

    def dh_slot(i):
        for e in range(2):
            DQ[i, 64 * e:64 * e + 64] = turn_back(RQ1[e, i].astype(full)).astype(low)
            DQ[i, 128 + 64 * e:192 + 64 * e] = turn_back(RKV[e, i, 0].astype(full)).astype(low)
            DQ[i, 256 + 64 * e:320 + 64 * e] = RKV[e, i, 1]
        t = dot(DQ[i], WQT[...], 0, 0) + PH[i]
        TH[i] = t.astype(low).reshape(4, 128, 1024)
        g_shift = jnp.sum(t, axis=0, keepdims=True)
        g_gain = jnp.sum(t * XH[i].reshape(BLK, 1024).astype(full), axis=0, keepdims=True)
        return g_shift, g_gain, jnp.sum(DQ[i].astype(full), axis=1, keepdims=True)

    a_shift, a_gain, a_bq = dh_slot(1 - w)
    hpair = remote(TH.at[1 - w], pin.at[1], pps.at[1], ppr.at[1], sib)
    hpair.start()
    b_shift, b_gain, b_bq = dh_slot(w)
    hpair.wait_recv()
    zh = pair_z(1, TH)

    gq = dot(DQ[0], HB[0].reshape(BLK, 1024), 1, 0) + dot(DQ[1], HB[1].reshape(BLK, 1024), 1, 0)
    d0, p0 = iota((128, 1024), 1), iota((128, 1024), 0)
    block = (d0 >= 8 * p0) & (d0 < 8 * p0 + 8)
    dt, lt = iota((1024, 128), 0), iota((1024, 128), 1)

    def spread_row(v, lane):
        a = jnp.where(block, jnp.broadcast_to(v, (128, 1024)), 0.0).astype(low)
        return dot(a, (lt == lane + (dt & 7)).astype(full).astype(low), 1, 0)

    small = spread_row(a_gain + b_gain, 0) + spread_row(a_shift + b_shift, 8) + spread_row(gb_out, 16)
    f0, pf = iota((128, 512), 1), iota((128, 512), 0)
    base = f0 - 4 * (pf - j)
    a = jnp.where(
        (((pf - j) & 7) == 0) & (base >= 0) & (base < 32), jnp.broadcast_to(gb1, (128, 512)), 0.0
    ).astype(low)
    ft, lf = iota((512, 128), 0), iota((512, 128), 1)
    small = small + dot(a, (lf == 48 + (ft & 31)).astype(full).astype(low), 1, 0)
    n0, pn = iota((128, 384), 1), iota((128, 384), 0)
    qk_at = (n0 // 128) * 1024 + 128 * j + (n0 & 127) - 16 * pn
    v_at = 128 * j + (n0 & 127) - 8 * pn
    owns = ((n0 < 256) & (qk_at >= 0) & (qk_at < 16)) | ((n0 >= 256) & (v_at >= 0) & (v_at < 8))
    nt, ln = iota((384, 128), 0), iota((384, 128), 1)
    lane = jnp.where(nt < 256, 24 + (nt & 15), 40 + (nt & 7))
    b = jnp.where(ln == lane, jnp.broadcast_to(a_bq + b_bq, (384, 128)), 0.0).astype(low)
    small = small + dot(owns.astype(full).astype(low), b, 1, 0)
    head_row = (dt == 8 * lt).astype(full).astype(low)
    pad = dot(head_row, small.astype(low), 1, 0)
    left = gq[:256].T
    right = jnp.concatenate([gq[256:].T, pad], axis=1)
    GQ[...] = jnp.concatenate(
        [left.reshape(128, 8, 256), right.reshape(128, 8, 256)], axis=1
    ).astype(low).reshape(2, 4, 2, 8, 16, 256)
    c_q = first_unit(1, GQ)

    mine_x = tok[0].astype(full)
    for cp in zo:
        cp.wait_recv()
    t = add4(TO[w, z], zin[0, 1], zin[0, 2], zin[0, 3])
    OUT[0] = (mine_x + t + VEC[1:2, :]).astype(low)
    mean = jnp.mean(mine_x, axis=-1, keepdims=True)
    cen = mine_x - mean
    inv = lax.rsqrt(jnp.mean(cen * cen, axis=-1, keepdims=True) + norm_eps)
    for cp in c_q:
        cp.wait_recv()
    d_q = second_unit(1, GQ)
    for cp in zh:
        cp.wait_recv()
    gh = add4(TH[w, z], zin[1, 1], zin[1, 2], zin[1, 3])
    hat = cen * inv
    gx = gh * VEC[0:1, :]
    gx = gx - jnp.mean(gx, axis=-1, keepdims=True) - hat * jnp.mean(gx * hat, axis=-1, keepdims=True)
    TG[0] = (YY[w, z].astype(full) + inv * gx).astype(low)
    for cp in d_q:
        cp.wait_recv()
    t_q = last_unit(1, Qf, RQ)
    for cp in t_f + t_q:
        cp.wait_recv()

    for e in range(2):
        for i in range(2):
            @pl.when(jnp.logical_not(head_target(e, i)[1]))
            def _():
                kv_copy(e, i).wait_send()
                q_copy(e, i).wait_send()
                do_copy(e, i).wait_send()

    @pl.when(j != jo)
    def _():
        oc[0].wait_send()

    for i in range(4):
        @pl.when(jnp.logical_not(at_home(i)))
        def _():
            remote(OB.at[i], RO.at[e_me, i_me], bs.at[i, 0], br.at[0, e_me, i_me], home(i)).wait_send()
            remote(DQB.at[i], RQ1.at[e_me, i_me], bs.at[i, 1], br.at[1, e_me, i_me], home(i)).wait_send()
            remote(summed.at[i], RKV.at[e_me, i_me], bs.at[i, 2], br2.at[e_me, i_me], home(i)).wait_send()
    for k in range(16):
        cp, me = owner_copy(k)

        @pl.when(jnp.logical_not(me))
        def _():
            cp.wait_send()
    for cp in oc[1:] + tq + tf + xc + yc + q1 + q2 + f1 + f2 + g1 + g2 + [xpair, ypair, swap, k0, k1, k2, k3]:
        cp.wait_send()
    for cp in [opair, hpair] + zo + zh + c_w2 + c_f + c_q + d_w2 + d_f + d_q + t_f + t_q:
        cp.wait_send()


def layer(*args):
    S = pltpu.SemaphoreType.DMA
    V = pltpu.VMEM
    sds = jax.ShapeDtypeStruct
    return pl.pallas_call(
        layer_kernel,
        name="layer",
        out_shape=(
            sds((1, 128, 1024), low),
            sds((1, 128, 1024), low),
            sds((8, 16, 256), low),
            sds((8, 16, 256), low),
            sds((32, 1024), full),
            sds((8, 1024), full),
        ),
        in_specs=[pl.BlockSpec(memory_space=pltpu.SMEM)] + [VM] * 9,
        out_specs=(VM,) * 6,
        scratch_shapes=[
            V((2, 4, 128, 1024), low),
            V((2, 4, 128, 1024), low),
            V((2, 4, 128, 1024), low),
            V((2, 4, 128, 1024), low),
            V((2, 4, 128, 512), low),
            V((2, 4, 128, 512), low),
            V((1024, 512), low),
            V((2, 4, 2, 32, 1024), low),
            V((384, 1024), low),
            V((128, 1024), low),
            V((8, 1024), full),
            V((8, BLK), full),
            V((2, 4, 2, 64, BLK), low),
            V((4, 2, 64, BLK), low),
            V((2, 4, 2, 8, 16, 256), low),
            V((2, 4, 2, 8, 16, 256), low),
            V((8, 16, 256), low),
            V((8, 16, 256), low),
            V((16, 512), low),
            V((16, 16, 512), low),
            V((2, 2, 2, 2, 64, BLK), low),
            V((4, 64, BLK), full),
            V((4, 64, BLK), low),
            V((4, 1, BLK), full),
            V((4, 1, BLK), full),
            V((2, 2, 64, BLK), low),
            V((2, 2, 64, BLK), low),
            V((2, 2, 2, 64, BLK), low),
            V((2, 2, 64, BLK), full),
            V((4, 2, 64, BLK), full),
            V((4, 64, BLK), full),
            V((4, 64, BLK), low),
            V((4, 2, 64, BLK), low),
            V((4, 2, 64, BLK), low),
            V((4, 2, 64, BLK), low),
            V((2, BLK, 1024), full),
            V((2, 384, BLK), low),
            V((2, 4, 128, 1024), low),
            V((2, 4, 128, 1024), low),
            V((2, 4, 128, 1024), low),
            V((2, 4, 128, 1024), low),
            V((2, 4, 2, 8, 16, 256), low),
            V((2, 4, 2, 8, 16, 256), low),
            V((2, 4, 2, 32, 1024), low),
            V((2, 4, 2, 2, 4, 16, 256), low),
            V((2, 4, 4, 4, 16, 256), low),
            V((4, 2, 2, 32, 512), low),
            V((4, 4, 32, 512), low),
            V((2, 2, 4, 4, 16, 256), low),
            V((2, 4, 32, 512), low),
            V((2, 2, 4, 4, 16, 256), low),
            V((2, 4, 32, 512), low),
            V((8, 16, 256), low),
            V((8, 16, 256), low),
            V((16, 16, 512), low),
            V((16, 16, 512), low),
            S((4,)), S((4,)), S((4,)), S((4,)), S((2,)), S((2,)), S((8,)), S((8,)), S((8,)), S((8,)), S((16,)),
            S((16,)), S((2, 4)), S((2, 4)), S((2, 4)), S((2, 4)), S((2, 4)), S((2, 4)), S((2, 4)), S((2, 4)),
            S((2, 4)), S((2, 4)), S((2, 4)), S((2, 4)), S((2, 2, 3)), S((4,)), S((4,)), S((4,)), S, S,
            S((4, 3)), S((2, 2, 2)), S((2, 2)), S((2,)), S((2,)), S((4,)), S((4,)), S((16,)), S((16,)),
            S((2, 4)), S((2, 4)), S((3, 2, 4)), S((3, 2, 4)), S((3, 2, 4)), S((3, 2, 4)), S((2, 8)), S((2, 8)),
        ],
        compiler_params=pltpu.CompilerParams(
            collective_id=0, has_side_effects=True, vmem_limit_bytes=62 << 20
        ),
    )(*args)


def finish_kernel(out, tg, RF, RQ, gfc2, gwo,
                  OUT, TG, GQKV, GFC1, GFC2, GWO, GG, GS, BQK, BV, BO, B1, B2):
    OUT[...] = out[...]
    TG[...] = tg[...]
    GFC2[...] = gfc2[...]
    GWO[...] = gwo[...]
    for rr in range(16):
        g = rr // 4
        c, half = g // 2, g % 2
        for hi in range(2):
            tiles = [RF[4 * hi + n, 8 * c:8 * c + 8, 128 * half:128 * half + 128].astype(full) for n in range(4)]
            col = 128 * (2 * rr + hi)
            GFC1[:, col:col + 128] = lane_mix(tiles, [32 * (n - rr % 4) for n in range(4)])
    tail = jnp.zeros((8, 128), full)
    for q in range(8):
        c = 128 * q
        GQKV[:, c:c + 128] = RQ[q, 0:8, 0:128].astype(full)
        GQKV[:, 1024 + c:1152 + c] = RQ[q, 0:8, 128:256].astype(full)
        GQKV[:, 2048 + c:2176 + c] = RQ[q, 8:16, 0:128].astype(full)
        tail = tail + RQ[q, 8:16, 128:256].astype(full)
    row = tail[0]
    GG[...] = row[0:8]
    GS[...] = row[8:16]
    BQK[...] = row[24:40]
    BV[...] = row[40:48]
    BO[...] = row[16:24]
    B1[...] = row[48:80]
    B2[...] = row[16:24]


def finish(*args):
    sds = jax.ShapeDtypeStruct
    return pl.pallas_call(
        finish_kernel,
        name="finish",
        out_shape=(
            sds((1, 128, 1024), low),
            sds((1, 128, 1024), low),
            sds((8, 3072), full),
            sds((8, 4096), full),
            sds((32, 1024), full),
            sds((8, 1024), full),
            sds((8,), full),
            sds((8,), full),
            sds((16,), full),
            sds((8,), full),
            sds((8,), full),
            sds((32,), full),
            sds((8,), full),
        ),
        in_specs=[VM] * 6,
        out_specs=(VM,) * 13,
    )(*args)


def shards(
    tokens, lengths, ln_gain, ln_bias, w_qkv, b_qkv, w_out, b_out, w_fc1, b_fc1, w_fc2, b_fc2, cotangent
):
    s, y, xh, z, w = place()
    j = z * 2 + w
    m = y * 2 + xh
    small = jnp.concatenate(
        [
            ln_gain, ln_bias, b_qkv, b_out, b_fc1, b_fc2,
            (lengths // 64).astype(full), (lengths % 64).astype(full), jnp.zeros((38,), full),
        ]
    )[None]
    pos = (m * BLK + jnp.arange(BLK)).astype(full)
    freq = jnp.power(rope_base, -2.0 * jnp.arange(8).astype(full) / ROT)
    angle = freq[:, None] * pos[None, :]
    cosine, sine = jnp.cos(angle), jnp.sin(angle)

    parts = layer(lengths, tokens, cotangent, small, w_qkv, w_out, w_fc1, w_fc2, cosine, sine)
    OUT, TG, GQKV, GFC1, GFC2, GWO, GG, GS, BQK, BV, BO, B1, B2 = finish(*parts)
    return (OUT, TG, GG, GS, GQKV, BQK, BV, GWO, BO, GFC1, B1, GFC2, B2)


def solution(mesh):
    rows, tok, par, vec = (
        P(("slot", "wsh")), P(("slot", "wsh"), "ctx", None), P(("slot", "ctx", "wsh"), None), P(("slot", "ctx", "wsh"))
    )
    return jax.shard_map(
        shards,
        mesh=mesh,
        in_specs=(tok, rows, vec, vec, par, vec, par, vec, par, vec, par, vec, tok),
        out_specs=(tok, tok, vec, vec, par, vec, vec, par, vec, par, vec, par, vec),
        check_vma=False,
    )
```

```python
import functools

import jax
import jax.numpy as jnp
import numpy as np
from jax import lax
from jax.experimental import pallas as pl
from jax.experimental.pallas import tpu as pltpu
from jax.sharding import PartitionSpec as P

HEADS = 16
HD = 64
ROT = 16
HQ = 1024
D = 1024
FF = 4096
BLK = 512

norm_eps = 1e-05
rope_base = 10000.0
MESH = pl.DeviceIdType.MESH
low = jnp.bfloat16
full = jnp.float32
VM = pl.BlockSpec(memory_space=pltpu.VMEM)
AN = pl.BlockSpec(memory_space=pl.ANY)


def place():
    s = lax.axis_index("slot")
    c = lax.axis_index("ctx")
    w = lax.axis_index("wsh")
    return s, c // 8, (c // 4) % 2, c % 4, w


def dev(s, y, xh, z, w):
    return (s, y * 8 + xh * 4 + z, w)


def x_dev(x, y, z, w):
    return dev(x % 2, y, x // 2, z, w)


def signal(barrier, target):
    pl.semaphore_signal(barrier, inc=1, device_id=target, device_id_type=MESH)


def remote(src, dst, send, recv, target):
    return pltpu.make_async_remote_copy(
        src_ref=src, dst_ref=dst, send_sem=send, recv_sem=recv,
        device_id=target, device_id_type=MESH,
    )


def iota(shape, axis):
    return lax.broadcasted_iota(jnp.int32, shape, axis)


def dot(a, b, ca, cb):
    return lax.dot_general(a, b, (((ca,), (cb,)), ((), ())), preferred_element_type=full)


def core_of(m):
    return ((m + 1) // 2) % 2


def owner_lanes(params, width, lanes, step):
    f, l = iota((128, width), 1), iota((128, width), 0)
    pick = (l == lanes[0] + (f & (step - 1)))
    for other in lanes[1:]:
        pick = pick | (l == other + (f & (step - 1)))
    return dot(params, pick.astype(full).astype(low), 1, 0), f, l


def lane_mix(tiles, shifts):
    lane = iota((8, 128), 1)
    out = jnp.zeros((8, 128), full)
    for g in range(4):
        t = tiles[g]
        if shifts[g] % 128:
            t = pltpu.roll(t, shifts[g] % 128, 1)
        out = jnp.where((lane >= 32 * g) & (lane < 32 * g + 32), t, out)
    return out


def layer_kernel(
    lens, tok, cot, lg, lb, bq, bo, bf, bg, wq, wo, w1, w2, turns, OUT, TG, RF, RQ, GFC2, GWO, PAD, ROPE, XX, YY, HB, XH, GA, DU,
    W1, W2, WQT, WOF, VEC, VAL, KV, QD, Q, F, Qs, Fs, wos, WO, HT, OF, OB, LSE, DLT, RO, RQ1, RKV, acc,
    acc_own, dqa, DQB, other, got, summed, PH, DQ, TO, TH, pin, zin, GF, GQ, GW, gi0, gi1, wi0, wi1, gm, wm,
    gi2, wi2, Ff, Qf, GO, fo_in, zs, zr, ys, yr, ps, pr, ts, tr, fs, fr, os, orr, q2s, q2r,
    f2s, f2r, w1s, w1r, w2s, w2r, hs, kr, qr, dr, ks, krp, bs, br, br2, pps, ppr, kss, ksr, gos, gor, zzs, zzr,
    g1s, g1r, g2s, g2r, tts, ttr,
):
    s, y, xh, z, w = place()
    x = xh * 2 + s
    r = s * 8 + y * 2 + xh
    j = z * 2 + w
    jo = r // 2
    m = y * 2 + xh
    core, spot = core_of(m), m // 2
    keep = (j == jo).astype(jnp.int32)
    mine = ((y // 2 == w) & (core == w)).astype(jnp.int32)
    sib = dev(s, y, xh, z, 1 - w)

    lo4, hi4 = pl.ds(0, 4), pl.ds(4, 4)
    lo5, hi5 = pl.ds(0, 512), pl.ds(512, 512)
    half = z // 2
    flip = 1 - half

    def ahead(k, q):
        return x_dev((x + k * flip) % 4, (y + k * half) % 4, q // 2, q % 2)

    def behind(k, q):
        if q < 4:
            return x_dev((x + 4 - k) % 4, y, q // 2, q % 2)
        return dev(s, (y + 4 - k) % 4, xh, q // 2, q % 2)

    barrier = pltpu.get_barrier_semaphore()
    for k in range(4):
        for q in range(8):
            if k == 0:
                @pl.when(j != q)
                def _():
                    signal(barrier, behind(k, q))
            else:
                signal(barrier, behind(k, q))
    for k in range(1, 4):
        signal(barrier, x_dev((x + k) % 4, y, z, w))
        signal(barrier, dev(s, (y + k) % 4, xh, z, w))

    def wo_source(k):
        rr = 2 * j + k // 8
        return rr // 8, (rr // 2) % 4, rr % 2, (k % 8) // 2, k % 2

    def wo_mine(k):
        ss, sy, sxh, sz, sw = wo_source(k)
        return (ss == s) & (sy == y) & (sxh == xh) & (sz == z) & (sw == w)

    def source(i):
        return dev(s, i, (i + w) % 2, z, y // 2)

    def my_source(i):
        return (y == i) & (xh == (i + w) % 2) & (w == y // 2)

    def sender(q):
        return dev(q // 8, (q // 2) % 4, q % 2, jo // 2, jo % 2)

    def home(i):
        return dev(s, i, (i + w) % 2, z, y // 2)

    def at_home(i):
        return (y == i) & (xh == (i + w) % 2) & (w == y // 2)

    def head_at(e, i):
        return dev(s, 2 * w + e, i, z, core)

    def head_here(e, i):
        return (y == 2 * w + e) & (xh == i) & (core == w)

    e_me, i_me = y % 2, xh
    XX[w, z] = tok[0]
    first_row = iota((8, 128), 0)
    PAD[...] = jnp.zeros_like(PAD)
    PAD[0:1, 0:8] = lg[...].reshape(1, 8)
    PAD[1:2, 0:8] = lb[...].reshape(1, 8)
    PAD[2:3, 0:24] = bq[...].reshape(1, 24)
    PAD[3:4, 0:8] = bo[...].reshape(1, 8)
    PAD[4:5, 0:32] = bf[...].reshape(1, 32)
    PAD[5:6, 0:8] = bg[...].reshape(1, 8)
    lane8 = iota((8, 128), 1)
    size = jnp.full((8, 128), lens[0], jnp.int32)
    padded = jnp.where(
        first_row == 6,
        jnp.where(lane8 == 0, (size >> 6).astype(full), jnp.where(lane8 == 1, (size & 63).astype(full), 0.0)),
        PAD[...],
    )
    for q in range(8):
        c = 128 * q
        top = jnp.concatenate([wq[:, c:c + 128], wq[:, 1024 + c:1152 + c]], axis=1)
        bot = jnp.concatenate([wq[:, 2048 + c:2176 + c], padded], axis=1)
        Qs[q] = jnp.concatenate([top, bot], axis=0).astype(low)

    W2[s, y, xh] = w2[...].astype(low)
    for q in range(8):
        tiles = []
        for g in range(4):
            parts = [w1[:, 128 * (2 * (4 * g + n) + q // 4):128 * (2 * (4 * g + n) + q // 4) + 128] for n in range(4)]
            tiles.append(lane_mix(parts, [32 * (n - q % 4) for n in range(4)]))
        top = jnp.concatenate(tiles[:2], axis=1)
        bot = jnp.concatenate(tiles[2:], axis=1)
        Fs[q] = jnp.concatenate([top, bot], axis=0).astype(low)
    F[s, y, xh, j] = Fs[j]

    def ring1(ref0, ref1, snd, rcv):
        out = []
        for k in (1, 3, 2):
            cp = remote(ref0, ref0, snd.at[0, k], rcv.at[0, k], x_dev((x + k) % 4, y, z, w))
            cp.start()
            out.append(cp)
            cp = remote(ref1, ref1, snd.at[1, k], rcv.at[1, k], dev(s, (y + k) % 4, xh, z, w))
            cp.start()
            out.append(cp)
        return out

    def ring2(ref0, ref1, snd, rcv):
        out = []
        for k in (1, 3, 2):
            cp = remote(ref0, ref0, snd.at[0, k], rcv.at[0, k], dev(s, (y + k) % 4, xh, z, w))
            cp.start()
            out.append(cp)
            cp = remote(ref1, ref1, snd.at[1, k], rcv.at[1, k], x_dev((x + k) % 4, y, z, w))
            cp.start()
            out.append(cp)
        return out

    with jax.named_scope("barrier"):
        pl.semaphore_wait(barrier, 31 + 6)

    slot = (r % 2) * 8 + j
    tq, tf, xc, yc, oc = [], [], [], [], []
    for k in (1, 3, 2, 0):
        for n in range(8):
            if k == 0 and n == 0:
                continue
            q = (j + n) % 8
            cp = remote(Qs.at[q], Q.at[s, y, xh, j], ts.at[k, n], tr.at[k, j], ahead(k, q))
            cp.start()
            tq.append(cp)
    for k in (1, 3, 2, 0):
        for n in range(8):
            if k == 0 and n == 0:
                continue
            q = (j + n) % 8
            cp = remote(Fs.at[q], F.at[s, y, xh, j], fs.at[k, n], fr.at[k, j], ahead(k, q))
            cp.start()
            tf.append(cp)
    g1 = ring1(W2.at[s, y, xh, :, lo5], W2.at[s, y, xh, :, hi5], w1s, w1r)
    for k in (1, 3, 2):
        cp = remote(XX.at[w, z], XX.at[w, z], zs.at[k], zr.at[k], dev(s, y, xh, (z + k) % 4, w))
        cp.start()
        xc.append(cp)
    Q[s, y, xh, j] = Qs[j]

    row = iota((128, 1024), 0) + (m * BLK + z * 128)
    YY[w, z] = jnp.where(row < lens[0], cot[0].astype(full), 0.0).astype(low)
    wos[...] = jnp.concatenate([wo[:, :512], wo[:, 512:]], axis=0).astype(low)
    c0, s0 = turns[0], turns[1]
    at_m = iota((8, 128), 1) == m
    cm = jnp.sum(jnp.where(at_m, turns[2, :, :128], 0.0), axis=1, keepdims=True)
    sm = jnp.sum(jnp.where(at_m, turns[3, :, :128], 0.0), axis=1, keepdims=True)
    ROPE[0] = cm * c0 - sm * s0
    ROPE[1] = sm * c0 + cm * s0

    def wait_units(buf, stage, snd, rcv):
        for k in range(4):
            for q in range(8):
                if q < 4:
                    bx = (x + 4 - k) % 4
                    here = buf.at[bx % 2, y, bx // 2, q]
                else:
                    here = buf.at[s, (y + 4 - k) % 4, xh, q]
                cp = remote(stage.at[0], here, snd.at[k, 0], rcv.at[k, q], behind(k, q))
                if k == 0:
                    @pl.when(j != q)
                    def _():
                        cp.wait_recv()
                else:
                    cp.wait_recv()

    with jax.named_scope("units"):
        wait_units(Q, Qs, ts, tr)
    q2 = ring2(Q.at[:, y, :, lo4], Q.at[s, :, xh, hi4], q2s, q2r)
    with jax.named_scope("funits"):
        wait_units(F, Fs, fs, fr)
        for cp in g1:
            cp.wait_recv()
    f2 = ring2(F.at[:, y, :, lo4], F.at[s, :, xh, hi4], f2s, f2r)
    g2 = ring2(W2.at[:, y, :, :, lo5], W2.at[s, :, xh, :, hi5], w2s, w2r)
    with jax.named_scope("x"):
        for cp in xc:
            cp.wait_recv()
    xpair = remote(XX.at[w], XX.at[w], ps.at[0], pr.at[0], sib)
    xpair.start()
    with jax.named_scope("ring2"):
        for cp in q2:
            cp.wait_recv()
    for k in (1, 3, 2):
        cp = remote(YY.at[w, z], YY.at[w, z], ys.at[k], yr.at[k], dev(s, y, xh, (z + k) % 4, w))
        cp.start()
        yc.append(cp)
    for k in range(16):
        q = (r + k) % 16
        cp = remote(wos, WO.at[slot], os.at[k], orr.at[slot], dev(q // 8, (q // 2) % 4, q % 2, jo // 2, jo % 2))
        oc.append(cp)
        if k == 0:
            @pl.when(j != jo)
            def _():
                cp.start()

            @pl.when(j == jo)
            def _():
                WO[slot] = wos[...]
        else:
            cp.start()

    units = Q[...].reshape(128, 16, 256).astype(full)
    left = units[:, :8].reshape(1024, 256)
    right = units[:, 8:].reshape(1024, 256)
    WQT[0:256, :] = left.T.astype(low)
    WQT[256:384, :] = right[:, :128].T.astype(low)
    pads = right[:, 128:].astype(low)

    def params_of(i):
        pick = (iota((128, 1024), 1) == 8 * iota((128, 1024), 0) + i).astype(full).astype(low)
        return dot(pick, pads, 1, 0).astype(low)

    def row_of(i):
        t, f, l = owner_lanes(params_of(i), 1024, (0,), 8)
        return jnp.sum(jnp.where((f >= 8 * l) & (f < 8 * l + 8), t, 0.0), axis=0, keepdims=True)

    gain = row_of(0)
    shift = row_of(1)
    n0, p0 = iota((384, 128), 0), iota((384, 128), 1)
    n0 = (n0 // 128) * 1024 + 128 * j + (n0 & 127)
    at = n0 - 24 * p0
    inside = ((at >= 0) & (at < 24)).astype(full)
    t = dot(inside.astype(low), params_of(2), 1, 0)
    lane_want = jnp.sum(inside * at.astype(full), axis=1, keepdims=True)
    bias_q = jnp.sum(jnp.where(p0.astype(full) == lane_want, t, 0.0), axis=1, keepdims=True)
    co, si = ROPE[0], ROPE[1]

    def norm_slot(wi):
        def one(zi, carry):
            v = XX[wi, zi].astype(full)
            mean = jnp.mean(v, axis=-1, keepdims=True)
            c = v - mean
            var = jnp.mean(c * c, axis=-1, keepdims=True)
            h = c * lax.rsqrt(var + norm_eps)
            XH[wi, zi] = h.astype(low)
            HB[wi, zi] = (h * gain + shift).astype(low)
            return carry

        lax.fori_loop(0, 4, one, 0)

    def turn(v):
        a, b = v[0:8], v[8:16]
        return jnp.concatenate([a * co - b * si, b * co + a * si, v[16:]], axis=0)

    def qkv_slot(wi):
        t = dot(WQT[...], HB[wi].reshape(BLK, 1024), 1, 1) + bias_q
        for e in range(2):
            HT[e, wi, 0, 0] = turn(t[128 + 64 * e:192 + 64 * e]).astype(low)
            HT[e, wi, 0, 1] = t[256 + 64 * e:320 + 64 * e].astype(low)
            HT[e, wi, 1, 0] = (turn(t[64 * e:64 + 64 * e]).astype(low).astype(full) * 0.125).astype(low)

    def head_target(e, i):
        return dev(s, 2 * w + e, i, z, core), (y == 2 * w + e) & (xh == i) & (core == w)

    def kv_copy(e, i):
        return remote(HT.at[e, i, 0], KV.at[core, spot], hs.at[e, i, 0], kr.at[spot], head_target(e, i)[0])

    def q_copy(e, i):
        return remote(HT.at[e, i, 1, 0], QD.at[spot, 0], hs.at[e, i, 1], qr.at[spot], head_target(e, i)[0])

    def do_copy(e, i):
        return remote(HT.at[e, i, 1, 1], QD.at[spot, 1], hs.at[e, i, 2], dr.at[spot], head_target(e, i)[0])

    def send_qkv(i):
        for e in range(2):
            me = head_target(e, i)[1]

            @pl.when(jnp.logical_not(me))
            def _():
                kv_copy(e, i).start()
                q_copy(e, i).start()

            @pl.when(me)
            def _():
                KV[core, spot] = HT[e, i, 0]
                QD[spot, 0] = HT[e, i, 1, 0]

    def send_do(i):
        t = dot(WOF[...], YY[i].reshape(BLK, 1024), 1, 1)
        for e in range(2):
            HT[e, i, 1, 1] = t[64 * e:64 + 64 * e].astype(low)
            me = head_target(e, i)[1]

            @pl.when(jnp.logical_not(me))
            def _():
                do_copy(e, i).start()

            @pl.when(me)
            def _():
                QD[spot, 1] = HT[e, i, 1, 1]

    norm_slot(w)
    qkv_slot(w)
    send_qkv(w)
    xpair.wait_recv()
    norm_slot(1 - w)
    qkv_slot(1 - w)
    send_qkv(1 - w)

    VEC[0:1, :] = gain
    VEC[1:2, :] = row_of(3) + row_of(5)
    t, f, l = owner_lanes(params_of(4), 512, (0,), 32)
    base = f - 4 * (l - j)
    bias_1 = jnp.sum(
        jnp.where((((l - j) & 7) == 0) & (base >= 0) & (base < 32), t, 0.0), axis=0, keepdims=True
    )
    lp, ll = iota((128, 128), 0), iota((128, 128), 1)
    tok_pos = (iota((1, BLK), 1) + m * BLK).astype(full)
    pf = params_of(6).astype(full)
    for i in range(2):
        here = lp == s * 64 + i
        size = jnp.sum(jnp.where(here & (ll == 0), pf, 0.0)) * 64.0 + jnp.sum(jnp.where(here & (ll == 1), pf, 0.0))
        VAL[i:i + 1, :] = jnp.where(tok_pos < size, 1.0, 0.0)

    with jax.named_scope("f2"):
        for cp in f2 + g2:
            cp.wait_recv()
        with jax.named_scope("dy"):
            for cp in yc:
                cp.wait_recv()
        ypair = remote(YY.at[w], YY.at[w], ps.at[1], pr.at[1], sib)
        ypair.start()
    units = F[...].reshape(128, 16, 256).astype(full)
    W1[:, :256] = units[:, :8].reshape(1024, 256).astype(low)
    W1[:, 256:] = units[:, 8:].reshape(1024, 256).astype(low)

    def hidden(n, carry):
        wi, zi = jnp.where(n < 4, w, 1 - w), n % 4
        u = dot(HB[wi, zi], W1[...], 1, 0) + bias_1
        dg = dot(YY[wi, zi], W2[...].reshape(512, 1024), 1, 1)
        c0 = 0.7978845608028654
        t = jnp.tanh(c0 * (u + 0.044715 * (u * u * u)))
        GA[wi, zi] = (0.5 * u * (1.0 + t)).astype(low)
        slope = 0.5 * (1.0 + t) + (0.5 * c0) * u * (1.0 - t * t) * (1.0 + (3.0 * 0.044715) * (u * u))
        DU[wi, zi] = (dg * slope).astype(low)
        return carry

    with jax.named_scope("hidden"):
        lax.fori_loop(0, 4, hidden, 0)
        ypair.wait_recv()
        lax.fori_loop(4, 8, hidden, 0)
    with jax.named_scope("kv"):
        for i in range(4):
            @pl.when(jnp.logical_not(my_source(i)))
            def _():
                remote(HT.at[0, 0, 0], KV.at[w, i], hs.at[0, 0, 0], kr.at[i], source(i)).wait_recv()
    swap = remote(KV.at[w], KV.at[w], ks, krp, sib)
    swap.start()
    with jax.named_scope("wgrads"):
        for k in range(16):
            @pl.when(jnp.logical_not(wo_mine(k)))
            def _():
                remote(wos, WO.at[k], os.at[0], orr.at[k], dev(*wo_source(k))).wait_recv()
        units = WO[...].astype(full)
        WOF[:, :512] = units[:, :8].reshape(128, 512).astype(low)
        WOF[:, 512:] = units[:, 8:].reshape(128, 512).astype(low)
        send_do(w)
        send_do(1 - w)

        ga = GA[...].reshape(1024, 512)

        def first_w2(h):
            t = dot(ga, YY[:, :, :, 512 * h:512 * h + 512].reshape(1024, 512), 0, 0).astype(low)
            GW[:, :, :, :, 512 * h:512 * h + 512] = t.reshape(2, 4, 2, 32, 512)
            out = []
            for k in (1, 3, 2):
                yy, xx = (y + k) % 4, (x + k) % 4
                if h == 0:
                    cp = remote(GW.at[:, yy, :, :, lo5], wi0.at[k], g1s.at[2, 0, k], g1r.at[2, 0, k], dev(s, yy, xh, z, w))
                else:
                    cp = remote(GW.at[xx % 2, :, xx // 2, :, hi5], wi1.at[k], g1s.at[2, 1, k], g1r.at[2, 1, k], x_dev(xx, y, z, w))
                cp.start()
                out.append(cp)
            return out

        def first_unit(g, buf):
            out = []
            for k in (1, 3, 2):
                yy, xx = (y + k) % 4, (x + k) % 4
                cp = remote(buf.at[:, yy, :, lo4], gi0.at[g, k], g1s.at[g, 0, k], g1r.at[g, 0, k], dev(s, yy, xh, z, w))
                cp.start()
                out.append(cp)
                cp = remote(buf.at[xx % 2, :, xx // 2, hi4], gi1.at[g, k], g1s.at[g, 1, k], g1r.at[g, 1, k], x_dev(xx, y, z, w))
                cp.start()
                out.append(cp)
            return out

        def add4(a, b, c, d):
            return a.astype(full) + b.astype(full) + c.astype(full) + d.astype(full)

        def second_unit(g, buf):
            gm[g, 0] = add4(
                buf[:, y, :, 0:4], gi0[g, 1], gi0[g, 2], gi0[g, 3]
            ).astype(low).reshape(4, 4, 16, 256)
            gm[g, 1] = add4(
                buf[s, :, xh, 4:8], gi1[g, 1], gi1[g, 2], gi1[g, 3]
            ).astype(low)
            out = []
            for k in (1, 3, 2):
                yy, xx = (y + k) % 4, (x + k) % 4
                cp = remote(gm.at[g, 0, 2 * (xx % 2) + xx // 2], gi2.at[g, 0, k], g2s.at[g, 0, k], g2r.at[g, 0, k], x_dev(xx, y, z, w))
                cp.start()
                out.append(cp)
                cp = remote(gm.at[g, 1, yy], gi2.at[g, 1, k], g2s.at[g, 1, k], g2r.at[g, 1, k], dev(s, yy, xh, z, w))
                cp.start()
                out.append(cp)
            return out

        def second_w2():
            wm[0] = add4(GW[:, y, :, :, :512], wi0[1], wi0[2], wi0[3]).astype(low).reshape(4, 32, 512)
            wm[1] = add4(GW[s, :, xh, :, 512:], wi1[1], wi1[2], wi1[3]).astype(low)
            out = []
            for k in (1, 3, 2):
                yy, xx = (y + k) % 4, (x + k) % 4
                cp = remote(wm.at[0, 2 * (xx % 2) + xx // 2], wi2.at[0, k], g2s.at[2, 0, k], g2r.at[2, 0, k], x_dev(xx, y, z, w))
                cp.start()
                out.append(cp)
                cp = remote(wm.at[1, yy], wi2.at[1, k], g2s.at[2, 1, k], g2r.at[2, 1, k], dev(s, yy, xh, z, w))
                cp.start()
                out.append(cp)
            return out

        def last_unit(g, fin, got_units):
            fin[0:4] = add4(gm[g, 0, 2 * s + xh], gi2[g, 0, 1], gi2[g, 0, 2], gi2[g, 0, 3]).astype(low)
            fin[4:8] = add4(gm[g, 1, y], gi2[g, 1, 1], gi2[g, 1, 2], gi2[g, 1, 3]).astype(low)
            out = []
            for k in range(1, 8):
                q = (j + k) % 8
                cp = remote(fin.at[q], got_units.at[j], tts.at[g, k], ttr.at[g, k], dev(s, y, xh, q // 2, q % 2))
                cp.start()
                out.append(cp)
            got_units[j] = fin[j]
            return out

        c_w2 = first_w2(0)
        c_w2 += first_w2(1)

        du = DU[...].reshape(1024, 512)
        for n in range(4):
            t = dot(HB[:, :, :, 256 * n:256 * n + 256].reshape(1024, 256), du, 0, 0)
            t = jnp.concatenate([t[:, :256].reshape(32, 8, 256), t[:, 256:].reshape(32, 8, 256)], axis=1)
            GF[n // 2, 2 * (n % 2):2 * (n % 2) + 2] = t.astype(low).reshape(2, 2, 8, 16, 256)
        c_f = first_unit(0, GF)
        gb1 = jnp.sum(du.astype(full), axis=0, keepdims=True)
        gb_out = jnp.sum(YY[w, z].astype(full), axis=0, keepdims=True)
    with jax.named_scope("q"):
        for i in range(4):
            @pl.when(jnp.logical_not(my_source(i)))
            def _():
                remote(HT.at[0, 0, 1, 0], QD.at[i, 0], hs.at[0, 0, 1], qr.at[i], source(i)).wait_recv()
    with jax.named_scope("kvswap"):
        swap.wait_recv()

    causal = iota((BLK, BLK), 0) <= iota((BLK, BLK), 1)

    def query_block(i, carry):
        mi = 2 * i + (i + w) % 2
        q = QD[i, 0]

        def fwd(n, state, masked):
            run_max, total, out = state
            c, t = core_of(n), n // 2
            sc = dot(KV[c, t, 0], q, 0, 0)
            if masked:
                sc = jnp.where(causal, sc, -1e30)
            new_max = jnp.maximum(run_max, jnp.max(sc, axis=0, keepdims=True))
            pr = jnp.exp(sc - new_max)
            fac = jnp.exp(run_max - new_max)
            total = total * fac + jnp.sum(pr, axis=0, keepdims=True)
            out = out * fac + dot(KV[c, t, 1], pr.astype(low), 1, 0)
            return new_max, total, out

        state = (
            jnp.full((1, BLK), -1e30, full),
            jnp.zeros((1, BLK), full),
            jnp.zeros((HD, BLK), full),
        )
        state = lax.fori_loop(0, mi, lambda n, st: fwd(n, st, False), state)
        run_max, total, out = fwd(mi, state, True)
        out = out / total
        OF[i] = out
        LSE[i] = run_max + jnp.log(total)
        OB[i] = out.astype(low)

        @pl.when(jnp.logical_not(at_home(i)))
        def _():
            remote(OB.at[i], RO.at[e_me, i_me], bs.at[i, 0], br.at[0, e_me, i_me], home(i)).start()

        @pl.when(at_home(i))
        def _():
            RO[e_me, i_me] = OB[i]

        return carry

    with jax.named_scope("forward"):
        lax.fori_loop(0, 4, query_block, 0)


    def mlp_parts(i, carry):
        PH[i] = dot(DU[i].reshape(BLK, 512), W1[...], 1, 1)
        return carry

    def wait_home(g, src, dst):
        for e in range(2):
            for i in range(2):
                @pl.when(jnp.logical_not(head_here(e, i)))
                def _():
                    remote(src.at[0], dst.at[e, i], bs.at[0, g], br.at[g, e, i], head_at(e, i)).wait_recv()

    lax.fori_loop(0, 2, mlp_parts, 0)
    with jax.named_scope("ohome"):
        wait_home(0, OB, RO)

    def out_slot(i):
        ob = jnp.concatenate([RO[0, i], RO[1, i]], axis=0).astype(full)
        ob = (ob * VAL[pl.ds(i, 1), :]).astype(low)
        t = dot(ob, WOF[...], 0, 0) + dot(GA[i].reshape(BLK, 512), W2[...].reshape(512, 1024), 1, 0)
        TO[i] = t.astype(low).reshape(4, 128, 1024)
        return dot(ob, YY[i].reshape(BLK, 1024), 1, 0)

    g_wo = out_slot(1 - w)
    opair = remote(TO.at[1 - w], pin.at[0], pps.at[0], ppr.at[0], sib)
    opair.start()
    g_wo = g_wo + out_slot(w)
    GO[...] = jnp.concatenate(
        [g_wo[:, :512].reshape(16, 8, 512), g_wo[:, 512:].reshape(16, 8, 512)], axis=1
    ).astype(low)

    def owner(k):
        rr = 2 * j + k // 8
        return rr // 8, (rr // 2) % 4, rr % 2, (k % 8) // 2, k % 2

    def owner_copy(k):
        os_, oy, oxh, oz, ow = owner(k)
        me = (os_ == s) & (oy == y) & (oxh == xh) & (oz == z) & (ow == w)
        return remote(GO.at[k], fo_in.at[r], gos.at[k], gor.at[r], dev(os_, oy, oxh, oz, ow)), me

    for k in range(16):
        cp, me = owner_copy(k)

        @pl.when(jnp.logical_not(me))
        def _():
            cp.start()

        @pl.when(me)
        def _():
            fo_in[r] = GO[k]

    for i in range(4):
        @pl.when(jnp.logical_not(my_source(i)))
        def _():
            remote(HT.at[0, 0, 1, 1], QD.at[i, 1], hs.at[0, 0, 2], dr.at[i], source(i)).wait_recv()
    for i in range(4):
        DLT[i] = jnp.sum(QD[i, 1].astype(full) * OF[i], axis=0, keepdims=True)
    dqa[...] = jnp.zeros_like(dqa)

    def pair_of(c, t, i, masked):
        k = KV[c, t, 0]
        q = QD[i, 0]
        do = QD[i, 1]
        pr = jnp.exp(dot(k, q, 0, 0) - LSE[i])
        if masked:
            pr = jnp.where(causal, pr, 0.0)
        dp = dot(KV[c, t, 1], do, 0, 0)
        ds = (pr * (dp - DLT[i])).astype(low)
        acc[c, 0] += dot(q, ds, 1, 1)
        acc[c, 1] += dot(do, pr.astype(low), 1, 1)
        dqa[i] += dot(k, ds, 1, 0)

    def kv_home(t):
        summed[t] = (acc_own[t] + got[t].astype(full)).astype(low)

        @pl.when(jnp.logical_not(at_home(t)))
        def _():
            remote(summed.at[t], RKV.at[e_me, i_me], bs.at[t, 2], br2.at[e_me, i_me], home(t)).start()

        @pl.when(at_home(t))
        def _():
            RKV[e_me, i_me] = summed[t]

    def step(t):
        acc[...] = jnp.zeros_like(acc)

        def rest(u, carry):
            pair_of(u % 2, t, t + 1 + u // 2, False)
            return carry

        if t < 3:
            lax.fori_loop(0, 2 * (3 - t), rest, 0)

        @pl.when((t + w) % 2 == 1)
        def _():
            pair_of(1 - w, t, t, False)

        pair_of(w, t, t, True)
        other[t] = acc[1 - w].astype(low)
        acc_own[t] = acc[w]
        cp = remote(other.at[t], got.at[t], kss.at[t], ksr.at[t], sib)
        cp.start()
        DQB[t] = (dqa[t] * 0.125).astype(low)

        @pl.when(jnp.logical_not(at_home(t)))
        def _():
            remote(DQB.at[t], RQ1.at[e_me, i_me], bs.at[t, 1], br.at[1, e_me, i_me], home(t)).start()

        @pl.when(at_home(t))
        def _():
            RQ1[e_me, i_me] = DQB[t]

        return cp

    with jax.named_scope("step0"):
        k0 = step(0)
    with jax.named_scope("opair"):
        opair.wait_recv()

    def pair_z(n, buf):
        def one(t, carry):
            buf[w, t] = (buf[w, t].astype(full) + pin[n, t].astype(full)).astype(low)
            return carry

        lax.fori_loop(0, 4, one, 0)
        out = []
        for k in (1, 3, 2):
            zz = (z + k) % 4
            cp = remote(buf.at[w, zz], zin.at[n, k], zzs.at[n, k], zzr.at[n, k], dev(s, y, xh, zz, w))
            cp.start()
            out.append(cp)
        return out

    zo = pair_z(0, TO)
    with jax.named_scope("step1"):
        k1 = step(1)
    k0.wait_recv()
    kv_home(0)
    with jax.named_scope("wf1"):
        for cp in c_w2 + c_f:
            cp.wait_recv()
    d_w2 = second_w2()
    d_f = second_unit(0, GF)
    with jax.named_scope("step2"):
        k2 = step(2)
    k1.wait_recv()
    kv_home(1)
    k3 = step(3)
    k2.wait_recv()
    kv_home(2)
    with jax.named_scope("k3"):
        k3.wait_recv()
    kv_home(3)

    def turn_back(v):
        a, b = v[0:8], v[8:16]
        return jnp.concatenate([a * ROPE[0] + b * ROPE[1], b * ROPE[0] - a * ROPE[1], v[16:]], axis=0)

    def wait_kv():
        for e in range(2):
            for i in range(2):
                @pl.when(jnp.logical_not(head_here(e, i)))
                def _():
                    remote(summed.at[0], RKV.at[e, i], bs.at[0, 2], br2.at[e, i], head_at(e, i)).wait_recv()

    with jax.named_scope("fill"):
        with jax.named_scope("wf2"):
            for cp in d_w2 + d_f:
                cp.wait_recv()
        GFC2[:, :512] = add4(wm[0, 2 * s + xh], wi2[0, 1], wi2[0, 2], wi2[0, 3])
        GFC2[:, 512:] = add4(wm[1, y], wi2[1, 1], wi2[1, 2], wi2[1, 3])
        t_f = last_unit(0, Ff, RF)
        for q in range(16):
            @pl.when(jnp.logical_not((q == r) & (j == jo)))
            def _():
                remote(GO.at[0], fo_in.at[q], gos.at[0], gor.at[q], sender(q)).wait_recv()
        t = lax.fori_loop(0, 16, lambda q, t: t + fo_in[q].astype(full), jnp.zeros((16, 512), full))
        GWO[:, :512] = t[:8]
        GWO[:, 512:] = t[8:]
        mine_x = tok[0].astype(full)
        with jax.named_scope("zo"):
            for cp in zo:
                cp.wait_recv()
        t = add4(TO[w, z], zin[0, 1], zin[0, 2], zin[0, 3])
        OUT[0] = (mine_x + t + VEC[1:2, :]).astype(low)
        mean = jnp.mean(mine_x, axis=-1, keepdims=True)
        cen = mine_x - mean
        inv = lax.rsqrt(jnp.mean(cen * cen, axis=-1, keepdims=True) + norm_eps)
    with jax.named_scope("home"):
        wait_home(1, DQB, RQ1)
        wait_kv()

    def dh_slot(i):
        for e in range(2):
            DQ[i, 64 * e:64 * e + 64] = turn_back(RQ1[e, i].astype(full)).astype(low)
            DQ[i, 128 + 64 * e:192 + 64 * e] = turn_back(RKV[e, i, 0].astype(full)).astype(low)
            DQ[i, 256 + 64 * e:320 + 64 * e] = RKV[e, i, 1]
        t = dot(DQ[i], WQT[...], 0, 0) + PH[i]
        TH[i] = t.astype(low).reshape(4, 128, 1024)
        g_shift = jnp.sum(t, axis=0, keepdims=True)
        g_gain = jnp.sum(t * XH[i].reshape(BLK, 1024).astype(full), axis=0, keepdims=True)
        return g_shift, g_gain, jnp.sum(DQ[i].astype(full), axis=1, keepdims=True)

    a_shift, a_gain, a_bq = dh_slot(1 - w)
    hpair = remote(TH.at[1 - w], pin.at[1], pps.at[1], ppr.at[1], sib)
    hpair.start()
    b_shift, b_gain, b_bq = dh_slot(w)

    gq = dot(DQ[0], HB[0].reshape(BLK, 1024), 1, 0) + dot(DQ[1], HB[1].reshape(BLK, 1024), 1, 0)
    d0, p0 = iota((128, 1024), 1), iota((128, 1024), 0)
    block = (d0 >= 8 * p0) & (d0 < 8 * p0 + 8)
    dt, lt = iota((1024, 128), 0), iota((1024, 128), 1)

    def spread_row(v, lane):
        a = jnp.where(block, jnp.broadcast_to(v, (128, 1024)), 0.0).astype(low)
        return dot(a, (lt == lane + (dt & 7)).astype(full).astype(low), 1, 0)

    small = spread_row(a_gain + b_gain, 0) + spread_row(a_shift + b_shift, 8) + spread_row(gb_out, 16)
    f0, pf = iota((128, 512), 1), iota((128, 512), 0)
    base = f0 - 4 * (pf - j)
    a = jnp.where(
        (((pf - j) & 7) == 0) & (base >= 0) & (base < 32), jnp.broadcast_to(gb1, (128, 512)), 0.0
    ).astype(low)
    ft, lf = iota((512, 128), 0), iota((512, 128), 1)
    small = small + dot(a, (lf == 48 + (ft & 31)).astype(full).astype(low), 1, 0)
    n0, pn = iota((128, 384), 1), iota((128, 384), 0)
    qk_at = (n0 // 128) * 1024 + 128 * j + (n0 & 127) - 16 * pn
    v_at = 128 * j + (n0 & 127) - 8 * pn
    owns = ((n0 < 256) & (qk_at >= 0) & (qk_at < 16)) | ((n0 >= 256) & (v_at >= 0) & (v_at < 8))
    nt, ln = iota((384, 128), 0), iota((384, 128), 1)
    lane = jnp.where(nt < 256, 24 + (nt & 15), 40 + (nt & 7))
    b = jnp.where(ln == lane, jnp.broadcast_to(a_bq + b_bq, (384, 128)), 0.0).astype(low)
    small = small + dot(owns.astype(full).astype(low), b, 1, 0)
    head_row = (dt == 8 * lt).astype(full).astype(low)
    pad = dot(head_row, small.astype(low), 1, 0)
    left = gq[:256].T
    right = jnp.concatenate([gq[256:].T, pad], axis=1)
    GQ[...] = jnp.concatenate(
        [left.reshape(128, 8, 256), right.reshape(128, 8, 256)], axis=1
    ).astype(low).reshape(2, 4, 2, 8, 16, 256)
    c_q = first_unit(1, GQ)

    with jax.named_scope("hpair"):
        hpair.wait_recv()
    zh = pair_z(1, TH)
    with jax.named_scope("gq1"):
        for cp in c_q:
            cp.wait_recv()
    d_q = second_unit(1, GQ)
    with jax.named_scope("gq2"):
        for cp in d_q:
            cp.wait_recv()
    t_q = last_unit(1, Qf, RQ)
    with jax.named_scope("zh"):
        for cp in zh:
            cp.wait_recv()
    gh = add4(TH[w, z], zin[1, 1], zin[1, 2], zin[1, 3])
    hat = cen * inv
    gx = gh * VEC[0:1, :]
    gx = gx - jnp.mean(gx, axis=-1, keepdims=True) - hat * jnp.mean(gx * hat, axis=-1, keepdims=True)
    TG[0] = (YY[w, z].astype(full) + inv * gx).astype(low)
    with jax.named_scope("last"):
        for cp in t_f + t_q:
            cp.wait_recv()

    for e in range(2):
        for i in range(2):
            @pl.when(jnp.logical_not(head_target(e, i)[1]))
            def _():
                kv_copy(e, i).wait_send()
                q_copy(e, i).wait_send()
                do_copy(e, i).wait_send()

    @pl.when(j != jo)
    def _():
        oc[0].wait_send()

    for i in range(4):
        @pl.when(jnp.logical_not(at_home(i)))
        def _():
            remote(OB.at[i], RO.at[e_me, i_me], bs.at[i, 0], br.at[0, e_me, i_me], home(i)).wait_send()
            remote(DQB.at[i], RQ1.at[e_me, i_me], bs.at[i, 1], br.at[1, e_me, i_me], home(i)).wait_send()
            remote(summed.at[i], RKV.at[e_me, i_me], bs.at[i, 2], br2.at[e_me, i_me], home(i)).wait_send()
    for k in range(16):
        cp, me = owner_copy(k)

        @pl.when(jnp.logical_not(me))
        def _():
            cp.wait_send()
    for cp in oc[1:] + tq + tf + xc + yc + q2 + f2 + g1 + g2 + [xpair, ypair, swap, k0, k1, k2, k3]:
        cp.wait_send()
    for cp in [opair, hpair] + zo + zh + c_w2 + c_f + c_q + d_w2 + d_f + d_q + t_f + t_q:
        cp.wait_send()


def layer(*args):
    S = pltpu.SemaphoreType.DMA
    V = pltpu.VMEM
    sds = jax.ShapeDtypeStruct
    return pl.pallas_call(
        layer_kernel,
        name="layer",
        out_shape=(
            sds((1, 128, 1024), low),
            sds((1, 128, 1024), low),
            sds((8, 16, 256), low),
            sds((8, 16, 256), low),
            sds((32, 1024), full),
            sds((8, 1024), full),
        ),
        in_specs=[pl.BlockSpec(memory_space=pltpu.SMEM)] + [VM] * 13,
        out_specs=(VM,) * 6,
        scratch_shapes=[
            V((8, 128), full),
            V((2, 8, BLK), full),
            V((2, 4, 128, 1024), low),
            V((2, 4, 128, 1024), low),
            V((2, 4, 128, 1024), low),
            V((2, 4, 128, 1024), low),
            V((2, 4, 128, 512), low),
            V((2, 4, 128, 512), low),
            V((1024, 512), low),
            V((2, 4, 2, 32, 1024), low),
            V((384, 1024), low),
            V((128, 1024), low),
            V((8, 1024), full),
            V((8, BLK), full),
            V((2, 4, 2, 64, BLK), low),
            V((4, 2, 64, BLK), low),
            V((2, 4, 2, 8, 16, 256), low),
            V((2, 4, 2, 8, 16, 256), low),
            V((8, 16, 256), low),
            V((8, 16, 256), low),
            V((16, 512), low),
            V((16, 16, 512), low),
            V((2, 2, 2, 2, 64, BLK), low),
            V((4, 64, BLK), full),
            V((4, 64, BLK), low),
            V((4, 1, BLK), full),
            V((4, 1, BLK), full),
            V((2, 2, 64, BLK), low),
            V((2, 2, 64, BLK), low),
            V((2, 2, 2, 64, BLK), low),
            V((2, 2, 64, BLK), full),
            V((4, 2, 64, BLK), full),
            V((4, 64, BLK), full),
            V((4, 64, BLK), low),
            V((4, 2, 64, BLK), low),
            V((4, 2, 64, BLK), low),
            V((4, 2, 64, BLK), low),
            V((2, BLK, 1024), full),
            V((2, 384, BLK), low),
            V((2, 4, 128, 1024), low),
            V((2, 4, 128, 1024), low),
            V((2, 4, 128, 1024), low),
            V((2, 4, 128, 1024), low),
            V((2, 4, 2, 8, 16, 256), low),
            V((2, 4, 2, 8, 16, 256), low),
            V((2, 4, 2, 32, 1024), low),
            V((2, 4, 2, 2, 4, 16, 256), low),
            V((2, 4, 4, 4, 16, 256), low),
            V((4, 2, 2, 32, 512), low),
            V((4, 4, 32, 512), low),
            V((2, 2, 4, 4, 16, 256), low),
            V((2, 4, 32, 512), low),
            V((2, 2, 4, 4, 16, 256), low),
            V((2, 4, 32, 512), low),
            V((8, 16, 256), low),
            V((8, 16, 256), low),
            V((16, 16, 512), low),
            V((16, 16, 512), low),
            S((4,)), S((4,)), S((4,)), S((4,)), S((2,)), S((2,)), S((4, 8)), S((4, 8)), S((4, 8)), S((4, 8)), S((16,)),
            S((16,)), S((2, 4)), S((2, 4)), S((2, 4)), S((2, 4)),
            S((2, 4)), S((2, 4)), S((2, 4)), S((2, 4)), S((2, 2, 3)), S((4,)), S((4,)), S((4,)), S, S,
            S((4, 3)), S((2, 2, 2)), S((2, 2)), S((2,)), S((2,)), S((4,)), S((4,)), S((16,)), S((16,)),
            S((2, 4)), S((2, 4)), S((3, 2, 4)), S((3, 2, 4)), S((3, 2, 4)), S((3, 2, 4)), S((2, 8)), S((2, 8)),
        ],
        compiler_params=pltpu.CompilerParams(
            collective_id=0, has_side_effects=True, vmem_limit_bytes=62 << 20
        ),
    )(*args)


def finish_kernel(out, tg, RF, RQ, gfc2, gwo,
                  OUT, TG, GQKV, GFC1, GFC2, GWO, GG, GS, BQK, BV, BO, B1, B2):
    OUT[...] = out[...]
    TG[...] = tg[...]
    GFC2[...] = gfc2[...]
    GWO[...] = gwo[...]
    for rr in range(16):
        g = rr // 4
        c, half = g // 2, g % 2
        for hi in range(2):
            tiles = [RF[4 * hi + n, 8 * c:8 * c + 8, 128 * half:128 * half + 128].astype(full) for n in range(4)]
            col = 128 * (2 * rr + hi)
            GFC1[:, col:col + 128] = lane_mix(tiles, [32 * (n - rr % 4) for n in range(4)])
    tail = jnp.zeros((8, 128), full)
    for q in range(8):
        c = 128 * q
        GQKV[:, c:c + 128] = RQ[q, 0:8, 0:128].astype(full)
        GQKV[:, 1024 + c:1152 + c] = RQ[q, 0:8, 128:256].astype(full)
        GQKV[:, 2048 + c:2176 + c] = RQ[q, 8:16, 0:128].astype(full)
        tail = tail + RQ[q, 8:16, 128:256].astype(full)
    row = tail[0]
    GG[...] = row[0:8]
    GS[...] = row[8:16]
    BQK[...] = row[24:40]
    BV[...] = row[40:48]
    BO[...] = row[16:24]
    B1[...] = row[48:80]
    B2[...] = row[16:24]


def finish(*args):
    sds = jax.ShapeDtypeStruct
    return pl.pallas_call(
        finish_kernel,
        name="finish",
        out_shape=(
            sds((1, 128, 1024), low),
            sds((1, 128, 1024), low),
            sds((8, 3072), full),
            sds((8, 4096), full),
            sds((32, 1024), full),
            sds((8, 1024), full),
            sds((8,), full),
            sds((8,), full),
            sds((16,), full),
            sds((8,), full),
            sds((8,), full),
            sds((32,), full),
            sds((8,), full),
        ),
        in_specs=[VM] * 6,
        out_specs=(VM,) * 13,
    )(*args)


def shards(
    tokens, lengths, ln_gain, ln_bias, w_qkv, b_qkv, w_out, b_out, w_fc1, b_fc1, w_fc2, b_fc2, cotangent
):
    freq = rope_base ** (-2.0 * np.arange(8) / ROT)
    near = freq[:, None] * np.arange(BLK)[None, :]
    far = freq[:, None] * (BLK * np.arange(BLK))[None, :]
    turns = jnp.asarray(np.stack([np.cos(near), np.sin(near), np.cos(far), np.sin(far)]).astype(np.float32))
    parts = layer(
        lengths, tokens, cotangent, ln_gain, ln_bias, b_qkv, b_out, b_fc1, b_fc2, w_qkv, w_out, w_fc1, w_fc2, turns
    )
    OUT, TG, GQKV, GFC1, GFC2, GWO, GG, GS, BQK, BV, BO, B1, B2 = finish(*parts)
    return (OUT, TG, GG, GS, GQKV, BQK, BV, GWO, BO, GFC1, B1, GFC2, B2)


def solution(mesh):
    rows, tok, par, vec = (
        P(("slot", "wsh")), P(("slot", "wsh"), "ctx", None), P(("slot", "ctx", "wsh"), None), P(("slot", "ctx", "wsh"))
    )
    return jax.shard_map(
        shards,
        mesh=mesh,
        in_specs=(tok, rows, vec, vec, par, vec, par, vec, par, vec, par, vec, tok),
        out_specs=(tok, tok, vec, vec, par, vec, vec, par, vec, par, vec, par, vec),
        check_vma=False,
    )
```

```python
import functools

import jax
import jax.numpy as jnp
import numpy as np
from jax import lax
from jax.experimental import pallas as pl
from jax.experimental.pallas import tpu as pltpu
from jax.sharding import PartitionSpec as P

HEADS = 16
HD = 64
ROT = 16
HQ = 1024
D = 1024
FF = 4096
BLK = 512

norm_eps = 1e-05
rope_base = 10000.0
MESH = pl.DeviceIdType.MESH
low = jnp.bfloat16
full = jnp.float32
VM = pl.BlockSpec(memory_space=pltpu.VMEM)
AN = pl.BlockSpec(memory_space=pl.ANY)


def place():
    s = lax.axis_index("slot")
    c = lax.axis_index("ctx")
    w = lax.axis_index("wsh")
    return s, c // 8, (c // 4) % 2, c % 4, w


def dev(s, y, xh, z, w):
    return (s, y * 8 + xh * 4 + z, w)


def x_dev(x, y, z, w):
    return dev(x % 2, y, x // 2, z, w)


def signal(barrier, target):
    pl.semaphore_signal(barrier, inc=1, device_id=target, device_id_type=MESH)


def remote(src, dst, send, recv, target):
    return pltpu.make_async_remote_copy(
        src_ref=src, dst_ref=dst, send_sem=send, recv_sem=recv,
        device_id=target, device_id_type=MESH,
    )


def iota(shape, axis):
    return lax.broadcasted_iota(jnp.int32, shape, axis)


def dot(a, b, ca, cb):
    return lax.dot_general(a, b, (((ca,), (cb,)), ((), ())), preferred_element_type=full)


def core_of(m):
    return ((m + 1) // 2) % 2


def owner_lanes(params, width, lanes, step):
    f, l = iota((128, width), 1), iota((128, width), 0)
    pick = (l == lanes[0] + (f & (step - 1)))
    for other in lanes[1:]:
        pick = pick | (l == other + (f & (step - 1)))
    return dot(params, pick.astype(full).astype(low), 1, 0), f, l


def lane_mix(tiles, shifts):
    lane = iota((8, 128), 1)
    out = jnp.zeros((8, 128), full)
    for g in range(4):
        t = tiles[g]
        if shifts[g] % 128:
            t = pltpu.roll(t, shifts[g] % 128, 1)
        out = jnp.where((lane >= 32 * g) & (lane < 32 * g + 32), t, out)
    return out


def layer_kernel(
    lens, tok, cot, lg, lb, bq, bo, bf, bg, wq, wo, w1, w2, turns, OUT, TG, RF, RQ, GFC2, GWO, PAD, ROPE, SL, XX, YY, HB, XH, GA, DU,
    W1, W2, WQT, WOF, VEC, VAL, KV, QD, Q, F, Qs, Fs, wos, WO, HT, OF, OB, LSE, DLT, RO, RQ1, RKV, acc,
    acc_own, dqa, DQB, other, got, summed, PH, DQ, TO, TH, pin, zin, GF, GQ, GW, gi0, gi1, wi0, wi1, gm, wm,
    gi2, wi2, Ff, QIN, GO, fo_in, zs, zr, ys, yr, ps, pr, ts, tr, fs, fr, os, orr, q2s, q2r, f1s, f1r,
    f2s, f2r, w1s, w1r, w2s, w2r, hs, kr, qr, dr, ks, krp, bs, br, br2, pps, ppr, hps, hpr, kss, ksr, gos, gor, zzs, zzr,
    g1s, g1r, g2s, g2r, tts, ttr, us, ur,
):
    s, y, xh, z, w = place()
    x = xh * 2 + s
    r = s * 8 + y * 2 + xh
    j = z * 2 + w
    jo = r // 2
    m = y * 2 + xh
    core, spot = core_of(m), m // 2
    keep = (j == jo).astype(jnp.int32)
    mine = ((y // 2 == w) & (core == w)).astype(jnp.int32)
    sib = dev(s, y, xh, z, 1 - w)

    lo4, hi4 = pl.ds(0, 4), pl.ds(4, 4)
    lo5, hi5 = pl.ds(0, 512), pl.ds(512, 512)
    half = z // 2
    flip = 1 - half

    def ahead(k, q):
        return x_dev((x + k * flip) % 4, (y + k * half) % 4, q // 2, q % 2)

    def behind(k, q):
        if q < 4:
            return x_dev((x + 4 - k) % 4, y, q // 2, q % 2)
        return dev(s, (y + 4 - k) % 4, xh, q // 2, q % 2)

    barrier = pltpu.get_barrier_semaphore()
    for k in range(4):
        for q in range(8):
            if k == 0:
                @pl.when(j != q)
                def _():
                    signal(barrier, behind(k, q))
            else:
                signal(barrier, behind(k, q))
    for k in range(1, 4):
        signal(barrier, x_dev((x + k) % 4, y, z, w))
        signal(barrier, dev(s, (y + k) % 4, xh, z, w))

    def wo_source(k):
        rr = 2 * j + k // 8
        return rr // 8, (rr // 2) % 4, rr % 2, (k % 8) // 2, k % 2

    def wo_mine(k):
        ss, sy, sxh, sz, sw = wo_source(k)
        return (ss == s) & (sy == y) & (sxh == xh) & (sz == z) & (sw == w)

    def source(i):
        return dev(s, i, (i + w) % 2, z, y // 2)

    def my_source(i):
        return (y == i) & (xh == (i + w) % 2) & (w == y // 2)

    def sender(q):
        return dev(q // 8, (q // 2) % 4, q % 2, jo // 2, jo % 2)

    def home(i):
        return dev(s, i, (i + w) % 2, z, y // 2)

    def at_home(i):
        return (y == i) & (xh == (i + w) % 2) & (w == y // 2)

    def head_at(e, i):
        return dev(s, 2 * w + e, i, z, core)

    def head_here(e, i):
        return (y == 2 * w + e) & (xh == i) & (core == w)

    e_me, i_me = y % 2, xh
    XX[w, z] = tok[0]
    first_row = iota((8, 128), 0)
    PAD[...] = jnp.zeros_like(PAD)
    PAD[0:1, 0:8] = lg[...].reshape(1, 8)
    PAD[1:2, 0:8] = lb[...].reshape(1, 8)
    PAD[2:3, 0:24] = bq[...].reshape(1, 24)
    PAD[3:4, 0:8] = bo[...].reshape(1, 8)
    PAD[4:5, 0:32] = bf[...].reshape(1, 32)
    PAD[5:6, 0:8] = bg[...].reshape(1, 8)
    lane8 = iota((8, 128), 1)
    size = jnp.full((8, 128), lens[0], jnp.int32)
    padded = jnp.where(
        first_row == 6,
        jnp.where(lane8 == 0, (size >> 6).astype(full), jnp.where(lane8 == 1, (size & 63).astype(full), 0.0)),
        PAD[...],
    )
    for q in range(8):
        c = 128 * q
        top = jnp.concatenate([wq[:, c:c + 128], wq[:, 1024 + c:1152 + c]], axis=1)
        bot = jnp.concatenate([wq[:, 2048 + c:2176 + c], padded], axis=1)
        Qs[q] = jnp.concatenate([top, bot], axis=0).astype(low)

    W2[s, y, xh] = w2[...].astype(low)
    for q in range(8):
        tiles = []
        for g in range(4):
            parts = [w1[:, 128 * (2 * (4 * g + n) + q // 4):128 * (2 * (4 * g + n) + q // 4) + 128] for n in range(4)]
            tiles.append(lane_mix(parts, [32 * (n - q % 4) for n in range(4)]))
        top = jnp.concatenate(tiles[:2], axis=1)
        bot = jnp.concatenate(tiles[2:], axis=1)
        Fs[q] = jnp.concatenate([top, bot], axis=0).astype(low)
    F[s, y, xh, j] = Fs[j]

    def ring1(ref0, ref1, snd, rcv):
        out = []
        for k in (1, 3, 2):
            cp = remote(ref0, ref0, snd.at[0, k], rcv.at[0, k], x_dev((x + k) % 4, y, z, w))
            cp.start()
            out.append(cp)
            cp = remote(ref1, ref1, snd.at[1, k], rcv.at[1, k], dev(s, (y + k) % 4, xh, z, w))
            cp.start()
            out.append(cp)
        return out

    def ring2(ref0, ref1, snd, rcv):
        out = []
        for k in (1, 3, 2):
            cp = remote(ref0, ref0, snd.at[0, k], rcv.at[0, k], dev(s, (y + k) % 4, xh, z, w))
            cp.start()
            out.append(cp)
            cp = remote(ref1, ref1, snd.at[1, k], rcv.at[1, k], x_dev((x + k) % 4, y, z, w))
            cp.start()
            out.append(cp)
        return out

    def z_near(buf, snd, rcv):
        out = []
        for k in (1, 3):
            cp = remote(buf.at[w, z], buf.at[w, z], snd.at[k], rcv.at[k], dev(s, y, xh, (z + k) % 4, w))
            cp.start()
            out.append(cp)
        return out

    def z_far(buf, snd, rcv):
        up, down = (z + 1) % 4, (z + 3) % 4
        a = buf.at[w, down, pl.ds(0, 64)]
        b = buf.at[w, up, pl.ds(64, 64)]
        out = [
            remote(a, a, snd.at[2], rcv.at[2], dev(s, y, xh, up, w)),
            remote(b, b, snd.at[0], rcv.at[0], dev(s, y, xh, down, w)),
        ]
        for cp in out:
            cp.start()
        return out

    with jax.named_scope("barrier"):
        pl.semaphore_wait(barrier, 31 + 6)

    slot = (r % 2) * 8 + j
    tq, tf, oc = [], [], []
    for k in (1, 3, 2, 0):
        for n in range(8):
            if k == 0 and n == 0:
                continue
            q = (j + n) % 8
            cp = remote(Qs.at[q], Q.at[s, y, xh, j], ts.at[k, n], tr.at[k, j], ahead(k, q))
            cp.start()
            tq.append(cp)
    for k in range(1, 8):
        q = (j + k) % 8
        cp = remote(Fs.at[q], F.at[s, y, xh, j], fs.at[k], fr.at[k], dev(s, y, xh, q // 2, q % 2))
        cp.start()
        tf.append(cp)
    g1 = ring1(W2.at[s, y, xh, :, lo5], W2.at[s, y, xh, :, hi5], w1s, w1r)
    xc = z_near(XX, zs, zr)
    Q[s, y, xh, j] = Qs[j]

    row = iota((128, 1024), 0) + (m * BLK + z * 128)
    YY[w, z] = jnp.where(row < lens[0], cot[0].astype(full), 0.0).astype(low)
    wos[...] = jnp.concatenate([wo[:, :512], wo[:, 512:]], axis=0).astype(low)
    c0, s0 = turns[0], turns[1]
    at_m = iota((8, 128), 1) == m
    cm = jnp.sum(jnp.where(at_m, turns[2, :, :128], 0.0), axis=1, keepdims=True)
    sm = jnp.sum(jnp.where(at_m, turns[3, :, :128], 0.0), axis=1, keepdims=True)
    ROPE[0] = cm * c0 - sm * s0
    ROPE[1] = sm * c0 + cm * s0

    def wait_units(buf, stage, snd, rcv):
        for k in range(4):
            for q in range(8):
                if q < 4:
                    bx = (x + 4 - k) % 4
                    here = buf.at[bx % 2, y, bx // 2, q]
                else:
                    here = buf.at[s, (y + 4 - k) % 4, xh, q]
                cp = remote(stage.at[0], here, snd.at[k, 0], rcv.at[k, q], behind(k, q))
                if k == 0:
                    @pl.when(j != q)
                    def _():
                        cp.wait_recv()
                else:
                    cp.wait_recv()

    with jax.named_scope("units"):
        wait_units(Q, Qs, ts, tr)
    with jax.named_scope("tf"):
        for cp in tf:
            cp.wait_recv()
    f1 = ring1(F.at[s, y, xh, lo4], F.at[s, y, xh, hi4], f1s, f1r)
    q2 = ring2(Q.at[:, y, :, lo4], Q.at[s, :, xh, hi4], q2s, q2r)
    with jax.named_scope("g1"):
        for cp in g1:
            cp.wait_recv()
    with jax.named_scope("f1"):
        for cp in f1:
            cp.wait_recv()
    f2 = ring2(F.at[:, y, :, lo4], F.at[s, :, xh, hi4], f2s, f2r)
    g2 = ring2(W2.at[:, y, :, :, lo5], W2.at[s, :, xh, :, hi5], w2s, w2r)
    with jax.named_scope("xnear"):
        for cp in xc:
            cp.wait_recv()
    xf = z_far(XX, zs, zr)
    yc = z_near(YY, ys, yr)
    for k in range(16):
        q = (r + k) % 16
        cp = remote(wos, WO.at[slot], os.at[k], orr.at[slot], dev(q // 8, (q // 2) % 4, q % 2, jo // 2, jo % 2))
        oc.append(cp)
        if k == 0:
            @pl.when(j != jo)
            def _():
                cp.start()

            @pl.when(j == jo)
            def _():
                WO[slot] = wos[...]
        else:
            cp.start()
    with jax.named_scope("x"):
        for cp in xf:
            cp.wait_recv()
    xpair = remote(XX.at[w], XX.at[w], ps.at[0], pr.at[0], sib)
    xpair.start()
    with jax.named_scope("ring2"):
        for cp in q2:
            cp.wait_recv()
    units = Q[...].reshape(128, 16, 256).astype(full)
    left = units[:, :8].reshape(1024, 256)
    right = units[:, 8:].reshape(1024, 256)
    WQT[0:256, :] = left.T.astype(low)
    WQT[256:384, :] = right[:, :128].T.astype(low)
    pads = right[:, 128:].astype(low)

    def params_of(i):
        pick = (iota((128, 1024), 1) == 8 * iota((128, 1024), 0) + i).astype(full).astype(low)
        return dot(pick, pads, 1, 0).astype(low)

    def row_of(i):
        t, f, l = owner_lanes(params_of(i), 1024, (0,), 8)
        return jnp.sum(jnp.where((f >= 8 * l) & (f < 8 * l + 8), t, 0.0), axis=0, keepdims=True)

    gain = row_of(0)
    shift = row_of(1)
    n0, p0 = iota((384, 128), 0), iota((384, 128), 1)
    n0 = (n0 // 128) * 1024 + 128 * j + (n0 & 127)
    at = n0 - 24 * p0
    inside = ((at >= 0) & (at < 24)).astype(full)
    t = dot(inside.astype(low), params_of(2), 1, 0)
    lane_want = jnp.sum(inside * at.astype(full), axis=1, keepdims=True)
    bias_q = jnp.sum(jnp.where(p0.astype(full) == lane_want, t, 0.0), axis=1, keepdims=True)
    co, si = ROPE[0], ROPE[1]

    def norm_slot(wi):
        def one(zi, carry):
            v = XX[wi, zi].astype(full)
            mean = jnp.mean(v, axis=-1, keepdims=True)
            c = v - mean
            var = jnp.mean(c * c, axis=-1, keepdims=True)
            h = c * lax.rsqrt(var + norm_eps)
            XH[wi, zi] = h.astype(low)
            HB[wi, zi] = (h * gain + shift).astype(low)
            return carry

        lax.fori_loop(0, 4, one, 0)

    def turn(v):
        a, b = v[0:8], v[8:16]
        return jnp.concatenate([a * co - b * si, b * co + a * si, v[16:]], axis=0)

    def qkv_slot(wi):
        t = dot(WQT[...], HB[wi].reshape(BLK, 1024), 1, 1) + bias_q
        for e in range(2):
            HT[e, wi, 0, 0] = turn(t[128 + 64 * e:192 + 64 * e]).astype(low)
            HT[e, wi, 0, 1] = t[256 + 64 * e:320 + 64 * e].astype(low)
            HT[e, wi, 1, 0] = (turn(t[64 * e:64 + 64 * e]).astype(low).astype(full) * 0.125).astype(low)

    def head_target(e, i):
        return dev(s, 2 * w + e, i, z, core), (y == 2 * w + e) & (xh == i) & (core == w)

    def kv_copy(e, i):
        return remote(HT.at[e, i, 0], KV.at[core, spot], hs.at[e, i, 0], kr.at[spot], head_target(e, i)[0])

    def q_copy(e, i):
        return remote(HT.at[e, i, 1, 0], QD.at[spot, 0], hs.at[e, i, 1], qr.at[spot], head_target(e, i)[0])

    def do_copy(e, i):
        return remote(HT.at[e, i, 1, 1], QD.at[spot, 1], hs.at[e, i, 2], dr.at[spot], head_target(e, i)[0])

    def send_qkv(i):
        for e in range(2):
            me = head_target(e, i)[1]

            @pl.when(jnp.logical_not(me))
            def _():
                kv_copy(e, i).start()
                q_copy(e, i).start()

            @pl.when(me)
            def _():
                KV[core, spot] = HT[e, i, 0]
                QD[spot, 0] = HT[e, i, 1, 0]

    def send_do(i):
        t = dot(WOF[...], YY[i].reshape(BLK, 1024), 1, 1)
        for e in range(2):
            HT[e, i, 1, 1] = t[64 * e:64 + 64 * e].astype(low)
            me = head_target(e, i)[1]

            @pl.when(jnp.logical_not(me))
            def _():
                do_copy(e, i).start()

            @pl.when(me)
            def _():
                QD[spot, 1] = HT[e, i, 1, 1]

    norm_slot(w)
    qkv_slot(w)
    send_qkv(w)
    xpair.wait_recv()
    norm_slot(1 - w)
    qkv_slot(1 - w)
    send_qkv(1 - w)

    with jax.named_scope("ynear"):
        for cp in yc:
            cp.wait_recv()
    yf = z_far(YY, ys, yr)
    VEC[0:1, :] = gain
    VEC[1:2, :] = row_of(3) + row_of(5)
    t, f, l = owner_lanes(params_of(4), 512, (0,), 32)
    base = f - 4 * (l - j)
    bias_1 = jnp.sum(
        jnp.where((((l - j) & 7) == 0) & (base >= 0) & (base < 32), t, 0.0), axis=0, keepdims=True
    )
    lp, ll = iota((128, 128), 0), iota((128, 128), 1)
    tok_pos = (iota((1, BLK), 1) + m * BLK).astype(full)
    pf = params_of(6).astype(full)
    for i in range(2):
        here = lp == s * 64 + i
        size = jnp.sum(jnp.where(here & (ll == 0), pf, 0.0)) * 64.0 + jnp.sum(jnp.where(here & (ll == 1), pf, 0.0))
        VAL[i:i + 1, :] = jnp.where(tok_pos < size, 1.0, 0.0)

    with jax.named_scope("f2"):
        for cp in f2 + g2:
            cp.wait_recv()
    units = F[...].reshape(128, 16, 256).astype(full)
    W1[:, :256] = units[:, :8].reshape(1024, 256).astype(low)
    W1[:, 256:] = units[:, 8:].reshape(1024, 256).astype(low)
    g0 = 0.7978845608028654

    def hidden_up(n, carry):
        wi, zi = n // 2, pl.ds(2 * (n % 2), 2)
        u = dot(HB[wi, zi].reshape(256, 1024), W1[...], 1, 0) + bias_1
        t = jnp.tanh(g0 * (u + 0.044715 * (u * u * u)))
        GA[wi, zi] = (0.5 * u * (1.0 + t)).astype(low).reshape(2, 128, 512)
        slope = 0.5 * (1.0 + t) + (0.5 * g0) * u * (1.0 - t * t) * (1.0 + (3.0 * 0.044715) * (u * u))
        SL[wi, zi] = slope.reshape(2, 128, 512)
        return carry

    with jax.named_scope("hidden_up"):
        lax.fori_loop(0, 4, hidden_up, 0)
    with jax.named_scope("dy"):
        for cp in yf:
            cp.wait_recv()
    ypair = remote(YY.at[w], YY.at[w], ps.at[1], pr.at[1], sib)
    ypair.start()

    def hidden_down(n, carry):
        wi, zi = jnp.where(n < 2, w, 1 - w), pl.ds(2 * (n % 2), 2)
        dg = dot(YY[wi, zi].reshape(256, 1024), W2[...].reshape(512, 1024), 1, 1)
        DU[wi, zi] = (dg.reshape(2, 128, 512) * SL[wi, zi]).astype(low)
        return carry

    with jax.named_scope("hidden_down"):
        lax.fori_loop(0, 2, hidden_down, 0)
        ypair.wait_recv()
        lax.fori_loop(2, 4, hidden_down, 0)
    with jax.named_scope("wgrads"):
        ga = GA[...].reshape(1024, 512)

        def first_w2(h):
            t = dot(ga, YY[:, :, :, 512 * h:512 * h + 512].reshape(1024, 512), 0, 0).astype(low)
            GW[:, :, :, :, 512 * h:512 * h + 512] = t.reshape(2, 4, 2, 32, 512)
            out = []
            for k in (1, 3, 2):
                yy, xx = (y + k) % 4, (x + k) % 4
                if h == 0:
                    cp = remote(GW.at[:, yy, :, :, lo5], wi0.at[k], g1s.at[2, 0, k], g1r.at[2, 0, k], dev(s, yy, xh, z, w))
                else:
                    cp = remote(GW.at[xx % 2, :, xx // 2, :, hi5], wi1.at[k], g1s.at[2, 1, k], g1r.at[2, 1, k], x_dev(xx, y, z, w))
                cp.start()
                out.append(cp)
            return out

        def first_unit(g, buf):
            out = []
            for k in (1, 3, 2):
                yy, xx = (y + k) % 4, (x + k) % 4
                cp = remote(buf.at[:, yy, :, lo4], gi0.at[g, k], g1s.at[g, 0, k], g1r.at[g, 0, k], dev(s, yy, xh, z, w))
                cp.start()
                out.append(cp)
                cp = remote(buf.at[xx % 2, :, xx // 2, hi4], gi1.at[g, k], g1s.at[g, 1, k], g1r.at[g, 1, k], x_dev(xx, y, z, w))
                cp.start()
                out.append(cp)
            return out

        def add4(a, b, c, d):
            return a.astype(full) + b.astype(full) + c.astype(full) + d.astype(full)

        def second_unit(g, buf):
            gm[g, 0] = add4(
                buf[:, y, :, 0:4], gi0[g, 1], gi0[g, 2], gi0[g, 3]
            ).astype(low).reshape(4, 4, 16, 256)
            gm[g, 1] = add4(
                buf[s, :, xh, 4:8], gi1[g, 1], gi1[g, 2], gi1[g, 3]
            ).astype(low)
            out = []
            for k in (1, 3, 2):
                yy, xx = (y + k) % 4, (x + k) % 4
                cp = remote(gm.at[g, 0, 2 * (xx % 2) + xx // 2], gi2.at[g, 0, k], g2s.at[g, 0, k], g2r.at[g, 0, k], x_dev(xx, y, z, w))
                cp.start()
                out.append(cp)
                cp = remote(gm.at[g, 1, yy], gi2.at[g, 1, k], g2s.at[g, 1, k], g2r.at[g, 1, k], dev(s, yy, xh, z, w))
                cp.start()
                out.append(cp)
            return out

        def second_w2():
            wm[0] = add4(GW[:, y, :, :, :512], wi0[1], wi0[2], wi0[3]).astype(low).reshape(4, 32, 512)
            wm[1] = add4(GW[s, :, xh, :, 512:], wi1[1], wi1[2], wi1[3]).astype(low)
            out = []
            for k in (1, 3, 2):
                yy, xx = (y + k) % 4, (x + k) % 4
                cp = remote(wm.at[0, 2 * (xx % 2) + xx // 2], wi2.at[0, k], g2s.at[2, 0, k], g2r.at[2, 0, k], x_dev(xx, y, z, w))
                cp.start()
                out.append(cp)
                cp = remote(wm.at[1, yy], wi2.at[1, k], g2s.at[2, 1, k], g2r.at[2, 1, k], dev(s, yy, xh, z, w))
                cp.start()
                out.append(cp)
            return out

        def last_unit(g, fin, got_units):
            fin[0:4] = add4(gm[g, 0, 2 * s + xh], gi2[g, 0, 1], gi2[g, 0, 2], gi2[g, 0, 3]).astype(low)
            fin[4:8] = add4(gm[g, 1, y], gi2[g, 1, 1], gi2[g, 1, 2], gi2[g, 1, 3]).astype(low)
            out = []
            for k in range(1, 8):
                q = (j + k) % 8
                cp = remote(fin.at[q], got_units.at[j], tts.at[g, k], ttr.at[g, k], dev(s, y, xh, q // 2, q % 2))
                cp.start()
                out.append(cp)
            got_units[j] = fin[j]
            return out

        c_w2 = first_w2(0)
        c_w2 += first_w2(1)

    with jax.named_scope("kv"):
        for i in range(4):
            @pl.when(jnp.logical_not(my_source(i)))
            def _():
                remote(HT.at[0, 0, 0], KV.at[w, i], hs.at[0, 0, 0], kr.at[i], source(i)).wait_recv()
    swap = remote(KV.at[w], KV.at[w], ks, krp, sib)
    swap.start()
    with jax.named_scope("do"):
        for k in range(16):
            @pl.when(jnp.logical_not(wo_mine(k)))
            def _():
                remote(wos, WO.at[k], os.at[0], orr.at[k], dev(*wo_source(k))).wait_recv()
        units = WO[...].astype(full)
        WOF[:, :512] = units[:, :8].reshape(128, 512).astype(low)
        WOF[:, 512:] = units[:, 8:].reshape(128, 512).astype(low)
        send_do(w)
        send_do(1 - w)
    with jax.named_scope("wgrads1"):
        du = DU[...].reshape(1024, 512)
        for n in range(4):
            t = dot(HB[:, :, :, 256 * n:256 * n + 256].reshape(1024, 256), du, 0, 0)
            t = jnp.concatenate([t[:, :256].reshape(32, 8, 256), t[:, 256:].reshape(32, 8, 256)], axis=1)
            GF[n // 2, 2 * (n % 2):2 * (n % 2) + 2] = t.astype(low).reshape(2, 2, 8, 16, 256)
        c_f = first_unit(0, GF)
        gb1 = jnp.sum(du.astype(full), axis=0, keepdims=True)
        gb_out = jnp.sum(YY[w, z].astype(full), axis=0, keepdims=True)

    with jax.named_scope("q"):
        for i in range(4):
            @pl.when(jnp.logical_not(my_source(i)))
            def _():
                remote(HT.at[0, 0, 1, 0], QD.at[i, 0], hs.at[0, 0, 1], qr.at[i], source(i)).wait_recv()
    with jax.named_scope("kvswap"):
        swap.wait_recv()

    causal = iota((BLK, BLK), 0) <= iota((BLK, BLK), 1)

    def query_block(i, carry):
        mi = 2 * i + (i + w) % 2
        q = QD[i, 0]

        def fwd(n, state, masked):
            run_max, total, out = state
            c, t = core_of(n), n // 2
            sc = dot(KV[c, t, 0], q, 0, 0)
            if masked:
                sc = jnp.where(causal, sc, -1e30)
            new_max = jnp.maximum(run_max, jnp.max(sc, axis=0, keepdims=True))
            pr = jnp.exp(sc - new_max)
            fac = jnp.exp(run_max - new_max)
            total = total * fac + jnp.sum(pr, axis=0, keepdims=True)
            out = out * fac + dot(KV[c, t, 1], pr.astype(low), 1, 0)
            return new_max, total, out

        state = (
            jnp.full((1, BLK), -1e30, full),
            jnp.zeros((1, BLK), full),
            jnp.zeros((HD, BLK), full),
        )
        state = lax.fori_loop(0, mi, lambda n, st: fwd(n, st, False), state)
        run_max, total, out = fwd(mi, state, True)
        out = out / total
        OF[i] = out
        LSE[i] = run_max + jnp.log(total)
        OB[i] = out.astype(low)

        @pl.when(jnp.logical_not(at_home(i)))
        def _():
            remote(OB.at[i], RO.at[e_me, i_me], bs.at[i, 0], br.at[0, e_me, i_me], home(i)).start()

        @pl.when(at_home(i))
        def _():
            RO[e_me, i_me] = OB[i]

        return carry

    with jax.named_scope("forward"):
        lax.fori_loop(0, 4, query_block, 0)


    def mlp_parts(i, carry):
        PH[i] = dot(DU[i].reshape(BLK, 512), W1[...], 1, 1)
        return carry

    def wait_home(g, src, dst):
        for e in range(2):
            for i in range(2):
                @pl.when(jnp.logical_not(head_here(e, i)))
                def _():
                    remote(src.at[0], dst.at[e, i], bs.at[0, g], br.at[g, e, i], head_at(e, i)).wait_recv()

    for i in range(4):
        @pl.when(jnp.logical_not(my_source(i)))
        def _():
            remote(HT.at[0, 0, 1, 1], QD.at[i, 1], hs.at[0, 0, 2], dr.at[i], source(i)).wait_recv()
    for i in range(4):
        DLT[i] = jnp.sum(QD[i, 1].astype(full) * OF[i], axis=0, keepdims=True)
    dqa[...] = jnp.zeros_like(dqa)

    def pair_of(c, t, i, masked):
        k = KV[c, t, 0]
        q = QD[i, 0]
        do = QD[i, 1]
        pr = jnp.exp(dot(k, q, 0, 0) - LSE[i])
        if masked:
            pr = jnp.where(causal, pr, 0.0)
        dp = dot(KV[c, t, 1], do, 0, 0)
        ds = (pr * (dp - DLT[i])).astype(low)
        acc[c, 0] += dot(q, ds, 1, 1)
        acc[c, 1] += dot(do, pr.astype(low), 1, 1)
        dqa[i] += dot(k, ds, 1, 0)

    def kv_home(t):
        summed[t] = (acc_own[t] + got[t].astype(full)).astype(low)

        @pl.when(jnp.logical_not(at_home(t)))
        def _():
            remote(summed.at[t], RKV.at[e_me, i_me], bs.at[t, 2], br2.at[e_me, i_me], home(t)).start()

        @pl.when(at_home(t))
        def _():
            RKV[e_me, i_me] = summed[t]

    final = 2 * e_me + i_me

    def dq_home(t):
        DQB[t] = (dqa[t] * 0.125).astype(low)

        @pl.when(jnp.logical_not(at_home(t)))
        def _():
            remote(DQB.at[t], RQ1.at[e_me, i_me], bs.at[t, 1], br.at[1, e_me, i_me], home(t)).start()

        @pl.when(at_home(t))
        def _():
            RQ1[e_me, i_me] = DQB[t]

    def step(p, before=None):
        t = final if p == 3 else p + (p >= final).astype(jnp.int32)
        acc[...] = jnp.zeros_like(acc)

        def rest(u, carry):
            pair_of(u % 2, t, t + 1 + u // 2, False)
            return carry

        lax.fori_loop(0, 2 * (3 - t), rest, 0)
        if before is not None:
            before[1].wait_recv()
            kv_home(before[0])

        @pl.when((t + w) % 2 == 1)
        def _():
            pair_of(1 - w, t, t, False)

        pair_of(w, t, t, True)
        other[t] = acc[1 - w].astype(low)
        acc_own[t] = acc[w]
        cp = remote(other.at[t], got.at[t], kss.at[t], ksr.at[t], sib)
        cp.start()
        if p < 3:
            @pl.when(t < final)
            def _():
                dq_home(t)
        else:
            for n in range(4):
                @pl.when(n >= final)
                def _():
                    dq_home(n)
        return t, cp

    with jax.named_scope("step0"):
        k0 = step(0)
    with jax.named_scope("wf1"):
        for cp in c_w2 + c_f:
            cp.wait_recv()
    d_w2 = second_w2()
    d_f = second_unit(0, GF)
    with jax.named_scope("ohome"):
        wait_home(0, OB, RO)

    def out_slot(i):
        ob = jnp.concatenate([RO[0, i], RO[1, i]], axis=0).astype(full)
        ob = (ob * VAL[pl.ds(i, 1), :]).astype(low)
        t = dot(ob, WOF[...], 0, 0) + dot(GA[i].reshape(BLK, 512), W2[...].reshape(512, 1024), 1, 0)
        TO[i] = t.astype(low).reshape(4, 128, 1024)
        return dot(ob, YY[i].reshape(BLK, 1024), 1, 0)

    g_wo = out_slot(1 - w)
    opair = remote(TO.at[1 - w], pin.at[0], pps.at[0], ppr.at[0], sib)
    opair.start()
    g_wo = g_wo + out_slot(w)
    GO[...] = jnp.concatenate(
        [g_wo[:, :512].reshape(16, 8, 512), g_wo[:, 512:].reshape(16, 8, 512)], axis=1
    ).astype(low)

    def owner(k):
        rr = 2 * j + k // 8
        return rr // 8, (rr // 2) % 4, rr % 2, (k % 8) // 2, k % 2

    def owner_copy(k):
        os_, oy, oxh, oz, ow = owner(k)
        me = (os_ == s) & (oy == y) & (oxh == xh) & (oz == z) & (ow == w)
        return remote(GO.at[k], fo_in.at[r], gos.at[k], gor.at[r], dev(os_, oy, oxh, oz, ow)), me

    for k in range(16):
        cp, me = owner_copy(k)

        @pl.when(jnp.logical_not(me))
        def _():
            cp.start()

        @pl.when(me)
        def _():
            fo_in[r] = GO[k]

    def pair_z(n, buf):
        def one(t, carry):
            buf[w, t] = (buf[w, t].astype(full) + pin[n, t].astype(full)).astype(low)
            return carry

        lax.fori_loop(0, 4, one, 0)
        out = []
        for k in (1, 3, 2):
            zz = (z + k) % 4
            cp = remote(buf.at[w, zz], zin.at[n, k], zzs.at[n, k], zzr.at[n, k], dev(s, y, xh, zz, w))
            cp.start()
            out.append(cp)
        return out

    with jax.named_scope("step1"):
        k1 = step(1, k0)
    with jax.named_scope("opair"):
        opair.wait_recv()
    zo = pair_z(0, TO)
    with jax.named_scope("step2"):
        k2 = step(2, k1)
    with jax.named_scope("step3"):
        k3 = step(3, k2)
    with jax.named_scope("k3"):
        k3[1].wait_recv()
    kv_home(k3[0])

    def turn_back(v):
        a, b = v[0:8], v[8:16]
        return jnp.concatenate([a * ROPE[0] + b * ROPE[1], b * ROPE[0] - a * ROPE[1], v[16:]], axis=0)

    def wait_kv():
        for e in range(2):
            for i in range(2):
                @pl.when(jnp.logical_not(head_here(e, i)))
                def _():
                    remote(summed.at[0], RKV.at[e, i], bs.at[0, 2], br2.at[e, i], head_at(e, i)).wait_recv()

    with jax.named_scope("fill"):
        lax.fori_loop(0, 2, mlp_parts, 0)
        with jax.named_scope("wf2"):
            for cp in d_w2 + d_f:
                cp.wait_recv()
        GFC2[:, :512] = add4(wm[0, 2 * s + xh], wi2[0, 1], wi2[0, 2], wi2[0, 3])
        GFC2[:, 512:] = add4(wm[1, y], wi2[1, 1], wi2[1, 2], wi2[1, 3])
        t_f = last_unit(0, Ff, RF)
        mine_x = tok[0].astype(full)
        mean = jnp.mean(mine_x, axis=-1, keepdims=True)
        cen = mine_x - mean
        inv = lax.rsqrt(jnp.mean(cen * cen, axis=-1, keepdims=True) + norm_eps)
    with jax.named_scope("home"):
        wait_home(1, DQB, RQ1)
        wait_kv()

    def dh_slot(i):
        for e in range(2):
            DQ[i, 64 * e:64 * e + 64] = turn_back(RQ1[e, i].astype(full)).astype(low)
            DQ[i, 128 + 64 * e:192 + 64 * e] = turn_back(RKV[e, i, 0].astype(full)).astype(low)
            DQ[i, 256 + 64 * e:320 + 64 * e] = RKV[e, i, 1]
        t = dot(DQ[i], WQT[...], 0, 0) + PH[i]
        TH[i] = t.astype(low).reshape(4, 128, 1024)
        g_shift = jnp.sum(t, axis=0, keepdims=True)
        g_gain = jnp.sum(t * XH[i].reshape(BLK, 1024).astype(full), axis=0, keepdims=True)
        return g_shift, g_gain, jnp.sum(DQ[i].astype(full), axis=1, keepdims=True)

    a_shift, a_gain, a_bq = dh_slot(1 - w)
    hp = []
    for k in (2, 1, 3, 0):
        zz = (z + k) % 4
        cp = remote(TH.at[1 - w, zz], pin.at[1, zz], hps.at[k], hpr.at[k], sib)
        cp.start()
        hp.append((k, cp))
    b_shift, b_gain, b_bq = dh_slot(w)
    up, down, across = (z + 1) % 4, (z + 3) % 4, (z + 2) % 4

    def add_hp(n):
        k, cp = hp[n]
        zz = (z + k) % 4
        cp.wait_recv()
        TH[w, zz] = (TH[w, zz].astype(full) + pin[1, zz].astype(full)).astype(low)

    with jax.named_scope("hpfirst"):
        add_hp(0)
    lo6, hi6 = pl.ds(0, 64), pl.ds(64, 64)
    zh = [
        remote(TH.at[w, across, lo6], zin.at[1, 2, lo6], zzs.at[1, 2], zzr.at[1, 2], dev(s, y, xh, up, w)),
        remote(TH.at[w, across, hi6], zin.at[1, 2, hi6], zzs.at[1, 0], zzr.at[1, 0], dev(s, y, xh, down, w)),
    ]
    for cp in zh:
        cp.start()
    gq = dot(DQ[0], HB[0].reshape(BLK, 1024), 1, 0) + dot(DQ[1], HB[1].reshape(BLK, 1024), 1, 0)
    d0, p0 = iota((128, 1024), 1), iota((128, 1024), 0)
    block = (d0 >= 8 * p0) & (d0 < 8 * p0 + 8)
    dt, lt = iota((1024, 128), 0), iota((1024, 128), 1)

    def spread_row(v, lane):
        a = jnp.where(block, jnp.broadcast_to(v, (128, 1024)), 0.0).astype(low)
        return dot(a, (lt == lane + (dt & 7)).astype(full).astype(low), 1, 0)

    small = spread_row(a_gain + b_gain, 0) + spread_row(a_shift + b_shift, 8) + spread_row(gb_out, 16)
    f0, pf = iota((128, 512), 1), iota((128, 512), 0)
    base = f0 - 4 * (pf - j)
    a = jnp.where(
        (((pf - j) & 7) == 0) & (base >= 0) & (base < 32), jnp.broadcast_to(gb1, (128, 512)), 0.0
    ).astype(low)
    ft, lf = iota((512, 128), 0), iota((512, 128), 1)
    small = small + dot(a, (lf == 48 + (ft & 31)).astype(full).astype(low), 1, 0)
    n0, pn = iota((128, 384), 1), iota((128, 384), 0)
    qk_at = (n0 // 128) * 1024 + 128 * j + (n0 & 127) - 16 * pn
    v_at = 128 * j + (n0 & 127) - 8 * pn
    owns = ((n0 < 256) & (qk_at >= 0) & (qk_at < 16)) | ((n0 >= 256) & (v_at >= 0) & (v_at < 8))
    nt, ln = iota((384, 128), 0), iota((384, 128), 1)
    lane = jnp.where(nt < 256, 24 + (nt & 15), 40 + (nt & 7))
    b = jnp.where(ln == lane, jnp.broadcast_to(a_bq + b_bq, (384, 128)), 0.0).astype(low)
    small = small + dot(owns.astype(full).astype(low), b, 1, 0)
    head_row = (dt == 8 * lt).astype(full).astype(low)
    pad = dot(head_row, small.astype(low), 1, 0)
    left = gq[:256].T
    right = jnp.concatenate([gq[256:].T, pad], axis=1)
    GQ[...] = jnp.concatenate(
        [left.reshape(128, 8, 256), right.reshape(128, 8, 256)], axis=1
    ).astype(low).reshape(2, 4, 2, 8, 16, 256)
    c_q = first_unit(1, GQ)
    with jax.named_scope("hpair"):
        for n in (1, 2, 3):
            add_hp(n)
    with jax.named_scope("hrelay"):
        for cp in zh:
            cp.wait_recv()
    TH[w, up, 0:64] = (TH[w, up, 0:64].astype(full) + zin[1, 2, 0:64].astype(full)).astype(low)
    TH[w, down, 64:128] = (TH[w, down, 64:128].astype(full) + zin[1, 2, 64:128].astype(full)).astype(low)
    zn = [
        remote(TH.at[w, up], zin.at[1, 1], zzs.at[1, 1], zzr.at[1, 1], dev(s, y, xh, up, w)),
        remote(TH.at[w, down], zin.at[1, 3], zzs.at[1, 3], zzr.at[1, 3], dev(s, y, xh, down, w)),
    ]
    for cp in zn:
        cp.start()
    with jax.named_scope("zo"):
        for cp in zo:
            cp.wait_recv()
    t = add4(TO[w, z], zin[0, 1], zin[0, 2], zin[0, 3])
    OUT[0] = (mine_x + t + VEC[1:2, :]).astype(low)
    with jax.named_scope("gq1"):
        for cp in c_q:
            cp.wait_recv()
    gm[1, 0] = add4(GQ[:, y, :, 0:4], gi0[1, 1], gi0[1, 2], gi0[1, 3]).astype(low).reshape(4, 4, 16, 256)
    gm[1, 1] = add4(GQ[s, :, xh, 4:8], gi1[1, 1], gi1[1, 2], gi1[1, 3]).astype(low)

    def last_copy(k, q):
        xx, yy = (x + k) % 4, (y + k) % 4
        if q < 4:
            here, target = gm.at[1, 0, 2 * (xx % 2) + xx // 2, q], x_dev(xx, y, q // 2, q % 2)
        else:
            here, target = gm.at[1, 1, yy, q - 4], dev(s, yy, xh, q // 2, q % 2)
        return remote(here, QIN.at[k, j], us.at[k, q], ur.at[k, j], target)

    for k in (2, 1, 3, 0):
        for q in range(8):
            if k == 0:
                @pl.when(j != q)
                def _():
                    last_copy(k, q).start()

                @pl.when(j == q)
                def _():
                    if q < 4:
                        QIN[0, j] = gm[1, 0, 2 * s + xh, q]
                    else:
                        QIN[0, j] = gm[1, 1, y, q - 4]
            else:
                last_copy(k, q).start()
    with jax.named_scope("go"):
        for q in range(16):
            @pl.when(jnp.logical_not((q == r) & (j == jo)))
            def _():
                remote(GO.at[0], fo_in.at[q], gos.at[0], gor.at[q], sender(q)).wait_recv()
        t = lax.fori_loop(0, 16, lambda q, t: t + fo_in[q].astype(full), jnp.zeros((16, 512), full))
        GWO[:, :512] = t[:8]
        GWO[:, 512:] = t[8:]
    with jax.named_scope("zh"):
        for cp in zn:
            cp.wait_recv()
    gh = TH[w, z].astype(full) + zin[1, 1].astype(full) + zin[1, 3].astype(full)
    hat = cen * inv
    gx = gh * VEC[0:1, :]
    gx = gx - jnp.mean(gx, axis=-1, keepdims=True) - hat * jnp.mean(gx * hat, axis=-1, keepdims=True)
    TG[0] = (YY[w, z].astype(full) + inv * gx).astype(low)
    with jax.named_scope("lastf"):
        for cp in t_f:
            cp.wait_recv()
    with jax.named_scope("last"):
        for k in range(4):
            for q in range(8):
                if k == 0:
                    @pl.when(j != q)
                    def _():
                        remote(gm.at[1, 0, 0, 0], QIN.at[k, q], us.at[k, q], ur.at[k, q], sib).wait_recv()
                else:
                    remote(gm.at[1, 0, 0, 0], QIN.at[k, q], us.at[k, q], ur.at[k, q], sib).wait_recv()
    RQ[...] = add4(QIN[0], QIN[1], QIN[2], QIN[3]).astype(low)

    for k in range(4):
        for q in range(8):
            if k == 0:
                @pl.when(j != q)
                def _():
                    last_copy(k, q).wait_send()
            else:
                last_copy(k, q).wait_send()
    for e in range(2):
        for i in range(2):
            @pl.when(jnp.logical_not(head_target(e, i)[1]))
            def _():
                kv_copy(e, i).wait_send()
                q_copy(e, i).wait_send()
                do_copy(e, i).wait_send()

    @pl.when(j != jo)
    def _():
        oc[0].wait_send()

    for i in range(4):
        @pl.when(jnp.logical_not(at_home(i)))
        def _():
            remote(OB.at[i], RO.at[e_me, i_me], bs.at[i, 0], br.at[0, e_me, i_me], home(i)).wait_send()
            remote(DQB.at[i], RQ1.at[e_me, i_me], bs.at[i, 1], br.at[1, e_me, i_me], home(i)).wait_send()
            remote(summed.at[i], RKV.at[e_me, i_me], bs.at[i, 2], br2.at[e_me, i_me], home(i)).wait_send()
    for k in range(16):
        cp, me = owner_copy(k)

        @pl.when(jnp.logical_not(me))
        def _():
            cp.wait_send()
    for cp in oc[1:] + tq + tf + xc + xf + yc + yf + q2 + f1 + f2 + g1 + g2 + [xpair, ypair, swap, k0[1], k1[1], k2[1], k3[1]]:
        cp.wait_send()
    for cp in [opair] + [cp for _, cp in hp] + zo + zh + zn + c_w2 + c_f + c_q + d_w2 + d_f + t_f:
        cp.wait_send()


def layer(*args):
    S = pltpu.SemaphoreType.DMA
    V = pltpu.VMEM
    sds = jax.ShapeDtypeStruct
    return pl.pallas_call(
        layer_kernel,
        name="layer",
        out_shape=(
            sds((1, 128, 1024), low),
            sds((1, 128, 1024), low),
            sds((8, 16, 256), low),
            sds((8, 16, 256), low),
            sds((32, 1024), full),
            sds((8, 1024), full),
        ),
        in_specs=[pl.BlockSpec(memory_space=pltpu.SMEM)] + [VM] * 13,
        out_specs=(VM,) * 6,
        scratch_shapes=[
            V((8, 128), full),
            V((2, 8, BLK), full),
            V((2, 4, 128, 512), full),
            V((2, 4, 128, 1024), low),
            V((2, 4, 128, 1024), low),
            V((2, 4, 128, 1024), low),
            V((2, 4, 128, 1024), low),
            V((2, 4, 128, 512), low),
            V((2, 4, 128, 512), low),
            V((1024, 512), low),
            V((2, 4, 2, 32, 1024), low),
            V((384, 1024), low),
            V((128, 1024), low),
            V((8, 1024), full),
            V((8, BLK), full),
            V((2, 4, 2, 64, BLK), low),
            V((4, 2, 64, BLK), low),
            V((2, 4, 2, 8, 16, 256), low),
            V((2, 4, 2, 8, 16, 256), low),
            V((8, 16, 256), low),
            V((8, 16, 256), low),
            V((16, 512), low),
            V((16, 16, 512), low),
            V((2, 2, 2, 2, 64, BLK), low),
            V((4, 64, BLK), full),
            V((4, 64, BLK), low),
            V((4, 1, BLK), full),
            V((4, 1, BLK), full),
            V((2, 2, 64, BLK), low),
            V((2, 2, 64, BLK), low),
            V((2, 2, 2, 64, BLK), low),
            V((2, 2, 64, BLK), full),
            V((4, 2, 64, BLK), full),
            V((4, 64, BLK), full),
            V((4, 64, BLK), low),
            V((4, 2, 64, BLK), low),
            V((4, 2, 64, BLK), low),
            V((4, 2, 64, BLK), low),
            V((2, BLK, 1024), full),
            V((2, 384, BLK), low),
            V((2, 4, 128, 1024), low),
            V((2, 4, 128, 1024), low),
            V((2, 4, 128, 1024), low),
            V((2, 4, 128, 1024), low),
            V((2, 4, 2, 8, 16, 256), low),
            V((2, 4, 2, 8, 16, 256), low),
            V((2, 4, 2, 32, 1024), low),
            V((2, 4, 2, 2, 4, 16, 256), low),
            V((2, 4, 4, 4, 16, 256), low),
            V((4, 2, 2, 32, 512), low),
            V((4, 4, 32, 512), low),
            V((2, 2, 4, 4, 16, 256), low),
            V((2, 4, 32, 512), low),
            V((2, 2, 4, 4, 16, 256), low),
            V((2, 4, 32, 512), low),
            V((8, 16, 256), low),
            V((4, 8, 16, 256), low),
            V((16, 16, 512), low),
            V((16, 16, 512), low),
            S((4,)), S((4,)), S((4,)), S((4,)), S((2,)), S((2,)), S((4, 8)), S((4, 8)), S((8,)), S((8,)), S((16,)),
            S((16,)), S((2, 4)), S((2, 4)), S((2, 4)), S((2, 4)), S((2, 4)), S((2, 4)),
            S((2, 4)), S((2, 4)), S((2, 4)), S((2, 4)), S((2, 2, 3)), S((4,)), S((4,)), S((4,)), S, S,
            S((4, 3)), S((2, 2, 2)), S((2, 2)), S((2,)), S((2,)), S((4,)), S((4,)), S((4,)), S((4,)), S((16,)), S((16,)),
            S((2, 4)), S((2, 4)), S((3, 2, 4)), S((3, 2, 4)), S((3, 2, 4)), S((3, 2, 4)), S((2, 8)), S((2, 8)),
            S((4, 8)), S((4, 8)),
        ],
        compiler_params=pltpu.CompilerParams(
            collective_id=0, has_side_effects=True, vmem_limit_bytes=62 << 20
        ),
    )(*args)


def finish_kernel(out, tg, RF, RQ, gfc2, gwo,
                  OUT, TG, GQKV, GFC1, GFC2, GWO, GG, GS, BQK, BV, BO, B1, B2):
    OUT[...] = out[...]
    TG[...] = tg[...]
    GFC2[...] = gfc2[...]
    GWO[...] = gwo[...]
    for rr in range(16):
        g = rr // 4
        c, half = g // 2, g % 2
        for hi in range(2):
            tiles = [RF[4 * hi + n, 8 * c:8 * c + 8, 128 * half:128 * half + 128].astype(full) for n in range(4)]
            col = 128 * (2 * rr + hi)
            GFC1[:, col:col + 128] = lane_mix(tiles, [32 * (n - rr % 4) for n in range(4)])
    tail = jnp.zeros((8, 128), full)
    for q in range(8):
        c = 128 * q
        GQKV[:, c:c + 128] = RQ[q, 0:8, 0:128].astype(full)
        GQKV[:, 1024 + c:1152 + c] = RQ[q, 0:8, 128:256].astype(full)
        GQKV[:, 2048 + c:2176 + c] = RQ[q, 8:16, 0:128].astype(full)
        tail = tail + RQ[q, 8:16, 128:256].astype(full)
    row = tail[0]
    GG[...] = row[0:8]
    GS[...] = row[8:16]
    BQK[...] = row[24:40]
    BV[...] = row[40:48]
    BO[...] = row[16:24]
    B1[...] = row[48:80]
    B2[...] = row[16:24]


def finish(*args):
    sds = jax.ShapeDtypeStruct
    return pl.pallas_call(
        finish_kernel,
        name="finish",
        out_shape=(
            sds((1, 128, 1024), low),
            sds((1, 128, 1024), low),
            sds((8, 3072), full),
            sds((8, 4096), full),
            sds((32, 1024), full),
            sds((8, 1024), full),
            sds((8,), full),
            sds((8,), full),
            sds((16,), full),
            sds((8,), full),
            sds((8,), full),
            sds((32,), full),
            sds((8,), full),
        ),
        in_specs=[VM] * 6,
        out_specs=(VM,) * 13,
    )(*args)


def shards(
    tokens, lengths, ln_gain, ln_bias, w_qkv, b_qkv, w_out, b_out, w_fc1, b_fc1, w_fc2, b_fc2, cotangent
):
    freq = rope_base ** (-2.0 * np.arange(8) / ROT)
    near = freq[:, None] * np.arange(BLK)[None, :]
    far = freq[:, None] * (BLK * np.arange(BLK))[None, :]
    turns = jnp.asarray(np.stack([np.cos(near), np.sin(near), np.cos(far), np.sin(far)]).astype(np.float32))
    parts = layer(
        lengths, tokens, cotangent, ln_gain, ln_bias, b_qkv, b_out, b_fc1, b_fc2, w_qkv, w_out, w_fc1, w_fc2, turns
    )
    OUT, TG, GQKV, GFC1, GFC2, GWO, GG, GS, BQK, BV, BO, B1, B2 = finish(*parts)
    return (OUT, TG, GG, GS, GQKV, BQK, BV, GWO, BO, GFC1, B1, GFC2, B2)


def solution(mesh):
    rows, tok, par, vec = (
        P(("slot", "wsh")), P(("slot", "wsh"), "ctx", None), P(("slot", "ctx", "wsh"), None), P(("slot", "ctx", "wsh"))
    )
    return jax.shard_map(
        shards,
        mesh=mesh,
        in_specs=(tok, rows, vec, vec, par, vec, par, vec, par, vec, par, vec, tok),
        out_specs=(tok, tok, vec, vec, par, vec, vec, par, vec, par, vec, par, vec),
        check_vma=False,
    )
```

```python
import functools

import jax
import jax.numpy as jnp
import numpy as np
from jax import lax
from jax.experimental import pallas as pl
from jax.experimental.pallas import tpu as pltpu
from jax.sharding import PartitionSpec as P

HEADS = 16
HD = 64
ROT = 16
HQ = 1024
D = 1024
FF = 4096
BLK = 512

norm_eps = 1e-05
rope_base = 10000.0
MESH = pl.DeviceIdType.MESH
low = jnp.bfloat16
full = jnp.float32
VM = pl.BlockSpec(memory_space=pltpu.VMEM)
AN = pl.BlockSpec(memory_space=pl.ANY)


def place():
    s = lax.axis_index("slot")
    c = lax.axis_index("ctx")
    w = lax.axis_index("wsh")
    return s, c // 8, (c // 4) % 2, c % 4, w


def dev(s, y, xh, z, w):
    return (s, y * 8 + xh * 4 + z, w)


def x_dev(x, y, z, w):
    return dev(x % 2, y, x // 2, z, w)


def signal(barrier, target):
    pl.semaphore_signal(barrier, inc=1, device_id=target, device_id_type=MESH)


def local(src, dst, sem):
    pltpu.make_async_copy(src, dst, sem).start()


def drain(like, sem):
    pltpu.make_async_copy(like, like, sem).wait()


def remote(src, dst, send, recv, target):
    return pltpu.make_async_remote_copy(
        src_ref=src, dst_ref=dst, send_sem=send, recv_sem=recv,
        device_id=target, device_id_type=MESH,
    )


def iota(shape, axis):
    return lax.broadcasted_iota(jnp.int32, shape, axis)


def dot(a, b, ca, cb):
    return lax.dot_general(a, b, (((ca,), (cb,)), ((), ())), preferred_element_type=full)


def core_of(m):
    return ((m + 1) // 2) % 2


def owner_lanes(params, width, lanes, step):
    f, l = iota((128, width), 1), iota((128, width), 0)
    pick = (l == lanes[0] + (f & (step - 1)))
    for other in lanes[1:]:
        pick = pick | (l == other + (f & (step - 1)))
    return dot(params, pick.astype(full).astype(low), 1, 0), f, l


def lane_mix(tiles, shifts):
    lane = iota((8, 128), 1)
    out = jnp.zeros((8, 128), full)
    for g in range(4):
        t = tiles[g]
        if shifts[g] % 128:
            t = pltpu.roll(t, shifts[g] % 128, 1)
        out = jnp.where((lane >= 32 * g) & (lane < 32 * g + 32), t, out)
    return out


def layer_kernel(
    lens, tok, cot, lg, lb, bq, bo, bf, bg, wq, wo, w1, w2, turns, OUT, TG, RF, RQ, GFC2, GWO, PAD, ROPE, SL, XX, YY, HB, XH, GA, DU,
    W1, W2, WQT, WOF, VEC, VAL, KV, QD, Q, F, Qs, Fs, wos, WO, HT, OF, OB, LSE, DLT, RO, RQ1, RKV, acc,
    acc_own, dqa, DQB, other, got, summed, PH, DQ, TO, TH, pin, zin, GF, GQ, GW, gi0, gi1, wi0, wi1, gm, wm,
    gi2, wi2, Ff, QIN, GO, fo_in, zs, zr, ys, yr, ps, pr, ts, tr, fs, fr, os, orr, q2s, q2r, f1s, f1r,
    f2s, f2r, w1s, w1r, w2s, w2r, hs, kr, qr, dr, ks, krp, bs, br, br2, pps, ppr, hps, hpr, kss, ksr, gos, gor, zzs, zzr,
    g1s, g1r, g2s, g2r, tts, ttr, us, ur, spare, spare2, spare3, spare4, spare5, spare6,
):
    s, y, xh, z, w = place()
    x = xh * 2 + s
    r = s * 8 + y * 2 + xh
    j = z * 2 + w
    jo = r // 2
    m = y * 2 + xh
    core, spot = core_of(m), m // 2
    keep = (j == jo).astype(jnp.int32)
    mine = ((y // 2 == w) & (core == w)).astype(jnp.int32)
    sib = dev(s, y, xh, z, 1 - w)

    lo4, hi4 = pl.ds(0, 4), pl.ds(4, 4)
    lo5, hi5 = pl.ds(0, 512), pl.ds(512, 512)
    half = z // 2
    flip = 1 - half

    def ahead(k, q):
        return x_dev((x + k * flip) % 4, (y + k * half) % 4, q // 2, q % 2)

    def behind(k, q):
        if q < 4:
            return x_dev((x + 4 - k) % 4, y, q // 2, q % 2)
        return dev(s, (y + 4 - k) % 4, xh, q // 2, q % 2)

    barrier = pltpu.get_barrier_semaphore()
    for k in range(4):
        for q in range(8):
            if k == 0:
                @pl.when(j != q)
                def _():
                    signal(barrier, behind(k, q))
            else:
                signal(barrier, behind(k, q))
    for k in range(1, 4):
        signal(barrier, x_dev((x + k) % 4, y, z, w))
        signal(barrier, dev(s, (y + k) % 4, xh, z, w))

    def wo_source(k):
        rr = 2 * j + k // 8
        return rr // 8, (rr // 2) % 4, rr % 2, (k % 8) // 2, k % 2

    def wo_mine(k):
        ss, sy, sxh, sz, sw = wo_source(k)
        return (ss == s) & (sy == y) & (sxh == xh) & (sz == z) & (sw == w)

    def source(i):
        return dev(s, i, (i + w) % 2, z, y // 2)

    def my_source(i):
        return (y == i) & (xh == (i + w) % 2) & (w == y // 2)

    def sender(q):
        return dev(q // 8, (q // 2) % 4, q % 2, jo // 2, jo % 2)

    def home(i):
        return dev(s, i, (i + w) % 2, z, y // 2)

    def at_home(i):
        return (y == i) & (xh == (i + w) % 2) & (w == y // 2)

    def head_at(e, i):
        return dev(s, 2 * w + e, i, z, core)

    def head_here(e, i):
        return (y == 2 * w + e) & (xh == i) & (core == w)

    e_me, i_me = y % 2, xh
    XX[w, z] = tok[0]
    first_row = iota((8, 128), 0)
    PAD[...] = jnp.zeros_like(PAD)
    PAD[0:1, 0:8] = lg[...].reshape(1, 8)
    PAD[1:2, 0:8] = lb[...].reshape(1, 8)
    PAD[2:3, 0:24] = bq[...].reshape(1, 24)
    PAD[3:4, 0:8] = bo[...].reshape(1, 8)
    PAD[4:5, 0:32] = bf[...].reshape(1, 32)
    PAD[5:6, 0:8] = bg[...].reshape(1, 8)
    lane8 = iota((8, 128), 1)
    size = jnp.full((8, 128), lens[0], jnp.int32)
    padded = jnp.where(
        first_row == 6,
        jnp.where(lane8 == 0, (size >> 6).astype(full), jnp.where(lane8 == 1, (size & 63).astype(full), 0.0)),
        PAD[...],
    )
    for q in range(8):
        c = 128 * q
        top = jnp.concatenate([wq[:, c:c + 128], wq[:, 1024 + c:1152 + c]], axis=1)
        bot = jnp.concatenate([wq[:, 2048 + c:2176 + c], padded], axis=1)
        Qs[q] = jnp.concatenate([top, bot], axis=0).astype(low)

    W2[s, y, xh] = w2[...].astype(low)
    for q in range(8):
        tiles = []
        for g in range(4):
            parts = [w1[:, 128 * (2 * (4 * g + n) + q // 4):128 * (2 * (4 * g + n) + q // 4) + 128] for n in range(4)]
            tiles.append(lane_mix(parts, [32 * (n - q % 4) for n in range(4)]))
        top = jnp.concatenate(tiles[:2], axis=1)
        bot = jnp.concatenate(tiles[2:], axis=1)
        Fs[q] = jnp.concatenate([top, bot], axis=0).astype(low)

    def ring1(ref0, ref1, snd, rcv):
        for k in (1, 3, 2):
            cp = remote(ref0, ref0, snd, rcv, x_dev((x + k) % 4, y, z, w))
            cp.start()
            cp = remote(ref1, ref1, snd, rcv, dev(s, (y + k) % 4, xh, z, w))
            cp.start()

    def ring2(ref0, ref1, snd, rcv):
        for k in (1, 3, 2):
            cp = remote(ref0, ref0, snd, rcv, dev(s, (y + k) % 4, xh, z, w))
            cp.start()
            cp = remote(ref1, ref1, snd, rcv, x_dev((x + k) % 4, y, z, w))
            cp.start()

    def z_near(buf, snd, rcv):
        for k in (1, 3):
            cp = remote(buf.at[w, z], buf.at[w, z], snd.at[0], rcv.at[0], dev(s, y, xh, (z + k) % 4, w))
            cp.start()

    def z_far(buf, snd, rcv):
        up, down = (z + 1) % 4, (z + 3) % 4
        a = buf.at[w, down, pl.ds(0, 64)]
        b = buf.at[w, up, pl.ds(64, 64)]
        out = [
            remote(a, a, snd.at[1], rcv.at[1], dev(s, y, xh, up, w)),
            remote(b, b, snd.at[1], rcv.at[1], dev(s, y, xh, down, w)),
        ]
        for cp in out:
            cp.start()

    with jax.named_scope("barrier"):
        pl.semaphore_wait(barrier, 31 + 6)

    slot = (r % 2) * 8 + j
    for k in (1, 3, 2, 0):
        for n in range(8):
            if k == 0 and n == 0:
                continue
            q = (j + n) % 8
            remote(Qs.at[q], Q.at[s, y, xh, j], ts, tr, ahead(k, q)).start()
    for k in range(1, 8):
        q = (j + k) % 8
        remote(Fs.at[q], F.at[s, y, xh, j], fs, fr, dev(s, y, xh, q // 2, q % 2)).start()
    ring1(W2.at[s, y, xh, :, lo5], W2.at[s, y, xh, :, hi5], w1s, w1r)
    z_near(XX, zs, zr)
    local(Qs.at[j], Q.at[s, y, xh, j], tr)
    local(Qs.at[j], spare, ts)
    local(Fs.at[j], F.at[s, y, xh, j], fr)
    local(Fs.at[j], spare2, fs)

    row = iota((128, 1024), 0) + (m * BLK + z * 128)
    YY[w, z] = jnp.where(row < lens[0], cot[0].astype(full), 0.0).astype(low)
    wos[...] = jnp.concatenate([wo[:, :512], wo[:, 512:]], axis=0).astype(low)
    c0, s0 = turns[0], turns[1]
    at_m = iota((8, 128), 1) == m
    cm = jnp.sum(jnp.where(at_m, turns[2, :, :128], 0.0), axis=1, keepdims=True)
    sm = jnp.sum(jnp.where(at_m, turns[3, :, :128], 0.0), axis=1, keepdims=True)
    ROPE[0] = cm * c0 - sm * s0
    ROPE[1] = sm * c0 + cm * s0

    with jax.named_scope("units"):
        drain(QIN, tr)
    with jax.named_scope("tf"):
        drain(Fs, fr)
    ring1(F.at[s, y, xh, lo4], F.at[s, y, xh, hi4], f1s, f1r)
    ring2(Q.at[:, y, :, lo4], Q.at[s, :, xh, hi4], q2s, q2r)
    with jax.named_scope("g1"):
        drain(QIN.at[pl.ds(0, 3)], w1r)
    with jax.named_scope("f1"):
        drain(QIN.at[pl.ds(0, 3)], f1r)
    ring2(F.at[:, y, :, lo4], F.at[s, :, xh, hi4], f2s, f2r)
    ring2(W2.at[:, y, :, :, lo5], W2.at[s, :, xh, :, hi5], w2s, w2r)
    with jax.named_scope("xnear"):
        drain(XX.at[0, pl.ds(0, 2)], zr.at[0])
    z_far(XX, zs, zr)
    z_near(YY, ys, yr)
    for k in range(16):
        q = (r + k) % 16
        cp = remote(wos, WO.at[slot], os, orr, dev(q // 8, (q // 2) % 4, q % 2, jo // 2, jo % 2))
        if k == 0:
            @pl.when(j != jo)
            def _():
                cp.start()

            @pl.when(j == jo)
            def _():
                local(wos, WO.at[slot], orr)
                local(wos, spare3, os)
        else:
            cp.start()
    with jax.named_scope("x"):
        drain(XX.at[0, 0], zr.at[1])
    xpair = remote(XX.at[w], XX.at[w], ps.at[0], pr.at[0], sib)
    xpair.start()
    with jax.named_scope("ring2"):
        drain(Q.at[:, pl.ds(0, 3)], q2r)
    units = Q[...].reshape(128, 16, 256).astype(full)
    left = units[:, :8].reshape(1024, 256)
    right = units[:, 8:].reshape(1024, 256)
    WQT[0:256, :] = left.T.astype(low)
    WQT[256:384, :] = right[:, :128].T.astype(low)
    pads = right[:, 128:].astype(low)

    def params_of(i):
        pick = (iota((128, 1024), 1) == 8 * iota((128, 1024), 0) + i).astype(full).astype(low)
        return dot(pick, pads, 1, 0).astype(low)

    def row_of(i):
        t, f, l = owner_lanes(params_of(i), 1024, (0,), 8)
        return jnp.sum(jnp.where((f >= 8 * l) & (f < 8 * l + 8), t, 0.0), axis=0, keepdims=True)

    gain = row_of(0)
    shift = row_of(1)
    n0, p0 = iota((384, 128), 0), iota((384, 128), 1)
    n0 = (n0 // 128) * 1024 + 128 * j + (n0 & 127)
    at = n0 - 24 * p0
    inside = ((at >= 0) & (at < 24)).astype(full)
    t = dot(inside.astype(low), params_of(2), 1, 0)
    lane_want = jnp.sum(inside * at.astype(full), axis=1, keepdims=True)
    bias_q = jnp.sum(jnp.where(p0.astype(full) == lane_want, t, 0.0), axis=1, keepdims=True)
    co, si = ROPE[0], ROPE[1]

    def norm_slot(wi):
        def one(zi, carry):
            v = XX[wi, zi].astype(full)
            mean = jnp.mean(v, axis=-1, keepdims=True)
            c = v - mean
            var = jnp.mean(c * c, axis=-1, keepdims=True)
            h = c * lax.rsqrt(var + norm_eps)
            XH[wi, zi] = h.astype(low)
            HB[wi, zi] = (h * gain + shift).astype(low)
            return carry

        lax.fori_loop(0, 4, one, 0)

    def turn(v):
        a, b = v[0:8], v[8:16]
        return jnp.concatenate([a * co - b * si, b * co + a * si, v[16:]], axis=0)

    def qkv_slot(wi):
        t = dot(WQT[...], HB[wi].reshape(BLK, 1024), 1, 1) + bias_q
        for e in range(2):
            HT[e, wi, 0, 0] = turn(t[128 + 64 * e:192 + 64 * e]).astype(low)
            HT[e, wi, 0, 1] = t[256 + 64 * e:320 + 64 * e].astype(low)
            HT[e, wi, 1, 0] = (turn(t[64 * e:64 + 64 * e]).astype(low).astype(full) * 0.125).astype(low)

    def head_target(e, i):
        return dev(s, 2 * w + e, i, z, core), (y == 2 * w + e) & (xh == i) & (core == w)

    def kv_copy(e, i):
        return remote(HT.at[e, i, 0], KV.at[core, spot], hs.at[e, i, 0], kr.at[spot], head_target(e, i)[0])

    def q_copy(e, i):
        return remote(HT.at[e, i, 1, 0], QD.at[spot, 0], hs.at[e, i, 1], qr.at[spot], head_target(e, i)[0])

    def do_copy(e, i):
        return remote(HT.at[e, i, 1, 1], QD.at[spot, 1], hs.at[e, i, 2], dr.at[spot], head_target(e, i)[0])

    def send_qkv(i):
        for e in range(2):
            me = head_target(e, i)[1]

            @pl.when(jnp.logical_not(me))
            def _():
                kv_copy(e, i).start()
                q_copy(e, i).start()

            @pl.when(me)
            def _():
                KV[core, spot] = HT[e, i, 0]
                QD[spot, 0] = HT[e, i, 1, 0]

    def send_do(i):
        t = dot(WOF[...], YY[i].reshape(BLK, 1024), 1, 1)
        for e in range(2):
            HT[e, i, 1, 1] = t[64 * e:64 + 64 * e].astype(low)
            me = head_target(e, i)[1]

            @pl.when(jnp.logical_not(me))
            def _():
                do_copy(e, i).start()

            @pl.when(me)
            def _():
                QD[spot, 1] = HT[e, i, 1, 1]

    norm_slot(w)
    qkv_slot(w)
    send_qkv(w)
    xpair.wait_recv()
    norm_slot(1 - w)
    qkv_slot(1 - w)
    send_qkv(1 - w)

    with jax.named_scope("ynear"):
        drain(YY.at[0, pl.ds(0, 2)], yr.at[0])
    z_far(YY, ys, yr)
    VEC[0:1, :] = gain
    VEC[1:2, :] = row_of(3) + row_of(5)
    t, f, l = owner_lanes(params_of(4), 512, (0,), 32)
    base = f - 4 * (l - j)
    bias_1 = jnp.sum(
        jnp.where((((l - j) & 7) == 0) & (base >= 0) & (base < 32), t, 0.0), axis=0, keepdims=True
    )
    lp, ll = iota((128, 128), 0), iota((128, 128), 1)
    tok_pos = (iota((1, BLK), 1) + m * BLK).astype(full)
    pf = params_of(6).astype(full)
    for i in range(2):
        here = lp == s * 64 + i
        size = jnp.sum(jnp.where(here & (ll == 0), pf, 0.0)) * 64.0 + jnp.sum(jnp.where(here & (ll == 1), pf, 0.0))
        VAL[i:i + 1, :] = jnp.where(tok_pos < size, 1.0, 0.0)

    with jax.named_scope("f2"):
        drain(F.at[:, pl.ds(0, 3)], f2r)
        drain(F.at[:, pl.ds(0, 3)], w2r)
    units = F[...].reshape(128, 16, 256).astype(full)
    W1[:, :256] = units[:, :8].reshape(1024, 256).astype(low)
    W1[:, 256:] = units[:, 8:].reshape(1024, 256).astype(low)
    g0 = 0.7978845608028654

    def hidden_up(n, carry):
        wi, zi = n // 2, pl.ds(2 * (n % 2), 2)
        u = dot(HB[wi, zi].reshape(256, 1024), W1[...], 1, 0) + bias_1
        t = jnp.tanh(g0 * (u + 0.044715 * (u * u * u)))
        GA[wi, zi] = (0.5 * u * (1.0 + t)).astype(low).reshape(2, 128, 512)
        slope = 0.5 * (1.0 + t) + (0.5 * g0) * u * (1.0 - t * t) * (1.0 + (3.0 * 0.044715) * (u * u))
        SL[wi, zi] = slope.reshape(2, 128, 512)
        return carry

    with jax.named_scope("hidden_up"):
        lax.fori_loop(0, 4, hidden_up, 0)
    with jax.named_scope("dy"):
        drain(YY.at[0, 0], yr.at[1])
    ypair = remote(YY.at[w], YY.at[w], ps.at[1], pr.at[1], sib)
    ypair.start()

    def hidden_down(n, carry):
        wi, zi = jnp.where(n < 2, w, 1 - w), pl.ds(2 * (n % 2), 2)
        dg = dot(YY[wi, zi].reshape(256, 1024), W2[...].reshape(512, 1024), 1, 1)
        DU[wi, zi] = (dg.reshape(2, 128, 512) * SL[wi, zi]).astype(low)
        return carry

    with jax.named_scope("hidden_down"):
        lax.fori_loop(0, 2, hidden_down, 0)
        ypair.wait_recv()
        lax.fori_loop(2, 4, hidden_down, 0)
    with jax.named_scope("wgrads"):
        ga = GA[...].reshape(1024, 512)

        def first_w2(h):
            t = dot(ga, YY[:, :, :, 512 * h:512 * h + 512].reshape(1024, 512), 0, 0).astype(low)
            GW[:, :, :, :, 512 * h:512 * h + 512] = t.reshape(2, 4, 2, 32, 512)
            out = []
            for k in (1, 3, 2):
                yy, xx = (y + k) % 4, (x + k) % 4
                if h == 0:
                    cp = remote(GW.at[:, yy, :, :, lo5], wi0.at[k], g1s.at[2], g1r.at[2], dev(s, yy, xh, z, w))
                else:
                    cp = remote(GW.at[xx % 2, :, xx // 2, :, hi5], wi1.at[k], g1s.at[2], g1r.at[2], x_dev(xx, y, z, w))
                cp.start()
                out.append(cp)
            return out

        def first_unit(g, buf):
            out = []
            for k in (1, 3, 2):
                yy, xx = (y + k) % 4, (x + k) % 4
                cp = remote(buf.at[:, yy, :, lo4], gi0.at[g, k], g1s.at[g], g1r.at[g], dev(s, yy, xh, z, w))
                cp.start()
                out.append(cp)
                cp = remote(buf.at[xx % 2, :, xx // 2, hi4], gi1.at[g, k], g1s.at[g], g1r.at[g], x_dev(xx, y, z, w))
                cp.start()
                out.append(cp)
            return out

        def add4(a, b, c, d):
            return a.astype(full) + b.astype(full) + c.astype(full) + d.astype(full)

        def second_unit(g, buf):
            gm[g, 0] = add4(
                buf[:, y, :, 0:4], gi0[g, 1], gi0[g, 2], gi0[g, 3]
            ).astype(low).reshape(4, 4, 16, 256)
            gm[g, 1] = add4(
                buf[s, :, xh, 4:8], gi1[g, 1], gi1[g, 2], gi1[g, 3]
            ).astype(low)
            out = []
            for k in (1, 3, 2):
                yy, xx = (y + k) % 4, (x + k) % 4
                cp = remote(gm.at[g, 0, 2 * (xx % 2) + xx // 2], gi2.at[g, 0, k], g2s.at[g], g2r.at[g], x_dev(xx, y, z, w))
                cp.start()
                out.append(cp)
                cp = remote(gm.at[g, 1, yy], gi2.at[g, 1, k], g2s.at[g], g2r.at[g], dev(s, yy, xh, z, w))
                cp.start()
                out.append(cp)
            return out

        def second_w2():
            wm[0] = add4(GW[:, y, :, :, :512], wi0[1], wi0[2], wi0[3]).astype(low).reshape(4, 32, 512)
            wm[1] = add4(GW[s, :, xh, :, 512:], wi1[1], wi1[2], wi1[3]).astype(low)
            out = []
            for k in (1, 3, 2):
                yy, xx = (y + k) % 4, (x + k) % 4
                cp = remote(wm.at[0, 2 * (xx % 2) + xx // 2], wi2.at[0, k], g2s.at[2], g2r.at[2], x_dev(xx, y, z, w))
                cp.start()
                out.append(cp)
                cp = remote(wm.at[1, yy], wi2.at[1, k], g2s.at[2], g2r.at[2], dev(s, yy, xh, z, w))
                cp.start()
                out.append(cp)
            return out

        def last_unit(g, fin, got_units):
            fin[0:4] = add4(gm[g, 0, 2 * s + xh], gi2[g, 0, 1], gi2[g, 0, 2], gi2[g, 0, 3]).astype(low)
            fin[4:8] = add4(gm[g, 1, y], gi2[g, 1, 1], gi2[g, 1, 2], gi2[g, 1, 3]).astype(low)
            out = []
            for k in range(1, 8):
                q = (j + k) % 8
                cp = remote(fin.at[q], got_units.at[j], tts, ttr, dev(s, y, xh, q // 2, q % 2))
                cp.start()
                out.append(cp)
            local(fin.at[j], got_units.at[j], ttr)
            local(fin.at[j], spare4, tts)
            return out

        c_w2 = first_w2(0)
        c_w2 += first_w2(1)

    with jax.named_scope("kv"):
        for i in range(4):
            @pl.when(jnp.logical_not(my_source(i)))
            def _():
                remote(HT.at[0, 0, 0], KV.at[w, i], hs.at[0, 0, 0], kr.at[i], source(i)).wait_recv()
    swap = remote(KV.at[w], KV.at[w], ks, krp, sib)
    swap.start()
    with jax.named_scope("do"):
        drain(WO, orr)
        units = WO[...].astype(full)
        WOF[:, :512] = units[:, :8].reshape(128, 512).astype(low)
        WOF[:, 512:] = units[:, 8:].reshape(128, 512).astype(low)
        send_do(w)
        send_do(1 - w)
    with jax.named_scope("wgrads1"):
        du = DU[...].reshape(1024, 512)
        for n in range(4):
            t = dot(HB[:, :, :, 256 * n:256 * n + 256].reshape(1024, 256), du, 0, 0)
            t = jnp.concatenate([t[:, :256].reshape(32, 8, 256), t[:, 256:].reshape(32, 8, 256)], axis=1)
            GF[n // 2, 2 * (n % 2):2 * (n % 2) + 2] = t.astype(low).reshape(2, 2, 8, 16, 256)
        c_f = first_unit(0, GF)
        gb1 = jnp.sum(du.astype(full), axis=0, keepdims=True)
        gb_out = jnp.sum(YY[w, z].astype(full), axis=0, keepdims=True)

    with jax.named_scope("q"):
        for i in range(4):
            @pl.when(jnp.logical_not(my_source(i)))
            def _():
                remote(HT.at[0, 0, 1, 0], QD.at[i, 0], hs.at[0, 0, 1], qr.at[i], source(i)).wait_recv()
    with jax.named_scope("kvswap"):
        swap.wait_recv()

    causal = iota((BLK, BLK), 0) <= iota((BLK, BLK), 1)

    def query_block(i, carry):
        q = QD[i, 0]

        def many(blocks, state):
            run_max, total, out = state
            scores = []
            for c, t, masked in blocks:
                sc = dot(KV[c, t, 0], q, 0, 0)
                scores.append(jnp.where(causal, sc, -1e30) if masked else sc)
            new_max = run_max
            for sc in scores:
                new_max = jnp.maximum(new_max, jnp.max(sc, axis=0, keepdims=True))
            fac = jnp.exp(run_max - new_max)
            total, out = total * fac, out * fac
            for (c, t, _), sc in zip(blocks, scores):
                pr = jnp.exp(sc - new_max)
                total = total + jnp.sum(pr, axis=0, keepdims=True)
                out = out + dot(KV[c, t, 1], pr.astype(low), 1, 0)
            return new_max, total, out

        def two(t):
            return [(0, t, False), (1, t, False)]

        state = (
            jnp.full((1, BLK), -1e30, full),
            jnp.zeros((1, BLK), full),
            jnp.zeros((HD, BLK), full),
        )
        state = lax.fori_loop(0, i // 2, lambda t, st: many(two(2 * t) + two(2 * t + 1), st), state)
        state = lax.fori_loop(2 * (i // 2), i, lambda t, st: many(two(t), st), state)

        def keep_state(state):
            run_max, total, out = state
            out = out / total
            OF[i] = out
            LSE[i] = run_max + jnp.log(total)
            OB[i] = out.astype(low)

        @pl.when((i + w) % 2 == 1)
        def _():
            keep_state(many([(1 - w, i, False), (w, i, True)], state))

        @pl.when((i + w) % 2 == 0)
        def _():
            keep_state(many([(w, i, True)], state))

        @pl.when(jnp.logical_not(at_home(i)))
        def _():
            remote(OB.at[i], RO.at[e_me, i_me], bs.at[i, 0], br.at[0, e_me, i_me], home(i)).start()

        @pl.when(at_home(i))
        def _():
            RO[e_me, i_me] = OB[i]

        return carry

    with jax.named_scope("forward"):
        lax.fori_loop(0, 4, query_block, 0)


    def mlp_parts(i, carry):
        PH[i] = dot(DU[i].reshape(BLK, 512), W1[...], 1, 1)
        return carry

    def wait_home(g, src, dst):
        for e in range(2):
            for i in range(2):
                @pl.when(jnp.logical_not(head_here(e, i)))
                def _():
                    remote(src.at[0], dst.at[e, i], bs.at[0, g], br.at[g, e, i], head_at(e, i)).wait_recv()

    for i in range(4):
        @pl.when(jnp.logical_not(my_source(i)))
        def _():
            remote(HT.at[0, 0, 1, 1], QD.at[i, 1], hs.at[0, 0, 2], dr.at[i], source(i)).wait_recv()
    for i in range(4):
        DLT[i] = jnp.sum(QD[i, 1].astype(full) * OF[i], axis=0, keepdims=True)
    dqa[...] = jnp.zeros_like(dqa)

    def pairs(t, i, blocks):
        q, do, lse, dlt = QD[i, 0], QD[i, 1], LSE[i], DLT[i]
        scores = [dot(KV[c, t, 0], q, 0, 0) for c, _ in blocks]
        dps = [dot(KV[c, t, 1], do, 0, 0) for c, _ in blocks]
        dq = dqa[i]
        for (c, masked), sc, dp in zip(blocks, scores, dps):
            pr = jnp.exp(sc - lse)
            if masked:
                pr = jnp.where(causal, pr, 0.0)
            ds = (pr * (dp - dlt)).astype(low)
            acc[c, 0] += dot(q, ds, 1, 1)
            acc[c, 1] += dot(do, pr.astype(low), 1, 1)
            dq = dq + dot(KV[c, t, 0], ds, 1, 0)
        dqa[i] = dq

    def kv_home(t):
        summed[t] = (acc_own[t] + got[t].astype(full)).astype(low)

        @pl.when(jnp.logical_not(at_home(t)))
        def _():
            remote(summed.at[t], RKV.at[e_me, i_me], bs.at[t, 2], br2.at[e_me, i_me], home(t)).start()

        @pl.when(at_home(t))
        def _():
            RKV[e_me, i_me] = summed[t]

    final = 2 * e_me + i_me

    def dq_home(t):
        DQB[t] = (dqa[t] * 0.125).astype(low)

        @pl.when(jnp.logical_not(at_home(t)))
        def _():
            remote(DQB.at[t], RQ1.at[e_me, i_me], bs.at[t, 1], br.at[1, e_me, i_me], home(t)).start()

        @pl.when(at_home(t))
        def _():
            RQ1[e_me, i_me] = DQB[t]

    def step(p, before=None):
        t = final if p == 3 else p + (p >= final).astype(jnp.int32)
        acc[...] = jnp.zeros_like(acc)

        def rest(i, carry):
            pairs(t, i, [(0, False), (1, False)])
            return carry

        some = jnp.minimum(t + 2, 4)
        lax.fori_loop(t + 1, some, rest, 0)
        if before is not None:
            before[1].wait_recv()
            kv_home(before[0])
        if p != 2:
            lax.fori_loop(some, 4, rest, 0)

        @pl.when((t + w) % 2 == 1)
        def _():
            pairs(t, t, [(1 - w, False), (w, True)])

        @pl.when((t + w) % 2 == 0)
        def _():
            pairs(t, t, [(w, True)])

        other[t] = acc[1 - w].astype(low)
        acc_own[t] = acc[w]
        cp = remote(other.at[t], got.at[t], kss.at[t], ksr.at[t], sib)
        cp.start()
        if p < 3:
            @pl.when(t < final)
            def _():
                dq_home(t)
        else:
            for n in range(4):
                @pl.when(n >= final)
                def _():
                    dq_home(n)
        return t, cp

    with jax.named_scope("step0"):
        k0 = step(0)
    with jax.named_scope("wf1"):
        drain(F.at[:, pl.ds(0, 3)], g1r.at[2])
        drain(F.at[:, pl.ds(0, 3)], g1r.at[0])
    d_w2 = second_w2()
    d_f = second_unit(0, GF)
    with jax.named_scope("ohome"):
        wait_home(0, OB, RO)

    def out_slot(i):
        ob = jnp.concatenate([RO[0, i], RO[1, i]], axis=0).astype(full)
        ob = (ob * VAL[pl.ds(i, 1), :]).astype(low)
        t = dot(ob, WOF[...], 0, 0) + dot(GA[i].reshape(BLK, 512), W2[...].reshape(512, 1024), 1, 0)
        TO[i] = t.astype(low).reshape(4, 128, 1024)
        return dot(ob, YY[i].reshape(BLK, 1024), 1, 0)

    g_wo = out_slot(1 - w)
    opair = remote(TO.at[1 - w], pin.at[0], pps.at[0], ppr.at[0], sib)
    opair.start()
    g_wo = g_wo + out_slot(w)
    GO[...] = jnp.concatenate(
        [g_wo[:, :512].reshape(16, 8, 512), g_wo[:, 512:].reshape(16, 8, 512)], axis=1
    ).astype(low)

    def owner(k):
        rr = 2 * j + k // 8
        return rr // 8, (rr // 2) % 4, rr % 2, (k % 8) // 2, k % 2

    def owner_copy(k):
        os_, oy, oxh, oz, ow = owner(k)
        me = (os_ == s) & (oy == y) & (oxh == xh) & (oz == z) & (ow == w)
        return remote(GO.at[k], fo_in.at[r], gos, gor, dev(os_, oy, oxh, oz, ow)), me

    for k in range(16):
        cp, me = owner_copy(k)

        @pl.when(jnp.logical_not(me))
        def _():
            cp.start()

        @pl.when(me)
        def _():
            local(GO.at[k], fo_in.at[r], gor)
            local(GO.at[k], spare6, gos)

    def pair_z(n, buf):
        def one(t, carry):
            buf[w, t] = (buf[w, t].astype(full) + pin[n, t].astype(full)).astype(low)
            return carry

        lax.fori_loop(0, 4, one, 0)
        out = []
        for k in (1, 3, 2):
            zz = (z + k) % 4
            cp = remote(buf.at[w, zz], zin.at[n, k], zzs.at[0], zzr.at[0], dev(s, y, xh, zz, w))
            cp.start()
            out.append(cp)
        return out

    with jax.named_scope("step1"):
        k1 = step(1, k0)
    with jax.named_scope("opair"):
        opair.wait_recv()
    zo = pair_z(0, TO)
    with jax.named_scope("step2"):
        k2 = step(2, k1)
    with jax.named_scope("step3"):
        k3 = step(3, k2)
    with jax.named_scope("k3"):
        k3[1].wait_recv()
    kv_home(k3[0])

    def turn_back(v):
        a, b = v[0:8], v[8:16]
        return jnp.concatenate([a * ROPE[0] + b * ROPE[1], b * ROPE[0] - a * ROPE[1], v[16:]], axis=0)

    def wait_kv():
        for e in range(2):
            for i in range(2):
                @pl.when(jnp.logical_not(head_here(e, i)))
                def _():
                    remote(summed.at[0], RKV.at[e, i], bs.at[0, 2], br2.at[e, i], head_at(e, i)).wait_recv()

    with jax.named_scope("fill"):
        lax.fori_loop(0, 2, mlp_parts, 0)
        with jax.named_scope("wf2"):
            drain(QIN.at[pl.ds(0, 3)], g2r.at[2])
            drain(QIN.at[pl.ds(0, 3)], g2r.at[0])
        GFC2[:, :512] = add4(wm[0, 2 * s + xh], wi2[0, 1], wi2[0, 2], wi2[0, 3])
        GFC2[:, 512:] = add4(wm[1, y], wi2[1, 1], wi2[1, 2], wi2[1, 3])
        t_f = last_unit(0, Ff, RF)
        mine_x = tok[0].astype(full)
        mean = jnp.mean(mine_x, axis=-1, keepdims=True)
        cen = mine_x - mean
        inv = lax.rsqrt(jnp.mean(cen * cen, axis=-1, keepdims=True) + norm_eps)
    with jax.named_scope("home"):
        wait_home(1, DQB, RQ1)
        wait_kv()

    def dh_slot(i):
        for e in range(2):
            DQ[i, 64 * e:64 * e + 64] = turn_back(RQ1[e, i].astype(full)).astype(low)
            DQ[i, 128 + 64 * e:192 + 64 * e] = turn_back(RKV[e, i, 0].astype(full)).astype(low)
            DQ[i, 256 + 64 * e:320 + 64 * e] = RKV[e, i, 1]
        t = dot(DQ[i], WQT[...], 0, 0) + PH[i]
        TH[i] = t.astype(low).reshape(4, 128, 1024)
        g_shift = jnp.sum(t, axis=0, keepdims=True)
        g_gain = jnp.sum(t * XH[i].reshape(BLK, 1024).astype(full), axis=0, keepdims=True)
        return g_shift, g_gain, jnp.sum(DQ[i].astype(full), axis=1, keepdims=True)

    a_shift, a_gain, a_bq = dh_slot(1 - w)
    hp = []
    for k in (2, 1, 3, 0):
        zz = (z + k) % 4
        cp = remote(TH.at[1 - w, zz], pin.at[1, zz], hps.at[k], hpr.at[k], sib)
        cp.start()
        hp.append((k, cp))
    b_shift, b_gain, b_bq = dh_slot(w)
    up, down, across = (z + 1) % 4, (z + 3) % 4, (z + 2) % 4

    def add_hp(n):
        k, cp = hp[n]
        zz = (z + k) % 4
        cp.wait_recv()
        TH[w, zz] = (TH[w, zz].astype(full) + pin[1, zz].astype(full)).astype(low)

    with jax.named_scope("hpfirst"):
        add_hp(0)
    lo6, hi6 = pl.ds(0, 64), pl.ds(64, 64)
    zh = [
        remote(TH.at[w, across, lo6], zin.at[1, 2, lo6], zzs.at[1], zzr.at[1], dev(s, y, xh, up, w)),
        remote(TH.at[w, across, hi6], zin.at[1, 2, hi6], zzs.at[1], zzr.at[1], dev(s, y, xh, down, w)),
    ]
    for cp in zh:
        cp.start()
    gq = dot(DQ[0], HB[0].reshape(BLK, 1024), 1, 0) + dot(DQ[1], HB[1].reshape(BLK, 1024), 1, 0)
    d0, p0 = iota((128, 1024), 1), iota((128, 1024), 0)
    block = (d0 >= 8 * p0) & (d0 < 8 * p0 + 8)
    dt, lt = iota((1024, 128), 0), iota((1024, 128), 1)

    def spread_row(v, lane):
        a = jnp.where(block, jnp.broadcast_to(v, (128, 1024)), 0.0).astype(low)
        return dot(a, (lt == lane + (dt & 7)).astype(full).astype(low), 1, 0)

    small = spread_row(a_gain + b_gain, 0) + spread_row(a_shift + b_shift, 8) + spread_row(gb_out, 16)
    f0, pf = iota((128, 512), 1), iota((128, 512), 0)
    base = f0 - 4 * (pf - j)
    a = jnp.where(
        (((pf - j) & 7) == 0) & (base >= 0) & (base < 32), jnp.broadcast_to(gb1, (128, 512)), 0.0
    ).astype(low)
    ft, lf = iota((512, 128), 0), iota((512, 128), 1)
    small = small + dot(a, (lf == 48 + (ft & 31)).astype(full).astype(low), 1, 0)
    n0, pn = iota((128, 384), 1), iota((128, 384), 0)
    qk_at = (n0 // 128) * 1024 + 128 * j + (n0 & 127) - 16 * pn
    v_at = 128 * j + (n0 & 127) - 8 * pn
    owns = ((n0 < 256) & (qk_at >= 0) & (qk_at < 16)) | ((n0 >= 256) & (v_at >= 0) & (v_at < 8))
    nt, ln = iota((384, 128), 0), iota((384, 128), 1)
    lane = jnp.where(nt < 256, 24 + (nt & 15), 40 + (nt & 7))
    b = jnp.where(ln == lane, jnp.broadcast_to(a_bq + b_bq, (384, 128)), 0.0).astype(low)
    small = small + dot(owns.astype(full).astype(low), b, 1, 0)
    head_row = (dt == 8 * lt).astype(full).astype(low)
    pad = dot(head_row, small.astype(low), 1, 0)
    left = gq[:256].T
    right = jnp.concatenate([gq[256:].T, pad], axis=1)
    GQ[...] = jnp.concatenate(
        [left.reshape(128, 8, 256), right.reshape(128, 8, 256)], axis=1
    ).astype(low).reshape(2, 4, 2, 8, 16, 256)
    c_q = first_unit(1, GQ)
    with jax.named_scope("hpair"):
        for n in (1, 2, 3):
            add_hp(n)
    with jax.named_scope("hrelay"):
        drain(TH.at[0, 0], zzr.at[1])
    TH[w, up, 0:64] = (TH[w, up, 0:64].astype(full) + zin[1, 2, 0:64].astype(full)).astype(low)
    TH[w, down, 64:128] = (TH[w, down, 64:128].astype(full) + zin[1, 2, 64:128].astype(full)).astype(low)
    zn = [
        remote(TH.at[w, up], zin.at[1, 1], zzs.at[2], zzr.at[2], dev(s, y, xh, up, w)),
        remote(TH.at[w, down], zin.at[1, 3], zzs.at[2], zzr.at[2], dev(s, y, xh, down, w)),
    ]
    for cp in zn:
        cp.start()
    with jax.named_scope("zo"):
        drain(TO.at[0, pl.ds(0, 3)], zzr.at[0])
    t = add4(TO[w, z], zin[0, 1], zin[0, 2], zin[0, 3])
    OUT[0] = (mine_x + t + VEC[1:2, :]).astype(low)
    with jax.named_scope("gq1"):
        drain(F.at[:, pl.ds(0, 3)], g1r.at[1])
    gm[1, 0] = add4(GQ[:, y, :, 0:4], gi0[1, 1], gi0[1, 2], gi0[1, 3]).astype(low).reshape(4, 4, 16, 256)
    gm[1, 1] = add4(GQ[s, :, xh, 4:8], gi1[1, 1], gi1[1, 2], gi1[1, 3]).astype(low)

    def last_copy(k, q):
        xx, yy = (x + k) % 4, (y + k) % 4
        if q < 4:
            here, target = gm.at[1, 0, 2 * (xx % 2) + xx // 2, q], x_dev(xx, y, q // 2, q % 2)
        else:
            here, target = gm.at[1, 1, yy, q - 4], dev(s, yy, xh, q // 2, q % 2)
        return remote(here, QIN.at[k, j], us, ur, target)

    for k in (2, 1, 3, 0):
        for q in range(8):
            if k == 0:
                @pl.when(j != q)
                def _():
                    last_copy(k, q).start()

                @pl.when(j == q)
                def _():
                    here = gm.at[1, 0, 2 * s + xh, q] if q < 4 else gm.at[1, 1, y, q - 4]
                    local(here, QIN.at[0, j], ur)
                    local(here, spare5, us)
            else:
                last_copy(k, q).start()
    with jax.named_scope("go"):
        drain(fo_in, gor)
        t = lax.fori_loop(0, 16, lambda q, t: t + fo_in[q].astype(full), jnp.zeros((16, 512), full))
        GWO[:, :512] = t[:8]
        GWO[:, 512:] = t[8:]
    with jax.named_scope("zh"):
        drain(TH.at[0, pl.ds(0, 2)], zzr.at[2])
    gh = TH[w, z].astype(full) + zin[1, 1].astype(full) + zin[1, 3].astype(full)
    hat = cen * inv
    gx = gh * VEC[0:1, :]
    gx = gx - jnp.mean(gx, axis=-1, keepdims=True) - hat * jnp.mean(gx * hat, axis=-1, keepdims=True)
    TG[0] = (YY[w, z].astype(full) + inv * gx).astype(low)
    with jax.named_scope("lastf"):
        drain(RF, ttr)
    with jax.named_scope("last"):
        drain(QIN, ur)
    RQ[...] = add4(QIN[0], QIN[1], QIN[2], QIN[3]).astype(low)

    for e in range(2):
        for i in range(2):
            @pl.when(jnp.logical_not(head_target(e, i)[1]))
            def _():
                kv_copy(e, i).wait_send()
                q_copy(e, i).wait_send()
                do_copy(e, i).wait_send()

    for i in range(4):
        @pl.when(jnp.logical_not(at_home(i)))
        def _():
            remote(OB.at[i], RO.at[e_me, i_me], bs.at[i, 0], br.at[0, e_me, i_me], home(i)).wait_send()
            remote(DQB.at[i], RQ1.at[e_me, i_me], bs.at[i, 1], br.at[1, e_me, i_me], home(i)).wait_send()
            remote(summed.at[i], RKV.at[e_me, i_me], bs.at[i, 2], br2.at[e_me, i_me], home(i)).wait_send()
    for like, sem in (
        (QIN, ts), (QIN, us), (Fs, fs), (Fs, tts), (WO, os), (WO, gos),
        (QIN.at[pl.ds(0, 3)], f1s), (QIN.at[pl.ds(0, 3)], w1s),
        (QIN.at[pl.ds(0, 3)], g2s.at[0]), (QIN.at[pl.ds(0, 3)], g2s.at[2]),
        (F.at[:, pl.ds(0, 3)], q2s), (F.at[:, pl.ds(0, 3)], f2s), (F.at[:, pl.ds(0, 3)], w2s),
        (F.at[:, pl.ds(0, 3)], g1s.at[0]), (F.at[:, pl.ds(0, 3)], g1s.at[1]), (F.at[:, pl.ds(0, 3)], g1s.at[2]),
        (XX.at[0, pl.ds(0, 2)], zs.at[0]), (XX.at[0, 0], zs.at[1]),
        (XX.at[0, pl.ds(0, 2)], ys.at[0]), (XX.at[0, 0], ys.at[1]),
        (TO.at[0, pl.ds(0, 3)], zzs.at[0]), (TH.at[0, 0], zzs.at[1]), (TH.at[0, pl.ds(0, 2)], zzs.at[2]),
    ):
        drain(like, sem)
    for cp in [xpair, ypair, swap, k0[1], k1[1], k2[1], k3[1], opair] + [cp for _, cp in hp]:
        cp.wait_send()


def layer(*args):
    S = pltpu.SemaphoreType.DMA
    V = pltpu.VMEM
    sds = jax.ShapeDtypeStruct
    return pl.pallas_call(
        layer_kernel,
        name="layer",
        out_shape=(
            sds((1, 128, 1024), low),
            sds((1, 128, 1024), low),
            sds((8, 16, 256), low),
            sds((8, 16, 256), low),
            sds((32, 1024), full),
            sds((8, 1024), full),
        ),
        in_specs=[pl.BlockSpec(memory_space=pltpu.SMEM)] + [VM] * 13,
        out_specs=(VM,) * 6,
        scratch_shapes=[
            V((8, 128), full),
            V((2, 8, BLK), full),
            V((2, 4, 128, 512), full),
            V((2, 4, 128, 1024), low),
            V((2, 4, 128, 1024), low),
            V((2, 4, 128, 1024), low),
            V((2, 4, 128, 1024), low),
            V((2, 4, 128, 512), low),
            V((2, 4, 128, 512), low),
            V((1024, 512), low),
            V((2, 4, 2, 32, 1024), low),
            V((384, 1024), low),
            V((128, 1024), low),
            V((8, 1024), full),
            V((8, BLK), full),
            V((2, 4, 2, 64, BLK), low),
            V((4, 2, 64, BLK), low),
            V((2, 4, 2, 8, 16, 256), low),
            V((2, 4, 2, 8, 16, 256), low),
            V((8, 16, 256), low),
            V((8, 16, 256), low),
            V((16, 512), low),
            V((16, 16, 512), low),
            V((2, 2, 2, 2, 64, BLK), low),
            V((4, 64, BLK), full),
            V((4, 64, BLK), low),
            V((4, 1, BLK), full),
            V((4, 1, BLK), full),
            V((2, 2, 64, BLK), low),
            V((2, 2, 64, BLK), low),
            V((2, 2, 2, 64, BLK), low),
            V((2, 2, 64, BLK), full),
            V((4, 2, 64, BLK), full),
            V((4, 64, BLK), full),
            V((4, 64, BLK), low),
            V((4, 2, 64, BLK), low),
            V((4, 2, 64, BLK), low),
            V((4, 2, 64, BLK), low),
            V((2, BLK, 1024), full),
            V((2, 384, BLK), low),
            V((2, 4, 128, 1024), low),
            V((2, 4, 128, 1024), low),
            V((2, 4, 128, 1024), low),
            V((2, 4, 128, 1024), low),
            V((2, 4, 2, 8, 16, 256), low),
            V((2, 4, 2, 8, 16, 256), low),
            V((2, 4, 2, 32, 1024), low),
            V((2, 4, 2, 2, 4, 16, 256), low),
            V((2, 4, 4, 4, 16, 256), low),
            V((4, 2, 2, 32, 512), low),
            V((4, 4, 32, 512), low),
            V((2, 2, 4, 4, 16, 256), low),
            V((2, 4, 32, 512), low),
            V((2, 2, 4, 4, 16, 256), low),
            V((2, 4, 32, 512), low),
            V((8, 16, 256), low),
            V((4, 8, 16, 256), low),
            V((16, 16, 512), low),
            V((16, 16, 512), low),
            S((2,)), S((2,)), S((2,)), S((2,)), S((2,)), S((2,)), S, S, S, S, S, S, S, S, S, S, S, S, S, S, S, S,
            S((2, 2, 3)), S((4,)), S((4,)), S((4,)), S, S, S((4, 3)), S((2, 2, 2)), S((2, 2)), S((2,)), S((2,)),
            S((4,)), S((4,)), S((4,)), S((4,)), S, S, S((3,)), S((3,)), S((3,)), S((3,)), S((3,)), S((3,)), S, S,
            S, S, V((16, 256), low), V((16, 256), low), V((16, 512), low),
            V((16, 256), low), V((16, 256), low), V((16, 512), low),
        ],
        compiler_params=pltpu.CompilerParams(
            collective_id=0, has_side_effects=True, vmem_limit_bytes=62 << 20
        ),
    )(*args)


def finish_kernel(out, tg, RF, RQ, gfc2, gwo,
                  OUT, TG, GQKV, GFC1, GFC2, GWO, GG, GS, BQK, BV, BO, B1, B2):
    OUT[...] = out[...]
    TG[...] = tg[...]
    GFC2[...] = gfc2[...]
    GWO[...] = gwo[...]
    for rr in range(16):
        g = rr // 4
        c, half = g // 2, g % 2
        for hi in range(2):
            tiles = [RF[4 * hi + n, 8 * c:8 * c + 8, 128 * half:128 * half + 128].astype(full) for n in range(4)]
            col = 128 * (2 * rr + hi)
            GFC1[:, col:col + 128] = lane_mix(tiles, [32 * (n - rr % 4) for n in range(4)])
    tail = jnp.zeros((8, 128), full)
    for q in range(8):
        c = 128 * q
        GQKV[:, c:c + 128] = RQ[q, 0:8, 0:128].astype(full)
        GQKV[:, 1024 + c:1152 + c] = RQ[q, 0:8, 128:256].astype(full)
        GQKV[:, 2048 + c:2176 + c] = RQ[q, 8:16, 0:128].astype(full)
        tail = tail + RQ[q, 8:16, 128:256].astype(full)
    row = tail[0]
    GG[...] = row[0:8]
    GS[...] = row[8:16]
    BQK[...] = row[24:40]
    BV[...] = row[40:48]
    BO[...] = row[16:24]
    B1[...] = row[48:80]
    B2[...] = row[16:24]


def finish(*args):
    sds = jax.ShapeDtypeStruct
    return pl.pallas_call(
        finish_kernel,
        name="finish",
        out_shape=(
            sds((1, 128, 1024), low),
            sds((1, 128, 1024), low),
            sds((8, 3072), full),
            sds((8, 4096), full),
            sds((32, 1024), full),
            sds((8, 1024), full),
            sds((8,), full),
            sds((8,), full),
            sds((16,), full),
            sds((8,), full),
            sds((8,), full),
            sds((32,), full),
            sds((8,), full),
        ),
        in_specs=[VM] * 6,
        out_specs=(VM,) * 13,
    )(*args)


def shards(
    tokens, lengths, ln_gain, ln_bias, w_qkv, b_qkv, w_out, b_out, w_fc1, b_fc1, w_fc2, b_fc2, cotangent
):
    freq = rope_base ** (-2.0 * np.arange(8) / ROT)
    near = freq[:, None] * np.arange(BLK)[None, :]
    far = freq[:, None] * (BLK * np.arange(BLK))[None, :]
    turns = jnp.asarray(np.stack([np.cos(near), np.sin(near), np.cos(far), np.sin(far)]).astype(np.float32))
    parts = layer(
        lengths, tokens, cotangent, ln_gain, ln_bias, b_qkv, b_out, b_fc1, b_fc2, w_qkv, w_out, w_fc1, w_fc2, turns
    )
    OUT, TG, GQKV, GFC1, GFC2, GWO, GG, GS, BQK, BV, BO, B1, B2 = finish(*parts)
    return (OUT, TG, GG, GS, GQKV, BQK, BV, GWO, BO, GFC1, B1, GFC2, B2)


def solution(mesh):
    rows, tok, par, vec = (
        P(("slot", "wsh")), P(("slot", "wsh"), "ctx", None), P(("slot", "ctx", "wsh"), None), P(("slot", "ctx", "wsh"))
    )
    return jax.shard_map(
        shards,
        mesh=mesh,
        in_specs=(tok, rows, vec, vec, par, vec, par, vec, par, vec, par, vec, tok),
        out_specs=(tok, tok, vec, vec, par, vec, vec, par, vec, par, vec, par, vec),
        check_vma=False,
    )
```

```python
import functools

import jax
import jax.numpy as jnp
import numpy as np
from jax import lax
from jax.experimental import pallas as pl
from jax.experimental.pallas import tpu as pltpu
from jax.sharding import PartitionSpec as P

HEADS = 16
HD = 64
ROT = 16
HQ = 1024
D = 1024
FF = 4096
BLK = 512

norm_eps = 1e-05
rope_base = 10000.0
MESH = pl.DeviceIdType.MESH
low = jnp.bfloat16
full = jnp.float32
VM = pl.BlockSpec(memory_space=pltpu.VMEM)
AN = pl.BlockSpec(memory_space=pl.ANY)


def place():
    s = lax.axis_index("slot")
    c = lax.axis_index("ctx")
    w = lax.axis_index("wsh")
    return s, c // 8, (c // 4) % 2, c % 4, w


def dev(s, y, xh, z, w):
    return (s, y * 8 + xh * 4 + z, w)


def x_dev(x, y, z, w):
    return dev(x % 2, y, x // 2, z, w)


def signal(barrier, target):
    pl.semaphore_signal(barrier, inc=1, device_id=target, device_id_type=MESH)


def local(src, dst, sem):
    pltpu.make_async_copy(src, dst, sem).start()


def drain(like, sem):
    pltpu.make_async_copy(like, like, sem).wait()


def remote(src, dst, send, recv, target):
    return pltpu.make_async_remote_copy(
        src_ref=src, dst_ref=dst, send_sem=send, recv_sem=recv,
        device_id=target, device_id_type=MESH,
    )


def iota(shape, axis):
    return lax.broadcasted_iota(jnp.int32, shape, axis)


def dot(a, b, ca, cb):
    return lax.dot_general(a, b, (((ca,), (cb,)), ((), ())), preferred_element_type=full)


def core_of(m):
    return ((m + 1) // 2) % 2


def owner_lanes(params, width, lanes, step):
    f, l = iota((128, width), 1), iota((128, width), 0)
    pick = (l == lanes[0] + (f & (step - 1)))
    for other in lanes[1:]:
        pick = pick | (l == other + (f & (step - 1)))
    return dot(params, pick.astype(full).astype(low), 1, 0), f, l


def lane_mix(tiles, shifts):
    lane = iota((8, 128), 1)
    out = jnp.zeros((8, 128), full)
    for g in range(4):
        t = tiles[g]
        if shifts[g] % 128:
            t = pltpu.roll(t, shifts[g] % 128, 1)
        out = jnp.where((lane >= 32 * g) & (lane < 32 * g + 32), t, out)
    return out


def layer_kernel(
    lens, tok_in, cot_in, lg, lb, bq, bo, bf, bg, wq_in, wo_in, w1_in, w2_in, turns_in, OUT, TG, RF, RQ, GFC2, GWO, tok, cot, wq, wo, w1, w2, turns, fetch, PAD, ROPE, SL, XX, YY, HB, XH, GA, DU,
    W1, W2, WQT, WOF, VEC, VAL, KV, QD, Q, F, Qs, Fs, wos, WO, HT, OF, OB, LSE, DLT, RO, RQ1, RKV, acc,
    acc_own, dqa, DQB, other, got, summed, PH, DQ, TO, TH, pin, zin, GF, GQ, GW, gi0, gi1, wi0, wi1, gm, wm,
    gi2, wi2, Ff, QIN, GO, fo_in, zs, zr, ys, yr, ps, pr, yps, ypr, ts, tr, fs, fr, os, orr, q2s, q2r, f1s, f1r,
    f2s, f2r, w1s, w1r, w2s, w2r, hs, kr, qr, dr, ks, krp, bs, br, br2, pps, ppr, hps, hpr, kss, ksr, gos, gor, zzs, zzr,
    g1s, g1r, g2s, g2r, tts, ttr, us, ur, spare, spare2, spare3, spare4, spare5, spare6,
):
    fetches = [
        pltpu.make_async_copy(a, b, fetch.at[n])
        for n, (a, b) in enumerate(
            ((wq_in, wq), (tok_in, tok), (w2_in, w2), (w1_in, w1), (wo_in, wo), (cot_in, cot), (turns_in, turns))
        )
    ]
    for cp in fetches:
        cp.start()
    s, y, xh, z, w = place()
    x = xh * 2 + s
    r = s * 8 + y * 2 + xh
    j = z * 2 + w
    jo = r // 2
    m = y * 2 + xh
    core, spot = core_of(m), m // 2
    keep = (j == jo).astype(jnp.int32)
    mine = ((y % 2 == w) & (core == w)).astype(jnp.int32)
    sib = dev(s, y, xh, z, 1 - w)

    lo4, hi4 = pl.ds(0, 4), pl.ds(4, 4)
    lo5, hi5 = pl.ds(0, 512), pl.ds(512, 512)
    half = z // 2
    flip = 1 - half

    def ahead(k, q):
        return x_dev((x + k * flip) % 4, (y + k * half) % 4, q // 2, q % 2)

    def behind(k, q):
        if q < 4:
            return x_dev((x + 4 - k) % 4, y, q // 2, q % 2)
        return dev(s, (y + 4 - k) % 4, xh, q // 2, q % 2)

    barrier = pltpu.get_barrier_semaphore()
    for k in range(4):
        for q in range(8):
            if k == 0:
                @pl.when(j != q)
                def _():
                    signal(barrier, behind(k, q))
            else:
                signal(barrier, behind(k, q))
    for k in range(1, 4):
        signal(barrier, x_dev((x + k) % 4, y, z, w))
        signal(barrier, dev(s, (y + k) % 4, xh, z, w))

    def wo_source(k):
        rr = 2 * j + k // 8
        return rr // 8, (rr // 2) % 4, rr % 2, (k % 8) // 2, k % 2

    def wo_mine(k):
        ss, sy, sxh, sz, sw = wo_source(k)
        return (ss == s) & (sy == y) & (sxh == xh) & (sz == z) & (sw == w)

    def source(i):
        return dev(s, i, (i + w) % 2, z, y % 2)

    def my_source(i):
        return (y == i) & (xh == (i + w) % 2) & (w == y % 2)

    def sender(q):
        return dev(q // 8, (q // 2) % 4, q % 2, jo // 2, jo % 2)

    def home(i):
        return dev(s, i, (i + w) % 2, z, y % 2)

    def at_home(i):
        return (y == i) & (xh == (i + w) % 2) & (w == y % 2)

    def head_at(e, i):
        return dev(s, 2 * e + w, i, z, core)

    def head_here(e, i):
        return (y == 2 * e + w) & (xh == i) & (core == w)

    e_me, i_me = y // 2, xh
    for cp in fetches:
        cp.wait()
    XX[w, z] = tok[0]
    first_row = iota((8, 128), 0)
    PAD[...] = jnp.zeros_like(PAD)
    PAD[0:1, 0:8] = lg[...].reshape(1, 8)
    PAD[1:2, 0:8] = lb[...].reshape(1, 8)
    PAD[2:3, 0:24] = bq[...].reshape(1, 24)
    PAD[3:4, 0:8] = bo[...].reshape(1, 8)
    PAD[4:5, 0:32] = bf[...].reshape(1, 32)
    PAD[5:6, 0:8] = bg[...].reshape(1, 8)
    lane8 = iota((8, 128), 1)
    size = jnp.full((8, 128), lens[0], jnp.int32)
    padded = jnp.where(
        first_row == 6,
        jnp.where(lane8 == 0, (size >> 6).astype(full), jnp.where(lane8 == 1, (size & 63).astype(full), 0.0)),
        PAD[...],
    )
    for q in range(8):
        c = 128 * q
        top = jnp.concatenate([wq[:, c:c + 128], wq[:, 1024 + c:1152 + c]], axis=1)
        bot = jnp.concatenate([wq[:, 2048 + c:2176 + c], padded], axis=1)
        Qs[q] = jnp.concatenate([top, bot], axis=0).astype(low)

    W2[s, y, xh] = w2[...].astype(low)
    for q in range(8):
        tiles = []
        for g in range(4):
            parts = [w1[:, 128 * (2 * (4 * g + n) + q // 4):128 * (2 * (4 * g + n) + q // 4) + 128] for n in range(4)]
            tiles.append(lane_mix(parts, [32 * (n - q % 4) for n in range(4)]))
        top = jnp.concatenate(tiles[:2], axis=1)
        bot = jnp.concatenate(tiles[2:], axis=1)
        Fs[q] = jnp.concatenate([top, bot], axis=0).astype(low)

    def ring1(ref0, ref1, snd, rcv):
        for k in (1, 3, 2):
            cp = remote(ref0, ref0, snd, rcv, x_dev((x + k) % 4, y, z, w))
            cp.start()
            cp = remote(ref1, ref1, snd, rcv, dev(s, (y + k) % 4, xh, z, w))
            cp.start()

    def ring2(ref0, ref1, snd, rcv):
        for k in (1, 3, 2):
            cp = remote(ref0, ref0, snd, rcv, dev(s, (y + k) % 4, xh, z, w))
            cp.start()
            cp = remote(ref1, ref1, snd, rcv, x_dev((x + k) % 4, y, z, w))
            cp.start()

    def z_near(buf, snd, rcv):
        for k in (1, 3):
            cp = remote(buf.at[w, z], buf.at[w, z], snd.at[0], rcv.at[0], dev(s, y, xh, (z + k) % 4, w))
            cp.start()

    def z_far(buf, snd, rcv):
        up, down = (z + 1) % 4, (z + 3) % 4
        a = buf.at[w, down, pl.ds(0, 64)]
        b = buf.at[w, up, pl.ds(64, 64)]
        out = [
            remote(a, a, snd.at[1], rcv.at[1], dev(s, y, xh, up, w)),
            remote(b, b, snd.at[1], rcv.at[1], dev(s, y, xh, down, w)),
        ]
        for cp in out:
            cp.start()

    with jax.named_scope("barrier"):
        pl.semaphore_wait(barrier, 31 + 6)

    slot = (r % 2) * 8 + j
    for n in (1, 2, 3, 4, 5, 6, 7, 0):
        for k in (1, 3, 2, 0):
            if k == 0 and n == 0:
                continue
            q = (j + n) % 8
            remote(Qs.at[q], Q.at[s, y, xh, j], ts, tr, ahead(k, q)).start()
    for k in range(1, 8):
        q = (j + k) % 8
        remote(Fs.at[q], F.at[s, y, xh, j], fs, fr, dev(s, y, xh, q // 2, q % 2)).start()
    ring1(W2.at[s, y, xh, :, lo5], W2.at[s, y, xh, :, hi5], w1s, w1r)
    z_near(XX, zs, zr)
    local(Qs.at[j], Q.at[s, y, xh, j], tr)
    local(Qs.at[j], spare, ts)
    local(Fs.at[j], F.at[s, y, xh, j], fr)
    local(Fs.at[j], spare2, fs)

    row = iota((128, 1024), 0) + (m * BLK + z * 128)
    YY[w, z] = jnp.where(row < lens[0], cot[0].astype(full), 0.0).astype(low)
    wos[...] = jnp.concatenate([wo[:, :512], wo[:, 512:]], axis=0).astype(low)
    c0, s0 = turns[0], turns[1]
    at_m = iota((8, 128), 1) == m
    cm = jnp.sum(jnp.where(at_m, turns[2, :, :128], 0.0), axis=1, keepdims=True)
    sm = jnp.sum(jnp.where(at_m, turns[3, :, :128], 0.0), axis=1, keepdims=True)
    ROPE[0] = cm * c0 - sm * s0
    ROPE[1] = sm * c0 + cm * s0

    with jax.named_scope("units"):
        drain(QIN, tr)
    with jax.named_scope("tf"):
        drain(Fs, fr)
    ring1(F.at[s, y, xh, lo4], F.at[s, y, xh, hi4], f1s, f1r)
    ring2(Q.at[:, y, :, lo4], Q.at[s, :, xh, hi4], q2s, q2r)
    with jax.named_scope("g1"):
        drain(QIN.at[pl.ds(0, 3)], w1r)
    with jax.named_scope("f1"):
        drain(QIN.at[pl.ds(0, 3)], f1r)
    ring2(F.at[:, y, :, lo4], F.at[s, :, xh, hi4], f2s, f2r)
    ring2(W2.at[:, y, :, :, lo5], W2.at[s, :, xh, :, hi5], w2s, w2r)
    with jax.named_scope("xnear"):
        drain(XX.at[0, pl.ds(0, 2)], zr.at[0])
    z_far(XX, zs, zr)
    z_near(YY, ys, yr)
    for k in range(16):
        q = (r + k) % 16
        cp = remote(wos, WO.at[slot], os, orr, dev(q // 8, (q // 2) % 4, q % 2, jo // 2, jo % 2))
        if k == 0:
            @pl.when(j != jo)
            def _():
                cp.start()

            @pl.when(j == jo)
            def _():
                local(wos, WO.at[slot], orr)
                local(wos, spare3, os)
        else:
            cp.start()
    with jax.named_scope("x"):
        drain(XX.at[0, 0], zr.at[1])
    xpair = remote(XX.at[w], XX.at[w], ps.at[0], pr.at[0], sib)
    xpair.start()
    with jax.named_scope("ring2"):
        drain(Q.at[:, pl.ds(0, 3)], q2r)
    units = Q[...].reshape(128, 16, 256).astype(full)
    left = units[:, :8].reshape(1024, 256)
    right = units[:, 8:].reshape(1024, 256)
    WQT[0:256, :] = left.T.astype(low)
    WQT[256:384, :] = right[:, :128].T.astype(low)
    pads = right[:, 128:].astype(low)

    def params_of(i):
        pick = (iota((128, 1024), 1) == 8 * iota((128, 1024), 0) + i).astype(full).astype(low)
        return dot(pick, pads, 1, 0).astype(low)

    def row_of(i):
        t, f, l = owner_lanes(params_of(i), 1024, (0,), 8)
        return jnp.sum(jnp.where((f >= 8 * l) & (f < 8 * l + 8), t, 0.0), axis=0, keepdims=True)

    gain = row_of(0)
    shift = row_of(1)
    n0, p0 = iota((384, 128), 0), iota((384, 128), 1)
    n0 = (n0 // 128) * 1024 + 128 * j + (n0 & 127)
    at = n0 - 24 * p0
    inside = ((at >= 0) & (at < 24)).astype(full)
    t = dot(inside.astype(low), params_of(2), 1, 0)
    lane_want = jnp.sum(inside * at.astype(full), axis=1, keepdims=True)
    bias_q = jnp.sum(jnp.where(p0.astype(full) == lane_want, t, 0.0), axis=1, keepdims=True)
    co, si = ROPE[0], ROPE[1]

    def norm_slot(wi):
        def one(zi, carry):
            v = XX[wi, zi].astype(full)
            mean = jnp.mean(v, axis=-1, keepdims=True)
            c = v - mean
            var = jnp.mean(c * c, axis=-1, keepdims=True)
            h = c * lax.rsqrt(var + norm_eps)
            XH[wi, zi] = h.astype(low)
            HB[wi, zi] = (h * gain + shift).astype(low)
            return carry

        lax.fori_loop(0, 4, one, 0)

    def turn(v):
        a, b = v[0:8], v[8:16]
        return jnp.concatenate([a * co - b * si, b * co + a * si, v[16:]], axis=0)

    def qkv_slot(wi):
        t = dot(WQT[...], HB[wi].reshape(BLK, 1024), 1, 1) + bias_q
        for e in range(2):
            HT[e, wi, 0, 0] = turn(t[128 + 64 * e:192 + 64 * e]).astype(low)
            HT[e, wi, 0, 1] = t[256 + 64 * e:320 + 64 * e].astype(low)
            HT[e, wi, 1, 0] = (turn(t[64 * e:64 + 64 * e]).astype(low).astype(full) * 0.125).astype(low)

    def head_target(e, i):
        return dev(s, 2 * e + w, i, z, core), (y == 2 * e + w) & (xh == i) & (core == w)

    def kv_copy(e, i):
        return remote(HT.at[e, i, 0], KV.at[core, spot], hs.at[e, i, 0], kr.at[spot], head_target(e, i)[0])

    def q_copy(e, i):
        return remote(HT.at[e, i, 1, 0], QD.at[spot, 0], hs.at[e, i, 1], qr.at[spot], head_target(e, i)[0])

    def do_copy(e, i):
        return remote(HT.at[e, i, 1, 1], QD.at[spot, 1], hs.at[e, i, 2], dr.at[spot], head_target(e, i)[0])

    def send_qkv(i):
        for e in range(2):
            me = head_target(e, i)[1]

            @pl.when(jnp.logical_not(me))
            def _():
                kv_copy(e, i).start()
                q_copy(e, i).start()

            @pl.when(me)
            def _():
                KV[core, spot] = HT[e, i, 0]
                QD[spot, 0] = HT[e, i, 1, 0]

    def send_do(i):
        t = dot(WOF[...], YY[i].reshape(BLK, 1024), 1, 1)
        for e in range(2):
            HT[e, i, 1, 1] = t[64 * e:64 + 64 * e].astype(low)
            me = head_target(e, i)[1]

            @pl.when(jnp.logical_not(me))
            def _():
                do_copy(e, i).start()

            @pl.when(me)
            def _():
                QD[spot, 1] = HT[e, i, 1, 1]

    norm_slot(w)
    qkv_slot(w)
    send_qkv(w)
    xpair.wait_recv()
    norm_slot(1 - w)
    qkv_slot(1 - w)
    send_qkv(1 - w)

    with jax.named_scope("ynear"):
        drain(YY.at[0, pl.ds(0, 2)], yr.at[0])
    for k in (0, 1, 3):
        here = YY.at[w, (z + k) % 4]
        remote(here, here, yps.at[0], ypr.at[0], sib).start()
    z_far(YY, ys, yr)
    VEC[0:1, :] = gain
    VEC[1:2, :] = row_of(3) + row_of(5)
    t, f, l = owner_lanes(params_of(4), 512, (0,), 32)
    base = f - 4 * (l - j)
    bias_1 = jnp.sum(
        jnp.where((((l - j) & 7) == 0) & (base >= 0) & (base < 32), t, 0.0), axis=0, keepdims=True
    )
    lp, ll = iota((128, 128), 0), iota((128, 128), 1)
    tok_pos = (iota((1, BLK), 1) + m * BLK).astype(full)
    pf = params_of(6).astype(full)
    for i in range(2):
        here = lp == s * 64 + i
        size = jnp.sum(jnp.where(here & (ll == 0), pf, 0.0)) * 64.0 + jnp.sum(jnp.where(here & (ll == 1), pf, 0.0))
        VAL[i:i + 1, :] = jnp.where(tok_pos < size, 1.0, 0.0)

    with jax.named_scope("f2"):
        drain(F.at[:, pl.ds(0, 3)], f2r)
        drain(F.at[:, pl.ds(0, 3)], w2r)
    units = F[...].reshape(128, 16, 256).astype(full)
    W1[:, :256] = units[:, :8].reshape(1024, 256).astype(low)
    W1[:, 256:] = units[:, 8:].reshape(1024, 256).astype(low)
    g0 = 0.7978845608028654

    def hidden_up(n, carry):
        wi, zi = n // 2, pl.ds(2 * (n % 2), 2)
        u = dot(HB[wi, zi].reshape(256, 1024), W1[...], 1, 0) + bias_1
        t = jnp.tanh(g0 * (u + 0.044715 * (u * u * u)))
        GA[wi, zi] = (0.5 * u * (1.0 + t)).astype(low).reshape(2, 128, 512)
        slope = 0.5 * (1.0 + t) + (0.5 * g0) * u * (1.0 - t * t) * (1.0 + (3.0 * 0.044715) * (u * u))
        SL[wi, zi] = slope.reshape(2, 128, 512)
        return carry

    with jax.named_scope("hidden_up"):
        lax.fori_loop(0, 4, hidden_up, 0)
    with jax.named_scope("dy"):
        drain(YY.at[0, 0], yr.at[1])
    ypair = remote(YY.at[w, (z + 2) % 4], YY.at[w, (z + 2) % 4], ps.at[1], pr.at[1], sib)
    ypair.start()

    def hidden_down(n, carry):
        wi, zi = jnp.where(n < 2, w, 1 - w), pl.ds(2 * (n % 2), 2)
        dg = dot(YY[wi, zi].reshape(256, 1024), W2[...].reshape(512, 1024), 1, 1)
        DU[wi, zi] = (dg.reshape(2, 128, 512) * SL[wi, zi]).astype(low)
        return carry

    with jax.named_scope("hidden_down"):
        lax.fori_loop(0, 2, hidden_down, 0)
        drain(YY.at[0, pl.ds(0, 3)], ypr.at[0])
        ypair.wait_recv()
        lax.fori_loop(2, 4, hidden_down, 0)
    with jax.named_scope("wgrads"):
        ga = GA[...].reshape(1024, 512)

        def first_w2(h):
            t = dot(ga, YY[:, :, :, 512 * h:512 * h + 512].reshape(1024, 512), 0, 0).astype(low)
            GW[:, :, :, :, 512 * h:512 * h + 512] = t.reshape(2, 4, 2, 32, 512)
            out = []
            for k in (1, 3, 2):
                yy, xx = (y + k) % 4, (x + k) % 4
                if h == 0:
                    cp = remote(GW.at[:, yy, :, :, lo5], wi0.at[k], g1s.at[2], g1r.at[2], dev(s, yy, xh, z, w))
                else:
                    cp = remote(GW.at[xx % 2, :, xx // 2, :, hi5], wi1.at[k], g1s.at[2], g1r.at[2], x_dev(xx, y, z, w))
                cp.start()
                out.append(cp)
            return out

        def first_unit(g, buf):
            out = []
            for k in (1, 3, 2):
                yy, xx = (y + k) % 4, (x + k) % 4
                cp = remote(buf.at[:, yy, :, lo4], gi0.at[g, k], g1s.at[g], g1r.at[g], dev(s, yy, xh, z, w))
                cp.start()
                out.append(cp)
                cp = remote(buf.at[xx % 2, :, xx // 2, hi4], gi1.at[g, k], g1s.at[g], g1r.at[g], x_dev(xx, y, z, w))
                cp.start()
                out.append(cp)
            return out

        def add4(a, b, c, d):
            return a.astype(full) + b.astype(full) + c.astype(full) + d.astype(full)

        def second_unit(g, buf):
            gm[g, 0] = add4(
                buf[:, y, :, 0:4], gi0[g, 1], gi0[g, 2], gi0[g, 3]
            ).astype(low).reshape(4, 4, 16, 256)
            gm[g, 1] = add4(
                buf[s, :, xh, 4:8], gi1[g, 1], gi1[g, 2], gi1[g, 3]
            ).astype(low)
            out = []
            for k in (1, 3, 2):
                yy, xx = (y + k) % 4, (x + k) % 4
                cp = remote(gm.at[g, 0, 2 * (xx % 2) + xx // 2], gi2.at[g, 0, k], g2s.at[g], g2r.at[g], x_dev(xx, y, z, w))
                cp.start()
                out.append(cp)
                cp = remote(gm.at[g, 1, yy], gi2.at[g, 1, k], g2s.at[g], g2r.at[g], dev(s, yy, xh, z, w))
                cp.start()
                out.append(cp)
            return out

        def second_w2():
            wm[0] = add4(GW[:, y, :, :, :512], wi0[1], wi0[2], wi0[3]).astype(low).reshape(4, 32, 512)
            wm[1] = add4(GW[s, :, xh, :, 512:], wi1[1], wi1[2], wi1[3]).astype(low)
            out = []
            for k in (1, 3, 2):
                yy, xx = (y + k) % 4, (x + k) % 4
                cp = remote(wm.at[0, 2 * (xx % 2) + xx // 2], wi2.at[0, k], g2s.at[2], g2r.at[2], x_dev(xx, y, z, w))
                cp.start()
                out.append(cp)
                cp = remote(wm.at[1, yy], wi2.at[1, k], g2s.at[2], g2r.at[2], dev(s, yy, xh, z, w))
                cp.start()
                out.append(cp)
            return out

        def last_unit(g, fin, got_units):
            fin[0:4] = add4(gm[g, 0, 2 * s + xh], gi2[g, 0, 1], gi2[g, 0, 2], gi2[g, 0, 3]).astype(low)
            fin[4:8] = add4(gm[g, 1, y], gi2[g, 1, 1], gi2[g, 1, 2], gi2[g, 1, 3]).astype(low)
            out = []
            for k in range(1, 8):
                q = (j + k) % 8
                cp = remote(fin.at[q], got_units.at[j], tts, ttr, dev(s, y, xh, q // 2, q % 2))
                cp.start()
                out.append(cp)
            local(fin.at[j], got_units.at[j], ttr)
            local(fin.at[j], spare4, tts)
            return out

        c_w2 = first_w2(0)
        c_w2 += first_w2(1)

    with jax.named_scope("kv"):
        for i in range(4):
            @pl.when(jnp.logical_not(my_source(i)))
            def _():
                remote(HT.at[0, 0, 0], KV.at[w, i], hs.at[0, 0, 0], kr.at[i], source(i)).wait_recv()
    swap = remote(KV.at[w], KV.at[w], ks, krp, sib)
    swap.start()
    with jax.named_scope("do"):
        drain(WO, orr)
        units = WO[...].astype(full)
        WOF[:, :512] = units[:, :8].reshape(128, 512).astype(low)
        WOF[:, 512:] = units[:, 8:].reshape(128, 512).astype(low)
        send_do(w)
        send_do(1 - w)
    with jax.named_scope("wgrads1"):
        du = DU[...].reshape(1024, 512)
        for n in range(4):
            t = dot(HB[:, :, :, 256 * n:256 * n + 256].reshape(1024, 256), du, 0, 0)
            t = jnp.concatenate([t[:, :256].reshape(32, 8, 256), t[:, 256:].reshape(32, 8, 256)], axis=1)
            GF[n // 2, 2 * (n % 2):2 * (n % 2) + 2] = t.astype(low).reshape(2, 2, 8, 16, 256)
        c_f = first_unit(0, GF)
        gb1 = jnp.sum(du.astype(full), axis=0, keepdims=True)
        gb_out = jnp.sum(YY[w, z].astype(full), axis=0, keepdims=True)

    with jax.named_scope("q"):
        for i in range(4):
            @pl.when(jnp.logical_not(my_source(i)))
            def _():
                remote(HT.at[0, 0, 1, 0], QD.at[i, 0], hs.at[0, 0, 1], qr.at[i], source(i)).wait_recv()
    with jax.named_scope("kvswap"):
        swap.wait_recv()

    causal = iota((BLK, BLK), 0) <= iota((BLK, BLK), 1)

    def query_block(i, carry):
        q = QD[i, 0]

        def many(blocks, state):
            run_max, total, out = state
            scores = []
            for c, t, masked in blocks:
                sc = dot(KV[c, t, 0], q, 0, 0)
                scores.append(jnp.where(causal, sc, -1e30) if masked else sc)
            new_max = run_max
            for sc in scores:
                new_max = jnp.maximum(new_max, jnp.max(sc, axis=0, keepdims=True))
            fac = jnp.exp(run_max - new_max)
            total, out = total * fac, out * fac
            for (c, t, _), sc in zip(blocks, scores):
                pr = jnp.exp(sc - new_max)
                total = total + jnp.sum(pr, axis=0, keepdims=True)
                out = out + dot(KV[c, t, 1], pr.astype(low), 1, 0)
            return new_max, total, out

        def two(t):
            return [(0, t, False), (1, t, False)]

        state = (
            jnp.full((1, BLK), -1e30, full),
            jnp.zeros((1, BLK), full),
            jnp.zeros((HD, BLK), full),
        )
        state = lax.fori_loop(0, i // 2, lambda t, st: many(two(2 * t) + two(2 * t + 1), st), state)
        state = lax.fori_loop(2 * (i // 2), i, lambda t, st: many(two(t), st), state)

        def keep_state(state):
            run_max, total, out = state
            out = out / total
            OF[i] = out
            LSE[i] = run_max + jnp.log(total)
            OB[i] = out.astype(low)

        @pl.when((i + w) % 2 == 1)
        def _():
            keep_state(many([(1 - w, i, False), (w, i, True)], state))

        @pl.when((i + w) % 2 == 0)
        def _():
            keep_state(many([(w, i, True)], state))

        @pl.when(jnp.logical_not(at_home(i)))
        def _():
            remote(OB.at[i], RO.at[e_me, i_me], bs.at[i, 0], br.at[0, e_me, i_me], home(i)).start()

        @pl.when(at_home(i))
        def _():
            RO[e_me, i_me] = OB[i]

        return carry

    with jax.named_scope("forward"):
        lax.fori_loop(0, 4, query_block, 0)


    def mlp_parts(i, carry):
        PH[i] = dot(DU[i].reshape(BLK, 512), W1[...], 1, 1)
        return carry

    def wait_home(g, src, dst):
        for e in range(2):
            for i in range(2):
                @pl.when(jnp.logical_not(head_here(e, i)))
                def _():
                    remote(src.at[0], dst.at[e, i], bs.at[0, g], br.at[g, e, i], head_at(e, i)).wait_recv()

    for i in range(4):
        @pl.when(jnp.logical_not(my_source(i)))
        def _():
            remote(HT.at[0, 0, 1, 1], QD.at[i, 1], hs.at[0, 0, 2], dr.at[i], source(i)).wait_recv()
    for i in range(4):
        DLT[i] = jnp.sum(QD[i, 1].astype(full) * OF[i], axis=0, keepdims=True)
    dqa[...] = jnp.zeros_like(dqa)

    def pairs(t, i, blocks):
        q, do, lse, dlt = QD[i, 0], QD[i, 1], LSE[i], DLT[i]
        scores = [dot(KV[c, t, 0], q, 0, 0) for c, _ in blocks]
        dps = [dot(KV[c, t, 1], do, 0, 0) for c, _ in blocks]
        dq = dqa[i]
        for (c, masked), sc, dp in zip(blocks, scores, dps):
            pr = jnp.exp(sc - lse)
            if masked:
                pr = jnp.where(causal, pr, 0.0)
            ds = (pr * (dp - dlt)).astype(low)
            acc[c, 0] += dot(q, ds, 1, 1)
            acc[c, 1] += dot(do, pr.astype(low), 1, 1)
            dq = dq + dot(KV[c, t, 0], ds, 1, 0)
        dqa[i] = dq

    def kv_home(t):
        summed[t] = (acc_own[t] + got[t].astype(full)).astype(low)

        @pl.when(jnp.logical_not(at_home(t)))
        def _():
            remote(summed.at[t], RKV.at[e_me, i_me], bs.at[t, 2], br2.at[e_me, i_me], home(t)).start()

        @pl.when(at_home(t))
        def _():
            RKV[e_me, i_me] = summed[t]

    final = 2 * e_me + i_me

    def dq_home(t):
        DQB[t] = (dqa[t] * 0.125).astype(low)

        @pl.when(jnp.logical_not(at_home(t)))
        def _():
            remote(DQB.at[t], RQ1.at[e_me, i_me], bs.at[t, 1], br.at[1, e_me, i_me], home(t)).start()

        @pl.when(at_home(t))
        def _():
            RQ1[e_me, i_me] = DQB[t]

    def step(p, before=None):
        t = final if p == 3 else p + (p >= final).astype(jnp.int32)
        acc[...] = jnp.zeros_like(acc)

        def rest(i, carry):
            pairs(t, i, [(0, False), (1, False)])
            return carry

        some = jnp.minimum(t + 2, 4)
        lax.fori_loop(t + 1, some, rest, 0)
        if before is not None:
            before[1].wait_recv()
            kv_home(before[0])
        if p != 2:
            lax.fori_loop(some, 4, rest, 0)

        @pl.when((t + w) % 2 == 1)
        def _():
            pairs(t, t, [(1 - w, False), (w, True)])

        @pl.when((t + w) % 2 == 0)
        def _():
            pairs(t, t, [(w, True)])

        other[t] = acc[1 - w].astype(low)
        acc_own[t] = acc[w]
        cp = remote(other.at[t], got.at[t], kss.at[t], ksr.at[t], sib)
        cp.start()
        if p < 3:
            @pl.when(t < final)
            def _():
                dq_home(t)
        else:
            for n in range(4):
                @pl.when(n >= final)
                def _():
                    dq_home(n)
        return t, cp

    with jax.named_scope("step0"):
        k0 = step(0)
    with jax.named_scope("wf1"):
        drain(F.at[:, pl.ds(0, 3)], g1r.at[2])
        drain(F.at[:, pl.ds(0, 3)], g1r.at[0])
    d_w2 = second_w2()
    d_f = second_unit(0, GF)
    with jax.named_scope("ohome"):
        wait_home(0, OB, RO)

    def out_slot(i):
        ob = jnp.concatenate([RO[0, i], RO[1, i]], axis=0).astype(full)
        ob = (ob * VAL[pl.ds(i, 1), :]).astype(low)
        t = dot(ob, WOF[...], 0, 0) + dot(GA[i].reshape(BLK, 512), W2[...].reshape(512, 1024), 1, 0)
        TO[i] = t.astype(low).reshape(4, 128, 1024)
        return dot(ob, YY[i].reshape(BLK, 1024), 1, 0)

    g_wo = out_slot(1 - w)
    opair = remote(TO.at[1 - w], pin.at[0], pps.at[0], ppr.at[0], sib)
    opair.start()
    g_wo = g_wo + out_slot(w)
    GO[...] = jnp.concatenate(
        [g_wo[:, :512].reshape(16, 8, 512), g_wo[:, 512:].reshape(16, 8, 512)], axis=1
    ).astype(low)

    def owner(k):
        rr = 2 * j + k // 8
        return rr // 8, (rr // 2) % 4, rr % 2, (k % 8) // 2, k % 2

    def owner_copy(k):
        os_, oy, oxh, oz, ow = owner(k)
        me = (os_ == s) & (oy == y) & (oxh == xh) & (oz == z) & (ow == w)
        return remote(GO.at[k], fo_in.at[r], gos, gor, dev(os_, oy, oxh, oz, ow)), me

    for k in range(16):
        cp, me = owner_copy(k)

        @pl.when(jnp.logical_not(me))
        def _():
            cp.start()

        @pl.when(me)
        def _():
            local(GO.at[k], fo_in.at[r], gor)
            local(GO.at[k], spare6, gos)

    def pair_z(n, buf):
        def one(t, carry):
            buf[w, t] = (buf[w, t].astype(full) + pin[n, t].astype(full)).astype(low)
            return carry

        lax.fori_loop(0, 4, one, 0)
        out = []
        for k in (1, 3, 2):
            zz = (z + k) % 4
            cp = remote(buf.at[w, zz], zin.at[n, k], zzs.at[0], zzr.at[0], dev(s, y, xh, zz, w))
            cp.start()
            out.append(cp)
        return out

    with jax.named_scope("step1"):
        k1 = step(1, k0)
    with jax.named_scope("opair"):
        opair.wait_recv()
    zo = pair_z(0, TO)
    with jax.named_scope("step2"):
        k2 = step(2, k1)
    with jax.named_scope("step3"):
        k3 = step(3, k2)
    with jax.named_scope("k3"):
        k3[1].wait_recv()
    kv_home(k3[0])

    def turn_back(v):
        a, b = v[0:8], v[8:16]
        return jnp.concatenate([a * ROPE[0] + b * ROPE[1], b * ROPE[0] - a * ROPE[1], v[16:]], axis=0)

    def wait_kv():
        for e in range(2):
            for i in range(2):
                @pl.when(jnp.logical_not(head_here(e, i)))
                def _():
                    remote(summed.at[0], RKV.at[e, i], bs.at[0, 2], br2.at[e, i], head_at(e, i)).wait_recv()

    d0, p0 = iota((128, 1024), 1), iota((128, 1024), 0)
    block = (d0 >= 8 * p0) & (d0 < 8 * p0 + 8)
    dt, lt = iota((1024, 128), 0), iota((1024, 128), 1)

    def spread_row(v, lane):
        a = jnp.where(block, jnp.broadcast_to(v, (128, 1024)), 0.0).astype(low)
        return dot(a, (lt == lane + (dt & 7)).astype(full).astype(low), 1, 0)

    f0, pf = iota((128, 512), 1), iota((128, 512), 0)
    base = f0 - 4 * (pf - j)
    a = jnp.where(
        (((pf - j) & 7) == 0) & (base >= 0) & (base < 32), jnp.broadcast_to(gb1, (128, 512)), 0.0
    ).astype(low)
    ft, lf = iota((512, 128), 0), iota((512, 128), 1)
    small_early = spread_row(gb_out, 16) + dot(a, (lf == 48 + (ft & 31)).astype(full).astype(low), 1, 0)
    with jax.named_scope("fill"):
        lax.fori_loop(0, 2, mlp_parts, 0)
        with jax.named_scope("wf2"):
            drain(QIN.at[pl.ds(0, 3)], g2r.at[2])
            drain(QIN.at[pl.ds(0, 3)], g2r.at[0])
        GFC2[:, :512] = add4(wm[0, 2 * s + xh], wi2[0, 1], wi2[0, 2], wi2[0, 3])
        GFC2[:, 512:] = add4(wm[1, y], wi2[1, 1], wi2[1, 2], wi2[1, 3])
        t_f = last_unit(0, Ff, RF)
        mine_x = tok[0].astype(full)
        mean = jnp.mean(mine_x, axis=-1, keepdims=True)
        cen = mine_x - mean
        inv = lax.rsqrt(jnp.mean(cen * cen, axis=-1, keepdims=True) + norm_eps)
    with jax.named_scope("home"):
        wait_home(1, DQB, RQ1)
        wait_kv()

    def dh_slot(i):
        for e in range(2):
            DQ[i, 64 * e:64 * e + 64] = turn_back(RQ1[e, i].astype(full)).astype(low)
            DQ[i, 128 + 64 * e:192 + 64 * e] = turn_back(RKV[e, i, 0].astype(full)).astype(low)
            DQ[i, 256 + 64 * e:320 + 64 * e] = RKV[e, i, 1]
        t = dot(DQ[i], WQT[...], 0, 0) + PH[i]
        TH[i] = t.astype(low).reshape(4, 128, 1024)
        g_shift = jnp.sum(t, axis=0, keepdims=True)
        g_gain = jnp.sum(t * XH[i].reshape(BLK, 1024).astype(full), axis=0, keepdims=True)
        return g_shift, g_gain, jnp.sum(DQ[i].astype(full), axis=1, keepdims=True)

    a_shift, a_gain, a_bq = dh_slot(1 - w)
    hp = []
    for k in (2, 1, 3, 0):
        zz = (z + k) % 4
        cp = remote(TH.at[1 - w, zz], pin.at[1, zz], hps.at[k], hpr.at[k], sib)
        cp.start()
        hp.append((k, cp))
    b_shift, b_gain, b_bq = dh_slot(w)
    up, down, across = (z + 1) % 4, (z + 3) % 4, (z + 2) % 4

    def add_hp(n):
        k, cp = hp[n]
        zz = (z + k) % 4
        cp.wait_recv()
        TH[w, zz] = (TH[w, zz].astype(full) + pin[1, zz].astype(full)).astype(low)

    with jax.named_scope("hpfirst"):
        add_hp(0)
    lo6, hi6 = pl.ds(0, 64), pl.ds(64, 64)
    zh = [
        remote(TH.at[w, across, lo6], zin.at[1, 2, lo6], zzs.at[1], zzr.at[1], dev(s, y, xh, up, w)),
        remote(TH.at[w, across, hi6], zin.at[1, 2, hi6], zzs.at[1], zzr.at[1], dev(s, y, xh, down, w)),
    ]
    for cp in zh:
        cp.start()
    gq = dot(DQ[0], HB[0].reshape(BLK, 1024), 1, 0) + dot(DQ[1], HB[1].reshape(BLK, 1024), 1, 0)
    small = spread_row(a_gain + b_gain, 0) + spread_row(a_shift + b_shift, 8) + small_early
    n0, pn = iota((128, 384), 1), iota((128, 384), 0)
    qk_at = (n0 // 128) * 1024 + 128 * j + (n0 & 127) - 16 * pn
    v_at = 128 * j + (n0 & 127) - 8 * pn
    owns = ((n0 < 256) & (qk_at >= 0) & (qk_at < 16)) | ((n0 >= 256) & (v_at >= 0) & (v_at < 8))
    nt, ln = iota((384, 128), 0), iota((384, 128), 1)
    lane = jnp.where(nt < 256, 24 + (nt & 15), 40 + (nt & 7))
    b = jnp.where(ln == lane, jnp.broadcast_to(a_bq + b_bq, (384, 128)), 0.0).astype(low)
    small = small + dot(owns.astype(full).astype(low), b, 1, 0)
    head_row = (dt == 8 * lt).astype(full).astype(low)
    pad = dot(head_row, small.astype(low), 1, 0)
    left = gq[:256].T
    right = jnp.concatenate([gq[256:].T, pad], axis=1)
    GQ[...] = jnp.concatenate(
        [left.reshape(128, 8, 256), right.reshape(128, 8, 256)], axis=1
    ).astype(low).reshape(2, 4, 2, 8, 16, 256)
    c_q = first_unit(1, GQ)
    with jax.named_scope("hpair"):
        for n in (1, 2, 3):
            add_hp(n)

    def to_near(k, target, part, sem):
        zz = (z + k) % 4
        remote(TH.at[w, zz, part], zin.at[1, k, part], zzs.at[sem], zzr.at[sem], dev(s, y, xh, zz, w)).start()

    to_near(1, up, hi6, 2)
    to_near(3, down, lo6, 2)
    with jax.named_scope("hrelay"):
        drain(TH.at[0, 0], zzr.at[1])
    TH[w, up, 0:64] = (TH[w, up, 0:64].astype(full) + zin[1, 2, 0:64].astype(full)).astype(low)
    TH[w, down, 64:128] = (TH[w, down, 64:128].astype(full) + zin[1, 2, 64:128].astype(full)).astype(low)
    to_near(1, up, lo6, 3)
    to_near(3, down, hi6, 3)
    with jax.named_scope("zo"):
        drain(TO.at[0, pl.ds(0, 3)], zzr.at[0])
    t = add4(TO[w, z], zin[0, 1], zin[0, 2], zin[0, 3])
    OUT[0] = (mine_x + t + VEC[1:2, :]).astype(low)
    with jax.named_scope("gq1"):
        drain(F.at[:, pl.ds(0, 3)], g1r.at[1])
    gm[1, 0] = add4(GQ[:, y, :, 0:4], gi0[1, 1], gi0[1, 2], gi0[1, 3]).astype(low).reshape(4, 4, 16, 256)
    gm[1, 1] = add4(GQ[s, :, xh, 4:8], gi1[1, 1], gi1[1, 2], gi1[1, 3]).astype(low)

    def last_copy(k, q):
        xx, yy = (x + k) % 4, (y + k) % 4
        if q < 4:
            here, target = gm.at[1, 0, 2 * (xx % 2) + xx // 2, q], x_dev(xx, y, q // 2, q % 2)
        else:
            here, target = gm.at[1, 1, yy, q - 4], dev(s, yy, xh, q // 2, q % 2)
        return remote(here, QIN.at[k, j], us, ur, target)

    for q in (0, 4, 1, 5, 2, 6, 3, 7):
        for k in (1, 3, 2, 0):
            if k == 0:
                @pl.when(j != q)
                def _():
                    last_copy(k, q).start()

                @pl.when(j == q)
                def _():
                    here = gm.at[1, 0, 2 * s + xh, q] if q < 4 else gm.at[1, 1, y, q - 4]
                    local(here, QIN.at[0, j], ur)
                    local(here, spare5, us)
            else:
                last_copy(k, q).start()
    with jax.named_scope("go"):
        drain(fo_in, gor)
        t = lax.fori_loop(0, 16, lambda q, t: t + fo_in[q].astype(full), jnp.zeros((16, 512), full))
        GWO[:, :512] = t[:8]
        GWO[:, 512:] = t[8:]
    with jax.named_scope("zh"):
        drain(TH.at[0, 0], zzr.at[2])
        drain(TH.at[0, 0], zzr.at[3])
    gh = TH[w, z].astype(full) + zin[1, 1].astype(full) + zin[1, 3].astype(full)
    hat = cen * inv
    gx = gh * VEC[0:1, :]
    gx = gx - jnp.mean(gx, axis=-1, keepdims=True) - hat * jnp.mean(gx * hat, axis=-1, keepdims=True)
    TG[0] = (YY[w, z].astype(full) + inv * gx).astype(low)
    with jax.named_scope("lastf"):
        drain(RF, ttr)
    with jax.named_scope("last"):
        drain(QIN, ur)
    RQ[...] = add4(QIN[0], QIN[1], QIN[2], QIN[3]).astype(low)

    for e in range(2):
        for i in range(2):
            @pl.when(jnp.logical_not(head_target(e, i)[1]))
            def _():
                kv_copy(e, i).wait_send()
                q_copy(e, i).wait_send()
                do_copy(e, i).wait_send()

    for i in range(4):
        @pl.when(jnp.logical_not(at_home(i)))
        def _():
            remote(OB.at[i], RO.at[e_me, i_me], bs.at[i, 0], br.at[0, e_me, i_me], home(i)).wait_send()
            remote(DQB.at[i], RQ1.at[e_me, i_me], bs.at[i, 1], br.at[1, e_me, i_me], home(i)).wait_send()
            remote(summed.at[i], RKV.at[e_me, i_me], bs.at[i, 2], br2.at[e_me, i_me], home(i)).wait_send()
    for like, sem in (
        (QIN, ts), (QIN, us), (Fs, fs), (Fs, tts), (WO, os), (WO, gos),
        (QIN.at[pl.ds(0, 3)], f1s), (QIN.at[pl.ds(0, 3)], w1s),
        (QIN.at[pl.ds(0, 3)], g2s.at[0]), (QIN.at[pl.ds(0, 3)], g2s.at[2]),
        (F.at[:, pl.ds(0, 3)], q2s), (F.at[:, pl.ds(0, 3)], f2s), (F.at[:, pl.ds(0, 3)], w2s),
        (F.at[:, pl.ds(0, 3)], g1s.at[0]), (F.at[:, pl.ds(0, 3)], g1s.at[1]), (F.at[:, pl.ds(0, 3)], g1s.at[2]),
        (XX.at[0, pl.ds(0, 2)], zs.at[0]), (XX.at[0, 0], zs.at[1]),
        (YY.at[0, pl.ds(0, 3)], yps.at[0]), (XX.at[0, pl.ds(0, 2)], ys.at[0]), (XX.at[0, 0], ys.at[1]),
        (TO.at[0, pl.ds(0, 3)], zzs.at[0]), (TH.at[0, 0], zzs.at[1]), (TH.at[0, 0], zzs.at[2]), (TH.at[0, 0], zzs.at[3]),
    ):
        drain(like, sem)
    for cp in [xpair, ypair, swap, k0[1], k1[1], k2[1], k3[1], opair] + [cp for _, cp in hp]:
        cp.wait_send()


def layer(*args):
    S = pltpu.SemaphoreType.DMA
    V = pltpu.VMEM
    sds = jax.ShapeDtypeStruct
    return pl.pallas_call(
        layer_kernel,
        name="layer",
        out_shape=(
            V((1, 128, 1024), low),
            V((1, 128, 1024), low),
            V((8, 16, 256), low),
            V((8, 16, 256), low),
            V((32, 1024), full),
            V((8, 1024), full),
        ),
        in_specs=[pl.BlockSpec(memory_space=pltpu.SMEM), AN, AN] + [VM] * 6 + [AN] * 5,
        out_specs=(VM,) * 6,
        scratch_shapes=[
            V((1, 128, 1024), low),
            V((1, 128, 1024), low),
            V((8, 3072), full),
            V((8, 1024), full),
            V((8, 4096), full),
            V((32, 1024), full),
            V((4, 8, BLK), full),
            S((7,)),
            V((8, 128), full),
            V((2, 8, BLK), full),
            V((2, 4, 128, 512), full),
            V((2, 4, 128, 1024), low),
            V((2, 4, 128, 1024), low),
            V((2, 4, 128, 1024), low),
            V((2, 4, 128, 1024), low),
            V((2, 4, 128, 512), low),
            V((2, 4, 128, 512), low),
            V((1024, 512), low),
            V((2, 4, 2, 32, 1024), low),
            V((384, 1024), low),
            V((128, 1024), low),
            V((8, 1024), full),
            V((8, BLK), full),
            V((2, 4, 2, 64, BLK), low),
            V((4, 2, 64, BLK), low),
            V((2, 4, 2, 8, 16, 256), low),
            V((2, 4, 2, 8, 16, 256), low),
            V((8, 16, 256), low),
            V((8, 16, 256), low),
            V((16, 512), low),
            V((16, 16, 512), low),
            V((2, 2, 2, 2, 64, BLK), low),
            V((4, 64, BLK), full),
            V((4, 64, BLK), low),
            V((4, 1, BLK), full),
            V((4, 1, BLK), full),
            V((2, 2, 64, BLK), low),
            V((2, 2, 64, BLK), low),
            V((2, 2, 2, 64, BLK), low),
            V((2, 2, 64, BLK), full),
            V((4, 2, 64, BLK), full),
            V((4, 64, BLK), full),
            V((4, 64, BLK), low),
            V((4, 2, 64, BLK), low),
            V((4, 2, 64, BLK), low),
            V((4, 2, 64, BLK), low),
            V((2, BLK, 1024), full),
            V((2, 384, BLK), low),
            V((2, 4, 128, 1024), low),
            V((2, 4, 128, 1024), low),
            V((2, 4, 128, 1024), low),
            V((2, 4, 128, 1024), low),
            V((2, 4, 2, 8, 16, 256), low),
            V((2, 4, 2, 8, 16, 256), low),
            V((2, 4, 2, 32, 1024), low),
            V((2, 4, 2, 2, 4, 16, 256), low),
            V((2, 4, 4, 4, 16, 256), low),
            V((4, 2, 2, 32, 512), low),
            V((4, 4, 32, 512), low),
            V((2, 2, 4, 4, 16, 256), low),
            V((2, 4, 32, 512), low),
            V((2, 2, 4, 4, 16, 256), low),
            V((2, 4, 32, 512), low),
            V((8, 16, 256), low),
            V((4, 8, 16, 256), low),
            V((16, 16, 512), low),
            V((16, 16, 512), low),
            S((2,)), S((2,)), S((2,)), S((2,)), S((2,)), S((2,)), S((1,)), S((1,)), S, S, S, S, S, S, S, S, S, S, S, S, S, S, S, S,
            S((2, 2, 3)), S((4,)), S((4,)), S((4,)), S, S, S((4, 3)), S((2, 2, 2)), S((2, 2)), S((2,)), S((2,)),
            S((4,)), S((4,)), S((4,)), S((4,)), S, S, S((4,)), S((4,)), S((3,)), S((3,)), S((3,)), S((3,)), S, S,
            S, S, V((16, 256), low), V((16, 256), low), V((16, 512), low),
            V((16, 256), low), V((16, 256), low), V((16, 512), low),
        ],
        compiler_params=pltpu.CompilerParams(
            collective_id=0, has_side_effects=True, vmem_limit_bytes=62 << 20
        ),
    )(*args)


def finish_kernel(out, tg, RF, RQ, gfc2, gwo,
                  OUT, TG, GQKV, GFC1, GFC2, GWO, GG, GS, BQK, BV, BO, B1, B2):
    OUT[...] = out[...]
    TG[...] = tg[...]
    GFC2[...] = gfc2[...]
    GWO[...] = gwo[...]
    for rr in range(16):
        g = rr // 4
        c, half = g // 2, g % 2
        for hi in range(2):
            tiles = [RF[4 * hi + n, 8 * c:8 * c + 8, 128 * half:128 * half + 128].astype(full) for n in range(4)]
            col = 128 * (2 * rr + hi)
            GFC1[:, col:col + 128] = lane_mix(tiles, [32 * (n - rr % 4) for n in range(4)])
    tail = jnp.zeros((8, 128), full)
    for q in range(8):
        c = 128 * q
        GQKV[:, c:c + 128] = RQ[q, 0:8, 0:128].astype(full)
        GQKV[:, 1024 + c:1152 + c] = RQ[q, 0:8, 128:256].astype(full)
        GQKV[:, 2048 + c:2176 + c] = RQ[q, 8:16, 0:128].astype(full)
        tail = tail + RQ[q, 8:16, 128:256].astype(full)
    row = tail[0]
    GG[...] = row[0:8]
    GS[...] = row[8:16]
    BQK[...] = row[24:40]
    BV[...] = row[40:48]
    BO[...] = row[16:24]
    B1[...] = row[48:80]
    B2[...] = row[16:24]


def finish(*args):
    sds = jax.ShapeDtypeStruct
    return pl.pallas_call(
        finish_kernel,
        name="finish",
        out_shape=(
            sds((1, 128, 1024), low),
            sds((1, 128, 1024), low),
            sds((8, 3072), full),
            sds((8, 4096), full),
            sds((32, 1024), full),
            sds((8, 1024), full),
            sds((8,), full),
            sds((8,), full),
            sds((16,), full),
            sds((8,), full),
            sds((8,), full),
            sds((32,), full),
            sds((8,), full),
        ),
        in_specs=[VM] * 6,
        out_specs=(VM,) * 13,
    )(*args)


def shards(
    tokens, lengths, ln_gain, ln_bias, w_qkv, b_qkv, w_out, b_out, w_fc1, b_fc1, w_fc2, b_fc2, cotangent
):
    freq = rope_base ** (-2.0 * np.arange(8) / ROT)
    near = freq[:, None] * np.arange(BLK)[None, :]
    far = freq[:, None] * (BLK * np.arange(BLK))[None, :]
    turns = jnp.asarray(np.stack([np.cos(near), np.sin(near), np.cos(far), np.sin(far)]).astype(np.float32))
    parts = layer(
        lengths, tokens, cotangent, ln_gain, ln_bias, b_qkv, b_out, b_fc1, b_fc2, w_qkv, w_out, w_fc1, w_fc2, turns
    )
    OUT, TG, GQKV, GFC1, GFC2, GWO, GG, GS, BQK, BV, BO, B1, B2 = finish(*[pltpu.with_memory_space_constraint(a, pltpu.VMEM) for a in parts])
    return (OUT, TG, GG, GS, GQKV, BQK, BV, GWO, BO, GFC1, B1, GFC2, B2)


def solution(mesh):
    rows, tok, par, vec = (
        P(("slot", "wsh")), P(("slot", "wsh"), "ctx", None), P(("slot", "ctx", "wsh"), None), P(("slot", "ctx", "wsh"))
    )
    return jax.shard_map(
        shards,
        mesh=mesh,
        in_specs=(tok, rows, vec, vec, par, vec, par, vec, par, vec, par, vec, tok),
        out_specs=(tok, tok, vec, vec, par, vec, vec, par, vec, par, vec, par, vec),
        check_vma=False,
    )
```

```python
import functools

import jax
import jax.numpy as jnp
import numpy as np
from jax import lax
from jax.experimental import pallas as pl
from jax.experimental.pallas import tpu as pltpu
from jax.sharding import PartitionSpec as P

HEADS = 16
HD = 64
ROT = 16
HQ = 1024
D = 1024
FF = 4096
BLK = 512

norm_eps = 1e-05
rope_base = 10000.0
MESH = pl.DeviceIdType.MESH
low = jnp.bfloat16
full = jnp.float32
VM = pl.BlockSpec(memory_space=pltpu.VMEM)
AN = pl.BlockSpec(memory_space=pl.ANY)


def place():
    s = lax.axis_index("slot")
    c = lax.axis_index("ctx")
    w = lax.axis_index("wsh")
    return s, c // 8, (c // 4) % 2, c % 4, w


def dev(s, y, xh, z, w):
    return (s, y * 8 + xh * 4 + z, w)


def x_dev(x, y, z, w):
    return dev(x % 2, y, x // 2, z, w)


def signal(barrier, target):
    pl.semaphore_signal(barrier, inc=1, device_id=target, device_id_type=MESH)


def local(src, dst, sem):
    pltpu.make_async_copy(src, dst, sem).start()


def drain(like, sem):
    pltpu.make_async_copy(like, like, sem).wait()


def remote(src, dst, send, recv, target):
    return pltpu.make_async_remote_copy(
        src_ref=src, dst_ref=dst, send_sem=send, recv_sem=recv,
        device_id=target, device_id_type=MESH,
    )


def iota(shape, axis):
    return lax.broadcasted_iota(jnp.int32, shape, axis)


def dot(a, b, ca, cb):
    return lax.dot_general(a, b, (((ca,), (cb,)), ((), ())), preferred_element_type=full)


def core_of(m):
    return ((m + 1) // 2) % 2


def owner_lanes(params, width, lanes, step):
    f, l = iota((128, width), 1), iota((128, width), 0)
    pick = (l == lanes[0] + (f & (step - 1)))
    for other in lanes[1:]:
        pick = pick | (l == other + (f & (step - 1)))
    return dot(params, pick.astype(full).astype(low), 1, 0), f, l


def lane_mix(tiles, shifts):
    lane = iota((8, 128), 1)
    out = jnp.zeros((8, 128), full)
    for g in range(4):
        t = tiles[g]
        if shifts[g] % 128:
            t = pltpu.roll(t, shifts[g] % 128, 1)
        out = jnp.where((lane >= 32 * g) & (lane < 32 * g + 32), t, out)
    return out


def layer_kernel(
    lens, tok_in, cot_in, lg, lb, bq, bo, bf, bg, wq_in, wo_in, w1_in, w2_in, turns_in, OUT, TG, RF, RQ, GFC2, GWO, tok, cot, wq, wo, w1, w2, turns, fetch, PAD, ROPE, SL, XX, YY, HB, XH, GA, DU,
    W1, W2, WQT, WOF, VEC, VAL, KV, QD, Q, F, Qs, Fs, wos, WO, HT, OF, OB, LSE, DLT, RO, RQ1, RKV, acc,
    acc_own, dqa, DQB, other, got, summed, PH, DQ, TO, TH, pin, zin, GF, GQ, GW, gi0, gi1, wi0, wi1, gm, wm,
    gi2, wi2, Ff, QIN, GO, fo_in, zs, zr, ys, yr, ps, pr, yps, ypr, ts, tr, fs, fr, os, orr, q2s, q2r, f1s, f1r,
    f2s, f2r, w1s, w1r, w2s, w2r, hs, kr, qr, dr, ks, krp, bs, br, br2, pps, ppr, hps, hpr, kss, ksr, gos, gor, zzs, zzr,
    g1s, g1r, g2s, g2r, tts, ttr, us, ur, spare, spare2, spare3, spare4, spare5, spare6,
):
    fetches = [
        pltpu.make_async_copy(a, b, fetch.at[n])
        for n, (a, b) in enumerate(
            ((wq_in, wq), (tok_in, tok), (w2_in, w2), (w1_in, w1), (wo_in, wo), (cot_in, cot), (turns_in, turns))
        )
    ]
    for cp in fetches:
        cp.start()
    s, y, xh, z, w = place()
    x = xh * 2 + s
    r = s * 8 + y * 2 + xh
    j = z * 2 + w
    jo = r // 2
    m = y * 2 + xh
    core, spot = core_of(m), m // 2
    keep = (j == jo).astype(jnp.int32)
    mine = ((y % 2 == w) & (core == w)).astype(jnp.int32)
    sib = dev(s, y, xh, z, 1 - w)

    lo4, hi4 = pl.ds(0, 4), pl.ds(4, 4)
    lo5, hi5 = pl.ds(0, 512), pl.ds(512, 512)
    half = z // 2
    flip = 1 - half

    def ahead(k, q):
        return x_dev((x + k * flip) % 4, (y + k * half) % 4, q // 2, q % 2)

    def behind(k, q):
        if q < 4:
            return x_dev((x + 4 - k) % 4, y, q // 2, q % 2)
        return dev(s, (y + 4 - k) % 4, xh, q // 2, q % 2)

    barrier = pltpu.get_barrier_semaphore()
    for k in range(4):
        for q in range(8):
            if k == 0:
                @pl.when(j != q)
                def _():
                    signal(barrier, behind(k, q))
            else:
                signal(barrier, behind(k, q))
    for k in range(1, 4):
        signal(barrier, x_dev((x + k) % 4, y, z, w))
        signal(barrier, dev(s, (y + k) % 4, xh, z, w))

    def wo_source(k):
        rr = 2 * j + k // 8
        return rr // 8, (rr // 2) % 4, rr % 2, (k % 8) // 2, k % 2

    def wo_mine(k):
        ss, sy, sxh, sz, sw = wo_source(k)
        return (ss == s) & (sy == y) & (sxh == xh) & (sz == z) & (sw == w)

    def source(i):
        return dev(s, i, (i + w) % 2, z, y % 2)

    def my_source(i):
        return (y == i) & (xh == (i + w) % 2) & (w == y % 2)

    def sender(q):
        return dev(q // 8, (q // 2) % 4, q % 2, jo // 2, jo % 2)

    def home(i):
        return dev(s, i, (i + w) % 2, z, y % 2)

    def at_home(i):
        return (y == i) & (xh == (i + w) % 2) & (w == y % 2)

    def head_at(e, i):
        return dev(s, 2 * e + w, i, z, core)

    def head_here(e, i):
        return (y == 2 * e + w) & (xh == i) & (core == w)

    e_me, i_me = y // 2, xh
    for cp in fetches:
        cp.wait()
    XX[w, z] = tok[0]
    first_row = iota((8, 128), 0)
    PAD[...] = jnp.zeros_like(PAD)
    PAD[0:1, 0:8] = lg[...].reshape(1, 8)
    PAD[1:2, 0:8] = lb[...].reshape(1, 8)
    PAD[2:3, 0:24] = bq[...].reshape(1, 24)
    PAD[3:4, 0:8] = bo[...].reshape(1, 8)
    PAD[4:5, 0:32] = bf[...].reshape(1, 32)
    PAD[5:6, 0:8] = bg[...].reshape(1, 8)
    lane8 = iota((8, 128), 1)
    size = jnp.full((8, 128), lens[0], jnp.int32)
    padded = jnp.where(
        first_row == 6,
        jnp.where(lane8 == 0, (size >> 6).astype(full), jnp.where(lane8 == 1, (size & 63).astype(full), 0.0)),
        PAD[...],
    )
    for q in range(8):
        c = 128 * q
        top = jnp.concatenate([wq[:, c:c + 128], wq[:, 1024 + c:1152 + c]], axis=1)
        bot = jnp.concatenate([wq[:, 2048 + c:2176 + c], padded], axis=1)
        Qs[q] = jnp.concatenate([top, bot], axis=0).astype(low)

    W2[s, y, xh] = w2[...].astype(low)
    for q in range(8):
        tiles = []
        for g in range(4):
            parts = [w1[:, 128 * (2 * (4 * g + n) + q // 4):128 * (2 * (4 * g + n) + q // 4) + 128] for n in range(4)]
            tiles.append(lane_mix(parts, [32 * (n - q % 4) for n in range(4)]))
        top = jnp.concatenate(tiles[:2], axis=1)
        bot = jnp.concatenate(tiles[2:], axis=1)
        Fs[q] = jnp.concatenate([top, bot], axis=0).astype(low)

    def ring1(ref0, ref1, snd, rcv):
        for k in (1, 3, 2):
            cp = remote(ref0, ref0, snd, rcv, x_dev((x + k) % 4, y, z, w))
            cp.start()
            cp = remote(ref1, ref1, snd, rcv, dev(s, (y + k) % 4, xh, z, w))
            cp.start()

    def ring2(ref0, ref1, snd, rcv):
        for k in (1, 3, 2):
            cp = remote(ref0, ref0, snd, rcv, dev(s, (y + k) % 4, xh, z, w))
            cp.start()
            cp = remote(ref1, ref1, snd, rcv, x_dev((x + k) % 4, y, z, w))
            cp.start()

    def z_near(buf, snd, rcv):
        for k in (1, 3):
            cp = remote(buf.at[w, z], buf.at[w, z], snd.at[0], rcv.at[0], dev(s, y, xh, (z + k) % 4, w))
            cp.start()

    def z_far(buf, snd, rcv):
        up, down = (z + 1) % 4, (z + 3) % 4
        a = buf.at[w, down, pl.ds(0, 64)]
        b = buf.at[w, up, pl.ds(64, 64)]
        out = [
            remote(a, a, snd.at[1], rcv.at[1], dev(s, y, xh, up, w)),
            remote(b, b, snd.at[1], rcv.at[1], dev(s, y, xh, down, w)),
        ]
        for cp in out:
            cp.start()

    with jax.named_scope("barrier"):
        pl.semaphore_wait(barrier, 31 + 6)

    slot = (r % 2) * 8 + j
    for n in (1, 2, 3, 4, 5, 6, 7, 0):
        for k in (1, 3, 2, 0):
            if k == 0 and n == 0:
                continue
            q = (j + n) % 8
            remote(Qs.at[q], Q.at[s, y, xh, j], ts, tr, ahead(k, q)).start()
    for k in range(1, 8):
        q = (j + k) % 8
        remote(Fs.at[q], F.at[s, y, xh, j], fs, fr, dev(s, y, xh, q // 2, q % 2)).start()
    ring1(W2.at[s, y, xh, :, lo5], W2.at[s, y, xh, :, hi5], w1s, w1r)
    z_near(XX, zs, zr)
    local(Qs.at[j], Q.at[s, y, xh, j], tr)
    local(Qs.at[j], spare, ts)
    local(Fs.at[j], F.at[s, y, xh, j], fr)
    local(Fs.at[j], spare2, fs)

    row = iota((128, 1024), 0) + (m * BLK + z * 128)
    YY[w, z] = jnp.where(row < lens[0], cot[0].astype(full), 0.0).astype(low)
    wos[...] = jnp.concatenate([wo[:, :512], wo[:, 512:]], axis=0).astype(low)
    c0, s0 = turns[0], turns[1]
    at_m = iota((8, 128), 1) == m
    cm = jnp.sum(jnp.where(at_m, turns[2, :, :128], 0.0), axis=1, keepdims=True)
    sm = jnp.sum(jnp.where(at_m, turns[3, :, :128], 0.0), axis=1, keepdims=True)
    ROPE[0] = cm * c0 - sm * s0
    ROPE[1] = sm * c0 + cm * s0

    with jax.named_scope("units"):
        drain(QIN, tr)
    with jax.named_scope("tf"):
        drain(Fs, fr)
    ring1(F.at[s, y, xh, lo4], F.at[s, y, xh, hi4], f1s, f1r)
    ring2(Q.at[:, y, :, lo4], Q.at[s, :, xh, hi4], q2s, q2r)
    with jax.named_scope("g1"):
        drain(QIN.at[pl.ds(0, 3)], w1r)
    with jax.named_scope("f1"):
        drain(QIN.at[pl.ds(0, 3)], f1r)
    ring2(F.at[:, y, :, lo4], F.at[s, :, xh, hi4], f2s, f2r)
    ring2(W2.at[:, y, :, :, lo5], W2.at[s, :, xh, :, hi5], w2s, w2r)
    with jax.named_scope("xnear"):
        drain(XX.at[0, pl.ds(0, 2)], zr.at[0])
    z_far(XX, zs, zr)
    z_near(YY, ys, yr)
    for k in range(16):
        q = (r + k) % 16
        cp = remote(wos, WO.at[slot], os, orr, dev(q // 8, (q // 2) % 4, q % 2, jo // 2, jo % 2))
        if k == 0:
            @pl.when(j != jo)
            def _():
                cp.start()

            @pl.when(j == jo)
            def _():
                local(wos, WO.at[slot], orr)
                local(wos, spare3, os)
        else:
            cp.start()
    with jax.named_scope("x"):
        drain(XX.at[0, 0], zr.at[1])
    xpair = remote(XX.at[w], XX.at[w], ps.at[0], pr.at[0], sib)
    xpair.start()
    with jax.named_scope("ring2"):
        drain(Q.at[:, pl.ds(0, 3)], q2r)
    units = Q[...].reshape(128, 16, 256).astype(full)
    left = units[:, :8].reshape(1024, 256)
    right = units[:, 8:].reshape(1024, 256)
    WQT[0:256, :] = left.T.astype(low)
    WQT[256:384, :] = right[:, :128].T.astype(low)
    pads = right[:, 128:].astype(low)

    def params_of(i):
        pick = (iota((128, 1024), 1) == 8 * iota((128, 1024), 0) + i).astype(full).astype(low)
        return dot(pick, pads, 1, 0).astype(low)

    def row_of(i):
        t, f, l = owner_lanes(params_of(i), 1024, (0,), 8)
        return jnp.sum(jnp.where((f >= 8 * l) & (f < 8 * l + 8), t, 0.0), axis=0, keepdims=True)

    gain = row_of(0)
    shift = row_of(1)
    n0, p0 = iota((384, 128), 0), iota((384, 128), 1)
    n0 = (n0 // 128) * 1024 + 128 * j + (n0 & 127)
    at = n0 - 24 * p0
    inside = ((at >= 0) & (at < 24)).astype(full)
    t = dot(inside.astype(low), params_of(2), 1, 0)
    lane_want = jnp.sum(inside * at.astype(full), axis=1, keepdims=True)
    bias_q = jnp.sum(jnp.where(p0.astype(full) == lane_want, t, 0.0), axis=1, keepdims=True)
    co, si = ROPE[0], ROPE[1]

    def norm_slot(wi):
        def one(zi, carry):
            v = XX[wi, zi].astype(full)
            mean = jnp.mean(v, axis=-1, keepdims=True)
            c = v - mean
            var = jnp.mean(c * c, axis=-1, keepdims=True)
            h = c * lax.rsqrt(var + norm_eps)
            XH[wi, zi] = h.astype(low)
            HB[wi, zi] = (h * gain + shift).astype(low)
            return carry

        lax.fori_loop(0, 4, one, 0)

    def turn(v):
        a, b = v[0:8], v[8:16]
        return jnp.concatenate([a * co - b * si, b * co + a * si, v[16:]], axis=0)

    def qkv_slot(wi):
        t = dot(WQT[...], HB[wi].reshape(BLK, 1024), 1, 1) + bias_q
        for e in range(2):
            HT[e, wi, 0, 0] = turn(t[128 + 64 * e:192 + 64 * e]).astype(low)
            HT[e, wi, 0, 1] = t[256 + 64 * e:320 + 64 * e].astype(low)
            HT[e, wi, 1, 0] = (turn(t[64 * e:64 + 64 * e]).astype(low).astype(full) * 0.125).astype(low)

    def head_target(e, i):
        return dev(s, 2 * e + w, i, z, core), (y == 2 * e + w) & (xh == i) & (core == w)

    def kv_copy(e, i):
        return remote(HT.at[e, i, 0], KV.at[core, spot], hs.at[e, i, 0], kr.at[spot], head_target(e, i)[0])

    def q_copy(e, i):
        return remote(HT.at[e, i, 1, 0], QD.at[spot, 0], hs.at[e, i, 1], qr.at[spot], head_target(e, i)[0])

    def do_copy(e, i):
        return remote(HT.at[e, i, 1, 1], QD.at[spot, 1], hs.at[e, i, 2], dr.at[spot], head_target(e, i)[0])

    def send_qkv(i):
        for e in range(2):
            me = head_target(e, i)[1]

            @pl.when(jnp.logical_not(me))
            def _():
                kv_copy(e, i).start()
                q_copy(e, i).start()

            @pl.when(me)
            def _():
                KV[core, spot] = HT[e, i, 0]
                QD[spot, 0] = HT[e, i, 1, 0]

    def send_do(i):
        t = dot(WOF[...], YY[i].reshape(BLK, 1024), 1, 1)
        for e in range(2):
            HT[e, i, 1, 1] = t[64 * e:64 + 64 * e].astype(low)
            me = head_target(e, i)[1]

            @pl.when(jnp.logical_not(me))
            def _():
                do_copy(e, i).start()

            @pl.when(me)
            def _():
                QD[spot, 1] = HT[e, i, 1, 1]

    norm_slot(w)
    qkv_slot(w)
    send_qkv(w)
    xpair.wait_recv()
    norm_slot(1 - w)
    qkv_slot(1 - w)
    send_qkv(1 - w)

    with jax.named_scope("ynear"):
        drain(YY.at[0, pl.ds(0, 2)], yr.at[0])
    for k in (0, 1, 3):
        here = YY.at[w, (z + k) % 4]
        remote(here, here, yps.at[0], ypr.at[0], sib).start()
    z_far(YY, ys, yr)
    VEC[0:1, :] = gain
    VEC[1:2, :] = row_of(3) + row_of(5)
    t, f, l = owner_lanes(params_of(4), 512, (0,), 32)
    base = f - 4 * (l - j)
    bias_1 = jnp.sum(
        jnp.where((((l - j) & 7) == 0) & (base >= 0) & (base < 32), t, 0.0), axis=0, keepdims=True
    )
    lp, ll = iota((128, 128), 0), iota((128, 128), 1)
    tok_pos = (iota((1, BLK), 1) + m * BLK).astype(full)
    pf = params_of(6).astype(full)
    for i in range(2):
        here = lp == s * 64 + i
        size = jnp.sum(jnp.where(here & (ll == 0), pf, 0.0)) * 64.0 + jnp.sum(jnp.where(here & (ll == 1), pf, 0.0))
        VAL[i:i + 1, :] = jnp.where(tok_pos < size, 1.0, 0.0)

    with jax.named_scope("f2"):
        drain(F.at[:, pl.ds(0, 3)], f2r)
    units = F[...].reshape(128, 16, 256).astype(full)
    W1[:, :256] = units[:, :8].reshape(1024, 256).astype(low)
    W1[:, 256:] = units[:, 8:].reshape(1024, 256).astype(low)
    g0 = 0.7978845608028654

    def hidden_up(n, carry):
        wi, zi = n // 2, pl.ds(2 * (n % 2), 2)
        u = dot(HB[wi, zi].reshape(256, 1024), W1[...], 1, 0) + bias_1
        t = jnp.tanh(g0 * (u + 0.044715 * (u * u * u)))
        GA[wi, zi] = (0.5 * u * (1.0 + t)).astype(low).reshape(2, 128, 512)
        slope = 0.5 * (1.0 + t) + (0.5 * g0) * u * (1.0 - t * t) * (1.0 + (3.0 * 0.044715) * (u * u))
        SL[wi, zi] = slope.reshape(2, 128, 512)
        return carry

    with jax.named_scope("hidden_up"):
        lax.fori_loop(0, 4, hidden_up, 0)
    with jax.named_scope("w2"):
        drain(F.at[:, pl.ds(0, 3)], w2r)
    with jax.named_scope("dy"):
        drain(YY.at[0, 0], yr.at[1])
    ypair = remote(YY.at[w, (z + 2) % 4], YY.at[w, (z + 2) % 4], ps.at[1], pr.at[1], sib)
    ypair.start()

    def hidden_down(n, carry):
        wi, zi = jnp.where(n < 2, w, 1 - w), pl.ds(2 * (n % 2), 2)
        dg = dot(YY[wi, zi].reshape(256, 1024), W2[...].reshape(512, 1024), 1, 1)
        DU[wi, zi] = (dg.reshape(2, 128, 512) * SL[wi, zi]).astype(low)
        return carry

    with jax.named_scope("hidden_down"):
        lax.fori_loop(0, 2, hidden_down, 0)
        drain(YY.at[0, pl.ds(0, 3)], ypr.at[0])
        ypair.wait_recv()
        lax.fori_loop(2, 4, hidden_down, 0)
    with jax.named_scope("wgrads"):
        ga = GA[...].reshape(1024, 512)

        def first_w2(h):
            t = dot(ga, YY[:, :, :, 512 * h:512 * h + 512].reshape(1024, 512), 0, 0).astype(low)
            GW[:, :, :, :, 512 * h:512 * h + 512] = t.reshape(2, 4, 2, 32, 512)
            out = []
            for k in (1, 3, 2):
                yy, xx = (y + k) % 4, (x + k) % 4
                if h == 0:
                    cp = remote(GW.at[:, yy, :, :, lo5], wi0.at[k], g1s.at[2], g1r.at[2], dev(s, yy, xh, z, w))
                else:
                    cp = remote(GW.at[xx % 2, :, xx // 2, :, hi5], wi1.at[k], g1s.at[2], g1r.at[2], x_dev(xx, y, z, w))
                cp.start()
                out.append(cp)
            return out

        def first_unit(g, buf):
            out = []
            for k in (1, 3, 2):
                yy, xx = (y + k) % 4, (x + k) % 4
                cp = remote(buf.at[:, yy, :, lo4], gi0.at[g, k], g1s.at[g], g1r.at[g], dev(s, yy, xh, z, w))
                cp.start()
                out.append(cp)
                cp = remote(buf.at[xx % 2, :, xx // 2, hi4], gi1.at[g, k], g1s.at[g], g1r.at[g], x_dev(xx, y, z, w))
                cp.start()
                out.append(cp)
            return out

        def add4(a, b, c, d):
            return a.astype(full) + b.astype(full) + c.astype(full) + d.astype(full)

        def second_unit(g, buf):
            gm[g, 0] = add4(
                buf[:, y, :, 0:4], gi0[g, 1], gi0[g, 2], gi0[g, 3]
            ).astype(low).reshape(4, 4, 16, 256)
            gm[g, 1] = add4(
                buf[s, :, xh, 4:8], gi1[g, 1], gi1[g, 2], gi1[g, 3]
            ).astype(low)
            out = []
            for k in (1, 3, 2):
                yy, xx = (y + k) % 4, (x + k) % 4
                cp = remote(gm.at[g, 0, 2 * (xx % 2) + xx // 2], gi2.at[g, 0, k], g2s.at[g], g2r.at[g], x_dev(xx, y, z, w))
                cp.start()
                out.append(cp)
                cp = remote(gm.at[g, 1, yy], gi2.at[g, 1, k], g2s.at[g], g2r.at[g], dev(s, yy, xh, z, w))
                cp.start()
                out.append(cp)
            return out

        def second_w2():
            wm[0] = add4(GW[:, y, :, :, :512], wi0[1], wi0[2], wi0[3]).astype(low).reshape(4, 32, 512)
            wm[1] = add4(GW[s, :, xh, :, 512:], wi1[1], wi1[2], wi1[3]).astype(low)
            out = []
            for k in (1, 3, 2):
                yy, xx = (y + k) % 4, (x + k) % 4
                cp = remote(wm.at[0, 2 * (xx % 2) + xx // 2], wi2.at[0, k], g2s.at[2], g2r.at[2], x_dev(xx, y, z, w))
                cp.start()
                out.append(cp)
                cp = remote(wm.at[1, yy], wi2.at[1, k], g2s.at[2], g2r.at[2], dev(s, yy, xh, z, w))
                cp.start()
                out.append(cp)
            return out

        def last_unit(g, fin, got_units):
            fin[0:4] = add4(gm[g, 0, 2 * s + xh], gi2[g, 0, 1], gi2[g, 0, 2], gi2[g, 0, 3]).astype(low)
            fin[4:8] = add4(gm[g, 1, y], gi2[g, 1, 1], gi2[g, 1, 2], gi2[g, 1, 3]).astype(low)
            out = []
            for k in range(1, 8):
                q = (j + k) % 8
                cp = remote(fin.at[q], got_units.at[j], tts, ttr, dev(s, y, xh, q // 2, q % 2))
                cp.start()
                out.append(cp)
            local(fin.at[j], got_units.at[j], ttr)
            local(fin.at[j], spare4, tts)
            return out

        c_w2 = first_w2(0)
        c_w2 += first_w2(1)

    with jax.named_scope("wgrads1"):
        du = DU[...].reshape(1024, 512)
        for n in range(4):
            t = dot(HB[:, :, :, 256 * n:256 * n + 256].reshape(1024, 256), du, 0, 0)
            t = jnp.concatenate([t[:, :256].reshape(32, 8, 256), t[:, 256:].reshape(32, 8, 256)], axis=1)
            GF[n // 2, 2 * (n % 2):2 * (n % 2) + 2] = t.astype(low).reshape(2, 2, 8, 16, 256)
        gb1 = jnp.sum(du.astype(full), axis=0, keepdims=True)
        gb_out = jnp.sum(YY[w, z].astype(full), axis=0, keepdims=True)

    with jax.named_scope("kv"):
        for i in range(4):
            @pl.when(jnp.logical_not(my_source(i)))
            def _():
                remote(HT.at[0, 0, 0], KV.at[w, i], hs.at[0, 0, 0], kr.at[i], source(i)).wait_recv()

            remote(KV.at[w, i], KV.at[w, i], ks, krp, sib).start()
    swap = remote(KV.at[w], KV.at[w], ks, krp, sib)
    with jax.named_scope("do"):
        drain(WO, orr)
        units = WO[...].astype(full)
        WOF[:, :512] = units[:, :8].reshape(128, 512).astype(low)
        WOF[:, 512:] = units[:, 8:].reshape(128, 512).astype(low)
        send_do(w)
        send_do(1 - w)
    c_f = first_unit(0, GF)
    with jax.named_scope("q"):
        for i in range(4):
            @pl.when(jnp.logical_not(my_source(i)))
            def _():
                remote(HT.at[0, 0, 1, 0], QD.at[i, 0], hs.at[0, 0, 1], qr.at[i], source(i)).wait_recv()
    with jax.named_scope("kvswap"):
        swap.wait_recv()

    causal = iota((BLK, BLK), 0) <= iota((BLK, BLK), 1)

    def query_block(i, carry):
        q = QD[i, 0]

        def many(blocks, state):
            run_max, total, out = state
            scores = []
            for c, t, masked in blocks:
                sc = dot(KV[c, t, 0], q, 0, 0)
                scores.append(jnp.where(causal, sc, -1e30) if masked else sc)
            new_max = run_max
            for sc in scores:
                new_max = jnp.maximum(new_max, jnp.max(sc, axis=0, keepdims=True))
            fac = jnp.exp(run_max - new_max)
            total, out = total * fac, out * fac
            for (c, t, _), sc in zip(blocks, scores):
                pr = jnp.exp(sc - new_max)
                total = total + jnp.sum(pr, axis=0, keepdims=True)
                out = out + dot(KV[c, t, 1], pr.astype(low), 1, 0)
            return new_max, total, out

        def two(t):
            return [(0, t, False), (1, t, False)]

        state = (
            jnp.full((1, BLK), -1e30, full),
            jnp.zeros((1, BLK), full),
            jnp.zeros((HD, BLK), full),
        )
        state = lax.fori_loop(0, i // 2, lambda t, st: many(two(2 * t) + two(2 * t + 1), st), state)
        state = lax.fori_loop(2 * (i // 2), i, lambda t, st: many(two(t), st), state)

        def keep_state(state):
            run_max, total, out = state
            out = out / total
            OF[i] = out
            LSE[i] = run_max + jnp.log(total)
            OB[i] = out.astype(low)

        @pl.when((i + w) % 2 == 1)
        def _():
            keep_state(many([(1 - w, i, False), (w, i, True)], state))

        @pl.when((i + w) % 2 == 0)
        def _():
            keep_state(many([(w, i, True)], state))

        @pl.when(jnp.logical_not(at_home(i)))
        def _():
            remote(OB.at[i], RO.at[e_me, i_me], bs.at[i, 0], br.at[0, e_me, i_me], home(i)).start()

        @pl.when(at_home(i))
        def _():
            RO[e_me, i_me] = OB[i]

        return carry

    with jax.named_scope("forward"):
        lax.fori_loop(0, 4, query_block, 0)


    def mlp_parts(i, carry):
        PH[i] = dot(DU[i].reshape(BLK, 512), W1[...], 1, 1)
        return carry

    def wait_home(g, src, dst):
        for e in range(2):
            for i in range(2):
                @pl.when(jnp.logical_not(head_here(e, i)))
                def _():
                    remote(src.at[0], dst.at[e, i], bs.at[0, g], br.at[g, e, i], head_at(e, i)).wait_recv()

    for i in range(4):
        @pl.when(jnp.logical_not(my_source(i)))
        def _():
            remote(HT.at[0, 0, 1, 1], QD.at[i, 1], hs.at[0, 0, 2], dr.at[i], source(i)).wait_recv()
    for i in range(4):
        DLT[i] = jnp.sum(QD[i, 1].astype(full) * OF[i], axis=0, keepdims=True)
    dqa[...] = jnp.zeros_like(dqa)

    def pairs(t, i, blocks):
        q, do, lse, dlt = QD[i, 0], QD[i, 1], LSE[i], DLT[i]
        scores = [dot(KV[c, t, 0], q, 0, 0) for c, _ in blocks]
        dps = [dot(KV[c, t, 1], do, 0, 0) for c, _ in blocks]
        dq = dqa[i]
        for (c, masked), sc, dp in zip(blocks, scores, dps):
            pr = jnp.exp(sc - lse)
            if masked:
                pr = jnp.where(causal, pr, 0.0)
            ds = (pr * (dp - dlt)).astype(low)
            acc[c, 0] += dot(q, ds, 1, 1)
            acc[c, 1] += dot(do, pr.astype(low), 1, 1)
            dq = dq + dot(KV[c, t, 0], ds, 1, 0)
        dqa[i] = dq

    def kv_home(t):
        summed[t] = (acc_own[t] + got[t].astype(full)).astype(low)

        @pl.when(jnp.logical_not(at_home(t)))
        def _():
            remote(summed.at[t], RKV.at[e_me, i_me], bs.at[t, 2], br2.at[e_me, i_me], home(t)).start()

        @pl.when(at_home(t))
        def _():
            RKV[e_me, i_me] = summed[t]

    final = 2 * e_me + i_me

    def dq_home(t):
        DQB[t] = (dqa[t] * 0.125).astype(low)

        @pl.when(jnp.logical_not(at_home(t)))
        def _():
            remote(DQB.at[t], RQ1.at[e_me, i_me], bs.at[t, 1], br.at[1, e_me, i_me], home(t)).start()

        @pl.when(at_home(t))
        def _():
            RQ1[e_me, i_me] = DQB[t]

    def step(p, before=None):
        t = final if p == 3 else p + (p >= final).astype(jnp.int32)
        acc[...] = jnp.zeros_like(acc)

        def rest(i, carry):
            pairs(t, i, [(0, False), (1, False)])
            return carry

        some = jnp.minimum(t + 2, 4)
        lax.fori_loop(t + 1, some, rest, 0)
        if before is not None:
            before[1].wait_recv()
            kv_home(before[0])
        if p != 2:
            lax.fori_loop(some, 4, rest, 0)

        @pl.when((t + w) % 2 == 1)
        def _():
            pairs(t, t, [(1 - w, False), (w, True)])

        @pl.when((t + w) % 2 == 0)
        def _():
            pairs(t, t, [(w, True)])

        other[t] = acc[1 - w].astype(low)
        acc_own[t] = acc[w]
        cp = remote(other.at[t], got.at[t], kss.at[t], ksr.at[t], sib)
        cp.start()
        if p < 3:
            @pl.when(t < final)
            def _():
                dq_home(t)
        else:
            for n in range(4):
                @pl.when(n >= final)
                def _():
                    dq_home(n)
        return t, cp

    with jax.named_scope("step0"):
        k0 = step(0)
    with jax.named_scope("wf1"):
        drain(F.at[:, pl.ds(0, 3)], g1r.at[2])
        drain(F.at[:, pl.ds(0, 3)], g1r.at[0])
    d_w2 = second_w2()
    d_f = second_unit(0, GF)
    with jax.named_scope("ohome"):
        wait_home(0, OB, RO)

    def out_slot(i):
        ob = jnp.concatenate([RO[0, i], RO[1, i]], axis=0).astype(full)
        ob = (ob * VAL[pl.ds(i, 1), :]).astype(low)
        t = dot(ob, WOF[...], 0, 0) + dot(GA[i].reshape(BLK, 512), W2[...].reshape(512, 1024), 1, 0)
        TO[i] = t.astype(low).reshape(4, 128, 1024)
        return dot(ob, YY[i].reshape(BLK, 1024), 1, 0)

    g_wo = out_slot(1 - w)
    opair = remote(TO.at[1 - w], pin.at[0], pps.at[0], ppr.at[0], sib)
    opair.start()
    g_wo = g_wo + out_slot(w)
    GO[...] = jnp.concatenate(
        [g_wo[:, :512].reshape(16, 8, 512), g_wo[:, 512:].reshape(16, 8, 512)], axis=1
    ).astype(low)

    def owner(k):
        rr = 2 * j + k // 8
        return rr // 8, (rr // 2) % 4, rr % 2, (k % 8) // 2, k % 2

    def owner_copy(k):
        os_, oy, oxh, oz, ow = owner(k)
        me = (os_ == s) & (oy == y) & (oxh == xh) & (oz == z) & (ow == w)
        return remote(GO.at[k], fo_in.at[r], gos, gor, dev(os_, oy, oxh, oz, ow)), me

    for k in range(16):
        cp, me = owner_copy(k)

        @pl.when(jnp.logical_not(me))
        def _():
            cp.start()

        @pl.when(me)
        def _():
            local(GO.at[k], fo_in.at[r], gor)
            local(GO.at[k], spare6, gos)

    def pair_z(n, buf):
        def one(t, carry):
            buf[w, t] = (buf[w, t].astype(full) + pin[n, t].astype(full)).astype(low)
            return carry

        lax.fori_loop(0, 4, one, 0)
        out = []
        for k in (1, 3, 2):
            zz = (z + k) % 4
            cp = remote(buf.at[w, zz], zin.at[n, k], zzs.at[0], zzr.at[0], dev(s, y, xh, zz, w))
            cp.start()
            out.append(cp)
        return out

    with jax.named_scope("step1"):
        k1 = step(1, k0)
    with jax.named_scope("opair"):
        opair.wait_recv()
    zo = pair_z(0, TO)
    with jax.named_scope("step2"):
        k2 = step(2, k1)
    with jax.named_scope("step3"):
        k3 = step(3, k2)
    with jax.named_scope("k3"):
        k3[1].wait_recv()
    kv_home(k3[0])

    def turn_back(v):
        a, b = v[0:8], v[8:16]
        return jnp.concatenate([a * ROPE[0] + b * ROPE[1], b * ROPE[0] - a * ROPE[1], v[16:]], axis=0)

    def wait_kv():
        for e in range(2):
            for i in range(2):
                @pl.when(jnp.logical_not(head_here(e, i)))
                def _():
                    remote(summed.at[0], RKV.at[e, i], bs.at[0, 2], br2.at[e, i], head_at(e, i)).wait_recv()

    d0, p0 = iota((128, 1024), 1), iota((128, 1024), 0)
    block = (d0 >= 8 * p0) & (d0 < 8 * p0 + 8)
    dt, lt = iota((1024, 128), 0), iota((1024, 128), 1)

    def spread_row(v, lane):
        a = jnp.where(block, jnp.broadcast_to(v, (128, 1024)), 0.0).astype(low)
        return dot(a, (lt == lane + (dt & 7)).astype(full).astype(low), 1, 0)

    f0, pf = iota((128, 512), 1), iota((128, 512), 0)
    base = f0 - 4 * (pf - j)
    a = jnp.where(
        (((pf - j) & 7) == 0) & (base >= 0) & (base < 32), jnp.broadcast_to(gb1, (128, 512)), 0.0
    ).astype(low)
    ft, lf = iota((512, 128), 0), iota((512, 128), 1)
    small_early = spread_row(gb_out, 16) + dot(a, (lf == 48 + (ft & 31)).astype(full).astype(low), 1, 0)
    with jax.named_scope("fill"):
        lax.fori_loop(0, 2, mlp_parts, 0)
        with jax.named_scope("wf2"):
            drain(QIN.at[pl.ds(0, 3)], g2r.at[2])
            drain(QIN.at[pl.ds(0, 3)], g2r.at[0])
        GFC2[:, :512] = add4(wm[0, 2 * s + xh], wi2[0, 1], wi2[0, 2], wi2[0, 3])
        GFC2[:, 512:] = add4(wm[1, y], wi2[1, 1], wi2[1, 2], wi2[1, 3])
        t_f = last_unit(0, Ff, RF)
        mine_x = tok[0].astype(full)
        mean = jnp.mean(mine_x, axis=-1, keepdims=True)
        cen = mine_x - mean
        inv = lax.rsqrt(jnp.mean(cen * cen, axis=-1, keepdims=True) + norm_eps)
    with jax.named_scope("home"):
        wait_home(1, DQB, RQ1)
        wait_kv()

    def dh_slot(i):
        for e in range(2):
            DQ[i, 64 * e:64 * e + 64] = turn_back(RQ1[e, i].astype(full)).astype(low)
            DQ[i, 128 + 64 * e:192 + 64 * e] = turn_back(RKV[e, i, 0].astype(full)).astype(low)
            DQ[i, 256 + 64 * e:320 + 64 * e] = RKV[e, i, 1]
        t = dot(DQ[i], WQT[...], 0, 0) + PH[i]
        TH[i] = t.astype(low).reshape(4, 128, 1024)
        g_shift = jnp.sum(t, axis=0, keepdims=True)
        g_gain = jnp.sum(t * XH[i].reshape(BLK, 1024).astype(full), axis=0, keepdims=True)
        return g_shift, g_gain, jnp.sum(DQ[i].astype(full), axis=1, keepdims=True)

    a_shift, a_gain, a_bq = dh_slot(1 - w)
    hp = []
    for k in (2, 1, 3, 0):
        zz = (z + k) % 4
        cp = remote(TH.at[1 - w, zz], pin.at[1, zz], hps.at[k], hpr.at[k], sib)
        cp.start()
        hp.append((k, cp))
    b_shift, b_gain, b_bq = dh_slot(w)
    gq = dot(DQ[0], HB[0].reshape(BLK, 1024), 1, 0) + dot(DQ[1], HB[1].reshape(BLK, 1024), 1, 0)
    small = spread_row(a_gain + b_gain, 0) + spread_row(a_shift + b_shift, 8) + small_early
    n0, pn = iota((128, 384), 1), iota((128, 384), 0)
    qk_at = (n0 // 128) * 1024 + 128 * j + (n0 & 127) - 16 * pn
    v_at = 128 * j + (n0 & 127) - 8 * pn
    owns = ((n0 < 256) & (qk_at >= 0) & (qk_at < 16)) | ((n0 >= 256) & (v_at >= 0) & (v_at < 8))
    nt, ln = iota((384, 128), 0), iota((384, 128), 1)
    lane = jnp.where(nt < 256, 24 + (nt & 15), 40 + (nt & 7))
    b = jnp.where(ln == lane, jnp.broadcast_to(a_bq + b_bq, (384, 128)), 0.0).astype(low)
    small = small + dot(owns.astype(full).astype(low), b, 1, 0)
    head_row = (dt == 8 * lt).astype(full).astype(low)
    pad = dot(head_row, small.astype(low), 1, 0)
    left = gq[:256].T
    right = jnp.concatenate([gq[256:].T, pad], axis=1)
    GQ[...] = jnp.concatenate(
        [left.reshape(128, 8, 256), right.reshape(128, 8, 256)], axis=1
    ).astype(low).reshape(2, 4, 2, 8, 16, 256)
    c_q = first_unit(1, GQ)
    up, down, across = (z + 1) % 4, (z + 3) % 4, (z + 2) % 4

    def add_hp(n):
        k, cp = hp[n]
        zz = (z + k) % 4
        cp.wait_recv()
        TH[w, zz] = (TH[w, zz].astype(full) + pin[1, zz].astype(full)).astype(low)

    with jax.named_scope("hpfirst"):
        add_hp(0)
    lo6, hi6 = pl.ds(0, 64), pl.ds(64, 64)
    zh = [
        remote(TH.at[w, across, lo6], zin.at[1, 2, lo6], zzs.at[1], zzr.at[1], dev(s, y, xh, up, w)),
        remote(TH.at[w, across, hi6], zin.at[1, 2, hi6], zzs.at[1], zzr.at[1], dev(s, y, xh, down, w)),
    ]
    for cp in zh:
        cp.start()
    with jax.named_scope("hpair"):
        for n in (1, 2, 3):
            add_hp(n)

    def to_near(k, target, part, sem):
        zz = (z + k) % 4
        remote(TH.at[w, zz, part], zin.at[1, k, part], zzs.at[sem], zzr.at[sem], dev(s, y, xh, zz, w)).start()

    to_near(1, up, hi6, 2)
    to_near(3, down, lo6, 2)
    with jax.named_scope("hrelay"):
        drain(TH.at[0, 0], zzr.at[1])
    TH[w, up, 0:64] = (TH[w, up, 0:64].astype(full) + zin[1, 2, 0:64].astype(full)).astype(low)
    TH[w, down, 64:128] = (TH[w, down, 64:128].astype(full) + zin[1, 2, 64:128].astype(full)).astype(low)
    to_near(1, up, lo6, 3)
    to_near(3, down, hi6, 3)
    with jax.named_scope("zo"):
        drain(TO.at[0, pl.ds(0, 3)], zzr.at[0])
    t = add4(TO[w, z], zin[0, 1], zin[0, 2], zin[0, 3])
    OUT[0] = (mine_x + t + VEC[1:2, :]).astype(low)
    with jax.named_scope("gq1"):
        drain(F.at[:, pl.ds(0, 3)], g1r.at[1])
    gm[1, 0] = add4(GQ[:, y, :, 0:4], gi0[1, 1], gi0[1, 2], gi0[1, 3]).astype(low).reshape(4, 4, 16, 256)
    gm[1, 1] = add4(GQ[s, :, xh, 4:8], gi1[1, 1], gi1[1, 2], gi1[1, 3]).astype(low)

    def last_copy(k, q):
        xx, yy = (x + k) % 4, (y + k) % 4
        if q < 4:
            here, target = gm.at[1, 0, 2 * (xx % 2) + xx // 2, q], x_dev(xx, y, q // 2, q % 2)
        else:
            here, target = gm.at[1, 1, yy, q - 4], dev(s, yy, xh, q // 2, q % 2)
        return remote(here, QIN.at[k, j], us, ur, target)

    for q in (0, 4, 1, 5, 2, 6, 3, 7):
        for k in (1, 3, 2, 0):
            if k == 0:
                @pl.when(j != q)
                def _():
                    last_copy(k, q).start()

                @pl.when(j == q)
                def _():
                    here = gm.at[1, 0, 2 * s + xh, q] if q < 4 else gm.at[1, 1, y, q - 4]
                    local(here, QIN.at[0, j], ur)
                    local(here, spare5, us)
            else:
                last_copy(k, q).start()
    with jax.named_scope("go"):
        drain(fo_in, gor)
        t = lax.fori_loop(0, 16, lambda q, t: t + fo_in[q].astype(full), jnp.zeros((16, 512), full))
        GWO[:, :512] = t[:8]
        GWO[:, 512:] = t[8:]
    with jax.named_scope("zh"):
        drain(TH.at[0, 0], zzr.at[2])
        drain(TH.at[0, 0], zzr.at[3])
    gh = TH[w, z].astype(full) + zin[1, 1].astype(full) + zin[1, 3].astype(full)
    hat = cen * inv
    gx = gh * VEC[0:1, :]
    gx = gx - jnp.mean(gx, axis=-1, keepdims=True) - hat * jnp.mean(gx * hat, axis=-1, keepdims=True)
    TG[0] = (YY[w, z].astype(full) + inv * gx).astype(low)
    with jax.named_scope("lastf"):
        drain(RF, ttr)
    with jax.named_scope("last"):
        drain(QIN, ur)
    RQ[...] = add4(QIN[0], QIN[1], QIN[2], QIN[3]).astype(low)

    for e in range(2):
        for i in range(2):
            @pl.when(jnp.logical_not(head_target(e, i)[1]))
            def _():
                kv_copy(e, i).wait_send()
                q_copy(e, i).wait_send()
                do_copy(e, i).wait_send()

    for i in range(4):
        @pl.when(jnp.logical_not(at_home(i)))
        def _():
            remote(OB.at[i], RO.at[e_me, i_me], bs.at[i, 0], br.at[0, e_me, i_me], home(i)).wait_send()
            remote(DQB.at[i], RQ1.at[e_me, i_me], bs.at[i, 1], br.at[1, e_me, i_me], home(i)).wait_send()
            remote(summed.at[i], RKV.at[e_me, i_me], bs.at[i, 2], br2.at[e_me, i_me], home(i)).wait_send()
    for like, sem in (
        (QIN, ts), (QIN, us), (Fs, fs), (Fs, tts), (WO, os), (WO, gos),
        (QIN.at[pl.ds(0, 3)], f1s), (QIN.at[pl.ds(0, 3)], w1s),
        (QIN.at[pl.ds(0, 3)], g2s.at[0]), (QIN.at[pl.ds(0, 3)], g2s.at[2]),
        (F.at[:, pl.ds(0, 3)], q2s), (F.at[:, pl.ds(0, 3)], f2s), (F.at[:, pl.ds(0, 3)], w2s),
        (F.at[:, pl.ds(0, 3)], g1s.at[0]), (F.at[:, pl.ds(0, 3)], g1s.at[1]), (F.at[:, pl.ds(0, 3)], g1s.at[2]),
        (XX.at[0, pl.ds(0, 2)], zs.at[0]), (XX.at[0, 0], zs.at[1]),
        (YY.at[0, pl.ds(0, 3)], yps.at[0]), (XX.at[0, pl.ds(0, 2)], ys.at[0]), (XX.at[0, 0], ys.at[1]),
        (TO.at[0, pl.ds(0, 3)], zzs.at[0]), (TH.at[0, 0], zzs.at[1]), (TH.at[0, 0], zzs.at[2]), (TH.at[0, 0], zzs.at[3]),
    ):
        drain(like, sem)
    for cp in [xpair, ypair, swap, k0[1], k1[1], k2[1], k3[1], opair] + [cp for _, cp in hp]:
        cp.wait_send()


def layer(*args):
    S = pltpu.SemaphoreType.DMA
    V = pltpu.VMEM
    sds = jax.ShapeDtypeStruct
    return pl.pallas_call(
        layer_kernel,
        name="layer",
        out_shape=(
            V((1, 128, 1024), low),
            V((1, 128, 1024), low),
            V((8, 16, 256), low),
            V((8, 16, 256), low),
            V((32, 1024), full),
            V((8, 1024), full),
        ),
        in_specs=[pl.BlockSpec(memory_space=pltpu.SMEM), AN, AN] + [VM] * 6 + [AN] * 5,
        out_specs=(VM,) * 6,
        scratch_shapes=[
            V((1, 128, 1024), low),
            V((1, 128, 1024), low),
            V((8, 3072), full),
            V((8, 1024), full),
            V((8, 4096), full),
            V((32, 1024), full),
            V((4, 8, BLK), full),
            S((7,)),
            V((8, 128), full),
            V((2, 8, BLK), full),
            V((2, 4, 128, 512), full),
            V((2, 4, 128, 1024), low),
            V((2, 4, 128, 1024), low),
            V((2, 4, 128, 1024), low),
            V((2, 4, 128, 1024), low),
            V((2, 4, 128, 512), low),
            V((2, 4, 128, 512), low),
            V((1024, 512), low),
            V((2, 4, 2, 32, 1024), low),
            V((384, 1024), low),
            V((128, 1024), low),
            V((8, 1024), full),
            V((8, BLK), full),
            V((2, 4, 2, 64, BLK), low),
            V((4, 2, 64, BLK), low),
            V((2, 4, 2, 8, 16, 256), low),
            V((2, 4, 2, 8, 16, 256), low),
            V((8, 16, 256), low),
            V((8, 16, 256), low),
            V((16, 512), low),
            V((16, 16, 512), low),
            V((2, 2, 2, 2, 64, BLK), low),
            V((4, 64, BLK), full),
            V((4, 64, BLK), low),
            V((4, 1, BLK), full),
            V((4, 1, BLK), full),
            V((2, 2, 64, BLK), low),
            V((2, 2, 64, BLK), low),
            V((2, 2, 2, 64, BLK), low),
            V((2, 2, 64, BLK), full),
            V((4, 2, 64, BLK), full),
            V((4, 64, BLK), full),
            V((4, 64, BLK), low),
            V((4, 2, 64, BLK), low),
            V((4, 2, 64, BLK), low),
            V((4, 2, 64, BLK), low),
            V((2, BLK, 1024), full),
            V((2, 384, BLK), low),
            V((2, 4, 128, 1024), low),
            V((2, 4, 128, 1024), low),
            V((2, 4, 128, 1024), low),
            V((2, 4, 128, 1024), low),
            V((2, 4, 2, 8, 16, 256), low),
            V((2, 4, 2, 8, 16, 256), low),
            V((2, 4, 2, 32, 1024), low),
            V((2, 4, 2, 2, 4, 16, 256), low),
            V((2, 4, 4, 4, 16, 256), low),
            V((4, 2, 2, 32, 512), low),
            V((4, 4, 32, 512), low),
            V((2, 2, 4, 4, 16, 256), low),
            V((2, 4, 32, 512), low),
            V((2, 2, 4, 4, 16, 256), low),
            V((2, 4, 32, 512), low),
            V((8, 16, 256), low),
            V((4, 8, 16, 256), low),
            V((16, 16, 512), low),
            V((16, 16, 512), low),
            S((2,)), S((2,)), S((2,)), S((2,)), S((2,)), S((2,)), S((1,)), S((1,)), S, S, S, S, S, S, S, S, S, S, S, S, S, S, S, S,
            S((2, 2, 3)), S((4,)), S((4,)), S((4,)), S, S, S((4, 3)), S((2, 2, 2)), S((2, 2)), S((2,)), S((2,)),
            S((4,)), S((4,)), S((4,)), S((4,)), S, S, S((4,)), S((4,)), S((3,)), S((3,)), S((3,)), S((3,)), S, S,
            S, S, V((16, 256), low), V((16, 256), low), V((16, 512), low),
            V((16, 256), low), V((16, 256), low), V((16, 512), low),
        ],
        compiler_params=pltpu.CompilerParams(
            collective_id=0, has_side_effects=True, vmem_limit_bytes=62 << 20
        ),
    )(*args)


def finish_kernel(out, tg, RF, RQ, gfc2, gwo,
                  OUT, TG, GQKV, GFC1, GFC2, GWO, GG, GS, BQK, BV, BO, B1, B2):
    OUT[...] = out[...]
    TG[...] = tg[...]
    GFC2[...] = gfc2[...]
    GWO[...] = gwo[...]
    for rr in range(16):
        g = rr // 4
        c, half = g // 2, g % 2
        for hi in range(2):
            tiles = [RF[4 * hi + n, 8 * c:8 * c + 8, 128 * half:128 * half + 128].astype(full) for n in range(4)]
            col = 128 * (2 * rr + hi)
            GFC1[:, col:col + 128] = lane_mix(tiles, [32 * (n - rr % 4) for n in range(4)])
    tail = jnp.zeros((8, 128), full)
    for q in range(8):
        c = 128 * q
        GQKV[:, c:c + 128] = RQ[q, 0:8, 0:128].astype(full)
        GQKV[:, 1024 + c:1152 + c] = RQ[q, 0:8, 128:256].astype(full)
        GQKV[:, 2048 + c:2176 + c] = RQ[q, 8:16, 0:128].astype(full)
        tail = tail + RQ[q, 8:16, 128:256].astype(full)
    row = tail[0]
    GG[...] = row[0:8]
    GS[...] = row[8:16]
    BQK[...] = row[24:40]
    BV[...] = row[40:48]
    BO[...] = row[16:24]
    B1[...] = row[48:80]
    B2[...] = row[16:24]


def finish(*args):
    sds = jax.ShapeDtypeStruct
    return pl.pallas_call(
        finish_kernel,
        name="finish",
        out_shape=(
            sds((1, 128, 1024), low),
            sds((1, 128, 1024), low),
            sds((8, 3072), full),
            sds((8, 4096), full),
            sds((32, 1024), full),
            sds((8, 1024), full),
            sds((8,), full),
            sds((8,), full),
            sds((16,), full),
            sds((8,), full),
            sds((8,), full),
            sds((32,), full),
            sds((8,), full),
        ),
        in_specs=[VM] * 6,
        out_specs=(VM,) * 13,
    )(*args)


def shards(
    tokens, lengths, ln_gain, ln_bias, w_qkv, b_qkv, w_out, b_out, w_fc1, b_fc1, w_fc2, b_fc2, cotangent
):
    freq = rope_base ** (-2.0 * np.arange(8) / ROT)
    near = freq[:, None] * np.arange(BLK)[None, :]
    far = freq[:, None] * (BLK * np.arange(BLK))[None, :]
    turns = jnp.asarray(np.stack([np.cos(near), np.sin(near), np.cos(far), np.sin(far)]).astype(np.float32))
    parts = layer(
        lengths, tokens, cotangent, ln_gain, ln_bias, b_qkv, b_out, b_fc1, b_fc2, w_qkv, w_out, w_fc1, w_fc2, turns
    )
    OUT, TG, GQKV, GFC1, GFC2, GWO, GG, GS, BQK, BV, BO, B1, B2 = finish(*[pltpu.with_memory_space_constraint(a, pltpu.VMEM) for a in parts])
    return (OUT, TG, GG, GS, GQKV, BQK, BV, GWO, BO, GFC1, B1, GFC2, B2)


def solution(mesh):
    rows, tok, par, vec = (
        P(("slot", "wsh")), P(("slot", "wsh"), "ctx", None), P(("slot", "ctx", "wsh"), None), P(("slot", "ctx", "wsh"))
    )
    return jax.shard_map(
        shards,
        mesh=mesh,
        in_specs=(tok, rows, vec, vec, par, vec, par, vec, par, vec, par, vec, tok),
        out_specs=(tok, tok, vec, vec, par, vec, vec, par, vec, par, vec, par, vec),
        check_vma=False,
    )
```
